32 devices in a mesh: stream: 2 (over core), batch: 16 (over z, y, x).
Axes of the slice: x: 2, y: 2, z: 4, core: 2. Of those that a mesh axis runs over, the one named last changes fastest.
Arguments:
- inputs: bfloat16 [2, 16, 1024, 768], P('stream', 'batch'), may hold values from -6 to 6
- lengths: int32 [16], P('batch'), may hold values from 128 to 1024, as said below
- cotangent: bfloat16 [2, 16, 1024, 768], P('stream', 'batch'), may hold values from -6 to 6
- qkv_weight: bfloat16 [768, 2304], replicated, may hold values from -0.21875 to 0.21875
- out_weight: bfloat16 [768, 768], replicated, may hold values from -2 to 2
- up_weight: bfloat16 [768, 3072], replicated, may hold values from -0.21875 to 0.21875
- down_weight: bfloat16 [3072, 768], replicated, may hold values from -0.109375 to 0.109375
- attn_gain: float32 [768], replicated, may hold values from 0.5 to 1.5
- mlp_gain: float32 [768], replicated, may hold values from 0.5 to 1.5
Outputs:
- outputs: bfloat16 [2, 16, 1024, 768], P('stream', 'batch')
- input_grad: bfloat16 [2, 16, 1024, 768], P('stream', 'batch')
- qkv_grad: float32 [768, 2304], P(('stream', 'batch'))
- out_grad: float32 [768, 768], P(('stream', 'batch'))
- up_grad: float32 [768, 3072], P(None, ('stream', 'batch'))
- down_grad: float32 [3072, 768], P(('stream', 'batch'))
- attn_gain_grad: float32 [768], replicated
- mlp_gain_grad: float32 [768], replicated
- rms: float32 [3], replicated
The draws below stay inside these ranges and needn't reach their ends.
Inputs may be any that keep to these rules, and one draw needn't show every extreme that they name: `lengths`: each length is a multiple of 16; some row has length 1024.
All inputs are finite; a program needn't handle non-finite values.
Results may differ from the reference program's by a relative error of at most 0.014.
Values may be sent and summed in bfloat16 or wider, within the bound.
No kernel may reach another device: no remote copies, remote signals or barrier semaphores. Data moves between devices by JAX's collectives and lax.ppermute only.
A program may use at most 384 MiB of HBM per device.

```python
import jax
import jax.numpy as jnp
from jax import lax

D = 768
H = 12
HD = 64
FF = 3072
BLK = 16
SEQ = 1024
MINLEN = 128
ROWS_ALL = 16


def draw_lengths(key, part):
    first, second = jax.random.split(jax.random.fold_in(key, 11))
    blocks = jax.random.randint(first, (ROWS_ALL,), MINLEN // BLK, SEQ // BLK + 1)
    chosen = jax.random.randint(second, (), 0, ROWS_ALL)
    blocks = jnp.where(jnp.arange(ROWS_ALL) == chosen, SEQ // BLK, blocks)
    return (blocks * BLK).astype(jnp.int32)


def block_levels(own_key, shape, shards, smallest, top_value):
    loudness = 1.0
    for axis_at, parts in shards:
        heights = jax.random.uniform(jax.random.fold_in(jax.random.fold_in(own_key, 6), axis_at), (parts,), jnp.float32, smallest / len(shards), top_value / len(shards))
        loudness = loudness * jnp.repeat(jnp.exp(heights), shape[axis_at] // parts).reshape((-1,) + (1,) * (len(shape) - 1 - axis_at))
    return loudness


def gaussian(own_key, dims, spread, reach, cuts=(), kind=jnp.bfloat16):
    array = spread * jax.random.normal(own_key, dims, jnp.float32)
    if cuts:
        array = array * block_levels(own_key, dims, cuts, -0.22, 0.18)
    return jnp.clip(array, -reach, reach).astype(kind)


def setup_inputs(seed: int = 0) -> dict:
    key_list = jax.random.split(jax.random.key(seed), 10)
    inputs = gaussian(key_list[0], (2, ROWS_ALL, SEQ, D), 1.0, 6.0, ((0, 2), (1, 16)))
    lengths = draw_lengths(jax.random.fold_in(key_list[9], 71), 0)
    cotangent = gaussian(key_list[2], (2, ROWS_ALL, SEQ, D), 1.0, 6.0, ((0, 2), (1, 16)))
    qkv_weight = gaussian(key_list[3], (D, 3 * D), D ** -0.5, 0.21875)
    out_weight = gaussian(key_list[4], (D, D), 8 ** -0.5, 2.0)
    up_weight = gaussian(key_list[5], (D, FF), D ** -0.5, 0.21875)
    down_weight = gaussian(key_list[6], (FF, D), FF ** -0.5, 0.109375)
    attn_gain = jnp.clip(1.0 + 0.1 * jax.random.normal(key_list[7], (D,), jnp.float32), 0.5, 1.5)
    mlp_gain = jnp.clip(1.0 + 0.1 * jax.random.normal(key_list[8], (D,), jnp.float32), 0.5, 1.5)
    return dict(inputs=inputs, lengths=lengths, cotangent=cotangent, qkv_weight=qkv_weight, out_weight=out_weight, up_weight=up_weight, down_weight=down_weight, attn_gain=attn_gain, mlp_gain=mlp_gain)


EPS = 1e-06
HIGH = lax.Precision.HIGHEST

@jax.custom_vjp
def low(v):
    return lax.optimization_barrier(v.astype(jnp.bfloat16)).astype(jnp.float32)

@jax.custom_vjp
def low_back(v):
    return v

def low_keep(v):
    return (low(v), None)

def low_pass(kept, grad):
    return (grad,)

def back_keep(v):
    return (v, None)

def back_low(kept, grad):
    return (low(grad),)
low.defvjp(low_keep, low_pass)
low_back.defvjp(back_keep, back_low)

def rms_norm(value, gain):
    return value * lax.rsqrt(lax.optimization_barrier(jnp.mean(value * value, axis=-1, keepdims=True)) + EPS) * gain

def rotary_tables():
    half = HD // 2
    freqs = jnp.exp(-jnp.log(10000.0) * jnp.arange(half, dtype=jnp.float32) / half)
    angles = jnp.arange(SEQ, dtype=jnp.float32)[:, None] * freqs[None, :]
    return (jnp.cos(angles)[:, None, :], jnp.sin(angles)[:, None, :])

def rotate(t, cosine, sine):
    half = HD // 2
    first = t[..., :half]
    second = t[..., half:]
    return jnp.concatenate([first * cosine - second * sine, second * cosine + first * sine], axis=-1)

def project(x, gain, wqkv, cosine, sine):
    h = low(rms_norm(x, gain))
    qkv = low_back(jnp.dot(h, wqkv, precision=HIGH))
    query = qkv[:, :D].reshape(SEQ, H, HD)
    key = qkv[:, D:2 * D].reshape(SEQ, H, HD)
    value = qkv[:, 2 * D:].reshape(SEQ, H, HD)
    return (low(rotate(query, cosine, sine)), low(rotate(key, cosine, sine)), low(value))

def attention(query, keys, values, mask):
    raw = jnp.einsum('qhd,khd->hqk', query, keys, precision=HIGH) * HD ** (-0.5)
    scores = jnp.where(mask[None], low_back(raw), -1e+30)
    top = lax.optimization_barrier(jnp.max(scores, axis=-1, keepdims=True))
    expo = jnp.exp(scores - top)
    prob = low(expo / lax.optimization_barrier(jnp.sum(expo, axis=-1, keepdims=True)))
    out = jnp.einsum('hqk,khd->qhd', prob, values, precision=HIGH).reshape(SEQ, D)
    return low(low_back(out))

def row_layer(pair, length, wqkv, wo, w1, w2, g1, g2):
    cosine, sine = rotary_tables()
    position = jnp.arange(SEQ, dtype=jnp.int32)
    block = position // BLK
    valid = position < length
    qc, kc, vc = project(pair[0], g1, wqkv, cosine, sine)
    qn, kn, vn = project(pair[1], g1, wqkv, cosine, sine)
    clean_mask = (block[None, :] <= block[:, None]) & valid[None, :]
    noisy_own = (block[None, :] == block[:, None]) & valid[None, :]
    noisy_clean = (block[None, :] < block[:, None]) & valid[None, :]
    oc = attention(qc, kc, vc, clean_mask)
    on = attention(qn, jnp.concatenate([kn, kc], 0), jnp.concatenate([vn, vc], 0), jnp.concatenate([noisy_own, noisy_clean], 1))
    weight = valid.astype(jnp.float32)[:, None]
    results = []
    sums = jnp.zeros((3,), jnp.float32)
    for x, o in ((pair[0], oc), (pair[1], on)):
        branch = low_back(jnp.dot(o, wo, precision=HIGH))
        x2 = x + branch
        h2 = low(rms_norm(x2, g2))
        upper = low_back(jnp.dot(h2, w1, precision=HIGH))
        act = low(jax.nn.gelu(upper, approximate=True))
        mixed = low_back(jnp.dot(act, w2, precision=HIGH))
        results.append(x2 + mixed)
        sums = sums + jnp.stack([jnp.sum(weight * x * x), jnp.sum(weight * branch * branch), jnp.sum(weight * mixed * mixed)])
    return (jnp.stack(results), sums)

def reference(inputs, lengths, cotangent, qkv_weight, out_weight, up_weight, down_weight, attn_gain, mlp_gain):

    def forward(xs, wqkv, wo, w1, w2, g1, g2):

        def one_row(carry, item):
            pair, length = item
            ypair, sums = row_layer(pair, length, wqkv, wo, w1, w2, g1, g2)
            return (carry + sums, ypair)
        sums, ys = lax.scan(jax.checkpoint(one_row), jnp.zeros((3,), jnp.float32), (jnp.swapaxes(xs, 0, 1), lengths))
        return (jnp.swapaxes(ys, 0, 1), sums)
    ys, pullback, sums = jax.vjp(forward, inputs.astype(jnp.float32), qkv_weight.astype(jnp.float32), out_weight.astype(jnp.float32), up_weight.astype(jnp.float32), down_weight.astype(jnp.float32), attn_gain, mlp_gain, has_aux=True)
    grads = pullback(cotangent.astype(jnp.float32))
    count = 2.0 * jnp.sum(lengths).astype(jnp.float32)
    rms = jnp.sqrt(sums / (count * D))
    return (ys.astype(jnp.bfloat16), grads[0].astype(jnp.bfloat16), grads[1], grads[2], grads[3], grads[4], grads[5], grads[6], rms)
```

```python
import functools

import jax
import jax.numpy as jnp
import numpy as np
from jax import lax
from jax.experimental import pallas as pl
from jax.experimental.pallas import tpu as pltpu
from jax.sharding import PartitionSpec as P

f32 = jnp.float32
bf16 = jnp.bfloat16

HD = 64
BLK = 16
EPS = 1e-06
NEG = -1e30
PW = 2 * HD
T = 128
R = 256
FC = 256
SCALE = HD**-0.5
GROUPS = 3

SMEM = pl.BlockSpec(memory_space=pltpu.SMEM)


def params(mib):
    return pltpu.CompilerParams(vmem_limit_bytes=mib << 20)


def shape(dims, dtype):
    return jax.ShapeDtypeStruct(dims, dtype)


def nn(a, b):
    return jnp.dot(a, b, preferred_element_type=f32)


def nt(a, b):
    return lax.dot_general(a, b, (((1,), (1,)), ((), ())), preferred_element_type=f32)


def tn(a, b):
    return lax.dot_general(a, b, (((0,), (0,)), ((), ())), preferred_element_type=f32)


def whole(dims):
    return pl.BlockSpec(dims, lambda *_: (0,) * len(dims), pipeline_mode=pl.Buffered(1))


def inv_rms(v):
    return lax.rsqrt(jnp.mean(v * v, axis=-1, keepdims=True) + EPS)


def norm_back(v, gain, grad):
    r = inv_rms(v)
    unit = v * r
    scaled = grad * gain
    inner = jnp.mean(scaled * unit, axis=-1, keepdims=True)
    return r * (scaled - unit * inner), grad * unit


def rotary_tables(length):
    half = HD // 2
    freqs = np.exp(-np.log(10000.0) * np.arange(half) / half).astype(np.float32)
    angles = (np.arange(length, dtype=np.float32)[:, None] * freqs[None, :]).astype(np.float64)
    cosine, sine = np.cos(angles), np.sin(angles)
    zero = np.zeros_like(sine)
    pair = lambda a, b: np.concatenate([a, b, a, b], axis=1).astype(np.float32)
    return pair(cosine, cosine), pair(-sine, zero), pair(zero, sine)


def rotated(v, cosine, minus, plus, sign):
    outs = []
    for c in range(0, v.shape[1], PW):
        part = v[:, c : c + PW]
        ahead = pltpu.roll(part, PW - HD // 2, 1)
        behind = pltpu.roll(part, HD // 2, 1)
        outs.append(part * cosine + (ahead * minus + behind * plus) * sign)
    return jnp.concatenate(outs, axis=1)


def token_weight(start, length, rows):
    return lax.broadcasted_iota(jnp.int32, (rows, 1), 0) + start < length


def row_sum(v):
    return jnp.sum(v, axis=0, keepdims=True)


def project_kernel(info, x, gain, wq, wk, wv, cosine, minus, plus, q, k, v, h1t, sums):
    at = pl.program_id(0)

    @pl.when(at == 0)
    def _():
        sums[...] = jnp.zeros_like(sums)

    value = x[...].astype(f32)
    h1 = (value * inv_rms(value) * gain[...]).astype(bf16)
    tables = (cosine[...], minus[...], plus[...], 1.0)
    q[...] = rotated(nn(h1, wq[...]), *tables).astype(bf16)
    k[...] = rotated(nn(h1, wk[...]), *tables).astype(bf16)
    v[...] = nn(h1, wv[...]).astype(bf16)
    h1t[...] = h1.T
    weight = token_weight(at * R, info[1], R)
    sums[0:1, :] += row_sum(jnp.where(weight, value * value, 0.0))


def project(info, x, gain, weight, tables):
    seq, width = x.shape
    rows = pl.BlockSpec((R, width), lambda i: (i, 0))
    table = pl.BlockSpec((R, PW), lambda i: (i, 0))
    third = lambda c: pl.BlockSpec((width, width), lambda i: (0, c), pipeline_mode=pl.Buffered(1))
    return pl.pallas_call(
        project_kernel,
        grid=(seq // R,),
        in_specs=[SMEM, rows, whole((1, width)), third(0), third(1), third(2), table, table, table],
        out_specs=[rows, rows, rows, pl.BlockSpec((width, R), lambda i: (0, i)), whole((8, width))],
        out_shape=[shape((seq, width), bf16)] * 3 + [shape((width, seq), bf16), shape((8, width), f32)],
        compiler_params=params(40),
        cost_estimate=pl.CostEstimate(
            flops=2 * seq * width * 3 * width, bytes_accessed=12 * seq * width, transcendentals=0
        ),
        name="project",
    )(info, x, gain, weight, weight, weight, *tables)


def clean_kv_kernel(info, x, received, gain, wk, wv, cosine, minus, plus, k, v):
    value = jnp.where(info[0] == 1, received[...].astype(f32), x[...].astype(f32))
    h1 = (value * inv_rms(value) * gain[...]).astype(bf16)
    k[...] = rotated(nn(h1, wk[...]), cosine[...], minus[...], plus[...], 1.0).astype(bf16)
    v[...] = nn(h1, wv[...]).astype(bf16)


def clean_kv(info, x, received, gain, weight, tables):
    seq, width = x.shape
    rows = pl.BlockSpec((R, width), lambda i: (i, 0))
    table = pl.BlockSpec((R, PW), lambda i: (i, 0))
    third = lambda c: pl.BlockSpec((width, width), lambda i: (0, c), pipeline_mode=pl.Buffered(1))
    return pl.pallas_call(
        clean_kv_kernel,
        grid=(seq // R,),
        in_specs=[SMEM, rows, rows, whole((1, width)), third(1), third(2), table, table, table],
        out_specs=[rows, rows],
        out_shape=[shape((seq, width), bf16)] * 2,
        compiler_params=params(40),
        cost_estimate=pl.CostEstimate(
            flops=2 * seq * width * 2 * width, bytes_accessed=10 * seq * width, transcendentals=0
        ),
        name="clean_kv",
    )(info, x, received, gain, weight, weight, *tables)


def stacked(tile, low):
    zero = jnp.zeros_like(tile)
    return jnp.concatenate([jnp.where(low, tile, zero), jnp.where(low, zero, tile)], axis=0)


def unstacked(tile_t):
    half = lax.broadcasted_iota(jnp.int32, (PW, 1), 0) < HD
    return jnp.where(half, tile_t[:, :T], tile_t[:, T:])


def chunks_of(i):
    out, j = [], 0
    while j < i:
        n = 2 if i - j >= 2 else 1
        out.append((j * T, n * T))
        j += n
    return out


def edge_masks(noisy):
    row = lax.broadcasted_iota(jnp.int32, (T, 2 * T), 0) // BLK
    col = (lax.broadcasted_iota(jnp.int32, (T, 2 * T), 1) % T) // BLK
    own = jnp.logical_or(row == col, jnp.logical_and(row < col, noisy == 0))
    other = jnp.logical_and(row < col, noisy == 1)
    return own, other


def masked(s, start, length):
    pos = lax.broadcasted_iota(jnp.int32, s.shape, 0) + start
    return jnp.where(pos < length, s, NEG)


def over_rows(op, v):
    return op(v.reshape(v.shape[0] // 8, 8, v.shape[1]), axis=0)


def attend_kernel(info, q, ko, vo, kc, vc, o, o_t, lse, vo_t, vc_t, scores):
    noisy, length = info[0], info[1]
    seq = q.shape[0]
    low = lax.broadcasted_iota(jnp.int32, (1, PW), 1) < HD
    own_mask, other_mask = edge_masks(noisy)
    vo_t[...] = vo[...].T
    vc_t[...] = vc[...].T
    for i in range(seq // T):
        at = pl.ds(i * T, T)
        q2 = stacked(q[at, :] * bf16(SCALE), low)
        buf = scores.at[i % 2]
        edge = nt(jnp.concatenate([ko[at, :], kc[at, :]], 0), q2)
        own = masked(jnp.where(own_mask, edge[:T], NEG), i * T, length)
        other = masked(jnp.where(other_mask, edge[T:], NEG), i * T, length)
        buf[pl.ds(0, T), :] = own
        buf[pl.ds(T, T), :] = other
        top = over_rows(jnp.max, jnp.maximum(own, other))
        for start, size in chunks_of(i):
            s = masked(nt(kc[pl.ds(start, size), :], q2), start, length)
            buf[pl.ds(2 * T + start, size), :] = s
            top = jnp.maximum(top, over_rows(jnp.max, s))
        top = jnp.max(top, axis=0, keepdims=True)
        p = jnp.exp(buf[pl.ds(0, 2 * T), :] - top)
        total = over_rows(jnp.sum, p)
        acc = nn(jnp.concatenate([vo_t[:, at], vc_t[:, at]], 1), p.astype(bf16))
        for start, size in chunks_of(i):
            p = jnp.exp(buf[pl.ds(2 * T + start, size), :] - top)
            total = total + over_rows(jnp.sum, p)
            acc = acc + nn(vc_t[:, pl.ds(start, size)], p.astype(bf16))
        total = row_sum(total)
        lse[0, pl.ds(i, 1), :] = top + jnp.log(total)
        out_t = unstacked(acc / total)
        o_t[:, at] = out_t.astype(bf16)
        o[at, :] = out_t.T.astype(bf16)


def attend(info, q, ko, vo, kc, vc):
    seq, width = q.shape
    pairs = width // PW
    cols = pl.BlockSpec((seq, PW), lambda h: (0, h))
    rows = pl.BlockSpec((PW, seq), lambda h: (h, 0))
    return pl.pallas_call(
        attend_kernel,
        grid=(pairs,),
        in_specs=[SMEM] + [cols] * 5,
        out_specs=[cols, rows, pl.BlockSpec((1, seq // T, 2 * T), lambda h: (h, 0, 0))],
        out_shape=[shape((seq, width), bf16), shape((width, seq), bf16), shape((pairs, seq // T, 2 * T), f32)],
        scratch_shapes=[
            pltpu.VMEM((PW, seq), bf16),
            pltpu.VMEM((PW, seq), bf16),
            pltpu.VMEM((2, seq + T, 2 * T), f32),
        ],
        compiler_params=params(40),
        cost_estimate=pl.CostEstimate(
            flops=4 * seq * seq * width, bytes_accessed=14 * seq * width, transcendentals=seq * seq * 8
        ),
        name="attend",
    )(info, q, ko, vo, kc, vc)


def attend_back_kernel(
    info, q, ko, vo, kc, vc, o, do, lse, dq, dko, dvo, dkc, dvc, ko_t, kc_t, dk_acc, dv_acc
):
    noisy, length = info[0], info[1]
    seq = q.shape[0]
    low = lax.broadcasted_iota(jnp.int32, (1, PW), 1) < HD
    own_mask, other_mask = edge_masks(noisy)
    ko_t[...] = ko[...].T
    kc_t[...] = kc[...].T
    for i in range(seq // T):
        at = pl.ds(i * T, T)
        q2 = stacked(q[at, :] * bf16(SCALE), low)
        do2 = stacked(do[at, :], low)
        prod = (do[at, :].astype(f32) * o[at, :].astype(f32)).T
        delta = jnp.concatenate([row_sum(prod[:HD]), row_sum(prod[HD:])], 1)
        norm = lse[0, pl.ds(i, 1), :]
        s = nt(jnp.concatenate([ko[at, :], kc[at, :]], 0), q2)
        own = masked(jnp.where(own_mask, s[:T], NEG), i * T, length)
        other = masked(jnp.where(other_mask, s[T:], NEG), i * T, length)
        p = jnp.exp(jnp.concatenate([own, other], 0) - norm)
        dp = nt(jnp.concatenate([vo[at, :], vc[at, :]], 0), do2)
        ds = (p * (dp - delta)).astype(bf16)
        dv = nn(p.astype(bf16), do2)
        dk = nn(ds, q2)
        dvo[at, :] = dv[:T]
        dko[at, :] = dk[:T]
        dv_acc[at, :] = dv[T:]
        dk_acc[at, :] = dk[T:]
        dq_t = nn(jnp.concatenate([ko_t[:, at], kc_t[:, at]], 1), ds)
        for start, size in chunks_of(i):
            rows = pl.ds(start, size)
            p = jnp.exp(masked(nt(kc[rows, :], q2), start, length) - norm)
            ds = (p * (nt(vc[rows, :], do2) - delta)).astype(bf16)
            dv_acc[rows, :] += nn(p.astype(bf16), do2)
            dk_acc[rows, :] += nn(ds, q2)
            dq_t = dq_t + nn(kc_t[:, rows], ds)
        dq[at, :] = unstacked(dq_t).T * SCALE
    dkc[...] = dk_acc[...].astype(dkc.dtype)
    dvc[...] = dv_acc[...].astype(dvc.dtype)


def attend_back(info, q, ko, vo, kc, vc, o, do, lse):
    seq, width = q.shape
    pairs = width // PW
    cols = pl.BlockSpec((seq, PW), lambda h: (0, h))
    return pl.pallas_call(
        attend_back_kernel,
        grid=(pairs,),
        in_specs=[SMEM] + [cols] * 7 + [pl.BlockSpec((1, seq // T, 2 * T), lambda h: (h, 0, 0))],
        out_specs=[cols] * 5,
        out_shape=[shape((seq, width), f32)] * 3 + [shape((seq, width), bf16)] * 2,
        scratch_shapes=[pltpu.VMEM((PW, seq), bf16)] * 2 + [pltpu.VMEM((seq, PW), f32)] * 2,
        compiler_params=params(40),
        cost_estimate=pl.CostEstimate(
            flops=8 * seq * seq * width, bytes_accessed=30 * seq * width, transcendentals=seq * seq * 8
        ),
        name="attend_back",
    )(info, q, ko, vo, kc, vc, o, do, lse)


def join_kernel(info, x, o, wo, gain, x2, h2, sums):
    at = pl.program_id(0)

    @pl.when(at == 0)
    def _():
        sums[...] = jnp.zeros_like(sums)

    branch = nn(o[...], wo[...])
    value = x[...].astype(f32) + branch
    x2[...] = value
    h2[...] = (value * inv_rms(value) * gain[...]).astype(bf16)
    weight = token_weight(at * R, info[1], R)
    sums[0:1, :] += row_sum(jnp.where(weight, branch * branch, 0.0))


def join(info, x, o, weight, gain):
    seq, width = x.shape
    rows = pl.BlockSpec((R, width), lambda i: (i, 0))
    return pl.pallas_call(
        join_kernel,
        grid=(seq // R,),
        in_specs=[SMEM, rows, rows, whole((width, width)), whole((1, width))],
        out_specs=[rows, rows, whole((8, width))],
        out_shape=[shape((seq, width), f32), shape((seq, width), bf16), shape((8, width), f32)],
        compiler_params=params(40),
        cost_estimate=pl.CostEstimate(
            flops=2 * seq * width * width, bytes_accessed=10 * seq * width, transcendentals=0
        ),
        name="join",
    )(info, x, o, weight, gain)


C0 = 0.7978845608028654
C1 = C0 * 0.044715


def feed_kernel(first, at, h2, dm, w1, w2, m_in, dh_in, m, dh, g_up, g_down, act_s, du_s):
    step = pl.program_id(0)

    @pl.when(step == 0)
    def _():
        if first:
            m[...] = jnp.zeros_like(m)
            dh[...] = jnp.zeros_like(dh)
        else:
            m[...] = m_in[...]
            dh[...] = dh_in[...]

    for t in range(0, h2.shape[0], R):
        rows = pl.ds(t, R)
        u = nn(h2[rows, :], w1[...])
        da = nt(dm[rows, :], w2[...])
        sq = u * u
        half = 0.5 * jnp.tanh(u * (C0 + C1 * sq)) + 0.5
        act = (u * half).astype(bf16)
        slope = half + u * (2.0 * half * (1.0 - half)) * (C0 + 3.0 * C1 * sq)
        du = (da * slope).astype(bf16)
        act_s[rows, :] = act
        du_s[rows, :] = du
        m[rows, :] += nn(act, w2[...])
        dh[rows, :] += nt(du, w1[...])
    g_down[...] = tn(act_s[...], dm[...]).astype(bf16)
    g_up[...] = tn(du_s[...], h2[...]).astype(bf16)


def feed(first, part, h2, dm, w1, w2, m_in, dh_in):
    seq, width = h2.shape
    hidden = w1.shape[1] // 2
    steps = hidden // FC
    held = whole((seq, width))
    grads = pl.BlockSpec((FC, width), lambda c, at: (c, 0))
    carried = [pl.BlockSpec(memory_space=pl.ANY)] * 2 if first else [held] * 2
    return pl.pallas_call(
        functools.partial(feed_kernel, first),
        grid_spec=pltpu.PrefetchScalarGridSpec(
            num_scalar_prefetch=1,
            grid=(steps,),
            in_specs=[
                held,
                held,
                pl.BlockSpec((width, FC), lambda c, at: (0, at[0] * steps + c)),
                pl.BlockSpec((FC, width), lambda c, at: (at[0] * steps + c, 0)),
            ]
            + carried,
            out_specs=[held, held, grads, grads],
            scratch_shapes=[pltpu.VMEM((seq, FC), bf16)] * 2,
        ),
        out_shape=[shape((seq, width), f32)] * 2 + [shape((hidden, width), bf16)] * 2,
        compiler_params=params(56),
        cost_estimate=pl.CostEstimate(
            flops=12 * seq * width * hidden, bytes_accessed=24 * seq * width, transcendentals=seq * hidden
        ),
        name="feed",
    )(part, h2, dm, w1, w2, m_in, dh_in)


def middle_kernel(info, x2, m, dh, dy, o_t, wo, gain, out, dx2, do, g_send, g_keep, sums, acc):
    at = pl.program_id(0)

    @pl.when(at == 0)
    def _():
        sums[...] = jnp.zeros_like(sums)
        acc[...] = jnp.zeros_like(acc)

    value = x2[...]
    mixed = m[...]
    out[...] = (value + mixed).astype(bf16)
    weight = token_weight(at * R, info[1], R)
    sums[0:1, :] += row_sum(jnp.where(weight, mixed * mixed, 0.0))
    grad, gain_terms = norm_back(value, gain[...], dh[...])
    sums[1:2, :] += row_sum(gain_terms)
    grad = grad + dy[...].astype(f32)
    dx2[...] = grad
    da = grad.astype(bf16)
    do[...] = nt(da, wo[...]).astype(bf16)
    acc[...] += nn(o_t[...], da)

    @pl.when(at == pl.num_programs(0) - 1)
    def _():
        half = acc.shape[0] // 2
        mine = pl.multiple_of(info[0] * half, half)
        g_keep[...] = acc[pl.ds(mine, half), :].astype(bf16)
        g_send[...] = acc[pl.ds(half - mine, half), :].astype(bf16)


def middle(info, x2, m, dh, dy, o_t, weight, gain):
    seq, width = x2.shape
    rows = pl.BlockSpec((R, width), lambda i: (i, 0))
    half = whole((width // 2, width))
    return pl.pallas_call(
        middle_kernel,
        grid=(seq // R,),
        in_specs=[
            SMEM,
            rows,
            rows,
            rows,
            rows,
            pl.BlockSpec((width, R), lambda i: (0, i)),
            whole((width, width)),
            whole((1, width)),
        ],
        out_specs=[rows, rows, rows, half, half, whole((8, width))],
        out_shape=[shape((seq, width), bf16), shape((seq, width), f32), shape((seq, width), bf16)]
        + [shape((width // 2, width), bf16)] * 2
        + [shape((8, width), f32)],
        scratch_shapes=[pltpu.VMEM((width, width), f32)],
        compiler_params=params(40),
        cost_estimate=pl.CostEstimate(
            flops=4 * seq * width * width, bytes_accessed=26 * seq * width, transcendentals=0
        ),
        name="middle",
    )(info, x2, m, dh, dy, o_t, weight, gain)


def finish_kernel(
    info, x, dx2, dq, dko, dvo, dkc, dvc, rk, rv, cosine, minus, plus, h1t, wqkv, gain,
    dx, g_send, g_keep, sums, acc,
):
    at = pl.program_id(0)

    @pl.when(at == 0)
    def _():
        sums[...] = jnp.zeros_like(sums)
        acc[...] = jnp.zeros_like(acc)

    tables = (cosine[...], minus[...], plus[...], -1.0)
    clean = (1 - info[0]).astype(f32)
    total = lambda own, local, other: own[...] + clean * (local[...].astype(f32) + other[...].astype(f32))
    grads = jnp.concatenate(
        [
            rotated(dq[...], *tables).astype(bf16),
            rotated(total(dko, dkc, rk), *tables).astype(bf16),
            total(dvo, dvc, rv).astype(bf16),
        ],
        axis=1,
    )
    acc[...] += nn(h1t[...], grads)
    grad, gain_terms = norm_back(x[...].astype(f32), gain[...], nt(grads, wqkv[...]))
    sums[0:1, :] += row_sum(gain_terms)
    dx[...] = (dx2[...] + grad).astype(bf16)

    @pl.when(at == pl.num_programs(0) - 1)
    def _():
        half = acc.shape[0] // 2
        mine = pl.multiple_of(info[0] * half, half)
        g_keep[...] = acc[pl.ds(mine, half), :].astype(bf16)
        g_send[...] = acc[pl.ds(half - mine, half), :].astype(bf16)


def finish(info, x, dx2, dq, dko, dvo, dkc, dvc, rk, rv, tables, h1t, weight, gain):
    seq, width = x.shape
    wide = weight.shape[1]
    rows = pl.BlockSpec((R, width), lambda i: (i, 0))
    table = pl.BlockSpec((R, PW), lambda i: (i, 0))
    half = whole((width // 2, wide))
    return pl.pallas_call(
        finish_kernel,
        grid=(seq // R,),
        in_specs=[SMEM]
        + [rows] * 9
        + [table] * 3
        + [pl.BlockSpec((width, R), lambda i: (0, i)), whole((width, wide)), whole((1, width))],
        out_specs=[rows, half, half, whole((8, width))],
        out_shape=[shape((seq, width), bf16)]
        + [shape((width // 2, wide), bf16)] * 2
        + [shape((8, width), f32)],
        scratch_shapes=[pltpu.VMEM((width, wide), f32)],
        compiler_params=params(56),
        cost_estimate=pl.CostEstimate(
            flops=4 * seq * width * wide, bytes_accessed=40 * seq * width, transcendentals=0
        ),
        name="finish",
    )(info, x, dx2, dq, dko, dvo, dkc, dvc, rk, rv, *tables, h1t, weight, gain)


def bit_orders(count):
    bits = [1 << i for i in range(count.bit_length() - 1)]
    if len(bits) == 4:
        x, y, z, far = bits
        return [(x, y, z, far), (y, x, z, far), (z, x, far, y)]
    return [tuple(bits[g:] + bits[:g]) for g in range(GROUPS)]


def exchange(value, axis, bit):
    size = lax.axis_size(axis)
    return lax.ppermute(value, axis, [(i, i ^ bit) for i in range(size)])


def distance(order, place):
    out = 0
    for i, bit in enumerate(order):
        out = out + ((place >> (len(order) - 1 - i)) & 1) * bit
    return out


def start_kernel(arrays, me, *refs):
    ins = refs[: 2 * 2 * arrays * GROUPS]
    outs = refs[2 * 2 * arrays * GROUPS :]
    for g in range(GROUPS):
        for side in range(2):
            row = 0
            for a in range(arrays):
                base = ((g * 2 + side) * arrays + a) * 2
                kept, got = ins[base], ins[base + 1]
                size = kept.shape[1]
                total = kept[0].astype(f32) + got[0].astype(f32)
                outs[g * 2 + side][0, row : row + size, :] = total.astype(bf16)
                row += size


def start_sum(me, kept, got, views, orders):
    count = 1 << len(orders[0])
    half = count // 2
    specs, args, rows = [], [], 0
    for g, order in enumerate(orders):
        for side in range(2):
            for array, other, (block, place) in zip(kept, got, views, strict=True):
                index = lambda r, me, order=order, side=side, g=g, place=place: place(
                    me[0] ^ distance(order, r + side * half), g
                )
                specs += [pl.BlockSpec(block, index)] * 2
                args += [array, other]
    rows = sum(block[1] for block, _ in views)
    width = views[0][0][2]
    out = pl.BlockSpec((1, rows, width), lambda r, me: (r, 0, 0))
    outs = pl.pallas_call(
        functools.partial(start_kernel, len(kept)),
        grid_spec=pltpu.PrefetchScalarGridSpec(
            num_scalar_prefetch=1, grid=(half,), in_specs=specs, out_specs=[out] * (2 * GROUPS)
        ),
        out_shape=[shape((half, rows, width), bf16)] * (2 * GROUPS),
        cost_estimate=pl.CostEstimate(
            flops=0, bytes_accessed=6 * GROUPS * count * rows * width, transcendentals=0
        ),
        name="start_sum",
    )(me, *args)
    return outs[0::2], outs[1::2]


def step_kernel(*refs):
    for g in range(GROUPS):
        low, high, got_low, got_high = refs[4 * g : 4 * g + 4]
        keep, send = refs[4 * GROUPS + 2 * g : 4 * GROUPS + 2 * g + 2]
        keep[...] = (low[...].astype(f32) + got_low[...].astype(f32)).astype(bf16)
        send[...] = (high[...].astype(f32) + got_high[...].astype(f32)).astype(bf16)


def step_sum(kept, got):
    count, rows, width = kept[0].shape
    half = count // 2
    steps = min(half, 2)
    block = (half // steps, rows, width)
    low = pl.BlockSpec(block, lambda r: (r, 0, 0))
    high = pl.BlockSpec(block, lambda r: (r + steps, 0, 0))
    args = []
    for a, b in zip(kept, got, strict=True):
        args += [a, a, b, b]
    outs = pl.pallas_call(
        step_kernel,
        grid=(steps,),
        in_specs=[low, high, low, high] * GROUPS,
        out_specs=[low, low] * GROUPS,
        out_shape=[shape((half, rows, width), bf16)] * (2 * GROUPS),
        cost_estimate=pl.CostEstimate(
            flops=0, bytes_accessed=6 * GROUPS * count * rows * width, transcendentals=0
        ),
        name="step_sum",
    )(*args)
    return outs[0::2], outs[1::2]


def sum_parts(me, kept, got, views):
    orders = bit_orders(lax.axis_size("batch"))
    keep, send = start_sum(me, kept, got, views, orders)
    for i in range(len(orders[0])):
        got = [exchange(s, "batch", order[i]) for s, order in zip(send, orders, strict=True)]
        if i < len(orders[0]) - 1:
            keep, send = step_sum(keep, got)
    return [a[0].astype(f32) + b[0].astype(f32) for a, b in zip(keep, got, strict=True)]


def sum_all(value):
    value = value + exchange(value, "stream", 1)
    for order in bit_orders(lax.axis_size("batch"))[0]:
        value = value + exchange(value, "batch", order)
    return value


def on_device(
    inputs, lengths, cotangent, qkv_weight, out_weight, up_weight, down_weight, attn_gain, mlp_gain
):
    seq, width = inputs.shape[2:]
    x = inputs[0, 0]
    dy = cotangent[0, 0]
    count = lax.axis_size("batch")
    stream = lax.axis_index("stream").astype(jnp.int32)
    me = lax.axis_index("batch").astype(jnp.int32).reshape(1)
    info = jnp.stack([stream, lengths[0]])
    gain1, gain2 = attn_gain.reshape(1, width), mlp_gain.reshape(1, width)
    tables = [jnp.asarray(t) for t in rotary_tables(seq)]

    received = lax.ppermute(x, "stream", [(0, 1)])
    q, ko, vo, h1t, sums_x = project(info, x, gain1, qkv_weight, tables)
    kc, vc = clean_kv(info, x, received, gain1, qkv_weight, tables)
    o, o_t, lse = attend(info, q, ko, vo, kc, vc)
    x2, h2, sums_a = join(info, x, o, out_weight, gain2)

    part = stream.reshape(1)
    none = jnp.zeros((8, 128), f32)
    m, dh, up_send, down_send = feed(True, 1 - part, h2, dy, up_weight, down_weight, none, none)
    up_got, down_got = (exchange(a, "stream", 1) for a in (up_send, down_send))
    m, dh, up_keep, down_keep = feed(False, part, h2, dy, up_weight, down_weight, m, dh)
    outputs, dx2, do, out_send, out_keep, sums_m = middle(info, x2, m, dh, dy, o_t, out_weight, gain2)
    out_got = exchange(out_send, "stream", 1)

    def by_rows(array):
        return array.reshape(count * GROUPS, array.shape[0] // (count * GROUPS), width)

    def rows_view(array):
        return ((1, array.shape[0] // (count * GROUPS), width), lambda part, g: (part * GROUPS + g, 0, 0))

    kept = [down_keep, up_keep, out_keep]
    early = sum_parts(
        me,
        [by_rows(a) for a in kept],
        [by_rows(a) for a in (down_got, up_got, out_got)],
        [rows_view(a) for a in kept],
    )

    dq, dko, dvo, dkc, dvc = attend_back(info, q, ko, vo, kc, vc, o, do, lse)
    rk, rv = (lax.ppermute(a, "stream", [(1, 0)]) for a in (dkc, dvc))
    dx, qkv_send, qkv_keep, sums_h = finish(
        info, x, dx2, dq, dko, dvo, dkc, dvc, rk, rv, tables, h1t, qkv_weight, gain1
    )
    qkv_got = exchange(qkv_send, "stream", 1)
    tall = width // (2 * count)
    split = lambda a: a.reshape(count, tall, 3 * width)
    late = sum_parts(
        me, [split(qkv_keep)], [split(qkv_got)], [((1, tall, width), lambda part, g: (part, 0, g))]
    )
    small = jnp.concatenate(
        [
            sums_x[:1],
            sums_a[:1],
            sums_m[:2],
            sums_h[:1],
            jnp.full((1, width), lengths[0].astype(f32)),
            jnp.zeros((2, width), f32),
        ]
    )
    small = sum_all(small)

    tall = down_keep.shape[0] // (count * GROUPS)
    down_grad = jnp.concatenate([e[:tall] for e in early])
    up_grad = jnp.concatenate([e[tall : 2 * tall] for e in early]).T
    out_grad = jnp.concatenate([e[2 * tall :] for e in early])
    qkv_grad = jnp.concatenate(late, axis=1)
    squares = jnp.sum(small[jnp.array([0, 1, 2])], axis=1)
    rms = jnp.sqrt(squares / (small[5, 0] * width))
    return (
        outputs[None, None],
        dx[None, None],
        qkv_grad,
        out_grad,
        up_grad,
        down_grad,
        small[4],
        small[3],
        rms,
    )


def solution(mesh):
    rows = P("stream", "batch", None, None)
    both = ("stream", "batch")
    return jax.shard_map(
        on_device,
        mesh=mesh,
        in_specs=(rows, P("batch"), rows, P(), P(), P(), P(), P(), P()),
        out_specs=(rows, rows, P(both, None), P(both, None), P(None, both), P(both, None), P(), P(), P()),
        check_vma=False,
    )
```

```python
import functools

import jax
import jax.numpy as jnp
import numpy as np
from jax import lax
from jax.experimental import pallas as pl
from jax.experimental.pallas import tpu as pltpu
from jax.sharding import PartitionSpec as P

f32 = jnp.float32
bf16 = jnp.bfloat16

HD = 64
BLK = 16
EPS = 1e-06
NEG = -1e30
PW = 2 * HD
T = 128
R = 256
FC = 256
SCALE = HD**-0.5
PARTS = (3, 2, 1)
GROUPS = 3

SMEM = pl.BlockSpec(memory_space=pltpu.SMEM)


def params(mib):
    return pltpu.CompilerParams(vmem_limit_bytes=mib << 20)


def shape(dims, dtype):
    return jax.ShapeDtypeStruct(dims, dtype)


def nn(a, b):
    return jnp.dot(a, b, preferred_element_type=f32)


def nt(a, b):
    return lax.dot_general(a, b, (((1,), (1,)), ((), ())), preferred_element_type=f32)


def tn(a, b):
    return lax.dot_general(a, b, (((0,), (0,)), ((), ())), preferred_element_type=f32)


def whole(dims):
    return pl.BlockSpec(dims, lambda *_: (0,) * len(dims), pipeline_mode=pl.Buffered(1))


def inv_rms(v):
    return lax.rsqrt(jnp.mean(v * v, axis=-1, keepdims=True) + EPS)


def norm_back(v, gain, grad):
    r = inv_rms(v)
    unit = v * r
    scaled = grad * gain
    inner = jnp.mean(scaled * unit, axis=-1, keepdims=True)
    return r * (scaled - unit * inner), grad * unit


def rotary_tables(length):
    half = HD // 2
    freqs = np.exp(-np.log(10000.0) * np.arange(half) / half).astype(np.float32)
    angles = (np.arange(length, dtype=np.float32)[:, None] * freqs[None, :]).astype(np.float64)
    cosine, sine = np.cos(angles), np.sin(angles)
    zero = np.zeros_like(sine)
    pair = lambda a, b: np.concatenate([a, b, a, b], axis=1).astype(np.float32)
    return pair(cosine, cosine), pair(-sine, zero), pair(zero, sine)


def rotated(v, cosine, minus, plus, sign):
    outs = []
    for c in range(0, v.shape[1], PW):
        part = v[:, c : c + PW]
        ahead = pltpu.roll(part, PW - HD // 2, 1)
        behind = pltpu.roll(part, HD // 2, 1)
        outs.append(part * cosine + (ahead * minus + behind * plus) * sign)
    return jnp.concatenate(outs, axis=1)


def token_weight(start, length, rows):
    return lax.broadcasted_iota(jnp.int32, (rows, 1), 0) + start < length


def row_sum(v):
    return jnp.sum(v, axis=0, keepdims=True)


def project_kernel(info, x, gain, wq, wk, wv, cosine, minus, plus, q, k, v, h1t, sums):
    at = pl.program_id(0)

    @pl.when(at == 0)
    def _():
        sums[...] = jnp.zeros_like(sums)

    value = x[...].astype(f32)
    h1 = (value * inv_rms(value) * gain[...]).astype(bf16)
    tables = (cosine[...], minus[...], plus[...], 1.0)
    q[...] = rotated(nn(h1, wq[...]), *tables).astype(bf16)
    k[...] = rotated(nn(h1, wk[...]), *tables).astype(bf16)
    v[...] = nn(h1, wv[...]).astype(bf16)
    h1t[...] = h1.T
    weight = token_weight(at * R, info[1], R)
    sums[0:1, :] += row_sum(jnp.where(weight, value * value, 0.0))


def project(info, x, gain, weight, tables):
    seq, width = x.shape
    rows = pl.BlockSpec((R, width), lambda i: (i, 0))
    table = pl.BlockSpec((R, PW), lambda i: (i, 0))
    third = lambda c: pl.BlockSpec((width, width), lambda i: (0, c), pipeline_mode=pl.Buffered(1))
    return pl.pallas_call(
        project_kernel,
        grid=(seq // R,),
        in_specs=[SMEM, rows, whole((1, width)), third(0), third(1), third(2), table, table, table],
        out_specs=[rows, rows, rows, pl.BlockSpec((width, R), lambda i: (0, i)), whole((8, width))],
        out_shape=[shape((seq, width), bf16)] * 3 + [shape((width, seq), bf16), shape((8, width), f32)],
        compiler_params=params(40),
        cost_estimate=pl.CostEstimate(
            flops=2 * seq * width * 3 * width, bytes_accessed=12 * seq * width, transcendentals=0
        ),
        name="project",
    )(info, x, gain, weight, weight, weight, *tables)


def clean_kv_kernel(info, x, received, gain, wk, wv, cosine, minus, plus, k, v):
    value = jnp.where(info[0] == 1, received[...].astype(f32), x[...].astype(f32))
    h1 = (value * inv_rms(value) * gain[...]).astype(bf16)
    k[...] = rotated(nn(h1, wk[...]), cosine[...], minus[...], plus[...], 1.0).astype(bf16)
    v[...] = nn(h1, wv[...]).astype(bf16)


def clean_kv(info, x, received, gain, weight, tables):
    seq, width = x.shape
    rows = pl.BlockSpec((R, width), lambda i: (i, 0))
    table = pl.BlockSpec((R, PW), lambda i: (i, 0))
    third = lambda c: pl.BlockSpec((width, width), lambda i: (0, c), pipeline_mode=pl.Buffered(1))
    return pl.pallas_call(
        clean_kv_kernel,
        grid=(seq // R,),
        in_specs=[SMEM, rows, rows, whole((1, width)), third(1), third(2), table, table, table],
        out_specs=[rows, rows],
        out_shape=[shape((seq, width), bf16)] * 2,
        compiler_params=params(40),
        cost_estimate=pl.CostEstimate(
            flops=2 * seq * width * 2 * width, bytes_accessed=10 * seq * width, transcendentals=0
        ),
        name="clean_kv",
    )(info, x, received, gain, weight, weight, *tables)


def stacked(tile, low):
    zero = jnp.zeros_like(tile)
    return jnp.concatenate([jnp.where(low, tile, zero), jnp.where(low, zero, tile)], axis=0)


def unstacked(tile_t):
    half = lax.broadcasted_iota(jnp.int32, (PW, 1), 0) < HD
    return jnp.where(half, tile_t[:, :T], tile_t[:, T:])


def chunks_of(i):
    out, j = [], 0
    while j < i:
        n = 2 if i - j >= 2 else 1
        out.append((j * T, n * T))
        j += n
    return out


def edge_masks(noisy):
    row = lax.broadcasted_iota(jnp.int32, (T, 2 * T), 0) // BLK
    col = (lax.broadcasted_iota(jnp.int32, (T, 2 * T), 1) % T) // BLK
    own = jnp.logical_or(row == col, jnp.logical_and(row < col, noisy == 0))
    other = jnp.logical_and(row < col, noisy == 1)
    return own, other


def masked(s, start, length):
    pos = lax.broadcasted_iota(jnp.int32, s.shape, 0) + start
    return jnp.where(pos < length, s, NEG)


def over_rows(op, v):
    return op(v.reshape(v.shape[0] // 8, 8, v.shape[1]), axis=0)


def attend_kernel(info, q, ko, vo, kc, vc, o, o_t, lse, vo_t, vc_t, scores):
    noisy, length = info[0], info[1]
    seq = q.shape[0]
    low = lax.broadcasted_iota(jnp.int32, (1, PW), 1) < HD
    own_mask, other_mask = edge_masks(noisy)
    vo_t[...] = vo[...].T
    vc_t[...] = vc[...].T
    for i in range(seq // T):
        at = pl.ds(i * T, T)
        q2 = stacked(q[at, :] * bf16(SCALE), low)
        buf = scores.at[i % 2]
        edge = nt(jnp.concatenate([ko[at, :], kc[at, :]], 0), q2)
        own = masked(jnp.where(own_mask, edge[:T], NEG), i * T, length)
        other = masked(jnp.where(other_mask, edge[T:], NEG), i * T, length)
        buf[pl.ds(0, T), :] = own
        buf[pl.ds(T, T), :] = other
        top = over_rows(jnp.max, jnp.maximum(own, other))
        for start, size in chunks_of(i):
            s = masked(nt(kc[pl.ds(start, size), :], q2), start, length)
            buf[pl.ds(2 * T + start, size), :] = s
            top = jnp.maximum(top, over_rows(jnp.max, s))
        top = jnp.max(top, axis=0, keepdims=True)
        p = jnp.exp(buf[pl.ds(0, 2 * T), :] - top)
        total = over_rows(jnp.sum, p)
        acc = nn(jnp.concatenate([vo_t[:, at], vc_t[:, at]], 1), p.astype(bf16))
        for start, size in chunks_of(i):
            p = jnp.exp(buf[pl.ds(2 * T + start, size), :] - top)
            total = total + over_rows(jnp.sum, p)
            acc = acc + nn(vc_t[:, pl.ds(start, size)], p.astype(bf16))
        total = row_sum(total)
        lse[0, pl.ds(i, 1), :] = top + jnp.log(total)
        out_t = unstacked(acc / total)
        o_t[:, at] = out_t.astype(bf16)
        o[at, :] = out_t.T.astype(bf16)


def attend(info, q, ko, vo, kc, vc):
    seq, width = q.shape
    pairs = width // PW
    cols = pl.BlockSpec((seq, PW), lambda h: (0, h))
    rows = pl.BlockSpec((PW, seq), lambda h: (h, 0))
    return pl.pallas_call(
        attend_kernel,
        grid=(pairs,),
        in_specs=[SMEM] + [cols] * 5,
        out_specs=[cols, rows, pl.BlockSpec((1, seq // T, 2 * T), lambda h: (h, 0, 0))],
        out_shape=[shape((seq, width), bf16), shape((width, seq), bf16), shape((pairs, seq // T, 2 * T), f32)],
        scratch_shapes=[
            pltpu.VMEM((PW, seq), bf16),
            pltpu.VMEM((PW, seq), bf16),
            pltpu.VMEM((2, seq + T, 2 * T), f32),
        ],
        compiler_params=params(40),
        cost_estimate=pl.CostEstimate(
            flops=4 * seq * seq * width, bytes_accessed=14 * seq * width, transcendentals=seq * seq * 8
        ),
        name="attend",
    )(info, q, ko, vo, kc, vc)


def attend_back_kernel(
    info, q, ko, vo, kc, vc, o, do, lse, dq, dko, dvo, dkc, dvc, ko_t, kc_t, dk_acc, dv_acc
):
    noisy, length = info[0], info[1]
    seq = q.shape[0]
    low = lax.broadcasted_iota(jnp.int32, (1, PW), 1) < HD
    own_mask, other_mask = edge_masks(noisy)
    ko_t[...] = ko[...].T
    kc_t[...] = kc[...].T
    for i in range(seq // T):
        at = pl.ds(i * T, T)
        q2 = stacked(q[at, :] * bf16(SCALE), low)
        do2 = stacked(do[at, :], low)
        prod = (do[at, :].astype(f32) * o[at, :].astype(f32)).T
        delta = jnp.concatenate([row_sum(prod[:HD]), row_sum(prod[HD:])], 1)
        norm = lse[0, pl.ds(i, 1), :]
        s = nt(jnp.concatenate([ko[at, :], kc[at, :]], 0), q2)
        own = masked(jnp.where(own_mask, s[:T], NEG), i * T, length)
        other = masked(jnp.where(other_mask, s[T:], NEG), i * T, length)
        p = jnp.exp(jnp.concatenate([own, other], 0) - norm)
        dp = nt(jnp.concatenate([vo[at, :], vc[at, :]], 0), do2)
        ds = (p * (dp - delta)).astype(bf16)
        dv = nn(p.astype(bf16), do2)
        dk = nn(ds, q2)
        dvo[at, :] = dv[:T]
        dko[at, :] = dk[:T]
        dv_acc[at, :] = dv[T:]
        dk_acc[at, :] = dk[T:]
        dq_t = nn(jnp.concatenate([ko_t[:, at], kc_t[:, at]], 1), ds)
        for start, size in chunks_of(i):
            rows = pl.ds(start, size)
            p = jnp.exp(masked(nt(kc[rows, :], q2), start, length) - norm)
            ds = (p * (nt(vc[rows, :], do2) - delta)).astype(bf16)
            dv_acc[rows, :] += nn(p.astype(bf16), do2)
            dk_acc[rows, :] += nn(ds, q2)
            dq_t = dq_t + nn(kc_t[:, rows], ds)
        dq[at, :] = unstacked(dq_t).T * SCALE
    dkc[...] = dk_acc[...].astype(dkc.dtype)
    dvc[...] = dv_acc[...].astype(dvc.dtype)


def attend_back(info, first, pairs, q, ko, vo, kc, vc, o, do, lse):
    seq = q.shape[0]
    width = pairs * PW
    source = pl.BlockSpec((seq, PW), lambda h: (0, first + h))
    cols = pl.BlockSpec((seq, PW), lambda h: (0, h))
    return pl.pallas_call(
        attend_back_kernel,
        grid=(pairs,),
        in_specs=[SMEM] + [source] * 7 + [pl.BlockSpec((1, seq // T, 2 * T), lambda h: (first + h, 0, 0))],
        out_specs=[cols] * 5,
        out_shape=[shape((seq, width), f32)] * 3 + [shape((seq, width), bf16)] * 2,
        scratch_shapes=[pltpu.VMEM((PW, seq), bf16)] * 2 + [pltpu.VMEM((seq, PW), f32)] * 2,
        compiler_params=params(40),
        cost_estimate=pl.CostEstimate(
            flops=8 * seq * seq * width, bytes_accessed=30 * seq * width, transcendentals=seq * seq * 8
        ),
        name="attend_back",
    )(info, q, ko, vo, kc, vc, o, do, lse)


def join_kernel(info, x, o, wo, gain, x2, h2, sums):
    at = pl.program_id(0)

    @pl.when(at == 0)
    def _():
        sums[...] = jnp.zeros_like(sums)

    branch = nn(o[...], wo[...])
    value = x[...].astype(f32) + branch
    x2[...] = value
    h2[...] = (value * inv_rms(value) * gain[...]).astype(bf16)
    weight = token_weight(at * R, info[1], R)
    sums[0:1, :] += row_sum(jnp.where(weight, branch * branch, 0.0))


def join(info, x, o, weight, gain):
    seq, width = x.shape
    rows = pl.BlockSpec((R, width), lambda i: (i, 0))
    return pl.pallas_call(
        join_kernel,
        grid=(seq // R,),
        in_specs=[SMEM, rows, rows, whole((width, width)), whole((1, width))],
        out_specs=[rows, rows, whole((8, width))],
        out_shape=[shape((seq, width), f32), shape((seq, width), bf16), shape((8, width), f32)],
        compiler_params=params(40),
        cost_estimate=pl.CostEstimate(
            flops=2 * seq * width * width, bytes_accessed=10 * seq * width, transcendentals=0
        ),
        name="join",
    )(info, x, o, weight, gain)


C0 = 0.7978845608028654
C1 = C0 * 0.044715


def feed_kernel(first, at, h2, dm, w1, w2, m_in, dh_in, m, dh, g_up, g_down, act_s, du_s):
    step = pl.program_id(0)

    @pl.when(step == 0)
    def _():
        if first:
            m[...] = jnp.zeros_like(m)
            dh[...] = jnp.zeros_like(dh)
        else:
            m[...] = m_in[...]
            dh[...] = dh_in[...]

    for t in range(0, h2.shape[0], R):
        rows = pl.ds(t, R)
        u = nn(h2[rows, :], w1[...])
        da = nt(dm[rows, :], w2[...])
        sq = u * u
        half = 0.5 * jnp.tanh(u * (C0 + C1 * sq)) + 0.5
        act = (u * half).astype(bf16)
        slope = half + u * (2.0 * half * (1.0 - half)) * (C0 + 3.0 * C1 * sq)
        du = (da * slope).astype(bf16)
        act_s[rows, :] = act
        du_s[rows, :] = du
        m[rows, :] += nn(act, w2[...])
        dh[rows, :] += nt(du, w1[...])
    g_down[...] = tn(act_s[...], dm[...]).astype(bf16)
    g_up[...] = tn(du_s[...], h2[...]).astype(bf16)


def feed(first, part, h2, dm, w1, w2, m_in, dh_in):
    seq, width = h2.shape
    hidden = w1.shape[1] // 2
    steps = hidden // FC
    held = whole((seq, width))
    grads = pl.BlockSpec((FC, width), lambda c, at: (c, 0))
    carried = [pl.BlockSpec(memory_space=pl.ANY)] * 2 if first else [held] * 2
    return pl.pallas_call(
        functools.partial(feed_kernel, first),
        grid_spec=pltpu.PrefetchScalarGridSpec(
            num_scalar_prefetch=1,
            grid=(steps,),
            in_specs=[
                held,
                held,
                pl.BlockSpec((width, FC), lambda c, at: (0, at[0] * steps + c)),
                pl.BlockSpec((FC, width), lambda c, at: (at[0] * steps + c, 0)),
            ]
            + carried,
            out_specs=[held, held, grads, grads],
            scratch_shapes=[pltpu.VMEM((seq, FC), bf16)] * 2,
        ),
        out_shape=[shape((seq, width), f32)] * 2 + [shape((hidden, width), bf16)] * 2,
        compiler_params=params(56),
        cost_estimate=pl.CostEstimate(
            flops=12 * seq * width * hidden, bytes_accessed=24 * seq * width, transcendentals=seq * hidden
        ),
        name="feed",
    )(part, h2, dm, w1, w2, m_in, dh_in)


def middle_kernel(info, x2, m, dh, dy, o_t, wo, gain, out, dx2, do, g_send, g_keep, sums, acc):
    at = pl.program_id(0)

    @pl.when(at == 0)
    def _():
        sums[...] = jnp.zeros_like(sums)
        acc[...] = jnp.zeros_like(acc)

    value = x2[...]
    mixed = m[...]
    out[...] = (value + mixed).astype(bf16)
    weight = token_weight(at * R, info[1], R)
    sums[0:1, :] += row_sum(jnp.where(weight, mixed * mixed, 0.0))
    grad, gain_terms = norm_back(value, gain[...], dh[...])
    sums[1:2, :] += row_sum(gain_terms)
    grad = grad + dy[...].astype(f32)
    dx2[...] = grad
    da = grad.astype(bf16)
    do[...] = nt(da, wo[...]).astype(bf16)
    acc[...] += nn(o_t[...], da)

    @pl.when(at == pl.num_programs(0) - 1)
    def _():
        half = acc.shape[0] // 2
        mine = pl.multiple_of(info[0] * half, half)
        g_keep[...] = acc[pl.ds(mine, half), :].astype(bf16)
        g_send[...] = acc[pl.ds(half - mine, half), :].astype(bf16)


def middle(info, x2, m, dh, dy, o_t, weight, gain):
    seq, width = x2.shape
    rows = pl.BlockSpec((R, width), lambda i: (i, 0))
    half = whole((width // 2, width))
    return pl.pallas_call(
        middle_kernel,
        grid=(seq // R,),
        in_specs=[
            SMEM,
            rows,
            rows,
            rows,
            rows,
            pl.BlockSpec((width, R), lambda i: (0, i)),
            whole((width, width)),
            whole((1, width)),
        ],
        out_specs=[rows, rows, rows, half, half, whole((8, width))],
        out_shape=[shape((seq, width), bf16), shape((seq, width), f32), shape((seq, width), bf16)]
        + [shape((width // 2, width), bf16)] * 2
        + [shape((8, width), f32)],
        scratch_shapes=[pltpu.VMEM((width, width), f32)],
        compiler_params=params(40),
        cost_estimate=pl.CostEstimate(
            flops=4 * seq * width * width, bytes_accessed=26 * seq * width, transcendentals=0
        ),
        name="middle",
    )(info, x2, m, dh, dy, o_t, weight, gain)


def finish_kernel(info, x, dx2, cosine, minus, plus, h1t, wqkv, gain, *refs):
    at = pl.program_id(0)
    dx, g_send, g_keep, sums, acc = refs[-5:]
    pieces = refs[:-5]

    @pl.when(at == 0)
    def _():
        sums[...] = jnp.zeros_like(sums)
        acc[...] = jnp.zeros_like(acc)

    tables = (cosine[...], minus[...], plus[...], -1.0)
    clean = (1 - info[0]).astype(f32)
    dqs, dks, dvs = [], [], []
    for p in range(0, len(pieces), 7):
        dq, dko, dvo, dkc, dvc, rk, rv = (ref[...] for ref in pieces[p : p + 7])
        dk = dko + clean * (dkc.astype(f32) + rk.astype(f32))
        dv = dvo + clean * (dvc.astype(f32) + rv.astype(f32))
        dqs.append(rotated(dq, *tables).astype(bf16))
        dks.append(rotated(dk, *tables).astype(bf16))
        dvs.append(dv.astype(bf16))
    grads = jnp.concatenate(dqs + dks + dvs, axis=1)
    acc[...] += nn(h1t[...], grads)
    grad, gain_terms = norm_back(x[...].astype(f32), gain[...], nt(grads, wqkv[...]))
    sums[0:1, :] += row_sum(gain_terms)
    dx[...] = (dx2[...] + grad).astype(bf16)

    @pl.when(at == pl.num_programs(0) - 1)
    def _():
        half = acc.shape[0] // 2
        mine = pl.multiple_of(info[0] * half, half)
        g_keep[...] = acc[pl.ds(mine, half), :].astype(bf16)
        g_send[...] = acc[pl.ds(half - mine, half), :].astype(bf16)


def finish(info, x, dx2, pieces, tables, h1t, weight, gain):
    seq, width = x.shape
    wide = weight.shape[1]
    rows = pl.BlockSpec((R, width), lambda i: (i, 0))
    table = pl.BlockSpec((R, PW), lambda i: (i, 0))
    half = whole((width // 2, wide))
    return pl.pallas_call(
        finish_kernel,
        grid=(seq // R,),
        in_specs=[SMEM]
        + [rows] * 2
        + [table] * 3
        + [pl.BlockSpec((width, R), lambda i: (0, i)), whole((width, wide)), whole((1, width))]
        + [pl.BlockSpec((R, a.shape[1]), lambda i: (i, 0)) for piece in pieces for a in piece],
        out_specs=[rows, half, half, whole((8, width))],
        out_shape=[shape((seq, width), bf16)]
        + [shape((width // 2, wide), bf16)] * 2
        + [shape((8, width), f32)],
        scratch_shapes=[pltpu.VMEM((width, wide), f32)],
        compiler_params=params(56),
        cost_estimate=pl.CostEstimate(
            flops=4 * seq * width * wide, bytes_accessed=40 * seq * width, transcendentals=0
        ),
        name="finish",
    )(info, x, dx2, *tables, h1t, weight, gain, *(a for piece in pieces for a in piece))


def bit_orders(count):
    bits = [1 << i for i in range(count.bit_length() - 1)]
    if len(bits) == 4:
        x, y, z, far = bits
        return [(x, y, z, far), (y, x, z, far), (z, x, far, y)]
    return [tuple(bits[g:] + bits[:g]) for g in range(GROUPS)]


def exchange(value, axis, bit):
    size = lax.axis_size(axis)
    return lax.ppermute(value, axis, [(i, i ^ bit) for i in range(size)])


def distance(order, place):
    out = 0
    for i, bit in enumerate(order):
        out = out + ((place >> (len(order) - 1 - i)) & 1) * bit
    return out


def start_kernel(arrays, me, *refs):
    ins = refs[: 2 * 2 * arrays * GROUPS]
    outs = refs[2 * 2 * arrays * GROUPS :]
    for g in range(GROUPS):
        for side in range(2):
            row = 0
            for a in range(arrays):
                base = ((g * 2 + side) * arrays + a) * 2
                kept, got = ins[base], ins[base + 1]
                size = kept.shape[1]
                total = kept[0].astype(f32) + got[0].astype(f32)
                outs[g * 2 + side][0, row : row + size, :] = total.astype(bf16)
                row += size


def start_sum(me, kept, got, views, orders):
    count = 1 << len(orders[0])
    half = count // 2
    specs, args, rows = [], [], 0
    for g, order in enumerate(orders):
        for side in range(2):
            for array, other, (block, place) in zip(kept, got, views, strict=True):
                index = lambda r, me, order=order, side=side, g=g, place=place: place(
                    me[0] ^ distance(order, r + side * half), g
                )
                specs += [pl.BlockSpec(block, index)] * 2
                args += [array, other]
    rows = sum(block[1] for block, _ in views)
    width = views[0][0][2]
    out = pl.BlockSpec((1, rows, width), lambda r, me: (r, 0, 0))
    outs = pl.pallas_call(
        functools.partial(start_kernel, len(kept)),
        grid_spec=pltpu.PrefetchScalarGridSpec(
            num_scalar_prefetch=1, grid=(half,), in_specs=specs, out_specs=[out] * (2 * GROUPS)
        ),
        out_shape=[shape((half, rows, width), bf16)] * (2 * GROUPS),
        cost_estimate=pl.CostEstimate(
            flops=0, bytes_accessed=6 * GROUPS * count * rows * width, transcendentals=0
        ),
        name="start_sum",
    )(me, *args)
    return outs[0::2], outs[1::2]


def step_kernel(*refs):
    for g in range(GROUPS):
        low, high, got_low, got_high = refs[4 * g : 4 * g + 4]
        keep, send = refs[4 * GROUPS + 2 * g : 4 * GROUPS + 2 * g + 2]
        keep[...] = (low[...].astype(f32) + got_low[...].astype(f32)).astype(bf16)
        send[...] = (high[...].astype(f32) + got_high[...].astype(f32)).astype(bf16)


def step_sum(kept, got):
    count, rows, width = kept[0].shape
    half = count // 2
    steps = min(half, 2)
    block = (half // steps, rows, width)
    low = pl.BlockSpec(block, lambda r: (r, 0, 0))
    high = pl.BlockSpec(block, lambda r: (r + steps, 0, 0))
    args = []
    for a, b in zip(kept, got, strict=True):
        args += [a, a, b, b]
    outs = pl.pallas_call(
        step_kernel,
        grid=(steps,),
        in_specs=[low, high, low, high] * GROUPS,
        out_specs=[low, low] * GROUPS,
        out_shape=[shape((half, rows, width), bf16)] * (2 * GROUPS),
        cost_estimate=pl.CostEstimate(
            flops=0, bytes_accessed=6 * GROUPS * count * rows * width, transcendentals=0
        ),
        name="step_sum",
    )(*args)
    return outs[0::2], outs[1::2]


def after(value, *earlier):
    return lax.optimization_barrier((value, earlier))[0]


def sum_parts(me, kept, got, views):
    orders = bit_orders(lax.axis_size("batch"))
    keep, send = start_sum(me, kept, got, views, orders)
    for i in range(len(orders[0])):
        got = [exchange(s, "batch", order[i]) for s, order in zip(send, orders, strict=True)]
        earlier = yield send[0]
        if earlier is not None:
            keep = after(keep, earlier)
        if i < len(orders[0]) - 1:
            keep, send = step_sum(keep, got)
    yield [a[0].astype(f32) + b[0].astype(f32) for a, b in zip(keep, got, strict=True)]


def finished(steps, earlier):
    out = steps.send(earlier)
    while not isinstance(out, list):
        out = steps.send(None)
    return out


def sum_all(value):
    value = value + exchange(value, "stream", 1)
    for order in bit_orders(lax.axis_size("batch"))[0]:
        value = value + exchange(value, "batch", order)
    return value


def on_device(
    inputs, lengths, cotangent, qkv_weight, out_weight, up_weight, down_weight, attn_gain, mlp_gain
):
    seq, width = inputs.shape[2:]
    x = inputs[0, 0]
    dy = cotangent[0, 0]
    count = lax.axis_size("batch")
    stream = lax.axis_index("stream").astype(jnp.int32)
    me = lax.axis_index("batch").astype(jnp.int32).reshape(1)
    info = jnp.stack([stream, lengths[0]])
    gain1, gain2 = attn_gain.reshape(1, width), mlp_gain.reshape(1, width)
    tables = [jnp.asarray(t) for t in rotary_tables(seq)]

    received = lax.ppermute(x, "stream", [(0, 1)])
    q, ko, vo, h1t, sums_x = project(info, x, gain1, qkv_weight, tables)
    kc, vc = clean_kv(info, x, received, gain1, qkv_weight, tables)
    o, o_t, lse = attend(info, q, ko, vo, kc, vc)
    x2, h2, sums_a = join(info, x, o, out_weight, gain2)

    part = stream.reshape(1)
    none = jnp.zeros((8, 128), f32)
    m, dh, up_send, down_send = feed(True, 1 - part, h2, dy, up_weight, down_weight, none, none)
    up_got, down_got = (exchange(a, "stream", 1) for a in (up_send, down_send))
    m, dh, up_keep, down_keep = feed(False, part, h2, dy, up_weight, down_weight, m, dh)
    outputs, dx2, do, out_send, out_keep, sums_m = middle(info, x2, m, dh, dy, o_t, out_weight, gain2)
    out_got = exchange(out_send, "stream", 1)

    def by_rows(array):
        return array.reshape(count * GROUPS, array.shape[0] // (count * GROUPS), width)

    def rows_view(array):
        return ((1, array.shape[0] // (count * GROUPS), width), lambda part, g: (part * GROUPS + g, 0, 0))

    kept = [down_keep, up_keep, out_keep]
    early = sum_parts(
        me,
        [by_rows(a) for a in kept],
        [by_rows(a) for a in (down_got, up_got, out_got)],
        [rows_view(a) for a in kept],
    )

    pieces, first, token = [], 0, next(early)
    for pairs in PARTS:
        do = after(do, token)
        piece = attend_back(info, first, pairs, q, ko, vo, kc, vc, o, do, lse)
        pieces.append(list(piece) + [lax.ppermute(a, "stream", [(1, 0)]) for a in piece[3:]])
        first += pairs
        token = early.send(piece[0])
    dx, qkv_send, qkv_keep, sums_h = finish(
        info, x, after(dx2, token), pieces, tables, h1t, qkv_weight, gain1
    )
    early = finished(early, dx)
    qkv_got = exchange(qkv_send, "stream", 1)
    tall = width // (2 * count)
    split = lambda a: a.reshape(count, tall, 3 * width)
    late = sum_parts(
        me, [split(qkv_keep)], [split(qkv_got)], [((1, tall, width), lambda part, g: (part, 0, g))]
    )
    next(late)
    late = finished(late, None)
    small = jnp.concatenate(
        [
            sums_x[:1],
            sums_a[:1],
            sums_m[:2],
            sums_h[:1],
            jnp.full((1, width), lengths[0].astype(f32)),
            jnp.zeros((2, width), f32),
        ]
    )
    small = sum_all(small)

    tall = down_keep.shape[0] // (count * GROUPS)
    down_grad = jnp.concatenate([e[:tall] for e in early])
    up_grad = jnp.concatenate([e[tall : 2 * tall] for e in early]).T
    out_grad = jnp.concatenate([e[2 * tall :] for e in early])
    qkv_grad = jnp.concatenate(late, axis=1)
    squares = jnp.sum(small[jnp.array([0, 1, 2])], axis=1)
    rms = jnp.sqrt(squares / (small[5, 0] * width))
    return (
        outputs[None, None],
        dx[None, None],
        qkv_grad,
        out_grad,
        up_grad,
        down_grad,
        small[4],
        small[3],
        rms,
    )


def solution(mesh):
    rows = P("stream", "batch", None, None)
    both = ("stream", "batch")
    return jax.shard_map(
        on_device,
        mesh=mesh,
        in_specs=(rows, P("batch"), rows, P(), P(), P(), P(), P(), P()),
        out_specs=(rows, rows, P(both, None), P(both, None), P(None, both), P(both, None), P(), P(), P()),
        check_vma=False,
    )
```

```python
import functools

import jax
import jax.numpy as jnp
import numpy as np
from jax import lax
from jax.experimental import pallas as pl
from jax.experimental.pallas import tpu as pltpu
from jax.sharding import PartitionSpec as P

f32 = jnp.float32
bf16 = jnp.bfloat16

HD = 64
BLK = 16
EPS = 1e-06
NEG = -1e30
PW = 2 * HD
T = 128
R = 256
FC = 512
SCALE = HD**-0.5
BIG = 60
GROUPS = 3

SMEM = pl.BlockSpec(memory_space=pltpu.SMEM)


def params(mib):
    return pltpu.CompilerParams(vmem_limit_bytes=mib << 20)


def shape(dims, dtype):
    return jax.ShapeDtypeStruct(dims, dtype)


def nn(a, b):
    return jnp.dot(a, b, preferred_element_type=f32)


def nt(a, b):
    return lax.dot_general(a, b, (((1,), (1,)), ((), ())), preferred_element_type=f32)


def tn(a, b):
    return lax.dot_general(a, b, (((0,), (0,)), ((), ())), preferred_element_type=f32)


def whole(dims):
    return pl.BlockSpec(dims, lambda *_: (0,) * len(dims), pipeline_mode=pl.Buffered(1))


def inv_rms(v):
    return lax.rsqrt(jnp.mean(v * v, axis=-1, keepdims=True) + EPS)


def norm_back(v, gain, grad):
    r = inv_rms(v)
    unit = v * r
    scaled = grad * gain
    inner = jnp.mean(scaled * unit, axis=-1, keepdims=True)
    return r * (scaled - unit * inner), grad * unit


def rotary_tables(length):
    half = HD // 2
    freqs = np.exp(-np.log(10000.0) * np.arange(half) / half).astype(np.float32)
    angles = (np.arange(length, dtype=np.float32)[:, None] * freqs[None, :]).astype(np.float64)
    return np.cos(angles).astype(np.float32), np.sin(angles).astype(np.float32)


def rotated(v, cosine, signed, sign):
    first = lax.broadcasted_iota(jnp.int32, (1, PW), 1) % HD < HD // 2
    outs = []
    for c in range(0, v.shape[1], PW):
        part = v[:, c : c + PW]
        partner = jnp.where(first, pltpu.roll(part, PW - HD // 2, 1), pltpu.roll(part, HD // 2, 1))
        outs.append(part * cosine + partner * (signed * sign))
    return outs[0] if len(outs) == 1 else jnp.concatenate(outs, axis=1)


def token_weight(start, length, rows):
    return lax.broadcasted_iota(jnp.int32, (rows, 1), 0) + start < length


def row_sum(v):
    return jnp.sum(v, axis=0, keepdims=True)


def project_kernel(info, x, gain, wq, wk, wv, cosine, signed, q, k, v, h1t, sums):
    at = pl.program_id(0)

    @pl.when(at == 0)
    def _():
        sums[...] = jnp.zeros_like(sums)

    value = x[...].astype(f32)
    h1 = (value * inv_rms(value) * gain[...]).astype(bf16)
    q[...] = rotated(nn(h1, wq[...]), cosine[...], signed[...], 1.0).astype(bf16)
    k[...] = rotated(nn(h1, wk[...]), cosine[...], signed[...], 1.0).astype(bf16)
    v[...] = nn(h1, wv[...]).astype(bf16)
    h1t[...] = h1.T
    weight = token_weight(at * R, info[1], R)
    sums[0:1, :] += row_sum(jnp.where(weight, value * value, 0.0))


def project(info, x, gain, weight, tables):
    seq, width = x.shape
    rows = pl.BlockSpec((R, width), lambda i: (i, 0))
    table = pl.BlockSpec((R, PW), lambda i: (i, 0))
    third = lambda c: pl.BlockSpec((width, width), lambda i: (0, c), pipeline_mode=pl.Buffered(1))
    return pl.pallas_call(
        project_kernel,
        grid=(seq // R,),
        in_specs=[SMEM, rows, whole((1, width)), third(0), third(1), third(2), table, table],
        out_specs=[rows, rows, rows, pl.BlockSpec((width, R), lambda i: (0, i)), whole((8, width))],
        out_shape=[shape((seq, width), bf16)] * 3 + [shape((width, seq), bf16), shape((8, width), f32)],
        compiler_params=params(BIG),
        cost_estimate=pl.CostEstimate(
            flops=2 * seq * width * 3 * width, bytes_accessed=12 * seq * width, transcendentals=0
        ),
        name="project",
    )(info, x, gain, weight, weight, weight, *tables)


def stacked(tile, low):
    zero = jnp.zeros_like(tile)
    return jnp.concatenate([jnp.where(low, tile, zero), jnp.where(low, zero, tile)], axis=0)


def unstacked(tile_t):
    half = lax.broadcasted_iota(jnp.int32, (PW, 1), 0) < HD
    return jnp.where(half, tile_t[:, :T], tile_t[:, T:])


def chunks_of(i):
    out, j = [], 0
    while j < i:
        n = 2 if i - j >= 2 else 1
        out.append((j * T, n * T))
        j += n
    return out


def edge_masks(noisy):
    row = lax.broadcasted_iota(jnp.int32, (T, 2 * T), 0) // BLK
    col = (lax.broadcasted_iota(jnp.int32, (T, 2 * T), 1) % T) // BLK
    own = jnp.logical_or(row == col, jnp.logical_and(row < col, noisy == 0))
    other = jnp.logical_and(row < col, noisy == 1)
    return own, other


def masked(s, start, length):
    pos = lax.broadcasted_iota(jnp.int32, s.shape, 0) + start
    return jnp.where(pos < length, s, NEG)


def over_rows(op, v):
    return op(v.reshape(v.shape[0] // 8, 8, v.shape[1]), axis=0)


def attend_pair(noisy, length, q, ko, vo, kc, vc, store, lse, vo_t, vc_t, scores):
    seq = q.shape[0]
    low = lax.broadcasted_iota(jnp.int32, (1, PW), 1) < HD
    own_mask, other_mask = edge_masks(noisy)
    vo_t[...] = vo[...].T
    vc_t[...] = vc[...].T
    for i in range(seq // T):
        at = pl.ds(i * T, T)
        q2 = stacked(q[at, :] * bf16(SCALE), low)
        buf = scores.at[i % 2]
        edge = nt(jnp.concatenate([ko[at, :], kc[at, :]], 0), q2)
        own = masked(jnp.where(own_mask, edge[:T], NEG), i * T, length)
        other = masked(jnp.where(other_mask, edge[T:], NEG), i * T, length)
        buf[pl.ds(0, T), :] = own
        buf[pl.ds(T, T), :] = other
        top = over_rows(jnp.max, jnp.maximum(own, other))
        for start, size in chunks_of(i):
            s = masked(nt(kc[pl.ds(start, size), :], q2), start, length)
            buf[pl.ds(2 * T + start, size), :] = s
            top = jnp.maximum(top, over_rows(jnp.max, s))
        top = jnp.max(top, axis=0, keepdims=True)
        p = jnp.exp(buf[pl.ds(0, 2 * T), :] - top)
        total = over_rows(jnp.sum, p)
        acc = nn(jnp.concatenate([vo_t[:, at], vc_t[:, at]], 1), p.astype(bf16))
        for start, size in chunks_of(i):
            p = jnp.exp(buf[pl.ds(2 * T + start, size), :] - top)
            total = total + over_rows(jnp.sum, p)
            acc = acc + nn(vc_t[:, pl.ds(start, size)], p.astype(bf16))
        total = row_sum(total)
        lse[0, pl.ds(i, 1), :] = top + jnp.log(total)
        store(at, unstacked(acc / total))


def turned_back(v, cosine, sine):
    quarter = HD // 2
    a, b, c, d = (v[i * quarter : (i + 1) * quarter] for i in range(4))
    return jnp.concatenate(
        [a * cosine + b * sine, b * cosine - a * sine, c * cosine + d * sine, d * cosine - c * sine]
    )


def attend_back_kernel(
    info, q, ko, vo, kc, vc, o, do, lse, cosine, sine, dq, keep, send, ko_t, kc_t, dko, dvo, dkc, dvc
):
    noisy, length = info[0], info[1]
    seq = q.shape[0]
    low = lax.broadcasted_iota(jnp.int32, (1, PW), 1) < HD
    own_mask, other_mask = edge_masks(noisy)
    ko_t[...] = ko[...].T
    kc_t[...] = kc[...].T
    for i in range(seq // T):
        at = pl.ds(i * T, T)
        q2 = stacked(q[at, :] * bf16(SCALE), low)
        do2 = stacked(do[at, :], low)
        prod = (do[at, :].astype(f32) * o[at, :].astype(f32)).T
        delta = jnp.concatenate([row_sum(prod[:HD]), row_sum(prod[HD:])], 1)
        norm = lse[0, pl.ds(i, 1), :]
        s = nt(jnp.concatenate([ko[at, :], kc[at, :]], 0), q2)
        own = masked(jnp.where(own_mask, s[:T], NEG), i * T, length)
        other = masked(jnp.where(other_mask, s[T:], NEG), i * T, length)
        p = jnp.exp(jnp.concatenate([own, other], 0) - norm)
        dp = nt(jnp.concatenate([vo[at, :], vc[at, :]], 0), do2)
        ds = (p * (dp - delta)).astype(bf16)
        dv = nn(p.astype(bf16), do2)
        dk = nn(ds, q2)
        dvo[at, :] = dv[:T]
        dko[at, :] = dk[:T]
        dvc[at, :] = dv[T:]
        dkc[at, :] = dk[T:]
        dq_t = nn(jnp.concatenate([ko_t[:, at], kc_t[:, at]], 1), ds)
        for start, size in chunks_of(i):
            rows = pl.ds(start, size)
            p = jnp.exp(masked(nt(kc[rows, :], q2), start, length) - norm)
            ds = (p * (nt(vc[rows, :], do2) - delta)).astype(bf16)
            dvc[rows, :] += nn(p.astype(bf16), do2)
            dkc[rows, :] += nn(ds, q2)
            dq_t = dq_t + nn(kc_t[:, rows], ds)
        dq[at, :] = (turned_back(unstacked(dq_t), cosine[:, at], sine[:, at]) * SCALE).T.astype(bf16)
    clean = (1 - noisy).astype(f32)
    for at, own, other in ((0, dko, dkc), (1, dvo, dvc)):
        keep[at] = (own[...] + clean * other[...]).astype(bf16)
        send[at] = other[...].astype(bf16)


def attend_back(info, first, pairs, q, ko, vo, kc, vc, o, do, lse, cosine, sine):
    seq = q.shape[0]
    width = pairs * PW
    source = pl.BlockSpec((seq, PW), lambda h: (0, first + h))
    both = pl.BlockSpec((2, seq, PW), lambda h: (0, 0, h))
    lines = pl.BlockSpec((1, seq // T, 2 * T), lambda h: (first + h, 0, 0))
    table = whole((HD // 2, seq))
    return pl.pallas_call(
        attend_back_kernel,
        grid=(pairs,),
        in_specs=[SMEM] + [source] * 7 + [lines, table, table],
        out_specs=[pl.BlockSpec((seq, PW), lambda h: (0, h)), both, both],
        out_shape=[shape((seq, width), bf16)] + [shape((2, seq, width), bf16)] * 2,
        scratch_shapes=[pltpu.VMEM((PW, seq), bf16)] * 2 + [pltpu.VMEM((seq, PW), f32)] * 4,
        compiler_params=params(BIG),
        cost_estimate=pl.CostEstimate(
            flops=8 * seq * seq * width, bytes_accessed=30 * seq * width, transcendentals=seq * seq * 8
        ),
        name="attend_back",
    )(info, q, ko, vo, kc, vc, o, do, lse, cosine, sine)


C0 = 0.7978845608028654
C1 = C0 * 0.044715


def layer_kernel(
    plan, info, x, received, gain1, gain2, wk, wv, cosine, signed, q, ko, vo, wo_any, dy_any, w1_any, w2_any,
    kc_out, vc_out, o_out, lse, out, dx2, do, up_send, up_keep, down_send, down_keep, g_send, g_keep, sums,
    kc, vc, vo_t, vc_t, scores, o, o_t, x2, h2, m, dh, act, du, acc, wo, dy, w1, w2, sem_a, sem_1, sem_2,
):
    step = pl.program_id(0)
    noisy, length = info[0], info[1]
    tiles, pairs, chunks = plan
    at_attend, at_join = tiles, tiles + pairs
    at_feed, at_middle = at_join + tiles, at_join + tiles + chunks
    seq = q.shape[0]

    def fetch(c):
        place = lax.rem(c + (chunks // 2) * (1 - noisy), chunks) * FC
        place = pl.multiple_of(place, FC)
        return (
            pltpu.make_async_copy(w1_any.at[:, pl.ds(place, FC)], w1.at[c], sem_1.at[c]),
            pltpu.make_async_copy(w2_any.at[pl.ds(place, FC), :], w2.at[c], sem_2.at[c]),
        )

    copies = (
        pltpu.make_async_copy(wo_any, wo, sem_a.at[0]),
        pltpu.make_async_copy(dy_any, dy, sem_a.at[1]),
    )

    @pl.when(step == 0)
    def _():
        for copy in copies:
            copy.start()
        for c in range(chunks):
            for copy in fetch(c):
                copy.start()
        sums[...] = jnp.zeros_like(sums)
        acc[...] = jnp.zeros_like(acc)

    @pl.when(step < at_attend)
    def _():
        rows = pl.ds(pl.multiple_of(step * R, R), R)
        value = jnp.where(noisy == 1, received[...].astype(f32), x[...].astype(f32))
        h1 = (value * inv_rms(value) * gain1[...]).astype(bf16)
        k = rotated(nn(h1, wk[...]), cosine[...], signed[...], 1.0).astype(bf16)
        v = nn(h1, wv[...]).astype(bf16)
        kc_out[...] = k
        vc_out[...] = v
        for p in range(pairs):
            kc[p, rows, :] = k[:, p * PW : (p + 1) * PW]
            vc[p, rows, :] = v[:, p * PW : (p + 1) * PW]

    @pl.when(jnp.logical_and(step >= at_attend, step < at_join))
    def _():
        p = step - at_attend
        lanes = pl.ds(pl.multiple_of(p * PW, PW), PW)

        def store(at, tile_t):
            o_t[lanes, at] = tile_t.astype(bf16)
            tile = tile_t.T.astype(bf16)
            o[at, lanes] = tile
            o_out[at, :] = tile

        attend_pair(noisy, length, q, ko, vo, kc.at[p], vc.at[p], store, lse, vo_t, vc_t, scores)

    @pl.when(step == at_join)
    def _():
        for copy in copies:
            copy.wait()

    @pl.when(jnp.logical_and(step >= at_join, step < at_feed))
    def _():
        start = pl.multiple_of((step - at_join) * R, R)
        rows = pl.ds(start, R)
        branch = nn(o[rows, :], wo[...])
        value = x[...].astype(f32) + branch
        x2[rows, :] = value
        h2[rows, :] = (value * inv_rms(value) * gain2[...]).astype(bf16)
        m[rows, :] = jnp.zeros_like(value)
        dh[rows, :] = jnp.zeros_like(value)
        weight = token_weight(start, length, R)
        sums[0:1, :] += row_sum(jnp.where(weight, branch * branch, 0.0))

    @pl.when(jnp.logical_and(step >= at_feed, step < at_middle))
    def _():
        c = step - at_feed
        for copy in fetch(c):
            copy.wait()
        up, down = w1.at[c], w2.at[c]
        for t in range(0, seq, R):
            rows = pl.ds(t, R)
            u = nn(h2[rows, :], up[...])
            da = nt(dy[rows, :], down[...])
            sq = u * u
            half = 0.5 * jnp.tanh(u * (C0 + C1 * sq)) + 0.5
            low = (u * half).astype(bf16)
            slope = half + u * (2.0 * half * (1.0 - half)) * (C0 + 3.0 * C1 * sq)
            back = (da * slope).astype(bf16)
            act[rows, :] = low
            du[rows, :] = back
            m[rows, :] += nn(low, down[...])
            dh[rows, :] += nt(back, up[...])
        down_grad = tn(act[...], dy[...]).astype(bf16)
        up_grad = tn(du[...], h2[...]).astype(bf16)

        @pl.when(c < chunks // 2)
        def _():
            down_send[...] = down_grad
            up_send[...] = up_grad

        @pl.when(c >= chunks // 2)
        def _():
            down_keep[...] = down_grad
            up_keep[...] = up_grad

    @pl.when(step >= at_middle)
    def _():
        start = pl.multiple_of((step - at_middle) * R, R)
        rows = pl.ds(start, R)
        value = x2[rows, :]
        mixed = m[rows, :]
        out[...] = (value + mixed).astype(bf16)
        weight = token_weight(start, length, R)
        sums[1:2, :] += row_sum(jnp.where(weight, mixed * mixed, 0.0))
        grad, gain_terms = norm_back(value, gain2[...], dh[rows, :])
        sums[2:3, :] += row_sum(gain_terms)
        grad = grad + dy[rows, :].astype(f32)
        dx2[...] = grad
        da = grad.astype(bf16)
        do[...] = nt(da, wo[...]).astype(bf16)
        acc[...] += nn(o_t[:, rows], da)

    @pl.when(step == at_middle + tiles - 1)
    def _():
        half = acc.shape[0] // 2
        mine = pl.multiple_of(noisy * half, half)
        g_keep[...] = acc[pl.ds(mine, half), :].astype(bf16)
        g_send[...] = acc[pl.ds(half - mine, half), :].astype(bf16)


def layer(info, x, received, gain1, gain2, wqkv, tables, q, ko, vo, wo, dy, w1, w2):
    seq, width = x.shape
    hidden = w1.shape[1]
    tiles, pairs, chunks = seq // R, width // PW, hidden // FC
    at_join = tiles + pairs
    at_feed, at_middle = at_join + tiles, at_join + tiles + chunks
    clip = lambda i, count: jnp.clip(i, 0, count - 1)
    early = lambda i: (clip(i, tiles), 0)
    late = lambda i: (clip(i - at_middle, tiles), 0)
    pair = lambda i: (0, clip(i - tiles, pairs))
    rows = (R, width)
    third = lambda c: pl.BlockSpec((width, width), lambda i: (0, c), pipeline_mode=pl.Buffered(1))
    table = pl.BlockSpec((R, PW), early)
    anywhere = pl.BlockSpec(memory_space=pl.ANY)
    head = pl.BlockSpec((seq, PW), pair)
    send = pl.BlockSpec((FC, width), lambda i: (clip(i - at_feed, chunks // 2), 0))
    keep = pl.BlockSpec((FC, width), lambda i: (clip(i - at_feed - chunks // 2, chunks // 2), 0))
    half = whole((width // 2, width))
    both = lambda i: (jnp.where(i < tiles, i, clip(i - at_join, tiles)), 0)
    vmem = pltpu.VMEM
    return pl.pallas_call(
        functools.partial(layer_kernel, (tiles, pairs, chunks)),
        grid=(at_middle + tiles,),
        in_specs=[SMEM, pl.BlockSpec(rows, both), pl.BlockSpec(rows, early), whole((1, width)), whole((1, width))]
        + [third(1), third(2), table, table, head, head, head]
        + [anywhere] * 4,
        out_specs=[pl.BlockSpec(rows, early)] * 2
        + [head, pl.BlockSpec((1, seq // T, 2 * T), lambda i: (clip(i - tiles, pairs), 0, 0))]
        + [pl.BlockSpec(rows, late)] * 3
        + [send, keep, send, keep, half, half, whole((8, width))],
        out_shape=[shape((seq, width), bf16)] * 3
        + [shape((pairs, seq // T, 2 * T), f32)]
        + [shape((seq, width), bf16), shape((seq, width), f32), shape((seq, width), bf16)]
        + [shape((hidden // 2, width), bf16)] * 4
        + [shape((width // 2, width), bf16)] * 2
        + [shape((8, width), f32)],
        scratch_shapes=[vmem((pairs, seq, PW), bf16)] * 2
        + [vmem((PW, seq), bf16)] * 2
        + [vmem((2, seq + T, 2 * T), f32), vmem((seq, width), bf16), vmem((width, seq), bf16)]
        + [vmem((seq, width), f32), vmem((seq, width), bf16)]
        + [vmem((seq, width), f32)] * 2
        + [vmem((seq, FC), bf16)] * 2
        + [vmem((width, width), f32), vmem((width, width), bf16), vmem((seq, width), bf16)]
        + [vmem((chunks, width, FC), bf16), vmem((chunks, FC, width), bf16)]
        + [pltpu.SemaphoreType.DMA((n,)) for n in (2, chunks, chunks)],
        compiler_params=params(BIG),
        cost_estimate=pl.CostEstimate(
            flops=seq * width * (12 * hidden + 12 * width + 4 * seq),
            bytes_accessed=60 * seq * width,
            transcendentals=seq * hidden + seq * seq * 8,
        ),
        name="layer",
    )(info, x, received, gain1, gain2, wqkv, wqkv, *tables, q, ko, vo, wo, dy, w1, w2)


def weigh_kernel(info, dq, keep, got, cosine, signed, h1t, dkv, g_send, g_keep):
    half = h1t.shape[0] // 2
    mine = pl.multiple_of(info[0] * half, half)
    dk = keep[0].astype(f32) + got[0].astype(f32)
    dk = rotated(dk, cosine[...], signed[...], -1.0).astype(bf16)
    dv = (keep[1].astype(f32) + got[1].astype(f32)).astype(bf16)
    dkv[0] = dk
    dkv[1] = dv
    grads = jnp.concatenate([dq[...], dk, dv], axis=1)
    for out, start in ((g_send, half - mine), (g_keep, mine)):
        total = nn(h1t[pl.ds(start, half), :], grads).astype(bf16)
        for i in range(3):
            out[i] = total[:, i * PW : (i + 1) * PW]


def weigh(info, piece, got, tables, h1t):
    dq, keep = piece
    seq, width = dq.shape
    tall = h1t.shape[0]
    both = pl.BlockSpec((2, seq, PW), lambda h: (0, 0, h))
    table = whole((seq, PW))
    half = pl.BlockSpec((3, tall // 2, PW), lambda h: (0, 0, h))
    return pl.pallas_call(
        weigh_kernel,
        grid=(width // PW,),
        in_specs=[SMEM, pl.BlockSpec((seq, PW), lambda h: (0, h)), both, both, table, table, whole((tall, seq))],
        out_specs=[both, half, half],
        out_shape=[shape((2, seq, width), bf16)] + [shape((3, tall // 2, width), bf16)] * 2,
        compiler_params=params(BIG),
        cost_estimate=pl.CostEstimate(
            flops=6 * seq * width * tall, bytes_accessed=16 * seq * width, transcendentals=0
        ),
        name="weigh",
    )(info, dq, keep, got, *tables, h1t)


def finish_kernel(parts, x, dx2, wqkv, gain, *refs):
    dx, sums = refs[-2:]

    @pl.when(pl.program_id(0) == 0)
    def _():
        sums[...] = jnp.zeros_like(sums)

    dqs, dkvs = refs[:parts], refs[parts : 2 * parts]
    grads = [r[...] for r in dqs] + [r[0] for r in dkvs] + [r[1] for r in dkvs]
    dh = nt(jnp.concatenate(grads, axis=1), wqkv[...])
    grad, gain_terms = norm_back(x[...].astype(f32), gain[...], dh)
    sums[0:1, :] += row_sum(gain_terms)
    dx[...] = (dx2[...] + grad).astype(bf16)


def finish(x, dx2, dqs, dkvs, weight, gain):
    seq, width = x.shape
    rows = pl.BlockSpec((R, width), lambda i: (i, 0))
    return pl.pallas_call(
        functools.partial(finish_kernel, len(dqs)),
        grid=(seq // R,),
        in_specs=[rows, rows, whole(weight.shape), whole((1, width))]
        + [pl.BlockSpec((R, a.shape[1]), lambda i: (i, 0)) for a in dqs]
        + [pl.BlockSpec((2, R, a.shape[2]), lambda i: (0, i, 0)) for a in dkvs],
        out_specs=[rows, whole((8, width))],
        out_shape=[shape((seq, width), bf16), shape((8, width), f32)],
        compiler_params=params(BIG),
        cost_estimate=pl.CostEstimate(
            flops=6 * seq * width * width, bytes_accessed=20 * seq * width, transcendentals=0
        ),
        name="finish",
    )(x, dx2, weight, gain, *dqs, *dkvs)


def bit_orders(count):
    bits = [1 << i for i in range(count.bit_length() - 1)]
    if len(bits) == 4:
        x, y, z, far = bits
        return [(x, y, z, far), (y, x, z, far), (z, x, far, y)]
    return [tuple(bits[g:] + bits[:g]) for g in range(GROUPS)]


def exchange(value, axis, bit):
    size = lax.axis_size(axis)
    return lax.ppermute(value, axis, [(i, i ^ bit) for i in range(size)])


def distance(order, place):
    out = 0
    for i, bit in enumerate(order):
        out = out + ((place >> (len(order) - 1 - i)) & 1) * bit
    return out


def start_kernel(orders, wheres, me, *refs):
    arrays = len(wheres)
    ins, outs = refs[: 2 * arrays], refs[2 * arrays :]
    half = outs[0].shape[0]
    for g, order in enumerate(orders):
        for side in range(2):

            def one(r, carry, g=g, order=order, side=side):
                part = me[0] ^ distance(order, r + side * half)
                row = 0
                for kept, got, where in zip(ins[::2], ins[1::2], wheres, strict=True):
                    place = where(part, g)
                    size = kept.shape[1]
                    total = kept[place].astype(f32) + got[place].astype(f32)
                    outs[g * 2 + side][r, row : row + size, :] = total.astype(bf16)
                    row += size
                return carry

            lax.fori_loop(0, half, one, 0)


def start_sum(me, kept, got, wheres, orders):
    count = 1 << len(orders[0])
    half = count // 2
    rows = sum(a.shape[1] for a in kept)
    width = kept[0].shape[2]
    cols = width // 3
    block = lambda a: pl.BlockSpec((a.shape[0], a.shape[1], cols), lambda c: (0, 0, c))
    out = pl.BlockSpec((half, rows, cols), lambda c: (0, 0, c))
    args = [a for pair in zip(kept, got, strict=True) for a in pair]
    outs = pl.pallas_call(
        functools.partial(start_kernel, orders, wheres),
        grid=(width // cols,),
        in_specs=[SMEM] + [block(a) for a in args],
        out_specs=[out] * (2 * GROUPS),
        out_shape=[shape((half, rows, width), bf16)] * (2 * GROUPS),
        compiler_params=params(BIG),
        cost_estimate=pl.CostEstimate(
            flops=0, bytes_accessed=6 * GROUPS * count * rows * width, transcendentals=0
        ),
        name="start_sum",
    )(me, *args)
    return outs[0::2], outs[1::2]


def step_kernel(*refs):
    for g in range(GROUPS):
        low, high, got_low, got_high = refs[4 * g : 4 * g + 4]
        keep, send = refs[4 * GROUPS + 2 * g : 4 * GROUPS + 2 * g + 2]
        keep[...] = (low[...].astype(f32) + got_low[...].astype(f32)).astype(bf16)
        send[...] = (high[...].astype(f32) + got_high[...].astype(f32)).astype(bf16)


def step_sum(kept, got):
    count, rows, width = kept[0].shape
    half = count // 2
    steps = min(half, 2)
    block = (half // steps, rows, width)
    low = pl.BlockSpec(block, lambda r: (r, 0, 0))
    high = pl.BlockSpec(block, lambda r: (r + steps, 0, 0))
    args = []
    for a, b in zip(kept, got, strict=True):
        args += [a, a, b, b]
    outs = pl.pallas_call(
        step_kernel,
        grid=(steps,),
        in_specs=[low, high, low, high] * GROUPS,
        out_specs=[low, low] * GROUPS,
        out_shape=[shape((half, rows, width), bf16)] * (2 * GROUPS),
        cost_estimate=pl.CostEstimate(
            flops=0, bytes_accessed=6 * GROUPS * count * rows * width, transcendentals=0
        ),
        name="step_sum",
    )(*args)
    return outs[0::2], outs[1::2]


def after(value, *earlier):
    return lax.optimization_barrier((value, earlier))[0]


def sum_parts(me, kept, got, wheres):
    orders = bit_orders(lax.axis_size("batch"))
    keep, send = start_sum(me, kept, got, wheres, orders)
    for i in range(len(orders[0])):
        got = [exchange(s, "batch", order[i]) for s, order in zip(send, orders, strict=True)]
        earlier = yield send[0]
        if earlier is not None:
            keep = after(keep, earlier)
        if i < len(orders[0]) - 1:
            keep, send = step_sum(keep, got)
    yield [a[0].astype(f32) + b[0].astype(f32) for a, b in zip(keep, got, strict=True)]


def finished(steps, earlier):
    out = steps.send(earlier)
    while not isinstance(out, list):
        out = steps.send(None)
    return out


def sum_all(value):
    value = value + exchange(value, "stream", 1)
    for order in bit_orders(lax.axis_size("batch"))[0]:
        value = value + exchange(value, "batch", order)
    return value


def on_device(
    inputs, lengths, cotangent, qkv_weight, out_weight, up_weight, down_weight, attn_gain, mlp_gain
):
    seq, width = inputs.shape[2:]
    x = inputs[0, 0]
    dy = cotangent[0, 0]
    count = lax.axis_size("batch")
    stream = lax.axis_index("stream").astype(jnp.int32)
    me = lax.axis_index("batch").astype(jnp.int32).reshape(1)
    info = jnp.stack([stream, lengths[0]])
    gain1, gain2 = attn_gain.reshape(1, width), mlp_gain.reshape(1, width)
    cosine, sine = rotary_tables(seq)
    tables = (
        jnp.asarray(np.concatenate([cosine] * 4, axis=1)),
        jnp.asarray(np.concatenate([-sine, sine] * 2, axis=1)),
    )
    tables_t = (jnp.asarray(cosine.T), jnp.asarray(sine.T))

    received = lax.ppermute(x, "stream", [(0, 1)])
    q, ko, vo, h1t, sums_x = project(info, x, gain1, qkv_weight, tables)
    (
        kc, vc, o, lse, outputs, dx2, do,
        up_send, up_keep, down_send, down_keep, out_send, out_keep, sums_m,
    ) = layer(
        info, x, received, gain1, gain2, qkv_weight, tables, q, ko, vo, out_weight, dy, up_weight, down_weight
    )
    down_got, up_got, out_got = (exchange(a, "stream", 1) for a in (down_send, up_send, out_send))

    def by_rows(array):
        return array.reshape(count * GROUPS, array.shape[0] // (count * GROUPS), width)

    heads = (q, ko, vo, kc, vc, o, do, lse, *tables_t)
    pairs = width // PW // 2
    dq1, keep1, send1 = attend_back(info, 0, pairs, *heads)
    got1 = lax.ppermute(send1, "stream", [(1, 0)])
    early = sum_parts(
        me,
        [by_rows(after(a, dq1)) for a in (down_keep, up_keep, out_keep)],
        [by_rows(a) for a in (down_got, up_got, out_got)],
        [lambda part, g: part * GROUPS + g] * 3,
    )
    token = next(early)
    dq2, keep2, send2 = attend_back(info, pairs, pairs, q, ko, vo, kc, vc, o, after(do, token), lse, *tables_t)
    got2 = lax.ppermute(send2, "stream", [(1, 0)])
    dkv1, qkv_send1, qkv_keep1 = weigh(info, (dq1, after(keep1, dq2)), got1, tables, h1t)
    qkv_got1 = exchange(qkv_send1, "stream", 1)
    token = early.send(dkv1)
    dkv2, qkv_send2, qkv_keep2 = weigh(info, (dq2, after(keep2, token)), got2, tables, h1t)
    qkv_got2 = exchange(qkv_send2, "stream", 1)
    dx, sums_h = finish(x, dx2, [dq1, dq2], [dkv1, dkv2], qkv_weight, gain1)

    tall = width // (2 * count)
    split = lambda a: a.reshape(GROUPS * count, tall, a.shape[2])
    late = sum_parts(
        me,
        [split(after(a, dx)) for a in (qkv_keep1, qkv_keep2)],
        [split(a) for a in (qkv_got1, qkv_got2)],
        [lambda part, g: g * count + part] * 2,
    )
    token = next(late)
    early.send(token)
    late.send(None)
    early = finished(early, None)
    late = finished(late, None)
    small = jnp.concatenate(
        [
            sums_x[:1],
            sums_m[:3],
            sums_h[:1],
            jnp.full((1, width), lengths[0].astype(f32)),
            jnp.zeros((2, width), f32),
        ]
    )
    small = sum_all(small)

    qkv_grad = jnp.concatenate([part for e in late for part in (e[:tall], e[tall:])], axis=1)
    tall = down_keep.shape[0] // (count * GROUPS)
    down_grad = jnp.concatenate([e[:tall] for e in early])
    up_grad = jnp.concatenate([e[tall : 2 * tall] for e in early]).T
    out_grad = jnp.concatenate([e[2 * tall :] for e in early])
    squares = jnp.sum(small[:3], axis=1)
    rms = jnp.sqrt(squares / (small[5, 0] * width))
    return (
        outputs[None, None],
        dx[None, None],
        qkv_grad,
        out_grad,
        up_grad,
        down_grad,
        small[4],
        small[3],
        rms,
    )


def solution(mesh):
    rows = P("stream", "batch", None, None)
    both = ("stream", "batch")
    return jax.shard_map(
        on_device,
        mesh=mesh,
        in_specs=(rows, P("batch"), rows, P(), P(), P(), P(), P(), P()),
        out_specs=(rows, rows, P(both, None), P(both, None), P(None, both), P(both, None), P(), P(), P()),
        check_vma=False,
    )
```

```python
import functools

import jax
import jax.numpy as jnp
import numpy as np
from jax import lax
from jax.experimental import pallas as pl
from jax.experimental.pallas import tpu as pltpu
from jax.sharding import PartitionSpec as P

f32 = jnp.float32
bf16 = jnp.bfloat16

HD = 64
BLK = 16
EPS = 1e-06
NEG = -1e30
PW = 2 * HD
T = 128
R = 256
FC = 512
SCALE = HD**-0.5
BIG = 60
GROUPS = 3

COST = pl.CostEstimate(flops=1 << 20, bytes_accessed=1 << 16, transcendentals=0)
LONG = pl.CostEstimate(flops=1 << 35, bytes_accessed=1 << 26, transcendentals=0)

SMEM = pl.BlockSpec(memory_space=pltpu.SMEM)


def params(mib):
    return pltpu.CompilerParams(vmem_limit_bytes=mib << 20)


def shape(dims, dtype):
    return jax.ShapeDtypeStruct(dims, dtype)


def pinned(*arrays):
    return [pltpu.with_memory_space_constraint(a, pltpu.HBM) for a in arrays]


def nn(a, b):
    return jnp.dot(a, b, preferred_element_type=f32)


def nt(a, b):
    return lax.dot_general(a, b, (((1,), (1,)), ((), ())), preferred_element_type=f32)


def tn(a, b):
    return lax.dot_general(a, b, (((0,), (0,)), ((), ())), preferred_element_type=f32)


def whole(dims):
    return pl.BlockSpec(dims, lambda *_: (0,) * len(dims), pipeline_mode=pl.Buffered(1))


def inv_rms(v):
    return lax.rsqrt(jnp.mean(v * v, axis=-1, keepdims=True) + EPS)


def norm_back(v, gain, grad):
    r = inv_rms(v)
    unit = v * r
    scaled = grad * gain
    inner = jnp.mean(scaled * unit, axis=-1, keepdims=True)
    return r * (scaled - unit * inner), grad * unit


def rotary_tables(length):
    half = HD // 2
    freqs = np.exp(-np.log(10000.0) * np.arange(half) / half).astype(np.float32)
    angles = (np.arange(length, dtype=np.float32)[:, None] * freqs[None, :]).astype(np.float64)
    return np.cos(angles).astype(np.float32), np.sin(angles).astype(np.float32)


def rotated(v, cosine, signed, sign):
    first = lax.broadcasted_iota(jnp.int32, (1, PW), 1) % HD < HD // 2
    outs = []
    for c in range(0, v.shape[1], PW):
        part = v[:, c : c + PW]
        partner = jnp.where(first, pltpu.roll(part, PW - HD // 2, 1), pltpu.roll(part, HD // 2, 1))
        outs.append(part * cosine + partner * (signed * sign))
    return outs[0] if len(outs) == 1 else jnp.concatenate(outs, axis=1)


def token_weight(start, length, rows):
    return lax.broadcasted_iota(jnp.int32, (rows, 1), 0) + start < length


def row_sum(v):
    return jnp.sum(v, axis=0, keepdims=True)


def project_kernel(info, x, gain, wq, wk, wv, cosine, signed, q, k, v, h1t, sums):
    at = pl.program_id(0)

    @pl.when(at == 0)
    def _():
        sums[...] = jnp.zeros_like(sums)

    value = x[...].astype(f32)
    h1 = (value * inv_rms(value) * gain[...]).astype(bf16)
    q[...] = rotated(nn(h1, wq[...]), cosine[...], signed[...], 1.0).astype(bf16)
    k[...] = rotated(nn(h1, wk[...]), cosine[...], signed[...], 1.0).astype(bf16)
    v[...] = nn(h1, wv[...]).astype(bf16)
    h1t[...] = h1.T
    weight = token_weight(at * R, info[1], R)
    sums[0:1, :] += row_sum(jnp.where(weight, value * value, 0.0))


def project(info, x, gain, weight, tables):
    seq, width = x.shape
    rows = pl.BlockSpec((R, width), lambda i: (i, 0))
    table = pl.BlockSpec((R, PW), lambda i: (i, 0))
    third = lambda c: pl.BlockSpec((width, width), lambda i: (0, c), pipeline_mode=pl.Buffered(1))
    return pl.pallas_call(
        project_kernel,
        grid=(seq // R,),
        in_specs=[SMEM, rows, whole((1, width)), third(0), third(1), third(2), table, table],
        out_specs=[rows, rows, rows, pl.BlockSpec((width, R), lambda i: (0, i)), whole((8, width))],
        out_shape=[shape((seq, width), bf16)] * 3 + [shape((width, seq), bf16), shape((8, width), f32)],
        compiler_params=params(BIG),
        cost_estimate=LONG,
        name="project",
    )(info, *pinned(x), gain, *pinned(weight, weight, weight, *tables))


def stacked(tile, low):
    zero = jnp.zeros_like(tile)
    return jnp.concatenate([jnp.where(low, tile, zero), jnp.where(low, zero, tile)], axis=0)


def unstacked(tile_t):
    half = lax.broadcasted_iota(jnp.int32, (PW, 1), 0) < HD
    return jnp.where(half, tile_t[:, :T], tile_t[:, T:])


def chunks_of(i):
    out, j = [], 0
    while j < i:
        n = 2 if i - j >= 2 else 1
        out.append((j * T, n * T))
        j += n
    return out


def edge_masks(noisy):
    row = lax.broadcasted_iota(jnp.int32, (T, 2 * T), 0) // BLK
    col = (lax.broadcasted_iota(jnp.int32, (T, 2 * T), 1) % T) // BLK
    own = jnp.logical_or(row == col, jnp.logical_and(row < col, noisy == 0))
    other = jnp.logical_and(row < col, noisy == 1)
    return own, other


def masked(s, start, length):
    pos = lax.broadcasted_iota(jnp.int32, s.shape, 0) + start
    return jnp.where(pos < length, s, NEG)


def over_rows(op, v):
    return op(v.reshape(v.shape[0] // 8, 8, v.shape[1]), axis=0)


def attend_pair(noisy, length, q, ko, vo, kc, vc, store, lse, vo_t, vc_t, scores):
    seq = q.shape[0]
    low = lax.broadcasted_iota(jnp.int32, (1, PW), 1) < HD
    own_mask, other_mask = edge_masks(noisy)
    vo_t[...] = vo[...].T
    vc_t[...] = vc[...].T
    for i in range(seq // T):
        at = pl.ds(i * T, T)
        q2 = stacked(q[at, :] * bf16(SCALE), low)
        buf = scores.at[i % 2]
        edge = nt(jnp.concatenate([ko[at, :], kc[at, :]], 0), q2)
        own = masked(jnp.where(own_mask, edge[:T], NEG), i * T, length)
        other = masked(jnp.where(other_mask, edge[T:], NEG), i * T, length)
        buf[pl.ds(0, T), :] = own
        buf[pl.ds(T, T), :] = other
        top = over_rows(jnp.max, jnp.maximum(own, other))
        for start, size in chunks_of(i):
            s = masked(nt(kc[pl.ds(start, size), :], q2), start, length)
            buf[pl.ds(2 * T + start, size), :] = s
            top = jnp.maximum(top, over_rows(jnp.max, s))
        top = jnp.max(top, axis=0, keepdims=True)
        p = jnp.exp(buf[pl.ds(0, 2 * T), :] - top)
        total = over_rows(jnp.sum, p)
        acc = nn(jnp.concatenate([vo_t[:, at], vc_t[:, at]], 1), p.astype(bf16))
        for start, size in chunks_of(i):
            p = jnp.exp(buf[pl.ds(2 * T + start, size), :] - top)
            total = total + over_rows(jnp.sum, p)
            acc = acc + nn(vc_t[:, pl.ds(start, size)], p.astype(bf16))
        total = row_sum(total)
        lse[0, pl.ds(i, 1), :] = top + jnp.log(total)
        store(at, unstacked(acc / total))


def turned_back(v, cosine, sine):
    quarter = HD // 2
    a, b, c, d = (v[i * quarter : (i + 1) * quarter] for i in range(4))
    return jnp.concatenate(
        [a * cosine + b * sine, b * cosine - a * sine, c * cosine + d * sine, d * cosine - c * sine]
    )


def attend_back_kernel(
    info, q, ko, vo, kc, vc, o, do, lse, cosine, sine, dq, keep, send, ko_t, kc_t, dko, dvo, dkc, dvc
):
    noisy, length = info[0], info[1]
    seq = q.shape[0]
    low = lax.broadcasted_iota(jnp.int32, (1, PW), 1) < HD
    own_mask, other_mask = edge_masks(noisy)
    ko_t[...] = ko[...].T
    kc_t[...] = kc[...].T
    for i in range(seq // T):
        at = pl.ds(i * T, T)
        q2 = stacked(q[at, :] * bf16(SCALE), low)
        do2 = stacked(do[at, :], low)
        prod = (do[at, :].astype(f32) * o[at, :].astype(f32)).T
        delta = jnp.concatenate([row_sum(prod[:HD]), row_sum(prod[HD:])], 1)
        norm = lse[0, pl.ds(i, 1), :]
        s = nt(jnp.concatenate([ko[at, :], kc[at, :]], 0), q2)
        own = masked(jnp.where(own_mask, s[:T], NEG), i * T, length)
        other = masked(jnp.where(other_mask, s[T:], NEG), i * T, length)
        p = jnp.exp(jnp.concatenate([own, other], 0) - norm)
        dp = nt(jnp.concatenate([vo[at, :], vc[at, :]], 0), do2)
        ds = (p * (dp - delta)).astype(bf16)
        dv = nn(p.astype(bf16), do2)
        dk = nn(ds, q2)
        dvo[at, :] = dv[:T]
        dko[at, :] = dk[:T]
        dvc[at, :] = dv[T:]
        dkc[at, :] = dk[T:]
        dq_t = nn(jnp.concatenate([ko_t[:, at], kc_t[:, at]], 1), ds)
        for start, size in chunks_of(i):
            rows = pl.ds(start, size)
            p = jnp.exp(masked(nt(kc[rows, :], q2), start, length) - norm)
            ds = (p * (nt(vc[rows, :], do2) - delta)).astype(bf16)
            dvc[rows, :] += nn(p.astype(bf16), do2)
            dkc[rows, :] += nn(ds, q2)
            dq_t = dq_t + nn(kc_t[:, rows], ds)
        dq[at, :] = (turned_back(unstacked(dq_t), cosine[:, at], sine[:, at]) * SCALE).T.astype(bf16)
    clean = (1 - noisy).astype(f32)
    for at, own, other in ((0, dko, dkc), (1, dvo, dvc)):
        keep[at] = (own[...] + clean * other[...]).astype(bf16)
        send[at] = other[...].astype(bf16)


def attend_back(info, first, pairs, q, ko, vo, kc, vc, o, do, lse, cosine, sine):
    seq = q.shape[0]
    width = pairs * PW
    source = pl.BlockSpec((seq, PW), lambda h: (0, first + h))
    both = pl.BlockSpec((2, seq, PW), lambda h: (0, 0, h))
    lines = pl.BlockSpec((1, seq // T, 2 * T), lambda h: (first + h, 0, 0))
    table = whole((HD // 2, seq))
    return pl.pallas_call(
        attend_back_kernel,
        grid=(pairs,),
        in_specs=[SMEM] + [source] * 7 + [lines, table, table],
        out_specs=[pl.BlockSpec((seq, PW), lambda h: (0, h)), both, both],
        out_shape=[shape((seq, width), bf16)] + [shape((2, seq, width), bf16)] * 2,
        scratch_shapes=[pltpu.VMEM((PW, seq), bf16)] * 2 + [pltpu.VMEM((seq, PW), f32)] * 4,
        compiler_params=params(24),
        cost_estimate=LONG,
        name="attend_back",
    )(info, *pinned(q, ko, vo, kc, vc, o, do), lse, cosine, sine)


C0 = 0.7978845608028654
C1 = C0 * 0.044715


def layer_kernel(
    plan, info, x, received, gain1, gain2, wk, wv, cosine, signed, q, ko, vo, wo_any, dy_any, w1_any, w2_any,
    kc_out, vc_out, o_out, lse, out, dx2, do, up_send, up_keep, down_send, down_keep, g_send, g_keep, sums,
    kc, vc, vo_t, vc_t, scores, o, o_t, x2, h2, m, dh, act, du, acc, wo, dy, w1, w2, sem_a, sem_1, sem_2,
):
    step = pl.program_id(0)
    noisy, length = info[0], info[1]
    tiles, pairs, chunks = plan
    at_attend, at_join = tiles, tiles + pairs
    at_feed, at_middle = at_join + tiles, at_join + tiles + chunks
    seq = q.shape[0]

    def fetch(c):
        place = lax.rem(c + (chunks // 2) * (1 - noisy), chunks) * FC
        place = pl.multiple_of(place, FC)
        return (
            pltpu.make_async_copy(w1_any.at[:, pl.ds(place, FC)], w1.at[c], sem_1.at[c]),
            pltpu.make_async_copy(w2_any.at[pl.ds(place, FC), :], w2.at[c], sem_2.at[c]),
        )

    copies = (
        pltpu.make_async_copy(wo_any, wo, sem_a.at[0]),
        pltpu.make_async_copy(dy_any, dy, sem_a.at[1]),
    )

    @pl.when(step == 0)
    def _():
        for copy in copies:
            copy.start()
        for c in range(chunks):
            for copy in fetch(c):
                copy.start()
        sums[...] = jnp.zeros_like(sums)
        acc[...] = jnp.zeros_like(acc)

    @pl.when(step < at_attend)
    def _():
        rows = pl.ds(pl.multiple_of(step * R, R), R)
        value = jnp.where(noisy == 1, received[...].astype(f32), x[...].astype(f32))
        h1 = (value * inv_rms(value) * gain1[...]).astype(bf16)
        k = rotated(nn(h1, wk[...]), cosine[...], signed[...], 1.0).astype(bf16)
        v = nn(h1, wv[...]).astype(bf16)
        kc_out[...] = k
        vc_out[...] = v
        for p in range(pairs):
            kc[p, rows, :] = k[:, p * PW : (p + 1) * PW]
            vc[p, rows, :] = v[:, p * PW : (p + 1) * PW]

    @pl.when(jnp.logical_and(step >= at_attend, step < at_join))
    def _():
        p = step - at_attend
        lanes = pl.ds(pl.multiple_of(p * PW, PW), PW)

        def store(at, tile_t):
            o_t[lanes, at] = tile_t.astype(bf16)
            tile = tile_t.T.astype(bf16)
            o[at, lanes] = tile
            o_out[at, :] = tile

        attend_pair(noisy, length, q, ko, vo, kc.at[p], vc.at[p], store, lse, vo_t, vc_t, scores)

    @pl.when(step == at_join)
    def _():
        for copy in copies:
            copy.wait()

    @pl.when(jnp.logical_and(step >= at_join, step < at_feed))
    def _():
        start = pl.multiple_of((step - at_join) * R, R)
        rows = pl.ds(start, R)
        branch = nn(o[rows, :], wo[...])
        value = x[...].astype(f32) + branch
        x2[rows, :] = value
        h2[rows, :] = (value * inv_rms(value) * gain2[...]).astype(bf16)
        m[rows, :] = jnp.zeros_like(value)
        dh[rows, :] = jnp.zeros_like(value)
        weight = token_weight(start, length, R)
        sums[0:1, :] += row_sum(jnp.where(weight, branch * branch, 0.0))

    @pl.when(jnp.logical_and(step >= at_feed, step < at_middle))
    def _():
        c = step - at_feed
        for copy in fetch(c):
            copy.wait()
        up, down = w1.at[c], w2.at[c]
        for t in range(0, seq, R):
            rows = pl.ds(t, R)
            u = nn(h2[rows, :], up[...])
            da = nt(dy[rows, :], down[...])
            sq = u * u
            half = 0.5 * jnp.tanh(u * (C0 + C1 * sq)) + 0.5
            low = (u * half).astype(bf16)
            slope = half + u * (2.0 * half * (1.0 - half)) * (C0 + 3.0 * C1 * sq)
            back = (da * slope).astype(bf16)
            act[rows, :] = low
            du[rows, :] = back
            m[rows, :] += nn(low, down[...])
            dh[rows, :] += nt(back, up[...])
        down_grad = tn(act[...], dy[...]).astype(bf16)
        up_grad = tn(du[...], h2[...]).astype(bf16)

        @pl.when(c < chunks // 2)
        def _():
            down_send[...] = down_grad
            up_send[...] = up_grad

        @pl.when(c >= chunks // 2)
        def _():
            down_keep[...] = down_grad
            up_keep[...] = up_grad

    @pl.when(step >= at_middle)
    def _():
        start = pl.multiple_of((step - at_middle) * R, R)
        rows = pl.ds(start, R)
        value = x2[rows, :]
        mixed = m[rows, :]
        out[...] = (value + mixed).astype(bf16)
        weight = token_weight(start, length, R)
        sums[1:2, :] += row_sum(jnp.where(weight, mixed * mixed, 0.0))
        grad, gain_terms = norm_back(value, gain2[...], dh[rows, :])
        sums[2:3, :] += row_sum(gain_terms)
        grad = grad + dy[rows, :].astype(f32)
        dx2[...] = grad
        da = grad.astype(bf16)
        do[...] = nt(da, wo[...]).astype(bf16)
        acc[...] += nn(o_t[:, rows], da)

    @pl.when(step == at_middle + tiles - 1)
    def _():
        half = acc.shape[0] // 2
        mine = pl.multiple_of(noisy * half, half)
        g_keep[...] = acc[pl.ds(mine, half), :].astype(bf16)
        g_send[...] = acc[pl.ds(half - mine, half), :].astype(bf16)


def layer(info, x, received, gain1, gain2, wqkv, tables, q, ko, vo, wo, dy, w1, w2):
    seq, width = x.shape
    hidden = w1.shape[1]
    tiles, pairs, chunks = seq // R, width // PW, hidden // FC
    at_join = tiles + pairs
    at_feed, at_middle = at_join + tiles, at_join + tiles + chunks
    clip = lambda i, count: jnp.clip(i, 0, count - 1)
    early = lambda i: (clip(i, tiles), 0)
    late = lambda i: (clip(i - at_middle, tiles), 0)
    pair = lambda i: (0, clip(i - tiles, pairs))
    rows = (R, width)
    third = lambda c: pl.BlockSpec((width, width), lambda i: (0, c), pipeline_mode=pl.Buffered(1))
    table = pl.BlockSpec((R, PW), early)
    anywhere = pl.BlockSpec(memory_space=pl.ANY)
    head = pl.BlockSpec((seq, PW), pair)
    send = pl.BlockSpec((FC, width), lambda i: (clip(i - at_feed, chunks // 2), 0))
    keep = pl.BlockSpec((FC, width), lambda i: (clip(i - at_feed - chunks // 2, chunks // 2), 0))
    half = whole((width // 2, width))
    both = lambda i: (jnp.where(i < tiles, i, clip(i - at_join, tiles)), 0)
    vmem = pltpu.VMEM
    return pl.pallas_call(
        functools.partial(layer_kernel, (tiles, pairs, chunks)),
        grid=(at_middle + tiles,),
        in_specs=[SMEM, pl.BlockSpec(rows, both), pl.BlockSpec(rows, early), whole((1, width)), whole((1, width))]
        + [third(1), third(2), table, table, head, head, head]
        + [anywhere] * 4,
        out_specs=[pl.BlockSpec(rows, early)] * 2
        + [head, pl.BlockSpec((1, seq // T, 2 * T), lambda i: (clip(i - tiles, pairs), 0, 0))]
        + [pl.BlockSpec(rows, late)] * 3
        + [send, keep, send, keep, half, half, whole((8, width))],
        out_shape=[shape((seq, width), bf16)] * 3
        + [shape((pairs, seq // T, 2 * T), f32)]
        + [shape((seq, width), bf16), shape((seq, width), f32), shape((seq, width), bf16)]
        + [shape((hidden // 2, width), bf16)] * 4
        + [shape((width // 2, width), bf16)] * 2
        + [shape((8, width), f32)],
        scratch_shapes=[vmem((pairs, seq, PW), bf16)] * 2
        + [vmem((PW, seq), bf16)] * 2
        + [vmem((2, seq + T, 2 * T), f32), vmem((seq, width), bf16), vmem((width, seq), bf16)]
        + [vmem((seq, width), f32), vmem((seq, width), bf16)]
        + [vmem((seq, width), f32)] * 2
        + [vmem((seq, FC), bf16)] * 2
        + [vmem((width, width), f32), vmem((width, width), bf16), vmem((seq, width), bf16)]
        + [vmem((chunks, width, FC), bf16), vmem((chunks, FC, width), bf16)]
        + [pltpu.SemaphoreType.DMA((n,)) for n in (2, chunks, chunks)],
        compiler_params=params(BIG),
        cost_estimate=LONG,
        name="layer",
    )(info, *pinned(x, received), gain1, gain2, *pinned(wqkv, wqkv, *tables, q, ko, vo, wo, dy, w1, w2))


def weigh_kernel(info, dq, keep, got, cosine, signed, h1t, dkv, g_send, g_keep):
    half = h1t.shape[0] // 2
    mine = pl.multiple_of(info[0] * half, half)
    dk = keep[0].astype(f32) + got[0].astype(f32)
    dk = rotated(dk, cosine[...], signed[...], -1.0).astype(bf16)
    dv = (keep[1].astype(f32) + got[1].astype(f32)).astype(bf16)
    dkv[0] = dk
    dkv[1] = dv
    grads = jnp.concatenate([dq[...], dk, dv], axis=1)
    for out, start in ((g_send, half - mine), (g_keep, mine)):
        total = nn(h1t[pl.ds(start, half), :], grads).astype(bf16)
        for i in range(3):
            out[i] = total[:, i * PW : (i + 1) * PW]


def weigh(info, piece, got, tables, h1t):
    dq, keep = piece
    seq, width = dq.shape
    tall = h1t.shape[0]
    both = pl.BlockSpec((2, seq, PW), lambda h: (0, 0, h))
    table = whole((seq, PW))
    half = pl.BlockSpec((3, tall // 2, PW), lambda h: (0, 0, h))
    return pl.pallas_call(
        weigh_kernel,
        grid=(width // PW,),
        in_specs=[SMEM, pl.BlockSpec((seq, PW), lambda h: (0, h)), both, both, table, table, whole((tall, seq))],
        out_specs=[both, half, half],
        out_shape=[shape((2, seq, width), bf16)] + [shape((3, tall // 2, width), bf16)] * 2,
        compiler_params=params(24),
        cost_estimate=LONG,
        name="weigh",
    )(info, *pinned(dq, keep), got, *pinned(*tables, h1t))


def finish_kernel(parts, x, dx2, wqkv, gain, *refs):
    dx, sums = refs[-2:]

    @pl.when(pl.program_id(0) == 0)
    def _():
        sums[...] = jnp.zeros_like(sums)

    dqs, dkvs = refs[:parts], refs[parts : 2 * parts]
    grads = [r[...] for r in dqs] + [r[0] for r in dkvs] + [r[1] for r in dkvs]
    dh = nt(jnp.concatenate(grads, axis=1), wqkv[...])
    grad, gain_terms = norm_back(x[...].astype(f32), gain[...], dh)
    sums[0:1, :] += row_sum(gain_terms)
    dx[...] = (dx2[...] + grad).astype(bf16)


def finish(x, dx2, dqs, dkvs, weight, gain):
    seq, width = x.shape
    rows = pl.BlockSpec((R, width), lambda i: (i, 0))
    return pl.pallas_call(
        functools.partial(finish_kernel, len(dqs)),
        grid=(seq // R,),
        in_specs=[rows, rows, whole(weight.shape), whole((1, width))]
        + [pl.BlockSpec((R, a.shape[1]), lambda i: (i, 0)) for a in dqs]
        + [pl.BlockSpec((2, R, a.shape[2]), lambda i: (0, i, 0)) for a in dkvs],
        out_specs=[rows, whole((8, width))],
        out_shape=[shape((seq, width), bf16), shape((8, width), f32)],
        compiler_params=params(24),
        cost_estimate=LONG,
        name="finish",
    )(*pinned(x, dx2, weight), gain, *pinned(*dqs, *dkvs))


def bit_orders(count):
    bits = [1 << i for i in range(count.bit_length() - 1)]
    if len(bits) == 4:
        x, y, z, far = bits
        return [(x, y, z, far), (y, x, z, far), (z, x, far, y)]
    return [tuple(bits[g:] + bits[:g]) for g in range(GROUPS)]


def exchange(value, axis, bit):
    size = lax.axis_size(axis)
    return lax.ppermute(value, axis, [(i, i ^ bit) for i in range(size)])


def distance(order, place):
    out = 0
    for i, bit in enumerate(order):
        out = out + ((place >> (len(order) - 1 - i)) & 1) * bit
    return out


def start_kernel(orders, wheres, me, *refs):
    arrays = len(wheres)
    ins, outs = refs[: 2 * arrays], refs[2 * arrays :]
    half = outs[0].shape[0]
    for g, order in enumerate(orders):
        for side in range(2):

            def one(r, carry, g=g, order=order, side=side):
                part = me[0] ^ distance(order, r + side * half)
                row = 0
                for kept, got, where in zip(ins[::2], ins[1::2], wheres, strict=True):
                    place = where(part, g)
                    size = kept.shape[1]
                    total = kept[place].astype(f32) + got[place].astype(f32)
                    outs[g * 2 + side][r, row : row + size, :] = total.astype(bf16)
                    row += size
                return carry

            lax.fori_loop(0, half, one, 0)


def start_sum(me, kept, got, wheres, orders):
    count = 1 << len(orders[0])
    half = count // 2
    rows = sum(a.shape[1] for a in kept)
    width = kept[0].shape[2]
    cols = width // 3
    block = lambda a: pl.BlockSpec((a.shape[0], a.shape[1], cols), lambda c: (0, 0, c))
    out = pl.BlockSpec((half, rows, cols), lambda c: (0, 0, c))
    args = [a for pair in zip(kept, got, strict=True) for a in pair]
    outs = pl.pallas_call(
        functools.partial(start_kernel, orders, wheres),
        grid=(width // cols,),
        in_specs=[SMEM] + [block(a) for a in args],
        out_specs=[out] * (2 * GROUPS),
        out_shape=[shape((half, rows, width), bf16)] * (2 * GROUPS),
        compiler_params=params(30),
        cost_estimate=COST,
        name="start_sum",
    )(me, *args)
    return outs[0::2], outs[1::2]


IN_VMEM = pl.BlockSpec(memory_space=pltpu.VMEM)


def step_kernel(*refs):
    half = refs[0].shape[0] // 2
    kept, got = refs[:GROUPS], refs[GROUPS : 2 * GROUPS]
    outs = refs[len(refs) - 2 * GROUPS - len(refs) % 2 :]
    for g in range(GROUPS):
        total = (kept[g][...].astype(f32) + got[g][...].astype(f32)).astype(bf16)
        outs[2 * g][...] = total[:half]
        outs[2 * g + 1][...] = total[half:]
    if len(refs) % 2:
        outs[-1][...] = refs[2 * GROUPS][...] + refs[2 * GROUPS + 1][...]


def step_sum(kept, got, small):
    count, rows, width = kept[0].shape
    args = [*kept, *got, *small]
    outs = pl.pallas_call(
        step_kernel,
        in_specs=[IN_VMEM] * len(args),
        out_specs=[IN_VMEM] * (2 * GROUPS + len(small) // 2),
        out_shape=[shape((count // 2, rows, width), bf16)] * (2 * GROUPS)
        + [shape(a.shape, f32) for a in small[:1]],
        compiler_params=params(16),
        cost_estimate=COST,
        name="step_sum",
    )(*args)
    return outs[0 : 2 * GROUPS : 2], outs[1 : 2 * GROUPS : 2], list(outs[2 * GROUPS :])


def feed_end_kernel(*refs):
    ins, (down, up, out) = refs[: 2 * GROUPS], refs[2 * GROUPS :]
    tall, few = down.shape[0] // GROUPS, out.shape[0] // GROUPS
    ups = []
    for g in range(GROUPS):
        total = ins[g][0].astype(f32) + ins[GROUPS + g][0].astype(f32)
        down[g * tall : (g + 1) * tall, :] = total[:tall]
        ups.append(total[tall : 2 * tall])
        out[g * few : (g + 1) * few, :] = total[2 * tall :]
    up[...] = jnp.concatenate(ups, axis=0).T


def feed_end(kept, got, tall, few):
    width = kept[0].shape[2]
    return pl.pallas_call(
        feed_end_kernel,
        in_specs=[IN_VMEM] * (2 * GROUPS),
        out_specs=[IN_VMEM] * 3,
        out_shape=[shape((tall, width), f32), shape((width, tall), f32), shape((few, width), f32)],
        compiler_params=params(16),
        cost_estimate=COST,
        name="feed_end",
    )(*kept, *got)


def qkv_end_kernel(*refs):
    ins, small, (out, sums) = refs[: 2 * GROUPS], refs[2 * GROUPS : 2 * GROUPS + 2], refs[2 * GROUPS + 2 :]
    tall = out.shape[0]
    cols = ins[0].shape[2]
    for g in range(GROUPS):
        total = ins[g][0].astype(f32) + ins[GROUPS + g][0].astype(f32)
        for part in range(total.shape[0] // tall):
            at = (2 * g + part) * cols
            out[:, at : at + cols] = total[part * tall : (part + 1) * tall]
    sums[...] = small[0][...] + small[1][...]


def qkv_end(kept, got, small, tall, wide):
    return pl.pallas_call(
        qkv_end_kernel,
        in_specs=[IN_VMEM] * (2 * GROUPS + 2),
        out_specs=[IN_VMEM] * 2,
        out_shape=[shape((tall, wide), f32), shape(small[0].shape, f32)],
        compiler_params=params(16),
        cost_estimate=COST,
        name="qkv_end",
    )(*kept, *got, *small)


def after(value, *earlier):
    return lax.optimization_barrier((value, earlier))[0]


def sum_parts(me, kept, got, wheres, small):
    orders = bit_orders(lax.axis_size("batch"))
    keep, send = start_sum(me, kept, got, wheres, orders)
    for i in range(len(orders[0])):
        got = [exchange(s, "batch", order[i]) for s, order in zip(send, orders, strict=True)]
        small = [small[0], exchange(small[0], "batch", orders[0][i])] if small else []
        if i == len(orders[0]) - 1:
            break
        earlier = yield send[0]
        if earlier is not None:
            keep = after(list(keep), earlier)
        keep, send, small = step_sum(keep, got, small)
    yield keep, got, small


def on_device(
    inputs, lengths, cotangent, qkv_weight, out_weight, up_weight, down_weight, attn_gain, mlp_gain
):
    seq, width = inputs.shape[2:]
    x = inputs[0, 0]
    dy = cotangent[0, 0]
    count = lax.axis_size("batch")
    stream = lax.axis_index("stream").astype(jnp.int32)
    me = lax.axis_index("batch").astype(jnp.int32).reshape(1)
    info = jnp.stack([stream, lengths[0]])
    gain1, gain2 = attn_gain.reshape(1, width), mlp_gain.reshape(1, width)
    cosine, sine = rotary_tables(seq)
    tables = (
        jnp.asarray(np.concatenate([cosine] * 4, axis=1)),
        jnp.asarray(np.concatenate([-sine, sine] * 2, axis=1)),
    )
    tables_t = (jnp.asarray(cosine.T), jnp.asarray(sine.T))

    received = lax.ppermute(x, "stream", [(0, 1)])
    q, ko, vo, h1t, sums_x = project(info, x, gain1, qkv_weight, tables)
    (
        kc, vc, o, lse, outputs, dx2, do,
        up_send, up_keep, down_send, down_keep, out_send, out_keep, sums_m,
    ) = layer(
        info, x, received, gain1, gain2, qkv_weight, tables, q, ko, vo, out_weight, dy, up_weight, down_weight
    )
    down_got, up_got, out_got = (exchange(a, "stream", 1) for a in (down_send, up_send, out_send))

    def by_rows(array):
        return array.reshape(count * GROUPS, array.shape[0] // (count * GROUPS), width)

    heads = (q, ko, vo, kc, vc, o, do, lse, *tables_t)
    pairs = width // PW // 2
    dq1, keep1, send1 = attend_back(info, 0, pairs, *heads)
    got1 = lax.ppermute(send1, "stream", [(1, 0)])
    early = sum_parts(
        me,
        [by_rows(after(a, dq1)) for a in (down_keep, up_keep, out_keep)],
        [by_rows(a) for a in (down_got, up_got, out_got)],
        [lambda part, g: part * GROUPS + g] * 3,
        [],
    )
    token = next(early)
    dq2, keep2, send2 = attend_back(info, pairs, pairs, q, ko, vo, kc, vc, o, after(do, token), lse, *tables_t)
    got2 = lax.ppermute(send2, "stream", [(1, 0)])
    token = early.send(dq2)
    dkv1, qkv_send1, qkv_keep1 = weigh(info, (dq1, after(keep1, token)), got1, tables, h1t)
    qkv_got1 = exchange(qkv_send1, "stream", 1)
    dkv2, qkv_send2, qkv_keep2 = weigh(info, (dq2, after(keep2, dkv1)), got2, tables, h1t)
    qkv_got2 = exchange(qkv_send2, "stream", 1)
    token = early.send(dkv2)
    dx, sums_h = finish(after(x, token), dx2, [dq1, dq2], [dkv1, dkv2], qkv_weight, gain1)

    small = jnp.concatenate(
        [
            sums_x[:1],
            sums_m[:3],
            sums_h[:1],
            jnp.full((1, width), lengths[0].astype(f32)),
            jnp.zeros((2, width), f32),
        ]
    )
    small_got = exchange(small, "stream", 1)
    tall = width // (2 * count)
    split = lambda a: a.reshape(GROUPS * count, tall, a.shape[2])
    late = sum_parts(
        me,
        [split(after(a, small)) for a in (qkv_keep1, qkv_keep2)],
        [split(a) for a in (qkv_got1, qkv_got2)],
        [lambda part, g: g * count + part] * 2,
        [small + small_got],
    )
    token = next(late)
    token = early.send(token)
    out = late.send(token if isinstance(token, jax.Array) else None)
    ends = token
    while not isinstance(ends, tuple):
        ends = early.send(out)
        if not isinstance(out, tuple):
            out = late.send(None if isinstance(ends, tuple) else ends)
    while not isinstance(out, tuple):
        out = late.send(None)
    up_cols = down_keep.shape[0] // count
    down_grad, up_grad, out_grad = feed_end(ends[0], ends[1], up_cols, tall)
    qkv_grad, small = qkv_end(*out, tall, 3 * width)

    squares = jnp.sum(small[:3], axis=1)
    rms = jnp.sqrt(squares / (small[5, 0] * width))
    return (
        outputs[None, None],
        dx[None, None],
        qkv_grad,
        out_grad,
        up_grad,
        down_grad,
        small[4],
        small[3],
        rms,
    )


def solution(mesh):
    rows = P("stream", "batch", None, None)
    both = ("stream", "batch")
    return jax.shard_map(
        on_device,
        mesh=mesh,
        in_specs=(rows, P("batch"), rows, P(), P(), P(), P(), P(), P()),
        out_specs=(rows, rows, P(both, None), P(both, None), P(None, both), P(both, None), P(), P(), P()),
        check_vma=False,
    )
```

```python
import functools

import jax
import jax.numpy as jnp
import numpy as np
from jax import lax
from jax.experimental import pallas as pl
from jax.experimental.pallas import tpu as pltpu
from jax.sharding import PartitionSpec as P

f32 = jnp.float32
bf16 = jnp.bfloat16

HD = 64
BLK = 16
EPS = 1e-06
NEG = -1e30
PW = 2 * HD
T = 128
R = 256
AHEAD = 2
FC = 512
SCALE = HD**-0.5
BIG = 60
GROUPS = 3

COST = pl.CostEstimate(flops=1 << 20, bytes_accessed=1 << 16, transcendentals=0)
LONG = pl.CostEstimate(flops=1 << 35, bytes_accessed=1 << 26, transcendentals=0)

SMEM = pl.BlockSpec(memory_space=pltpu.SMEM)
IN_VMEM = pl.BlockSpec(memory_space=pltpu.VMEM)


def params(mib):
    return pltpu.CompilerParams(vmem_limit_bytes=mib << 20)


def shape(dims, dtype):
    return jax.ShapeDtypeStruct(dims, dtype)


def pinned(*arrays):
    return [pltpu.with_memory_space_constraint(a, pltpu.HBM) for a in arrays]


def nn(a, b):
    return jnp.dot(a, b, preferred_element_type=f32)


def nt(a, b):
    return lax.dot_general(a, b, (((1,), (1,)), ((), ())), preferred_element_type=f32)


def tn(a, b):
    return lax.dot_general(a, b, (((0,), (0,)), ((), ())), preferred_element_type=f32)


def whole(dims):
    return pl.BlockSpec(dims, lambda *_: (0,) * len(dims), pipeline_mode=pl.Buffered(1))


def inv_rms(v):
    return lax.rsqrt(jnp.mean(v * v, axis=-1, keepdims=True) + EPS)


def norm_back(v, gain, grad):
    r = inv_rms(v)
    unit = v * r
    scaled = grad * gain
    inner = jnp.mean(scaled * unit, axis=-1, keepdims=True)
    return r * (scaled - unit * inner), grad * unit


def rotary_tables(length):
    half = HD // 2
    freqs = np.exp(-np.log(10000.0) * np.arange(half) / half).astype(np.float32)
    angles = (np.arange(length, dtype=np.float32)[:, None] * freqs[None, :]).astype(np.float64)
    return np.cos(angles).astype(np.float32), np.sin(angles).astype(np.float32)


def rotated(v, cosine, signed, sign):
    first = lax.broadcasted_iota(jnp.int32, (1, PW), 1) % HD < HD // 2
    outs = []
    for c in range(0, v.shape[1], PW):
        part = v[:, c : c + PW]
        partner = jnp.where(first, pltpu.roll(part, PW - HD // 2, 1), pltpu.roll(part, HD // 2, 1))
        outs.append(part * cosine + partner * (signed * sign))
    return outs[0] if len(outs) == 1 else jnp.concatenate(outs, axis=1)


def token_weight(start, length, rows):
    return lax.broadcasted_iota(jnp.int32, (rows, 1), 0) + start < length


def row_sum(v):
    return jnp.sum(v, axis=0, keepdims=True)


def by_pairs(ref, rows, value):
    for p in range(ref.shape[0]):
        ref[p, rows, :] = value[:, p * PW : (p + 1) * PW].astype(ref.dtype)


def project_kernel(info, x, gain, wq, wk, wv, cosine, signed, q, k, v, h1t, sums):
    at = pl.program_id(0)

    @pl.when(at == 0)
    def _():
        sums[...] = jnp.zeros_like(sums)

    value = x[...].astype(f32)
    h1 = (value * inv_rms(value) * gain[...]).astype(bf16)
    by_pairs(q, slice(None), rotated(nn(h1, wq[...]), cosine[...], signed[...], 1.0))
    by_pairs(k, slice(None), rotated(nn(h1, wk[...]), cosine[...], signed[...], 1.0))
    by_pairs(v, slice(None), nn(h1, wv[...]))
    h1t[...] = h1.T
    weight = token_weight(at * R, info[1], R)
    sums[0:1, :] += row_sum(jnp.where(weight, value * value, 0.0))


def project(info, x, gain, weight, tables):
    seq, width = x.shape
    rows = pl.BlockSpec((R, width), lambda i: (i, 0))
    table = pl.BlockSpec((R, PW), lambda i: (i, 0))
    heads = pl.BlockSpec((width // PW, R, PW), lambda i: (0, i, 0))
    third = lambda c: pl.BlockSpec((width, width), lambda i: (0, c), pipeline_mode=pl.Buffered(1))
    return pl.pallas_call(
        project_kernel,
        grid=(seq // R,),
        in_specs=[SMEM, rows, whole((1, width)), third(0), third(1), third(2), table, table],
        out_specs=[heads, heads, heads, pl.BlockSpec((width, R), lambda i: (0, i)), whole((8, width))],
        out_shape=[shape((width // PW, seq, PW), bf16)] * 3 + [shape((width, seq), bf16), shape((8, width), f32)],
        compiler_params=params(BIG),
        cost_estimate=LONG,
        name="project",
    )(info, *pinned(x), gain, *pinned(weight, weight, weight, *tables))


def stacked(tile, low):
    zero = jnp.zeros_like(tile)
    return jnp.concatenate([jnp.where(low, tile, zero), jnp.where(low, zero, tile)], axis=0)


def unstacked(tile_t):
    half = lax.broadcasted_iota(jnp.int32, (PW, 1), 0) < HD
    return jnp.where(half, tile_t[:, :T], tile_t[:, T:])


def chunks_of(i):
    out, j = [], 0
    while j < i:
        n = 2 if i - j >= 2 else 1
        out.append((j * T, n * T))
        j += n
    return out


def edge_bias(ref, noisy):
    row = lax.broadcasted_iota(jnp.int32, (T, 2 * T), 0) // BLK
    col = (lax.broadcasted_iota(jnp.int32, (T, 2 * T), 1) % T) // BLK
    own = jnp.logical_or(row == col, jnp.logical_and(row < col, noisy == 0))
    other = jnp.logical_and(row < col, noisy == 1)
    ref[:T, :] = jnp.where(own, 0.0, NEG)
    ref[T:, :] = jnp.where(other, 0.0, NEG)


def masked(s, start, length):
    pos = lax.broadcasted_iota(jnp.int32, s.shape, 0) + start
    return jnp.where(pos < length, s, NEG)


def over_rows(op, v):
    return op(v.reshape(v.shape[0] // 8, 8, v.shape[1]), axis=0)


def attend_pair(length, q, ko, vo, kc, vc, store, lse, vo_t, vc_t, scores, bias):
    seq = q.shape[0]
    low = lax.broadcasted_iota(jnp.int32, (1, PW), 1) < HD
    vo_t[...] = vo[...].T
    vc_t[...] = vc[...].T

    def score(i):
        at = pl.ds(i * T, T)
        q2 = stacked(q[at, :] * bf16(SCALE), low)
        buf = scores.at[i % AHEAD]
        edge = nt(jnp.concatenate([ko[at, :], kc[at, :]], 0), q2) + bias[...]
        own = masked(edge[:T], i * T, length)
        other = masked(edge[T:], i * T, length)
        buf[pl.ds(0, T), :] = own
        buf[pl.ds(T, T), :] = other
        top = over_rows(jnp.max, jnp.maximum(own, other))
        for start, size in chunks_of(i):
            s = masked(nt(kc[pl.ds(start, size), :], q2), start, length)
            buf[pl.ds(2 * T + start, size), :] = s
            top = jnp.maximum(top, over_rows(jnp.max, s))
        return jnp.max(top, axis=0, keepdims=True)

    def mix(i, top):
        at = pl.ds(i * T, T)
        buf = scores.at[i % AHEAD]
        p = jnp.exp(buf[pl.ds(0, 2 * T), :] - top)
        total = over_rows(jnp.sum, p)
        acc = nn(jnp.concatenate([vo_t[:, at], vc_t[:, at]], 1), p.astype(bf16))
        for start, size in chunks_of(i):
            p = jnp.exp(buf[pl.ds(2 * T + start, size), :] - top)
            total = total + over_rows(jnp.sum, p)
            acc = acc + nn(vc_t[:, pl.ds(start, size)], p.astype(bf16))
        total = row_sum(total)
        lse[0, pl.ds(i, 1), :] = top + jnp.log(total)
        store(at, unstacked(acc * (1.0 / total)))

    tops = {}
    for i in range(seq // T + AHEAD - 1):
        if i < seq // T:
            tops[i] = score(i)
        if i >= AHEAD - 1:
            mix(i - AHEAD + 1, tops.pop(i - AHEAD + 1))


def turned_back(v, cosine, sine):
    quarter = HD // 2
    a, b, c, d = (v[i * quarter : (i + 1) * quarter] for i in range(4))
    return jnp.concatenate(
        [a * cosine + b * sine, b * cosine - a * sine, c * cosine + d * sine, d * cosine - c * sine]
    )


def attend_back_kernel(
    info, q, ko, vo, kc, vc, o, do, lse, cosine, sine, dq, keep, send, ko_t, kc_t, dko, dvo, dkc, dvc, bias
):
    noisy, length = info[0], info[1]
    q, ko, vo, kc, vc = (ref.at[0] for ref in (q, ko, vo, kc, vc))
    seq = q.shape[0]
    low = lax.broadcasted_iota(jnp.int32, (1, PW), 1) < HD

    @pl.when(pl.program_id(0) == 0)
    def _():
        edge_bias(bias, noisy)

    ko_t[...] = ko[...].T
    kc_t[...] = kc[...].T

    def tile(i):
        at = pl.ds(i * T, T)
        prod = (do[at, :].astype(f32) * o[at, :].astype(f32)).T
        delta = jnp.concatenate([row_sum(prod[:HD]), row_sum(prod[HD:])], 1)
        q2 = stacked(q[at, :] * bf16(SCALE), low)
        return q2, stacked(do[at, :], low), lse[0, pl.ds(i, 1), :], delta

    def products(i, start, size, q2, do2):
        if start is None:
            at = pl.ds(i * T, T)
            s = nt(jnp.concatenate([ko[at, :], kc[at, :]], 0), q2) + bias[...]
            s = jnp.concatenate([masked(s[:T], i * T, length), masked(s[T:], i * T, length)], 0)
            return s, nt(jnp.concatenate([vo[at, :], vc[at, :]], 0), do2)
        rows = pl.ds(start, size)
        return masked(nt(kc[rows, :], q2), start, length), nt(vc[rows, :], do2)

    def gather(i, start, size, q2, do2, p, ds, dq_t):
        at = pl.ds(i * T, T)
        dv, dk = nn(p, do2), nn(ds, q2)
        if start is None:
            dvo[at, :] = dv[:T]
            dko[at, :] = dk[:T]
            dvc[at, :] = dv[T:]
            dkc[at, :] = dk[T:]
            return nn(jnp.concatenate([ko_t[:, at], kc_t[:, at]], 1), ds)
        rows = pl.ds(start, size)
        dvc[rows, :] += dv
        dkc[rows, :] += dk
        return dq_t + nn(kc_t[:, rows], ds)

    work = [(i, *c) for i in range(seq // T) for c in [(None, None)] + chunks_of(i)]
    tiles, made, weighed, dq_t = {}, {}, {}, None
    for n in range(len(work) + 2):
        if n < len(work):
            i = work[n][0]
            if i not in tiles:
                tiles[i] = tile(i)
            made[n] = products(*work[n], *tiles[i][:2])
        if 0 <= n - 1 < len(work):
            _, _, norm, delta = tiles[work[n - 1][0]]
            s, dp = made.pop(n - 1)
            p = jnp.exp(s - norm)
            weighed[n - 1] = p.astype(bf16), (p * (dp - delta)).astype(bf16)
        if n >= 2:
            i, start, size = work[n - 2]
            dq_t = gather(i, start, size, *tiles[i][:2], *weighed.pop(n - 2), dq_t)
            if n == len(work) + 1 or work[n - 1][0] != i:
                at = pl.ds(i * T, T)
                out = turned_back(unstacked(dq_t), cosine[:, at], sine[:, at]) * SCALE
                dq[at, :] = out.T.astype(bf16)
    clean = (1 - noisy).astype(f32)
    for at, own, other in ((0, dko, dkc), (1, dvo, dvc)):
        keep[at] = (own[...] + clean * other[...]).astype(bf16)
        send[at] = other[...].astype(bf16)


def attend_back(info, first, pairs, q, ko, vo, kc, vc, o, do, lse, cosine, sine):
    seq = q.shape[1]
    width = pairs * PW
    heads = pl.BlockSpec((1, seq, PW), lambda h: (first + h, 0, 0))
    source = pl.BlockSpec((seq, PW), lambda h: (0, first + h))
    both = pl.BlockSpec((2, seq, PW), lambda h: (0, 0, h))
    lines = pl.BlockSpec((1, seq // T, 2 * T), lambda h: (first + h, 0, 0))
    table = whole((HD // 2, seq))
    return pl.pallas_call(
        attend_back_kernel,
        grid=(pairs,),
        in_specs=[SMEM] + [heads] * 5 + [source] * 2 + [lines, table, table],
        out_specs=[pl.BlockSpec((seq, PW), lambda h: (0, h)), both, both],
        out_shape=[shape((seq, width), bf16)] + [shape((2, seq, width), bf16)] * 2,
        scratch_shapes=[pltpu.VMEM((PW, seq), bf16)] * 2
        + [pltpu.VMEM((seq, PW), f32)] * 4
        + [pltpu.VMEM((2 * T, 2 * T), f32)],
        compiler_params=params(24),
        cost_estimate=LONG,
        name="attend_back",
    )(info, *pinned(q, ko, vo, kc, vc, o, do), lse, cosine, sine)


C0 = 0.7978845608028654
C1 = C0 * 0.044715


def layer_kernel(
    info, gain1, gain2, x_any, received_any, wqkv_any, cosine_any, signed_any, q_any, ko_any, vo_any, wo_any,
    dy_any, w1_any, w2_any,
    kc_out, vc_out, o_out, lse_out, out_any, dx2_any, do_any,
    up_send, up_keep, down_send, down_keep, g_send, g_keep, sums,
    x, received, wkv, cosine, signed, q, ko, vo, wo, dy, w1, w2,
    kc, vc, vo_t, vc_t, scores, bias, o, o_t, lse, x2, h2, m, dh, act, du, up_grad, down_grad, half_grads,
    sem_in, sem_1, sem_2, sem_out, sem_up, sem_down, sem_tile,
):
    noisy, length = info[0], info[1]
    seq, width = x.shape
    chunks, pairs, tiles = w1.shape[0], kc.shape[0], seq // R
    copy = pltpu.make_async_copy

    def weights(c):
        place = lax.rem(c + (chunks // 2) * (1 - noisy), chunks) * FC
        place = pl.multiple_of(place, FC)
        return (
            copy(w1_any.at[:, pl.ds(place, FC)], w1.at[c], sem_1.at[c]),
            copy(w2_any.at[pl.ds(place, FC), :], w2.at[c], sem_2.at[c]),
        )

    sources = (
        (x_any, x),
        (received_any, received),
        (wqkv_any.at[:, pl.ds(width, 2 * width)], wkv),
        (cosine_any, cosine),
        (signed_any, signed),
        (q_any, q),
        (ko_any, ko),
        (vo_any, vo),
        (wo_any, wo),
        (dy_any, dy),
    )
    loads = [copy(a, b, sem_in.at[i]) for i, (a, b) in enumerate(sources)]
    for load in loads[:5]:
        load.start()
    sums[...] = jnp.zeros_like(sums)

    for load in loads[:5]:
        load.wait()
    for load in loads[5:]:
        load.start()

    def clean_rows(t, carry):
        rows = pl.ds(pl.multiple_of(t * R, R), R)
        value = jnp.where(noisy == 1, received[rows, :].astype(f32), x[rows, :].astype(f32))
        h1 = (value * inv_rms(value) * gain1[...]).astype(bf16)
        kv = nn(h1, wkv[...])
        by_pairs(kc, rows, rotated(kv[:, :width], cosine[rows, :], signed[rows, :], 1.0))
        by_pairs(vc, rows, kv[:, width:])
        return carry

    lax.fori_loop(0, tiles, clean_rows, 0)
    stores = [copy(kc, kc_out, sem_out.at[0]), copy(vc, vc_out, sem_out.at[1])]
    for store in stores:
        store.start()

    edge_bias(bias, noisy)
    for load in loads[5:8]:
        load.wait()
    for c in range(chunks):
        for load in weights(c):
            load.start()

    def one_pair(p, carry):
        lanes = pl.ds(pl.multiple_of(p * PW, PW), PW)

        def keep(at, tile_t):
            o_t[lanes, at] = tile_t.astype(bf16)
            o[at, lanes] = tile_t.T.astype(bf16)

        heads = (ref.at[p] for ref in (q, ko, vo, kc, vc))
        attend_pair(length, *heads, keep, lse.at[pl.ds(p, 1)], vo_t, vc_t, scores, bias)
        return carry

    lax.fori_loop(0, pairs, one_pair, 0)
    more = [copy(o, o_out, sem_out.at[2]), copy(lse, lse_out, sem_out.at[3])]
    for store in more:
        store.start()
    stores += more

    for load in loads[8:]:
        load.wait()

    def joined_rows(t, carry):
        start = pl.multiple_of(t * R, R)
        rows = pl.ds(start, R)
        branch = nn(o[rows, :], wo[...])
        value = x[rows, :].astype(f32) + branch
        x2[rows, :] = value
        h2[rows, :] = (value * inv_rms(value) * gain2[...]).astype(bf16)
        m[rows, :] = jnp.zeros_like(value)
        dh[rows, :] = jnp.zeros_like(value)
        weight = token_weight(start, length, R)
        sums[0:1, :] += row_sum(jnp.where(weight, branch * branch, 0.0))
        return carry

    lax.fori_loop(0, tiles, joined_rows, 0)

    def grad_stores(c, up, down):
        slot = lax.rem(c, 2)
        rows = pl.ds(pl.multiple_of(lax.rem(c, chunks // 2) * FC, FC), FC)
        return (
            copy(up_grad.at[slot], up.at[rows, :], sem_up.at[slot]),
            copy(down_grad.at[slot], down.at[rows, :], sem_down.at[slot]),
        )

    def one_chunk(c, carry):
        for load in weights(c):
            load.wait()
        up, down = w1.at[c], w2.at[c]
        for t in range(0, seq, R):
            rows = pl.ds(t, R)
            u = nn(h2[rows, :], up[...])
            da = nt(dy[rows, :], down[...])
            sq = u * u
            half = 0.5 * jnp.tanh(u * (C0 + C1 * sq)) + 0.5
            low = (u * half).astype(bf16)
            slope = half + u * (2.0 * half * (1.0 - half)) * (C0 + 3.0 * C1 * sq)
            back = (da * slope).astype(bf16)
            act[rows, :] = low
            du[rows, :] = back
            m[rows, :] += nn(low, down[...])
            dh[rows, :] += nt(back, up[...])

        @pl.when(c >= 2)
        def _():
            for store in grad_stores(c, up_send, down_send):
                store.wait()

        slot = lax.rem(c, 2)
        down_grad[slot] = tn(act[...], dy[...]).astype(bf16)
        up_grad[slot] = tn(du[...], h2[...]).astype(bf16)

        @pl.when(c < chunks // 2)
        def _():
            for store in grad_stores(c, up_send, down_send):
                store.start()

        @pl.when(c >= chunks // 2)
        def _():
            for store in grad_stores(c, up_keep, down_keep):
                store.start()

        return carry

    lax.fori_loop(0, chunks, one_chunk, 0)

    def tile_stores(t):
        rows = pl.ds(pl.multiple_of(t * R, R), R)
        return (
            copy(h2.at[rows, :], out_any.at[rows, :], sem_tile.at[t, 0]),
            copy(x2.at[rows, :], dx2_any.at[rows, :], sem_tile.at[t, 1]),
            copy(received.at[rows, :], do_any.at[rows, :], sem_tile.at[t, 2]),
        )

    def middle_rows(t, carry):
        start = pl.multiple_of(t * R, R)
        rows = pl.ds(start, R)
        value = x2[rows, :]
        mixed = m[rows, :]
        weight = token_weight(start, length, R)
        sums[1:2, :] += row_sum(jnp.where(weight, mixed * mixed, 0.0))
        grad, gain_terms = norm_back(value, gain2[...], dh[rows, :])
        sums[2:3, :] += row_sum(gain_terms)
        grad = grad + dy[rows, :].astype(f32)
        da = grad.astype(bf16)
        h2[rows, :] = (value + mixed).astype(bf16)
        x2[rows, :] = grad
        received[rows, :] = nt(da, wo[...]).astype(bf16)
        x[rows, :] = da
        for store in tile_stores(t):
            store.start()
        return carry

    lax.fori_loop(0, tiles, middle_rows, 0)
    half = width // 2
    mine = pl.multiple_of(noisy * half, half)
    half_grads[0] = nn(o_t[pl.ds(half - mine, half), :], x[...]).astype(bf16)
    half_grads[1] = nn(o_t[pl.ds(mine, half), :], x[...]).astype(bf16)
    more = [copy(half_grads.at[0], g_send, sem_out.at[4]), copy(half_grads.at[1], g_keep, sem_out.at[5])]
    for store in more:
        store.start()
    stores += more
    for c in range(chunks - 2, chunks):
        stores += grad_stores(c, up_keep, down_keep)
    for t in range(tiles):
        stores += tile_stores(t)
    for store in stores:
        store.wait()


def layer(info, x, received, gain1, gain2, wqkv, tables, q, ko, vo, wo, dy, w1, w2):
    seq, width = x.shape
    hidden = w1.shape[1]
    tiles, pairs, chunks = seq // R, width // PW, hidden // FC
    anywhere = pl.BlockSpec(memory_space=pl.ANY)
    vmem = pltpu.VMEM
    dma = pltpu.SemaphoreType.DMA
    heads = (pairs, seq, PW)
    outs = (
        [shape(heads, bf16)] * 2
        + [shape((seq, width), bf16), shape((pairs, seq // T, 2 * T), f32)]
        + [shape((seq, width), bf16), shape((seq, width), f32), shape((seq, width), bf16)]
        + [shape((hidden // 2, width), bf16)] * 4
        + [shape((width // 2, width), bf16)] * 2
        + [shape((8, width), f32)]
    )
    return pl.pallas_call(
        layer_kernel,
        in_specs=[SMEM, IN_VMEM, IN_VMEM] + [anywhere] * 12,
        out_specs=[anywhere] * 13 + [IN_VMEM],
        out_shape=outs,
        scratch_shapes=[vmem((seq, width), bf16)] * 2
        + [vmem((width, 2 * width), bf16), vmem((seq, PW), f32), vmem((seq, PW), f32)]
        + [vmem(heads, bf16)] * 3
        + [vmem((width, width), bf16), vmem((seq, width), bf16)]
        + [vmem((chunks, width, FC), bf16), vmem((chunks, FC, width), bf16)]
        + [vmem(heads, bf16)] * 2
        + [vmem((PW, seq), bf16)] * 2
        + [vmem((AHEAD, seq + T, 2 * T), f32), vmem((2 * T, 2 * T), f32)]
        + [vmem((seq, width), bf16), vmem((width, seq), bf16)]
        + [vmem((pairs, seq // T, 2 * T), f32)]
        + [vmem((seq, width), f32), vmem((seq, width), bf16)]
        + [vmem((seq, width), f32)] * 2
        + [vmem((seq, FC), bf16)] * 2
        + [vmem((2, FC, width), bf16)] * 2
        + [vmem((2, width // 2, width), bf16)]
        + [dma((10,)), dma((chunks,)), dma((chunks,)), dma((6,)), dma((2,)), dma((2,)), dma((tiles, 3))],
        compiler_params=params(BIG),
        cost_estimate=LONG,
        name="layer",
    )(info, gain1, gain2, *pinned(x, received, wqkv, *tables, q, ko, vo, wo, dy, w1, w2))


def weigh_kernel(info, dq, keep, got, cosine, signed, h1t, dkv, g_send, g_keep):
    half = h1t.shape[0] // 2
    mine = pl.multiple_of(info[0] * half, half)
    dk = keep[0].astype(f32) + got[0].astype(f32)
    dk = rotated(dk, cosine[...], signed[...], -1.0).astype(bf16)
    dv = (keep[1].astype(f32) + got[1].astype(f32)).astype(bf16)
    dkv[0] = dk
    dkv[1] = dv
    grads = jnp.concatenate([dq[...], dk, dv], axis=1)
    for out, start in ((g_send, half - mine), (g_keep, mine)):
        total = nn(h1t[pl.ds(start, half), :], grads).astype(bf16)
        for i in range(3):
            out[i] = total[:, i * PW : (i + 1) * PW]


def weigh(info, piece, got, tables, h1t):
    dq, keep = piece
    seq, width = dq.shape
    tall = h1t.shape[0]
    both = pl.BlockSpec((2, seq, PW), lambda h: (0, 0, h))
    table = whole((seq, PW))
    half = pl.BlockSpec((3, tall // 2, PW), lambda h: (0, 0, h))
    return pl.pallas_call(
        weigh_kernel,
        grid=(width // PW,),
        in_specs=[SMEM, pl.BlockSpec((seq, PW), lambda h: (0, h)), both, both, table, table, whole((tall, seq))],
        out_specs=[both, half, half],
        out_shape=[shape((2, seq, width), bf16)] + [shape((3, tall // 2, width), bf16)] * 2,
        compiler_params=params(24),
        cost_estimate=LONG,
        name="weigh",
    )(info, *pinned(dq, keep), got, *pinned(*tables, h1t))


def finish_kernel(parts, x, dx2, wqkv, gain, *refs):
    dx, sums = refs[-2:]

    @pl.when(pl.program_id(0) == 0)
    def _():
        sums[...] = jnp.zeros_like(sums)

    dqs, dkvs = refs[:parts], refs[parts : 2 * parts]
    grads = [r[...] for r in dqs] + [r[0] for r in dkvs] + [r[1] for r in dkvs]
    dh = nt(jnp.concatenate(grads, axis=1), wqkv[...])
    grad, gain_terms = norm_back(x[...].astype(f32), gain[...], dh)
    sums[0:1, :] += row_sum(gain_terms)
    dx[...] = (dx2[...] + grad).astype(bf16)


def finish(x, dx2, dqs, dkvs, weight, gain):
    seq, width = x.shape
    rows = pl.BlockSpec((R, width), lambda i: (i, 0))
    return pl.pallas_call(
        functools.partial(finish_kernel, len(dqs)),
        grid=(seq // R,),
        in_specs=[rows, rows, whole(weight.shape), whole((1, width))]
        + [pl.BlockSpec((R, a.shape[1]), lambda i: (i, 0)) for a in dqs]
        + [pl.BlockSpec((2, R, a.shape[2]), lambda i: (0, i, 0)) for a in dkvs],
        out_specs=[rows, whole((8, width))],
        out_shape=[shape((seq, width), bf16), shape((8, width), f32)],
        compiler_params=params(24),
        cost_estimate=LONG,
        name="finish",
    )(*pinned(x, dx2, weight), gain, *pinned(*dqs, *dkvs))


def bit_orders(count):
    bits = [1 << i for i in range(count.bit_length() - 1)]
    if len(bits) == 4:
        x, y, z, far = bits
        return [(x, y, z, far), (y, x, z, far), (z, x, far, y)]
    return [tuple(bits[g:] + bits[:g]) for g in range(GROUPS)]


def exchange(value, axis, bit):
    size = lax.axis_size(axis)
    return lax.ppermute(value, axis, [(i, i ^ bit) for i in range(size)])


def distance(order, place):
    out = 0
    for i, bit in enumerate(order):
        out = out + ((place >> (len(order) - 1 - i)) & 1) * bit
    return out


def start_kernel(orders, wheres, me, *refs):
    arrays = len(wheres)
    ins, outs = refs[: 2 * arrays], refs[2 * arrays :]
    half = outs[0].shape[0]
    for g, order in enumerate(orders):
        for side in range(2):

            def one(r, carry, g=g, order=order, side=side):
                part = me[0] ^ distance(order, r + side * half)
                row = 0
                for kept, got, where in zip(ins[::2], ins[1::2], wheres, strict=True):
                    place = where(part, g)
                    size = kept.shape[1]
                    total = kept[place].astype(f32) + got[place].astype(f32)
                    outs[g * 2 + side][r, row : row + size, :] = total.astype(bf16)
                    row += size
                return carry

            lax.fori_loop(0, half, one, 0)


def start_sum(me, kept, got, wheres, orders):
    count = 1 << len(orders[0])
    half = count // 2
    rows = sum(a.shape[1] for a in kept)
    width = kept[0].shape[2]
    cols = width // 3
    block = lambda a: pl.BlockSpec((a.shape[0], a.shape[1], cols), lambda c: (0, 0, c))
    out = pl.BlockSpec((half, rows, cols), lambda c: (0, 0, c))
    args = [a for pair in zip(kept, got, strict=True) for a in pair]
    outs = pl.pallas_call(
        functools.partial(start_kernel, orders, wheres),
        grid=(width // cols,),
        in_specs=[SMEM] + [block(a) for a in args],
        out_specs=[out] * (2 * GROUPS),
        out_shape=[shape((half, rows, width), bf16)] * (2 * GROUPS),
        compiler_params=params(30),
        cost_estimate=COST,
        name="start_sum",
    )(me, *args)
    return outs[0::2], outs[1::2]


def step_kernel(*refs):
    half = refs[0].shape[0] // 2
    kept, got = refs[:GROUPS], refs[GROUPS : 2 * GROUPS]
    outs = refs[len(refs) - 2 * GROUPS - len(refs) % 2 :]
    for g in range(GROUPS):
        total = (kept[g][...].astype(f32) + got[g][...].astype(f32)).astype(bf16)
        outs[2 * g][...] = total[:half]
        outs[2 * g + 1][...] = total[half:]
    if len(refs) % 2:
        outs[-1][...] = refs[2 * GROUPS][...] + refs[2 * GROUPS + 1][...]


def step_sum(kept, got, small):
    count, rows, width = kept[0].shape
    args = [*kept, *got, *small]
    outs = pl.pallas_call(
        step_kernel,
        in_specs=[IN_VMEM] * len(args),
        out_specs=[IN_VMEM] * (2 * GROUPS + len(small) // 2),
        out_shape=[shape((count // 2, rows, width), bf16)] * (2 * GROUPS)
        + [shape(a.shape, f32) for a in small[:1]],
        compiler_params=params(16),
        cost_estimate=COST,
        name="step_sum",
    )(*args)
    return outs[0 : 2 * GROUPS : 2], outs[1 : 2 * GROUPS : 2], list(outs[2 * GROUPS :])


def feed_end_kernel(*refs):
    ins, (down, up, out) = refs[: 2 * GROUPS], refs[2 * GROUPS :]
    tall, few = down.shape[0] // GROUPS, out.shape[0] // GROUPS
    ups = []
    for g in range(GROUPS):
        total = ins[g][0].astype(f32) + ins[GROUPS + g][0].astype(f32)
        down[g * tall : (g + 1) * tall, :] = total[:tall]
        ups.append(total[tall : 2 * tall])
        out[g * few : (g + 1) * few, :] = total[2 * tall :]
    up[...] = jnp.concatenate(ups, axis=0).T


def feed_end(kept, got, tall, few):
    width = kept[0].shape[2]
    return pl.pallas_call(
        feed_end_kernel,
        in_specs=[IN_VMEM] * (2 * GROUPS),
        out_specs=[IN_VMEM] * 3,
        out_shape=[shape((tall, width), f32), shape((width, tall), f32), shape((few, width), f32)],
        compiler_params=params(16),
        cost_estimate=COST,
        name="feed_end",
    )(*kept, *got)


def qkv_end_kernel(*refs):
    ins, small, (out, sums) = refs[: 2 * GROUPS], refs[2 * GROUPS : 2 * GROUPS + 2], refs[2 * GROUPS + 2 :]
    tall = out.shape[0]
    cols = ins[0].shape[2]
    for g in range(GROUPS):
        total = ins[g][0].astype(f32) + ins[GROUPS + g][0].astype(f32)
        for part in range(total.shape[0] // tall):
            at = (2 * g + part) * cols
            out[:, at : at + cols] = total[part * tall : (part + 1) * tall]
    sums[...] = small[0][...] + small[1][...]


def qkv_end(kept, got, small, tall, wide):
    return pl.pallas_call(
        qkv_end_kernel,
        in_specs=[IN_VMEM] * (2 * GROUPS + 2),
        out_specs=[IN_VMEM] * 2,
        out_shape=[shape((tall, wide), f32), shape(small[0].shape, f32)],
        compiler_params=params(16),
        cost_estimate=COST,
        name="qkv_end",
    )(*kept, *got, *small)


def after(value, *earlier):
    return lax.optimization_barrier((value, earlier))[0]


def sum_parts(me, kept, got, wheres, small):
    orders = bit_orders(lax.axis_size("batch"))
    keep, send = start_sum(me, kept, got, wheres, orders)
    for i in range(len(orders[0])):
        got = [exchange(s, "batch", order[i]) for s, order in zip(send, orders, strict=True)]
        small = [small[0], exchange(small[0], "batch", orders[0][i])] if small else []
        if i == len(orders[0]) - 1:
            break
        earlier = yield send[0]
        if earlier is not None:
            keep = after(list(keep), earlier)
        keep, send, small = step_sum(keep, got, small)
    yield keep, got, small


def on_device(
    inputs, lengths, cotangent, qkv_weight, out_weight, up_weight, down_weight, attn_gain, mlp_gain
):
    seq, width = inputs.shape[2:]
    x = inputs[0, 0]
    dy = cotangent[0, 0]
    count = lax.axis_size("batch")
    stream = lax.axis_index("stream").astype(jnp.int32)
    me = lax.axis_index("batch").astype(jnp.int32).reshape(1)
    info = jnp.stack([stream, lengths[0]])
    gain1, gain2 = attn_gain.reshape(1, width), mlp_gain.reshape(1, width)
    cosine, sine = rotary_tables(seq)
    tables = (
        jnp.asarray(np.concatenate([cosine] * 4, axis=1)),
        jnp.asarray(np.concatenate([-sine, sine] * 2, axis=1)),
    )
    tables_t = (jnp.asarray(cosine.T), jnp.asarray(sine.T))

    received = lax.ppermute(x, "stream", [(0, 1)])
    q, ko, vo, h1t, sums_x = project(info, x, gain1, qkv_weight, tables)
    (
        kc, vc, o, lse, outputs, dx2, do,
        up_send, up_keep, down_send, down_keep, out_send, out_keep, sums_m,
    ) = layer(
        info, x, received, gain1, gain2, qkv_weight, tables, q, ko, vo, out_weight, dy, up_weight, down_weight
    )
    down_got, up_got, out_got = (exchange(a, "stream", 1) for a in (down_send, up_send, out_send))

    def by_rows(array):
        return array.reshape(count * GROUPS, array.shape[0] // (count * GROUPS), width)

    heads = (q, ko, vo, kc, vc, o, do, lse, *tables_t)
    pairs = width // PW // 2
    dq1, keep1, send1 = attend_back(info, 0, pairs, *heads)
    got1 = lax.ppermute(send1, "stream", [(1, 0)])
    early = sum_parts(
        me,
        [by_rows(after(a, dq1)) for a in (down_keep, up_keep, out_keep)],
        [by_rows(a) for a in (down_got, up_got, out_got)],
        [lambda part, g: part * GROUPS + g] * 3,
        [],
    )
    token = next(early)
    dq2, keep2, send2 = attend_back(info, pairs, pairs, q, ko, vo, kc, vc, o, after(do, token), lse, *tables_t)
    got2 = lax.ppermute(send2, "stream", [(1, 0)])
    token = early.send(dq2)
    dkv1, qkv_send1, qkv_keep1 = weigh(info, (dq1, after(keep1, token)), got1, tables, h1t)
    qkv_got1 = exchange(qkv_send1, "stream", 1)
    dkv2, qkv_send2, qkv_keep2 = weigh(info, (dq2, after(keep2, dkv1)), got2, tables, h1t)
    qkv_got2 = exchange(qkv_send2, "stream", 1)
    token = early.send(dkv2)
    dx, sums_h = finish(after(x, token), dx2, [dq1, dq2], [dkv1, dkv2], qkv_weight, gain1)

    small = jnp.concatenate(
        [
            sums_x[:1],
            sums_m[:3],
            sums_h[:1],
            jnp.full((1, width), lengths[0].astype(f32)),
            jnp.zeros((2, width), f32),
        ]
    )
    small_got = exchange(small, "stream", 1)
    tall = width // (2 * count)
    split = lambda a: a.reshape(GROUPS * count, tall, a.shape[2])
    late = sum_parts(
        me,
        [split(after(a, small)) for a in (qkv_keep1, qkv_keep2)],
        [split(a) for a in (qkv_got1, qkv_got2)],
        [lambda part, g: g * count + part] * 2,
        [small + small_got],
    )
    token = next(late)
    token = early.send(token)
    out = late.send(token if isinstance(token, jax.Array) else None)
    ends = token
    while not isinstance(ends, tuple):
        ends = early.send(out)
        if not isinstance(out, tuple):
            out = late.send(None if isinstance(ends, tuple) else ends)
    while not isinstance(out, tuple):
        out = late.send(None)
    up_cols = down_keep.shape[0] // count
    down_grad, up_grad, out_grad = feed_end(ends[0], ends[1], up_cols, tall)
    qkv_grad, small = qkv_end(*out, tall, 3 * width)

    squares = jnp.sum(small[:3], axis=1)
    rms = jnp.sqrt(squares / (small[5, 0] * width))
    return (
        outputs[None, None],
        dx[None, None],
        qkv_grad,
        out_grad,
        up_grad,
        down_grad,
        small[4],
        small[3],
        rms,
    )


def solution(mesh):
    rows = P("stream", "batch", None, None)
    both = ("stream", "batch")
    return jax.shard_map(
        on_device,
        mesh=mesh,
        in_specs=(rows, P("batch"), rows, P(), P(), P(), P(), P(), P()),
        out_specs=(rows, rows, P(both, None), P(both, None), P(None, both), P(both, None), P(), P(), P()),
        check_vma=False,
    )
```

```python
import functools

import jax
import jax.numpy as jnp
import numpy as np
from jax import lax
from jax.experimental import pallas as pl
from jax.experimental.pallas import tpu as pltpu
from jax.sharding import PartitionSpec as P

f32 = jnp.float32
bf16 = jnp.bfloat16

HD = 64
BLK = 16
EPS = 1e-06
NEG = -1e30
PW = 2 * HD
T = 128
R = 256
AHEAD = 2
FC = 512
SCALE = HD**-0.5
BIG = 60
GROUPS = 3

COST = pl.CostEstimate(flops=1 << 20, bytes_accessed=1 << 16, transcendentals=0)
LONG = pl.CostEstimate(flops=1 << 35, bytes_accessed=1 << 26, transcendentals=0)

SMEM = pl.BlockSpec(memory_space=pltpu.SMEM)
IN_VMEM = pl.BlockSpec(memory_space=pltpu.VMEM)


def params(mib):
    return pltpu.CompilerParams(vmem_limit_bytes=mib << 20)


def shape(dims, dtype):
    return jax.ShapeDtypeStruct(dims, dtype)


def pinned(*arrays):
    return [pltpu.with_memory_space_constraint(a, pltpu.HBM) for a in arrays]


def nn(a, b):
    return jnp.dot(a, b, preferred_element_type=f32)


def nt(a, b):
    return lax.dot_general(a, b, (((1,), (1,)), ((), ())), preferred_element_type=f32)


def tn(a, b):
    return lax.dot_general(a, b, (((0,), (0,)), ((), ())), preferred_element_type=f32)


def whole(dims):
    return pl.BlockSpec(dims, lambda *_: (0,) * len(dims), pipeline_mode=pl.Buffered(1))


def inv_rms(v):
    return lax.rsqrt(jnp.mean(v * v, axis=-1, keepdims=True) + EPS)


def norm_back(v, gain, grad):
    r = inv_rms(v)
    unit = v * r
    scaled = grad * gain
    inner = jnp.mean(scaled * unit, axis=-1, keepdims=True)
    return r * (scaled - unit * inner), grad * unit


def rotary_tables(length):
    half = HD // 2
    freqs = np.exp(-np.log(10000.0) * np.arange(half) / half).astype(np.float32)
    angles = (np.arange(length, dtype=np.float32)[:, None] * freqs[None, :]).astype(np.float64)
    return np.cos(angles).astype(np.float32), np.sin(angles).astype(np.float32)


def rotated(v, cosine, signed, sign):
    first = lax.broadcasted_iota(jnp.int32, (1, PW), 1) % HD < HD // 2
    outs = []
    for c in range(0, v.shape[1], PW):
        part = v[:, c : c + PW]
        partner = jnp.where(first, pltpu.roll(part, PW - HD // 2, 1), pltpu.roll(part, HD // 2, 1))
        outs.append(part * cosine + partner * (signed * sign))
    return outs[0] if len(outs) == 1 else jnp.concatenate(outs, axis=1)


def token_weight(start, length, rows):
    return lax.broadcasted_iota(jnp.int32, (rows, 1), 0) + start < length


def row_sum(v):
    return jnp.sum(v, axis=0, keepdims=True)


def by_pairs(ref, rows, value):
    for p in range(ref.shape[0]):
        ref[p, rows, :] = value[:, p * PW : (p + 1) * PW].astype(ref.dtype)


def stacked(tile, low):
    zero = jnp.zeros_like(tile)
    return jnp.concatenate([jnp.where(low, tile, zero), jnp.where(low, zero, tile)], axis=0)


def unstacked(tile_t):
    half = lax.broadcasted_iota(jnp.int32, (PW, 1), 0) < HD
    return jnp.where(half, tile_t[:, :T], tile_t[:, T:])


def chunks_of(i):
    out, j = [], 0
    while j < i:
        n = 2 if i - j >= 2 else 1
        out.append((j * T, n * T))
        j += n
    return out


def edge_bias(ref, noisy):
    row = lax.broadcasted_iota(jnp.int32, (T, 2 * T), 0) // BLK
    col = (lax.broadcasted_iota(jnp.int32, (T, 2 * T), 1) % T) // BLK
    own = jnp.logical_or(row == col, jnp.logical_and(row < col, noisy == 0))
    other = jnp.logical_and(row < col, noisy == 1)
    ref[:T, :] = jnp.where(own, 0.0, NEG)
    ref[T:, :] = jnp.where(other, 0.0, NEG)


def masked(s, start, length):
    pos = lax.broadcasted_iota(jnp.int32, s.shape, 0) + start
    return jnp.where(pos < length, s, NEG)


def over_rows(op, v):
    return op(v.reshape(v.shape[0] // 8, 8, v.shape[1]), axis=0)


def attend_pair(length, q, ko, vo, kc, vc, store, lse, vo_t, vc_t, scores, bias):
    seq = q.shape[0]
    low = lax.broadcasted_iota(jnp.int32, (1, PW), 1) < HD
    vo_t[...] = vo[...].T
    vc_t[...] = vc[...].T

    def score(i):
        at = pl.ds(i * T, T)
        q2 = stacked(q[at, :] * bf16(SCALE), low)
        buf = scores.at[i % AHEAD]
        edge = nt(jnp.concatenate([ko[at, :], kc[at, :]], 0), q2) + bias[...]
        own = masked(edge[:T], i * T, length)
        other = masked(edge[T:], i * T, length)
        buf[pl.ds(0, T), :] = own
        buf[pl.ds(T, T), :] = other
        top = over_rows(jnp.max, jnp.maximum(own, other))
        for start, size in chunks_of(i):
            s = masked(nt(kc[pl.ds(start, size), :], q2), start, length)
            buf[pl.ds(2 * T + start, size), :] = s
            top = jnp.maximum(top, over_rows(jnp.max, s))
        return jnp.max(top, axis=0, keepdims=True)

    def mix(i, top):
        at = pl.ds(i * T, T)
        buf = scores.at[i % AHEAD]
        p = jnp.exp(buf[pl.ds(0, 2 * T), :] - top)
        total = over_rows(jnp.sum, p)
        acc = nn(jnp.concatenate([vo_t[:, at], vc_t[:, at]], 1), p.astype(bf16))
        for start, size in chunks_of(i):
            p = jnp.exp(buf[pl.ds(2 * T + start, size), :] - top)
            total = total + over_rows(jnp.sum, p)
            acc = acc + nn(vc_t[:, pl.ds(start, size)], p.astype(bf16))
        total = row_sum(total)
        lse[0, pl.ds(i, 1), :] = top + jnp.log(total)
        store(at, unstacked(acc * (1.0 / total)))

    tops = {}
    for i in range(seq // T + AHEAD - 1):
        if i < seq // T:
            tops[i] = score(i)
        if i >= AHEAD - 1:
            mix(i - AHEAD + 1, tops.pop(i - AHEAD + 1))


def turned_back(v, cosine, sine):
    quarter = HD // 2
    a, b, c, d = (v[i * quarter : (i + 1) * quarter] for i in range(4))
    return jnp.concatenate(
        [a * cosine + b * sine, b * cosine - a * sine, c * cosine + d * sine, d * cosine - c * sine]
    )


def attend_back_kernel(
    info, q, ko, vo, kc, vc, o, do, lse, cosine, sine, dq, keep, send, ko_t, kc_t, dko, dvo, dkc, dvc, bias
):
    noisy, length = info[0], info[1]
    q, ko, vo, kc, vc = (ref.at[0] for ref in (q, ko, vo, kc, vc))
    seq = q.shape[0]
    low = lax.broadcasted_iota(jnp.int32, (1, PW), 1) < HD

    @pl.when(pl.program_id(0) == 0)
    def _():
        edge_bias(bias, noisy)

    ko_t[...] = ko[...].T
    kc_t[...] = kc[...].T

    def tile(i):
        at = pl.ds(i * T, T)
        prod = (do[at, :].astype(f32) * o[at, :].astype(f32)).T
        delta = jnp.concatenate([row_sum(prod[:HD]), row_sum(prod[HD:])], 1)
        q2 = stacked(q[at, :] * bf16(SCALE), low)
        return q2, stacked(do[at, :], low), lse[0, pl.ds(i, 1), :], delta

    def products(i, start, size, q2, do2):
        if start is None:
            at = pl.ds(i * T, T)
            s = nt(jnp.concatenate([ko[at, :], kc[at, :]], 0), q2) + bias[...]
            s = jnp.concatenate([masked(s[:T], i * T, length), masked(s[T:], i * T, length)], 0)
            return s, nt(jnp.concatenate([vo[at, :], vc[at, :]], 0), do2)
        rows = pl.ds(start, size)
        return masked(nt(kc[rows, :], q2), start, length), nt(vc[rows, :], do2)

    def gather(i, start, size, q2, do2, p, ds, dq_t):
        at = pl.ds(i * T, T)
        dv, dk = nn(p, do2), nn(ds, q2)
        if start is None:
            dvo[at, :] = dv[:T]
            dko[at, :] = dk[:T]
            dvc[at, :] = dv[T:]
            dkc[at, :] = dk[T:]
            return nn(jnp.concatenate([ko_t[:, at], kc_t[:, at]], 1), ds)
        rows = pl.ds(start, size)
        dvc[rows, :] += dv
        dkc[rows, :] += dk
        return dq_t + nn(kc_t[:, rows], ds)

    work = [(i, *c) for i in range(seq // T) for c in [(None, None)] + chunks_of(i)]
    tiles, made, weighed, dq_t = {}, {}, {}, None
    for n in range(len(work) + 2):
        if n < len(work):
            i = work[n][0]
            if i not in tiles:
                tiles[i] = tile(i)
            made[n] = products(*work[n], *tiles[i][:2])
        if 0 <= n - 1 < len(work):
            _, _, norm, delta = tiles[work[n - 1][0]]
            s, dp = made.pop(n - 1)
            p = jnp.exp(s - norm)
            weighed[n - 1] = p.astype(bf16), (p * (dp - delta)).astype(bf16)
        if n >= 2:
            i, start, size = work[n - 2]
            dq_t = gather(i, start, size, *tiles[i][:2], *weighed.pop(n - 2), dq_t)
            if n == len(work) + 1 or work[n - 1][0] != i:
                at = pl.ds(i * T, T)
                out = turned_back(unstacked(dq_t), cosine[:, at], sine[:, at]) * SCALE
                dq[at, :] = out.T.astype(bf16)
    clean = (1 - noisy).astype(f32)
    for at, own, other in ((0, dko, dkc), (1, dvo, dvc)):
        keep[at] = (own[...] + clean * other[...]).astype(bf16)
        send[at] = other[...].astype(bf16)


def attend_back(info, first, pairs, q, ko, vo, kc, vc, o, do, lse, cosine, sine):
    seq = q.shape[1]
    width = pairs * PW
    heads = pl.BlockSpec((1, seq, PW), lambda h: (first + h, 0, 0))
    source = pl.BlockSpec((seq, PW), lambda h: (0, first + h))
    both = pl.BlockSpec((2, seq, PW), lambda h: (0, 0, h))
    lines = pl.BlockSpec((1, seq // T, 2 * T), lambda h: (first + h, 0, 0))
    table = whole((HD // 2, seq))
    return pl.pallas_call(
        attend_back_kernel,
        grid=(pairs,),
        in_specs=[SMEM] + [heads] * 5 + [source] * 2 + [lines, table, table],
        out_specs=[pl.BlockSpec((seq, PW), lambda h: (0, h)), both, both],
        out_shape=[shape((seq, width), bf16)] + [shape((2, seq, width), bf16)] * 2,
        scratch_shapes=[pltpu.VMEM((PW, seq), bf16)] * 2
        + [pltpu.VMEM((seq, PW), f32)] * 4
        + [pltpu.VMEM((2 * T, 2 * T), f32)],
        compiler_params=params(24),
        cost_estimate=LONG,
        name="attend_back",
    )(info, *pinned(q, ko, vo, kc, vc, o, do), lse, cosine, sine)


C0 = 0.7978845608028654
C1 = C0 * 0.044715


def layer_kernel(
    info, gain1_line, gain2_line, received_any, x_any, wqkv_any, cosine_any, signed_any, wo_any, dy_any,
    w1_any, w2_any,
    q_out, ko_out, vo_out, kc_out, vc_out, h1t_out, o_out, lse_out, out_any, dx2_any, do_any,
    up_send, up_keep, down_send, down_keep, g_send, g_keep, sums,
    x, received, wqkv, cosine, signed, q, ko, vo, h1t, wo, dy, w1, w2,
    kc, vc, vo_t, vc_t, scores, bias, o, o_t, lse, x2, h2, m, dh, act, du, up_grad, down_grad, half_grads,
    sem_in, sem_1, sem_2, sem_out, sem_up, sem_down, sem_tile,
):
    noisy, length = info[0], info[1]
    seq, width = x.shape
    chunks, pairs, tiles = w1.shape[0], kc.shape[0], seq // R
    copy = pltpu.make_async_copy
    gain1, gain2 = gain1_line[...].reshape(1, width), gain2_line[...].reshape(1, width)

    def weights(c):
        place = lax.rem(c + (chunks // 2) * (1 - noisy), chunks) * FC
        place = pl.multiple_of(place, FC)
        return (
            copy(w1_any.at[:, pl.ds(place, FC)], w1.at[c], sem_1.at[c]),
            copy(w2_any.at[pl.ds(place, FC), :], w2.at[c], sem_2.at[c]),
        )

    sources = (
        (x_any, x),
        (wqkv_any, wqkv),
        (cosine_any, cosine),
        (signed_any, signed),
        (received_any, received),
        (wo_any, wo),
        (dy_any, dy),
    )
    loads = [copy(a, b, sem_in.at[i]) for i, (a, b) in enumerate(sources)]
    for load in loads[:5]:
        load.start()
    sums[...] = jnp.zeros_like(sums)
    edge_bias(bias, noisy)

    for load in loads[:4]:
        load.wait()

    def own_rows(t, carry):
        start = pl.multiple_of(t * R, R)
        rows = pl.ds(start, R)
        value = x[rows, :].astype(f32)
        h1 = (value * inv_rms(value) * gain1).astype(bf16)
        h1t[:, rows] = h1.T
        tables = (cosine[rows, :], signed[rows, :], 1.0)
        by_pairs(q, rows, rotated(nn(h1, wqkv[:, :width]), *tables))
        by_pairs(ko, rows, rotated(nn(h1, wqkv[:, width : 2 * width]), *tables))
        by_pairs(vo, rows, nn(h1, wqkv[:, 2 * width :]))
        weight = token_weight(start, length, R)
        sums[0:1, :] += row_sum(jnp.where(weight, value * value, 0.0))
        return carry

    lax.fori_loop(0, tiles, own_rows, 0)
    stores = [copy(a, b, sem_out.at[6 + i]) for i, (a, b) in enumerate(((q, q_out), (ko, ko_out), (vo, vo_out), (h1t, h1t_out)))]
    for store in stores:
        store.start()
    loads[4].wait()

    def clean_rows(t, carry):
        rows = pl.ds(pl.multiple_of(t * R, R), R)
        value = jnp.where(noisy == 1, received[rows, :].astype(f32), x[rows, :].astype(f32))
        h1 = (value * inv_rms(value) * gain1).astype(bf16)
        by_pairs(kc, rows, rotated(nn(h1, wqkv[:, width : 2 * width]), cosine[rows, :], signed[rows, :], 1.0))
        by_pairs(vc, rows, nn(h1, wqkv[:, 2 * width :]))
        return carry

    lax.fori_loop(0, tiles, clean_rows, 0)
    for load in loads[5:]:
        load.start()
    more = [copy(kc, kc_out, sem_out.at[0]), copy(vc, vc_out, sem_out.at[1])]
    for store in more:
        store.start()
    stores += more

    for c in range(chunks):
        for load in weights(c):
            load.start()

    def one_pair(p, carry):
        lanes = pl.ds(pl.multiple_of(p * PW, PW), PW)

        def keep(at, tile_t):
            o_t[lanes, at] = tile_t.astype(bf16)
            o[at, lanes] = tile_t.T.astype(bf16)

        heads = (ref.at[p] for ref in (q, ko, vo, kc, vc))
        attend_pair(length, *heads, keep, lse.at[pl.ds(p, 1)], vo_t, vc_t, scores, bias)
        return carry

    lax.fori_loop(0, pairs, one_pair, 0)
    more = [copy(o, o_out, sem_out.at[2]), copy(lse, lse_out, sem_out.at[3])]
    for store in more:
        store.start()
    stores += more

    for load in loads[5:]:
        load.wait()

    def joined_rows(t, carry):
        start = pl.multiple_of(t * R, R)
        rows = pl.ds(start, R)
        branch = nn(o[rows, :], wo[...])
        value = x[rows, :].astype(f32) + branch
        x2[rows, :] = value
        h2[rows, :] = (value * inv_rms(value) * gain2).astype(bf16)
        m[rows, :] = jnp.zeros_like(value)
        dh[rows, :] = jnp.zeros_like(value)
        weight = token_weight(start, length, R)
        sums[1:2, :] += row_sum(jnp.where(weight, branch * branch, 0.0))
        return carry

    lax.fori_loop(0, tiles, joined_rows, 0)

    def grad_stores(c, up, down):
        slot = lax.rem(c, 2)
        rows = pl.ds(pl.multiple_of(lax.rem(c, chunks // 2) * FC, FC), FC)
        return (
            copy(up_grad.at[slot], up.at[rows, :], sem_up.at[slot]),
            copy(down_grad.at[slot], down.at[rows, :], sem_down.at[slot]),
        )

    def one_chunk(c, carry):
        for load in weights(c):
            load.wait()
        up, down = w1.at[c], w2.at[c]
        for t in range(0, seq, R):
            rows = pl.ds(t, R)
            u = nn(h2[rows, :], up[...])
            da = nt(dy[rows, :], down[...])
            sq = u * u
            half = 0.5 * jnp.tanh(u * (C0 + C1 * sq)) + 0.5
            low = (u * half).astype(bf16)
            slope = half + u * (2.0 * half * (1.0 - half)) * (C0 + 3.0 * C1 * sq)
            back = (da * slope).astype(bf16)
            act[rows, :] = low
            du[rows, :] = back
            m[rows, :] += nn(low, down[...])
            dh[rows, :] += nt(back, up[...])

        @pl.when(c >= 2)
        def _():
            for store in grad_stores(c, up_send, down_send):
                store.wait()

        slot = lax.rem(c, 2)
        down_grad[slot] = tn(act[...], dy[...]).astype(bf16)
        up_grad[slot] = tn(du[...], h2[...]).astype(bf16)

        @pl.when(c < chunks // 2)
        def _():
            for store in grad_stores(c, up_send, down_send):
                store.start()

        @pl.when(c >= chunks // 2)
        def _():
            for store in grad_stores(c, up_keep, down_keep):
                store.start()

        return carry

    lax.fori_loop(0, chunks, one_chunk, 0)

    def tile_stores(t):
        rows = pl.ds(pl.multiple_of(t * R, R), R)
        return (
            copy(h2.at[rows, :], out_any.at[rows, :], sem_tile.at[t, 0]),
            copy(x2.at[rows, :], dx2_any.at[rows, :], sem_tile.at[t, 1]),
            copy(received.at[rows, :], do_any.at[rows, :], sem_tile.at[t, 2]),
        )

    def middle_rows(t, carry):
        start = pl.multiple_of(t * R, R)
        rows = pl.ds(start, R)
        value = x2[rows, :]
        mixed = m[rows, :]
        weight = token_weight(start, length, R)
        sums[2:3, :] += row_sum(jnp.where(weight, mixed * mixed, 0.0))
        grad, gain_terms = norm_back(value, gain2, dh[rows, :])
        sums[3:4, :] += row_sum(gain_terms)
        grad = grad + dy[rows, :].astype(f32)
        da = grad.astype(bf16)
        h2[rows, :] = (value + mixed).astype(bf16)
        x2[rows, :] = grad
        received[rows, :] = nt(da, wo[...]).astype(bf16)
        x[rows, :] = da
        for store in tile_stores(t):
            store.start()
        return carry

    lax.fori_loop(0, tiles, middle_rows, 0)
    half = width // 2
    mine = pl.multiple_of(noisy * half, half)
    half_grads[0] = nn(o_t[pl.ds(half - mine, half), :], x[...]).astype(bf16)
    half_grads[1] = nn(o_t[pl.ds(mine, half), :], x[...]).astype(bf16)
    more = [copy(half_grads.at[0], g_send, sem_out.at[4]), copy(half_grads.at[1], g_keep, sem_out.at[5])]
    for store in more:
        store.start()
    stores += more
    for c in range(chunks - 2, chunks):
        stores += grad_stores(c, up_keep, down_keep)
    for t in range(tiles):
        stores += tile_stores(t)
    for store in stores:
        store.wait()


def layer(info, gain1, gain2, received, x, wqkv, tables, wo, dy, w1, w2):
    seq, width = x.shape
    hidden = w1.shape[1]
    tiles, pairs, chunks = seq // R, width // PW, hidden // FC
    anywhere = pl.BlockSpec(memory_space=pl.ANY)
    vmem = pltpu.VMEM
    dma = pltpu.SemaphoreType.DMA
    heads = (pairs, seq, PW)
    flat = (seq, width)
    outs = (
        [shape(heads, bf16)] * 5
        + [shape((width, seq), bf16), shape(flat, bf16), shape((pairs, seq // T, 2 * T), f32)]
        + [shape(flat, bf16), shape(flat, f32), shape(flat, bf16)]
        + [shape((hidden // 2, width), bf16)] * 4
        + [shape((width // 2, width), bf16)] * 2
        + [shape((8, width), f32)]
    )
    return pl.pallas_call(
        layer_kernel,
        in_specs=[SMEM, IN_VMEM, IN_VMEM] + [anywhere] * 9,
        out_specs=[anywhere] * 17 + [IN_VMEM],
        out_shape=outs,
        scratch_shapes=[vmem(flat, bf16)] * 2
        + [vmem(wqkv.shape, bf16), vmem((seq, PW), f32), vmem((seq, PW), f32)]
        + [vmem(heads, bf16)] * 3
        + [vmem((width, seq), bf16), vmem((width, width), bf16), vmem(flat, bf16)]
        + [vmem((chunks, width, FC), bf16), vmem((chunks, FC, width), bf16)]
        + [vmem(heads, bf16)] * 2
        + [vmem((PW, seq), bf16)] * 2
        + [vmem((AHEAD, seq + T, 2 * T), f32), vmem((2 * T, 2 * T), f32)]
        + [vmem(flat, bf16), vmem((width, seq), bf16)]
        + [vmem((pairs, seq // T, 2 * T), f32)]
        + [vmem(flat, f32), vmem(flat, bf16)]
        + [vmem(flat, f32)] * 2
        + [vmem((seq, FC), bf16)] * 2
        + [vmem((2, FC, width), bf16)] * 2
        + [vmem((2, width // 2, width), bf16)]
        + [dma((7,)), dma((chunks,)), dma((chunks,)), dma((10,)), dma((2,)), dma((2,)), dma((tiles, 3))],
        compiler_params=params(BIG),
        cost_estimate=LONG,
        name="layer",
    )(info, gain1, gain2, received, *pinned(x, wqkv, *tables, wo, dy, w1, w2))


def weigh_kernel(first, info, dq, keep, got, cosine, signed, h1t, wqkv, sums, dkv, g_send, g_keep, small):
    width, half = wqkv.shape[0], wqkv.shape[0] // 2
    mine = pl.multiple_of(info[0] * half, half)
    dk = keep[0].astype(f32) + got[0].astype(f32)
    dkv[0] = rotated(dk, cosine[...], signed[...], -1.0).astype(bf16)
    dkv[1] = (keep[1].astype(f32) + got[1].astype(f32)).astype(bf16)
    small[...] = sums[...]
    for out, start in ((g_send, half - mine), (g_keep, mine)):
        rows = pl.ds(start, half)
        terms = 0.0
        for i, part in enumerate((dq, dkv.at[0], dkv.at[1])):
            total = nn(h1t[rows, :], part[...])
            out[i] = total.astype(bf16)
            at = i * width + first * PW
            weighted = total * wqkv[rows, at : at + total.shape[1]].astype(f32)
            for c in range(0, total.shape[1], PW):
                terms = terms + weighted[:, c : c + PW]
        line = jnp.sum(terms.T, axis=0, keepdims=True)
        lanes = lax.broadcasted_iota(jnp.int32, (1, width), 1)
        inside = jnp.logical_and(lanes >= start, lanes < start + half)
        small[4:5, :] += jnp.where(inside, jnp.concatenate([line, line], axis=1), 0.0)
    small[5:6, :] = jnp.full((1, width), info[1].astype(f32))


def weigh(info, first, dq, keep, got, tables, h1t, wqkv, sums):
    seq, width = dq.shape
    tall = h1t.shape[0]
    return pl.pallas_call(
        functools.partial(weigh_kernel, first),
        in_specs=[SMEM] + [IN_VMEM] * 8,
        out_specs=[IN_VMEM] * 4,
        out_shape=[shape((2, seq, width), bf16)]
        + [shape((3, tall // 2, width), bf16)] * 2
        + [shape(sums.shape, f32)],
        compiler_params=params(24),
        cost_estimate=LONG,
        name="weigh",
    )(info, dq, keep, got, *tables, h1t, wqkv, sums)


def finish_kernel(parts, x, dx2, wqkv, gain_line, *refs):
    dx_any, dx, sem = refs[-3:]
    dqs, dkvs = refs[:parts], refs[parts : 2 * parts]
    tiles = sem.shape[0]
    gain = gain_line[...].reshape(1, x.shape[1])

    def store(t):
        rows = pl.ds(pl.multiple_of(t * R, R), R)
        return pltpu.make_async_copy(dx.at[rows, :], dx_any.at[rows, :], sem.at[t])

    def some_rows(t, carry):
        rows = pl.ds(pl.multiple_of(t * R, R), R)
        grads = [r[rows, :] for r in dqs] + [r[0, rows, :] for r in dkvs] + [r[1, rows, :] for r in dkvs]
        dh = nt(jnp.concatenate(grads, axis=1), wqkv[...])
        grad, _ = norm_back(x[rows, :].astype(f32), gain, dh)
        dx[rows, :] = (dx2[rows, :] + grad).astype(bf16)
        store(t).start()
        return carry

    lax.fori_loop(0, tiles, some_rows, 0)
    for t in range(tiles):
        store(t).wait()


def finish(x, dx2, dqs, dkvs, weight, gain):
    return pl.pallas_call(
        functools.partial(finish_kernel, len(dqs)),
        in_specs=[IN_VMEM] * (4 + len(dqs) + len(dkvs)),
        out_specs=pl.BlockSpec(memory_space=pl.ANY),
        out_shape=shape(x.shape, bf16),
        scratch_shapes=[pltpu.VMEM(x.shape, bf16), pltpu.SemaphoreType.DMA((x.shape[0] // R,))],
        compiler_params=params(24),
        cost_estimate=LONG,
        name="finish",
    )(x, dx2, weight, gain, *dqs, *dkvs)


def bit_orders(count):
    bits = [1 << i for i in range(count.bit_length() - 1)]
    if len(bits) == 4:
        x, y, z, far = bits
        return [(x, y, z, far), (y, z, x, far), (z, x, y, far)]
    return [tuple(bits[g:] + bits[:g]) for g in range(GROUPS)]


def exchange(value, axis, bit):
    size = lax.axis_size(axis)
    return lax.ppermute(value, axis, [(i, i ^ bit) for i in range(size)])


def distance(order, place):
    out = 0
    for i, bit in enumerate(order):
        out = out + ((place >> (len(order) - 1 - i)) & 1) * bit
    return out


def start_kernel(orders, wheres, me, *refs):
    arrays = len(wheres)
    ins, outs = refs[: 2 * arrays], refs[-2 * GROUPS :]
    half = outs[0].shape[0]
    if len(refs) > 2 * arrays + 2 * GROUPS:
        here, there, total = refs[2 * arrays : -2 * GROUPS]
        total[...] = here[...] + there[...]
    for g, order in enumerate(orders):
        for side in range(2):

            def one(r, carry, g=g, order=order, side=side):
                part = me[0] ^ distance(order, r + side * half)
                row = 0
                for kept, got, where in zip(ins[::2], ins[1::2], wheres, strict=True):
                    place = where(part, g)
                    size = kept.shape[1]
                    total = kept[place].astype(f32) + got[place].astype(f32)
                    outs[g * 2 + side][r, row : row + size, :] = total.astype(bf16)
                    row += size
                return carry

            lax.fori_loop(0, half, one, 0)


def start_sum(me, kept, got, wheres, orders, small):
    count = 1 << len(orders[0])
    half = count // 2
    rows = sum(a.shape[1] for a in kept)
    width = kept[0].shape[2]
    cols = width // 3
    args = [a for pair in zip(kept, got, strict=True) for a in pair]
    sums = [shape((half, rows, width), bf16)] * (2 * GROUPS)
    if small:
        specs = dict(
            in_specs=[SMEM] + [IN_VMEM] * (len(args) + 2),
            out_specs=[IN_VMEM] * (1 + 2 * GROUPS),
            out_shape=[shape(small[0].shape, f32)] + sums,
        )
    else:
        block = lambda a: pl.BlockSpec((a.shape[0], a.shape[1], cols), lambda c: (0, 0, c))
        specs = dict(
            grid=(width // cols,),
            in_specs=[SMEM] + [block(a) for a in args],
            out_specs=[pl.BlockSpec((half, rows, cols), lambda c: (0, 0, c))] * (2 * GROUPS),
            out_shape=sums,
        )
    outs = pl.pallas_call(
        functools.partial(start_kernel, orders, wheres),
        compiler_params=params(30),
        cost_estimate=COST,
        name="start_sum",
        **specs,
    )(me, *args, *small)
    small, outs = list(outs[: len(outs) - 2 * GROUPS]), outs[-2 * GROUPS :]
    return outs[0::2], outs[1::2], small


def step_kernel(*refs):
    half = refs[0].shape[0] // 2
    kept, got = refs[:GROUPS], refs[GROUPS : 2 * GROUPS]
    outs = refs[len(refs) - 2 * GROUPS - len(refs) % 2 :]
    for g in range(GROUPS):
        total = (kept[g][...].astype(f32) + got[g][...].astype(f32)).astype(bf16)
        outs[2 * g][...] = total[:half]
        outs[2 * g + 1][...] = total[half:]
    if len(refs) % 2:
        outs[-1][...] = refs[2 * GROUPS][...] + refs[2 * GROUPS + 1][...]


def step_sum(kept, got, small):
    count, rows, width = kept[0].shape
    args = [*kept, *got, *small]
    outs = pl.pallas_call(
        step_kernel,
        in_specs=[IN_VMEM] * len(args),
        out_specs=[IN_VMEM] * (2 * GROUPS + len(small) // 2),
        out_shape=[shape((count // 2, rows, width), bf16)] * (2 * GROUPS)
        + [shape(a.shape, f32) for a in small[:1]],
        compiler_params=params(16),
        cost_estimate=COST,
        name="step_sum",
    )(*args)
    return outs[0 : 2 * GROUPS : 2], outs[1 : 2 * GROUPS : 2], list(outs[2 * GROUPS :])


def feed_end_kernel(*refs):
    ins, (down, up, out) = refs[: 2 * GROUPS], refs[2 * GROUPS :]
    tall, few = down.shape[0] // GROUPS, out.shape[0] // GROUPS
    ups = []
    for g in range(GROUPS):
        total = ins[g][0].astype(f32) + ins[GROUPS + g][0].astype(f32)
        down[g * tall : (g + 1) * tall, :] = total[:tall]
        ups.append(total[tall : 2 * tall])
        out[g * few : (g + 1) * few, :] = total[2 * tall :]
    up[...] = jnp.concatenate(ups, axis=0).T


def feed_end(kept, got, tall, few):
    width = kept[0].shape[2]
    return pl.pallas_call(
        feed_end_kernel,
        in_specs=[IN_VMEM] * (2 * GROUPS),
        out_specs=[IN_VMEM] * 3,
        out_shape=[shape((tall, width), f32), shape((width, tall), f32), shape((few, width), f32)],
        compiler_params=params(16),
        cost_estimate=COST,
        name="feed_end",
    )(*kept, *got)


def qkv_end_kernel(gain_line, *refs):
    ins, small, outs = refs[: 2 * GROUPS], refs[2 * GROUPS : 2 * GROUPS + 2], refs[2 * GROUPS + 2 :]
    out, gain1, gain2, rms = outs
    tall = out.shape[0]
    width = gain1.shape[0]
    cols = ins[0].shape[2]
    for g in range(GROUPS):
        total = ins[g][0].astype(f32) + ins[GROUPS + g][0].astype(f32)
        for part in range(total.shape[0] // tall):
            at = (2 * g + part) * cols
            out[:, at : at + cols] = total[part * tall : (part + 1) * tall]
    sums = small[0][...] + small[1][...]
    gain2[...] = sums[3:4, :].reshape(width)
    gain1[...] = (sums[4:5, :] / gain_line[...].reshape(1, width)).reshape(width)
    count = jnp.max(sums[5:6, :], axis=1, keepdims=True) * width
    rms[...] = jnp.broadcast_to(jnp.sqrt(jnp.sum(sums, axis=1, keepdims=True) / count), rms.shape)


def qkv_end(gain, kept, got, small, tall, wide):
    return pl.pallas_call(
        qkv_end_kernel,
        in_specs=[IN_VMEM] * (2 * GROUPS + 3),
        out_specs=[IN_VMEM] * 4,
        out_shape=[shape((tall, wide), f32), shape(gain.shape, f32), shape(gain.shape, f32), shape((8, 128), f32)],
        compiler_params=params(16),
        cost_estimate=COST,
        name="qkv_end",
    )(gain, *kept, *got, *small)


def after(value, *earlier):
    return lax.optimization_barrier((value, earlier))[0]


def sum_parts(me, kept, got, wheres, small):
    orders = bit_orders(lax.axis_size("batch"))
    keep, send, small = start_sum(me, kept, got, wheres, orders, small)
    for i in range(len(orders[0])):
        got = [exchange(s, "batch", order[i]) for s, order in zip(send, orders, strict=True)]
        small = [small[0], exchange(small[0], "batch", orders[0][i])] if small else []
        if i == len(orders[0]) - 1:
            break
        earlier = yield send[0]
        if earlier is not None:
            keep = after(list(keep), earlier)
        keep, send, small = step_sum(keep, got, small)
    yield keep, got, small


def on_device(
    inputs, lengths, cotangent, qkv_weight, out_weight, up_weight, down_weight, attn_gain, mlp_gain
):
    seq, width = inputs.shape[2:]
    x = inputs[0, 0]
    dy = cotangent[0, 0]
    count = lax.axis_size("batch")
    stream = lax.axis_index("stream").astype(jnp.int32)
    me = lax.axis_index("batch").astype(jnp.int32).reshape(1)
    info = jnp.stack([stream, lengths[0]])
    cosine, sine = rotary_tables(seq)
    tables = (
        jnp.asarray(np.concatenate([cosine] * 4, axis=1)),
        jnp.asarray(np.concatenate([-sine, sine] * 2, axis=1)),
    )
    tables_t = (jnp.asarray(cosine.T), jnp.asarray(sine.T))

    received = lax.ppermute(x, "stream", [(0, 1)])
    (
        q, ko, vo, kc, vc, h1t, o, lse, outputs, dx2, do,
        up_send, up_keep, down_send, down_keep, out_send, out_keep, sums,
    ) = layer(
        info, attn_gain, mlp_gain, received, x, qkv_weight, tables, out_weight, dy, up_weight, down_weight
    )
    down_got, up_got, out_got = (exchange(a, "stream", 1) for a in (down_send, up_send, out_send))

    def by_rows(array):
        return array.reshape(count * GROUPS, array.shape[0] // (count * GROUPS), width)

    heads = (q, ko, vo, kc, vc, o)
    pairs = width // PW // 2
    dq1, keep1, send1 = attend_back(info, 0, pairs, *heads, do, lse, *tables_t)
    got1 = lax.ppermute(send1, "stream", [(1, 0)])
    early = sum_parts(
        me,
        [by_rows(after(a, dq1)) for a in (down_keep, up_keep, out_keep)],
        [by_rows(a) for a in (down_got, up_got, out_got)],
        [lambda part, g: part * GROUPS + g] * 3,
        [],
    )
    token = next(early)
    dq2, keep2, send2 = attend_back(info, pairs, pairs, *heads, after(do, token), lse, *tables_t)
    got2 = lax.ppermute(send2, "stream", [(1, 0)])
    token = early.send(dq2)
    dkv1, qkv_send1, qkv_keep1, small = weigh(info, 0, dq1, after(keep1, token), got1, tables, h1t, qkv_weight, sums)
    qkv_got1 = exchange(qkv_send1, "stream", 1)
    dkv2, qkv_send2, qkv_keep2, small = weigh(info, pairs, dq2, keep2, got2, tables, h1t, qkv_weight, small)
    qkv_got2 = exchange(qkv_send2, "stream", 1)
    small_got = exchange(small, "stream", 1)
    token = early.send(dkv2)

    tall = width // (2 * count)
    split = lambda a: a.reshape(GROUPS * count, tall, a.shape[2])
    late = sum_parts(
        me,
        [split(after(a, token)) for a in (qkv_keep1, qkv_keep2)],
        [split(a) for a in (qkv_got1, qkv_got2)],
        [lambda part, g: g * count + part] * 2,
        [small, small_got],
    )
    token = next(late)
    dx = finish(after(x, token), dx2, [dq1, dq2], [dkv1, dkv2], qkv_weight, attn_gain)
    late_out = late.send(dx)
    early_out = early.send(late_out)
    while not isinstance(late_out, tuple):
        late_out = late.send(None)
    while not isinstance(early_out, tuple):
        early_out = early.send(None)
    up_cols = down_keep.shape[0] // count
    down_grad, up_grad, out_grad = feed_end(*early_out[:2], up_cols, tall)
    qkv_grad, gain1_grad, gain2_grad, rms = qkv_end(attn_gain, *late_out, tall, 3 * width)
    return (
        outputs[None, None],
        dx[None, None],
        qkv_grad,
        out_grad,
        up_grad,
        down_grad,
        gain1_grad,
        gain2_grad,
        rms[:3, 0],
    )


def solution(mesh):
    rows = P("stream", "batch", None, None)
    both = ("stream", "batch")
    return jax.shard_map(
        on_device,
        mesh=mesh,
        in_specs=(rows, P("batch"), rows, P(), P(), P(), P(), P(), P()),
        out_specs=(rows, rows, P(both, None), P(both, None), P(None, both), P(both, None), P(), P(), P()),
        check_vma=False,
    )
```

```python
import functools

import jax
import jax.numpy as jnp
import numpy as np
from jax import lax
from jax.experimental import pallas as pl
from jax.experimental.pallas import tpu as pltpu
from jax.sharding import PartitionSpec as P

f32 = jnp.float32
bf16 = jnp.bfloat16

HD = 64
BLK = 16
EPS = 1e-06
NEG = -1e30
PW = 2 * HD
T = 128
R = 256
AHEAD = 2
FC = 512
SCALE = HD**-0.5
BIG = 57
GROUPS = 3

COST = pl.CostEstimate(flops=1 << 20, bytes_accessed=1 << 16, transcendentals=0)
LONG = pl.CostEstimate(flops=1 << 35, bytes_accessed=1 << 26, transcendentals=0)

SMEM = pl.BlockSpec(memory_space=pltpu.SMEM)
IN_VMEM = pl.BlockSpec(memory_space=pltpu.VMEM)


def params(mib):
    return pltpu.CompilerParams(vmem_limit_bytes=mib << 20)


def shape(dims, dtype):
    return jax.ShapeDtypeStruct(dims, dtype)


def pinned(*arrays):
    return [pltpu.with_memory_space_constraint(a, pltpu.HBM) for a in arrays]


def nn(a, b):
    return jnp.dot(a, b, preferred_element_type=f32)


def nt(a, b):
    return lax.dot_general(a, b, (((1,), (1,)), ((), ())), preferred_element_type=f32)


def tn(a, b):
    return lax.dot_general(a, b, (((0,), (0,)), ((), ())), preferred_element_type=f32)


def whole(dims):
    return pl.BlockSpec(dims, lambda *_: (0,) * len(dims), pipeline_mode=pl.Buffered(1))


def inv_rms(v):
    return lax.rsqrt(jnp.mean(v * v, axis=-1, keepdims=True) + EPS)


def norm_back(v, gain, grad):
    r = inv_rms(v)
    unit = v * r
    scaled = grad * gain
    inner = jnp.mean(scaled * unit, axis=-1, keepdims=True)
    return r * (scaled - unit * inner), grad * unit


def rotary_tables(length):
    half = HD // 2
    freqs = np.exp(-np.log(10000.0) * np.arange(half) / half).astype(np.float32)
    angles = (np.arange(length, dtype=np.float32)[:, None] * freqs[None, :]).astype(np.float64)
    return np.cos(angles).astype(np.float32), np.sin(angles).astype(np.float32)


def rotated(v, cosine, signed, sign):
    first = lax.broadcasted_iota(jnp.int32, (1, PW), 1) % HD < HD // 2
    outs = []
    for c in range(0, v.shape[1], PW):
        part = v[:, c : c + PW]
        partner = jnp.where(first, pltpu.roll(part, PW - HD // 2, 1), pltpu.roll(part, HD // 2, 1))
        outs.append(part * cosine + partner * (signed * sign))
    return outs[0] if len(outs) == 1 else jnp.concatenate(outs, axis=1)


def token_weight(start, length, rows):
    return lax.broadcasted_iota(jnp.int32, (rows, 1), 0) + start < length


def row_sum(v):
    return jnp.sum(v, axis=0, keepdims=True)


def by_pairs(ref, rows, value):
    for p in range(ref.shape[0]):
        ref[p, rows, :] = value[:, p * PW : (p + 1) * PW].astype(ref.dtype)


def stacked(tile, low):
    zero = jnp.zeros_like(tile)
    return jnp.concatenate([jnp.where(low, tile, zero), jnp.where(low, zero, tile)], axis=0)


def unstacked(tile_t):
    half = lax.broadcasted_iota(jnp.int32, (PW, 1), 0) < HD
    return jnp.where(half, tile_t[:, :T], tile_t[:, T:])


def chunks_of(i):
    out, j = [], 0
    while j < i:
        n = 2 if i - j >= 2 else 1
        out.append((j * T, n * T))
        j += n
    return out


def edge_bias(ref, noisy):
    row = lax.broadcasted_iota(jnp.int32, (T, 2 * T), 0) // BLK
    col = (lax.broadcasted_iota(jnp.int32, (T, 2 * T), 1) % T) // BLK
    own = jnp.logical_or(row == col, jnp.logical_and(row < col, noisy == 0))
    other = jnp.logical_and(row < col, noisy == 1)
    ref[:T, :] = jnp.where(own, 0.0, NEG)
    ref[T:, :] = jnp.where(other, 0.0, NEG)


def masked(s, start, length):
    pos = lax.broadcasted_iota(jnp.int32, s.shape, 0) + start
    return jnp.where(pos < length, s, NEG)


def over_rows(op, v):
    return op(v.reshape(v.shape[0] // 8, 8, v.shape[1]), axis=0)


def attend_pair(length, q, ko, vo, kc, vc, store, lse, vo_t, vc_t, scores, bias):
    seq = q.shape[0]
    low = lax.broadcasted_iota(jnp.int32, (1, PW), 1) < HD
    vo_t[...] = vo[...].T
    vc_t[...] = vc[...].T

    def score(i):
        at = pl.ds(i * T, T)
        q2 = stacked(q[at, :] * bf16(SCALE), low)
        buf = scores.at[i % AHEAD]
        edge = nt(jnp.concatenate([ko[at, :], kc[at, :]], 0), q2) + bias[...]
        own = masked(edge[:T], i * T, length)
        other = masked(edge[T:], i * T, length)
        buf[pl.ds(0, T), :] = own
        buf[pl.ds(T, T), :] = other
        top = over_rows(jnp.max, jnp.maximum(own, other))
        for start, size in chunks_of(i):
            s = masked(nt(kc[pl.ds(start, size), :], q2), start, length)
            buf[pl.ds(2 * T + start, size), :] = s
            top = jnp.maximum(top, over_rows(jnp.max, s))
        return jnp.max(top, axis=0, keepdims=True)

    def mix(i, top):
        at = pl.ds(i * T, T)
        buf = scores.at[i % AHEAD]
        p = jnp.exp(buf[pl.ds(0, 2 * T), :] - top)
        total = over_rows(jnp.sum, p)
        acc = nn(jnp.concatenate([vo_t[:, at], vc_t[:, at]], 1), p.astype(bf16))
        for start, size in chunks_of(i):
            p = jnp.exp(buf[pl.ds(2 * T + start, size), :] - top)
            total = total + over_rows(jnp.sum, p)
            acc = acc + nn(vc_t[:, pl.ds(start, size)], p.astype(bf16))
        total = row_sum(total)
        lse[0, pl.ds(i, 1), :] = top + jnp.log(total)
        store(at, unstacked(acc * (1.0 / total)))

    tops = {}
    for i in range(seq // T + AHEAD - 1):
        if i < seq // T:
            tops[i] = score(i)
        if i >= AHEAD - 1:
            mix(i - AHEAD + 1, tops.pop(i - AHEAD + 1))


def turned_back(v, cosine, sine):
    quarter = HD // 2
    a, b, c, d = (v[i * quarter : (i + 1) * quarter] for i in range(4))
    return jnp.concatenate(
        [a * cosine + b * sine, b * cosine - a * sine, c * cosine + d * sine, d * cosine - c * sine]
    )


def attend_back_kernel(
    info, q, ko, vo, kc, vc, o, do, lse, cosine, sine, dq, keep, send, ko_t, kc_t, dko, dvo, dkc, dvc, bias
):
    noisy, length = info[0], info[1]
    q, ko, vo, kc, vc = (ref.at[0] for ref in (q, ko, vo, kc, vc))
    seq = q.shape[0]
    low = lax.broadcasted_iota(jnp.int32, (1, PW), 1) < HD

    @pl.when(pl.program_id(0) == 0)
    def _():
        edge_bias(bias, noisy)

    ko_t[...] = ko[...].T
    kc_t[...] = kc[...].T

    def tile(i):
        at = pl.ds(i * T, T)
        prod = (do[at, :].astype(f32) * o[at, :].astype(f32)).T
        delta = jnp.concatenate([row_sum(prod[:HD]), row_sum(prod[HD:])], 1)
        q2 = stacked(q[at, :] * bf16(SCALE), low)
        return q2, stacked(do[at, :], low), lse[0, pl.ds(i, 1), :], delta

    def products(i, start, size, q2, do2):
        if start is None:
            at = pl.ds(i * T, T)
            s = nt(jnp.concatenate([ko[at, :], kc[at, :]], 0), q2) + bias[...]
            s = jnp.concatenate([masked(s[:T], i * T, length), masked(s[T:], i * T, length)], 0)
            return s, nt(jnp.concatenate([vo[at, :], vc[at, :]], 0), do2)
        rows = pl.ds(start, size)
        return masked(nt(kc[rows, :], q2), start, length), nt(vc[rows, :], do2)

    def gather(i, start, size, q2, do2, p, ds, dq_t):
        at = pl.ds(i * T, T)
        dv, dk = nn(p, do2), nn(ds, q2)
        if start is None:
            dvo[at, :] = dv[:T]
            dko[at, :] = dk[:T]
            dvc[at, :] = dv[T:]
            dkc[at, :] = dk[T:]
            return nn(jnp.concatenate([ko_t[:, at], kc_t[:, at]], 1), ds)
        rows = pl.ds(start, size)
        dvc[rows, :] += dv
        dkc[rows, :] += dk
        return dq_t + nn(kc_t[:, rows], ds)

    work = [(i, *c) for i in range(seq // T) for c in [(None, None)] + chunks_of(i)]
    tiles, made, weighed, dq_t = {}, {}, {}, None
    for n in range(len(work) + 2):
        if n < len(work):
            i = work[n][0]
            if i not in tiles:
                tiles[i] = tile(i)
            made[n] = products(*work[n], *tiles[i][:2])
        if 0 <= n - 1 < len(work):
            _, _, norm, delta = tiles[work[n - 1][0]]
            s, dp = made.pop(n - 1)
            p = jnp.exp(s - norm)
            weighed[n - 1] = p.astype(bf16), (p * (dp - delta)).astype(bf16)
        if n >= 2:
            i, start, size = work[n - 2]
            dq_t = gather(i, start, size, *tiles[i][:2], *weighed.pop(n - 2), dq_t)
            if n == len(work) + 1 or work[n - 1][0] != i:
                at = pl.ds(i * T, T)
                out = turned_back(unstacked(dq_t), cosine[:, at], sine[:, at]) * SCALE
                dq[at, :] = out.T.astype(bf16)
    clean = (1 - noisy).astype(f32)
    for at, own, other in ((0, dko, dkc), (1, dvo, dvc)):
        keep[at] = (own[...] + clean * other[...]).astype(bf16)
        send[at] = other[...].astype(bf16)


def attend_back(info, first, pairs, q, ko, vo, kc, vc, o, do, lse, cosine, sine):
    seq = q.shape[1]
    width = pairs * PW
    heads = pl.BlockSpec((1, seq, PW), lambda h: (first + h, 0, 0))
    source = pl.BlockSpec((seq, PW), lambda h: (0, first + h))
    both = pl.BlockSpec((2, seq, PW), lambda h: (0, 0, h))
    lines = pl.BlockSpec((1, seq // T, 2 * T), lambda h: (first + h, 0, 0))
    table = whole((HD // 2, seq))
    return pl.pallas_call(
        attend_back_kernel,
        grid=(pairs,),
        in_specs=[SMEM] + [heads] * 5 + [source] * 2 + [lines, table, table],
        out_specs=[pl.BlockSpec((seq, PW), lambda h: (0, h)), both, both],
        out_shape=[shape((seq, width), bf16)] + [shape((2, seq, width), bf16)] * 2,
        scratch_shapes=[pltpu.VMEM((PW, seq), bf16)] * 2
        + [pltpu.VMEM((seq, PW), f32)] * 4
        + [pltpu.VMEM((2 * T, 2 * T), f32)],
        compiler_params=params(24),
        cost_estimate=LONG,
        name="attend_back",
    )(info, *pinned(q, ko, vo, kc, vc, o, do), lse, cosine, sine)


C0 = 0.7978845608028654
C1 = C0 * 0.044715


def layer_kernel(
    info, gain1_line, gain2_line, received_any, x_any, wqkv_any, cosine_any, signed_any, wo_any, dy_any,
    w1_any, w2_any,
    q_out, ko_out, vo_out, kc_out, vc_out, h1t_out, o_out, lse_out, out_any, dx2_any, do_any,
    up_send, up_keep, down_send, down_keep, g_send, g_keep, sums,
    x, received, wqkv, cosine, signed, q, ko, vo, h1t, wo, dy, w1, w2,
    kc, vc, vo_t, vc_t, scores, bias, o, o_t, lse, x2, h2, m, dh, act, du, up_grad, down_grad, half_grads,
    sem_in, sem_1, sem_2, sem_out, sem_up, sem_down, sem_tile,
):
    noisy, length = info[0], info[1]
    seq, width = x.shape
    chunks, pairs, tiles = w1.shape[0], kc.shape[0], seq // R
    copy = pltpu.make_async_copy
    gain1, gain2 = gain1_line[...].reshape(1, width), gain2_line[...].reshape(1, width)

    def weights(c):
        place = lax.rem(c + (chunks // 2) * (1 - noisy), chunks) * FC
        place = pl.multiple_of(place, FC)
        return (
            copy(w1_any.at[:, pl.ds(place, FC)], w1.at[c], sem_1.at[c]),
            copy(w2_any.at[pl.ds(place, FC), :], w2.at[c], sem_2.at[c]),
        )

    sources = (
        (x_any, x),
        (wqkv_any, wqkv),
        (cosine_any, cosine),
        (signed_any, signed),
        (received_any, received),
        (wo_any, wo),
        (dy_any, dy),
    )
    loads = [copy(a, b, sem_in.at[i]) for i, (a, b) in enumerate(sources)]
    for load in loads[:5]:
        load.start()
    sums[...] = jnp.zeros_like(sums)
    edge_bias(bias, noisy)

    for load in loads[:4]:
        load.wait()

    def own_rows(t, carry):
        start = pl.multiple_of(t * R, R)
        rows = pl.ds(start, R)
        value = x[rows, :].astype(f32)
        h1 = (value * inv_rms(value) * gain1).astype(bf16)
        h1t[:, rows] = h1.T
        tables = (cosine[rows, :], signed[rows, :], 1.0)
        by_pairs(q, rows, rotated(nn(h1, wqkv[:, :width]), *tables))
        by_pairs(ko, rows, rotated(nn(h1, wqkv[:, width : 2 * width]), *tables))
        by_pairs(vo, rows, nn(h1, wqkv[:, 2 * width :]))
        weight = token_weight(start, length, R)
        sums[0:1, :] += row_sum(jnp.where(weight, value * value, 0.0))
        return carry

    lax.fori_loop(0, tiles, own_rows, 0)
    stores = [copy(a, b, sem_out.at[6 + i]) for i, (a, b) in enumerate(((q, q_out), (ko, ko_out), (vo, vo_out), (h1t, h1t_out)))]
    for store in stores:
        store.start()
    loads[4].wait()

    def clean_rows(t, carry):
        rows = pl.ds(pl.multiple_of(t * R, R), R)
        value = jnp.where(noisy == 1, received[rows, :].astype(f32), x[rows, :].astype(f32))
        h1 = (value * inv_rms(value) * gain1).astype(bf16)
        by_pairs(kc, rows, rotated(nn(h1, wqkv[:, width : 2 * width]), cosine[rows, :], signed[rows, :], 1.0))
        by_pairs(vc, rows, nn(h1, wqkv[:, 2 * width :]))
        return carry

    lax.fori_loop(0, tiles, clean_rows, 0)
    for load in loads[5:]:
        load.start()
    more = [copy(kc, kc_out, sem_out.at[0]), copy(vc, vc_out, sem_out.at[1])]
    for store in more:
        store.start()
    stores += more

    for c in range(chunks):
        for load in weights(c):
            load.start()

    def one_pair(p, carry):
        lanes = pl.ds(pl.multiple_of(p * PW, PW), PW)

        def keep(at, tile_t):
            o_t[lanes, at] = tile_t.astype(bf16)
            o[at, lanes] = tile_t.T.astype(bf16)

        heads = (ref.at[p] for ref in (q, ko, vo, kc, vc))
        attend_pair(length, *heads, keep, lse.at[pl.ds(p, 1)], vo_t, vc_t, scores, bias)
        return carry

    lax.fori_loop(0, pairs, one_pair, 0)
    more = [copy(o, o_out, sem_out.at[2]), copy(lse, lse_out, sem_out.at[3])]
    for store in more:
        store.start()
    stores += more

    for load in loads[5:]:
        load.wait()

    def joined_rows(t, carry):
        start = pl.multiple_of(t * R, R)
        rows = pl.ds(start, R)
        branch = nn(o[rows, :], wo[...])
        value = x[rows, :].astype(f32) + branch
        x2[rows, :] = value
        h2[rows, :] = (value * inv_rms(value) * gain2).astype(bf16)
        m[rows, :] = jnp.zeros_like(value)
        dh[rows, :] = jnp.zeros_like(value)
        weight = token_weight(start, length, R)
        sums[1:2, :] += row_sum(jnp.where(weight, branch * branch, 0.0))
        return carry

    lax.fori_loop(0, tiles, joined_rows, 0)

    def grad_stores(c, up, down):
        slot = lax.rem(c, 2)
        rows = pl.ds(pl.multiple_of(lax.rem(c, chunks // 2) * FC, FC), FC)
        return (
            copy(up_grad.at[slot], up.at[rows, :], sem_up.at[slot]),
            copy(down_grad.at[slot], down.at[rows, :], sem_down.at[slot]),
        )

    def one_chunk(c, carry):
        for load in weights(c):
            load.wait()
        up, down = w1.at[c], w2.at[c]
        for t in range(0, seq, R):
            rows = pl.ds(t, R)
            u = nn(h2[rows, :], up[...])
            da = nt(dy[rows, :], down[...])
            sq = u * u
            half = 0.5 * jnp.tanh(u * (C0 + C1 * sq)) + 0.5
            low = (u * half).astype(bf16)
            slope = half + u * (2.0 * half * (1.0 - half)) * (C0 + 3.0 * C1 * sq)
            back = (da * slope).astype(bf16)
            act[rows, :] = low
            du[rows, :] = back
            m[rows, :] += nn(low, down[...])
            dh[rows, :] += nt(back, up[...])

        @pl.when(c >= 2)
        def _():
            for store in grad_stores(c, up_send, down_send):
                store.wait()

        slot = lax.rem(c, 2)
        down_grad[slot] = tn(act[...], dy[...]).astype(bf16)
        up_grad[slot] = tn(du[...], h2[...]).astype(bf16)

        @pl.when(c < chunks // 2)
        def _():
            for store in grad_stores(c, up_send, down_send):
                store.start()

        @pl.when(c >= chunks // 2)
        def _():
            for store in grad_stores(c, up_keep, down_keep):
                store.start()

        return carry

    lax.fori_loop(0, chunks, one_chunk, 0)

    def tile_stores(t):
        rows = pl.ds(pl.multiple_of(t * R, R), R)
        return (
            copy(h2.at[rows, :], out_any.at[rows, :], sem_tile.at[t, 0]),
            copy(x2.at[rows, :], dx2_any.at[rows, :], sem_tile.at[t, 1]),
            copy(received.at[rows, :], do_any.at[rows, :], sem_tile.at[t, 2]),
        )

    def middle_rows(t, carry):
        start = pl.multiple_of(t * R, R)
        rows = pl.ds(start, R)
        value = x2[rows, :]
        mixed = m[rows, :]
        weight = token_weight(start, length, R)
        sums[2:3, :] += row_sum(jnp.where(weight, mixed * mixed, 0.0))
        grad, gain_terms = norm_back(value, gain2, dh[rows, :])
        sums[3:4, :] += row_sum(gain_terms)
        grad = grad + dy[rows, :].astype(f32)
        da = grad.astype(bf16)
        h2[rows, :] = (value + mixed).astype(bf16)
        x2[rows, :] = grad
        received[rows, :] = nt(da, wo[...]).astype(bf16)
        x[rows, :] = da
        for store in tile_stores(t):
            store.start()
        return carry

    lax.fori_loop(0, tiles, middle_rows, 0)
    half = width // 2
    mine = pl.multiple_of(noisy * half, half)
    half_grads[0] = nn(o_t[pl.ds(half - mine, half), :], x[...]).astype(bf16)
    half_grads[1] = nn(o_t[pl.ds(mine, half), :], x[...]).astype(bf16)
    more = [copy(half_grads.at[0], g_send, sem_out.at[4]), copy(half_grads.at[1], g_keep, sem_out.at[5])]
    for store in more:
        store.start()
    stores += more
    for c in range(chunks - 2, chunks):
        stores += grad_stores(c, up_keep, down_keep)
    for t in range(tiles):
        stores += tile_stores(t)
    for store in stores:
        store.wait()


def layer(info, gain1, gain2, received, x, wqkv, tables, wo, dy, w1, w2):
    seq, width = x.shape
    hidden = w1.shape[1]
    tiles, pairs, chunks = seq // R, width // PW, hidden // FC
    anywhere = pl.BlockSpec(memory_space=pl.ANY)
    vmem = pltpu.VMEM
    dma = pltpu.SemaphoreType.DMA
    heads = (pairs, seq, PW)
    flat = (seq, width)
    outs = (
        [shape(heads, bf16)] * 5
        + [shape((width, seq), bf16), shape(flat, bf16), shape((pairs, seq // T, 2 * T), f32)]
        + [shape(flat, bf16), shape(flat, f32), shape(flat, bf16)]
        + [shape((hidden // 2, width), bf16)] * 4
        + [shape((width // 2, width), bf16)] * 2
        + [shape((8, width), f32)]
    )
    return pl.pallas_call(
        layer_kernel,
        in_specs=[SMEM, IN_VMEM, IN_VMEM] + [anywhere] * 9,
        out_specs=[anywhere] * 17 + [IN_VMEM],
        out_shape=outs,
        scratch_shapes=[vmem(flat, bf16)] * 2
        + [vmem(wqkv.shape, bf16), vmem((seq, PW), f32), vmem((seq, PW), f32)]
        + [vmem(heads, bf16)] * 3
        + [vmem((width, seq), bf16), vmem((width, width), bf16), vmem(flat, bf16)]
        + [vmem((chunks, width, FC), bf16), vmem((chunks, FC, width), bf16)]
        + [vmem(heads, bf16)] * 2
        + [vmem((PW, seq), bf16)] * 2
        + [vmem((AHEAD, seq + T, 2 * T), f32), vmem((2 * T, 2 * T), f32)]
        + [vmem(flat, bf16), vmem((width, seq), bf16)]
        + [vmem((pairs, seq // T, 2 * T), f32)]
        + [vmem(flat, f32), vmem(flat, bf16)]
        + [vmem(flat, f32)] * 2
        + [vmem((seq, FC), bf16)] * 2
        + [vmem((2, FC, width), bf16)] * 2
        + [vmem((2, width // 2, width), bf16)]
        + [dma((7,)), dma((chunks,)), dma((chunks,)), dma((10,)), dma((2,)), dma((2,)), dma((tiles, 3))],
        compiler_params=params(BIG),
        cost_estimate=LONG,
        name="layer",
    )(info, gain1, gain2, received, *pinned(x, wqkv, *tables, wo, dy, w1, w2))


def weigh_kernel(first, info, dq, keep, got, cosine, signed, h1t, wqkv, sums, dkv, g_send, g_keep, small):
    width, half = wqkv.shape[0], wqkv.shape[0] // 2
    mine = pl.multiple_of(info[0] * half, half)
    dk = keep[0].astype(f32) + got[0].astype(f32)
    dkv[0] = rotated(dk, cosine[...], signed[...], -1.0).astype(bf16)
    dkv[1] = (keep[1].astype(f32) + got[1].astype(f32)).astype(bf16)
    small[...] = sums[...]
    for out, start in ((g_send, half - mine), (g_keep, mine)):
        rows = pl.ds(start, half)
        terms = 0.0
        for i, part in enumerate((dq, dkv.at[0], dkv.at[1])):
            total = nn(h1t[rows, :], part[...])
            out[i] = total.astype(bf16)
            at = i * width + first * PW
            weighted = total * wqkv[rows, at : at + total.shape[1]].astype(f32)
            for c in range(0, total.shape[1], PW):
                terms = terms + weighted[:, c : c + PW]
        line = jnp.sum(terms.T, axis=0, keepdims=True)
        lanes = lax.broadcasted_iota(jnp.int32, (1, width), 1)
        inside = jnp.logical_and(lanes >= start, lanes < start + half)
        small[4:5, :] += jnp.where(inside, jnp.concatenate([line, line], axis=1), 0.0)
    small[5:6, :] = jnp.full((1, width), info[1].astype(f32))


def weigh(info, first, dq, keep, got, tables, h1t, wqkv, sums):
    seq, width = dq.shape
    tall = h1t.shape[0]
    return pl.pallas_call(
        functools.partial(weigh_kernel, first),
        in_specs=[SMEM] + [IN_VMEM] * 8,
        out_specs=[IN_VMEM] * 4,
        out_shape=[shape((2, seq, width), bf16)]
        + [shape((3, tall // 2, width), bf16)] * 2
        + [shape(sums.shape, f32)],
        compiler_params=params(24),
        cost_estimate=LONG,
        name="weigh",
    )(info, dq, keep, got, *tables, h1t, wqkv, sums)


def finish_kernel(parts, x, dx2, wqkv, gain_line, *refs):
    dx_any, dx, sem = refs[-3:]
    dqs, dkvs = refs[:parts], refs[parts : 2 * parts]
    tiles = sem.shape[0]
    gain = gain_line[...].reshape(1, x.shape[1])

    def store(t):
        rows = pl.ds(pl.multiple_of(t * R, R), R)
        return pltpu.make_async_copy(dx.at[rows, :], dx_any.at[rows, :], sem.at[t])

    def some_rows(t, carry):
        rows = pl.ds(pl.multiple_of(t * R, R), R)
        grads = [r[rows, :] for r in dqs] + [r[0, rows, :] for r in dkvs] + [r[1, rows, :] for r in dkvs]
        dh = nt(jnp.concatenate(grads, axis=1), wqkv[...])
        grad, _ = norm_back(x[rows, :].astype(f32), gain, dh)
        dx[rows, :] = (dx2[rows, :] + grad).astype(bf16)
        store(t).start()
        return carry

    lax.fori_loop(0, tiles, some_rows, 0)
    for t in range(tiles):
        store(t).wait()


def finish(x, dx2, dqs, dkvs, weight, gain):
    return pl.pallas_call(
        functools.partial(finish_kernel, len(dqs)),
        in_specs=[IN_VMEM] * (4 + len(dqs) + len(dkvs)),
        out_specs=pl.BlockSpec(memory_space=pl.ANY),
        out_shape=shape(x.shape, bf16),
        scratch_shapes=[pltpu.VMEM(x.shape, bf16), pltpu.SemaphoreType.DMA((x.shape[0] // R,))],
        compiler_params=params(24),
        cost_estimate=LONG,
        name="finish",
    )(x, dx2, weight, gain, *dqs, *dkvs)


def bit_orders(count, groups):
    bits = [1 << i for i in range(count.bit_length() - 1)]
    if groups == 2:
        return [bits, bits[1::-1] + bits[2:]]
    return [bits[g:-1] + bits[:g] + bits[-1:] for g in range(groups)]


def exchange(value, axis, bit):
    size = lax.axis_size(axis)
    return lax.ppermute(value, axis, [(i, i ^ bit) for i in range(size)])


def distance(order, place):
    out = 0
    for i, bit in enumerate(order):
        out = out + ((place >> (len(order) - 1 - i)) & 1) * bit
    return out


LINES = 16


def halves(value):
    high = value.astype(bf16)
    return high, (value - high.astype(f32)).astype(bf16)


def put_sums(value, kept, block):
    high, low = halves(value)
    block[:LINES, :] = high
    block[LINES : 2 * LINES, :] = low
    kept[...] = high.astype(f32) + low.astype(f32)


def got_sums(block):
    return block[:LINES, :].astype(f32) + block[LINES : 2 * LINES, :].astype(f32)


def start_kernel(orders, sources, small, me, *refs):
    groups = len(orders)
    arrays = max(a for source in sources for a, _ in source) + 1
    ins, outs = refs[: 2 * arrays], refs[len(refs) - 2 * groups :]
    half = outs[0].shape[0]
    for g, order in enumerate(orders):
        for side in range(2):

            def one(r, carry, g=g, order=order, side=side):
                part = me[0] ^ distance(order, r + side * half)
                row = 0
                for a, where in sources[g]:
                    kept, got = ins[2 * a : 2 * a + 2]
                    place = where(part)
                    size = kept.shape[1]
                    total = kept[place].astype(f32) + got[place].astype(f32)
                    outs[2 * g + side][r, row : row + size, :] = total.astype(bf16)
                    row += size
                return carry

            lax.fori_loop(0, half, one, 0)
    if small:
        here, there, kept = refs[2 * arrays : 2 * arrays + 3]
        total = here[...] + there[...]
        if small == "rides":
            wide = total.shape[1] // 2
            total = jnp.concatenate([total[:, :wide], total[:, wide:]], axis=0)
            put_sums(total, kept, outs[1].at[half])
        else:
            kept[...] = total


def start_sum(me, kept, got, sources, orders, small, rides):
    count = 1 << len(orders[0])
    half = count // 2
    rows = [sum(kept[a].shape[1] for a, _ in source) for source in sources]
    width = kept[0].shape[2]
    cols = width // 3
    args = [a for pair in zip(kept, got, strict=True) for a in pair]
    sums = []
    for g in range(len(orders)):
        sums += [shape((half, rows[g], width), bf16), shape((half + (rides and g == 0), rows[g], width), bf16)]
    mode = "rides" if rides else "alone" if small else ""
    if small:
        lines = (LINES, width) if rides else small[0].shape
        specs = dict(
            in_specs=[SMEM] + [IN_VMEM] * (len(args) + 2),
            out_specs=[IN_VMEM] * (1 + len(sums)),
            out_shape=[shape(lines, f32)] + sums,
        )
    else:
        block = lambda a: pl.BlockSpec((a.shape[0], a.shape[1], cols), lambda c: (0, 0, c))
        specs = dict(
            grid=(width // cols,),
            in_specs=[SMEM] + [block(a) for a in args],
            out_specs=[block(a) for a in sums],
            out_shape=sums,
        )
    outs = pl.pallas_call(
        functools.partial(start_kernel, orders, sources, mode),
        compiler_params=params(30),
        cost_estimate=COST,
        name="start_sum",
        **specs,
    )(me, *args, *small)
    small, outs = list(outs[: len(outs) - len(sums)]), outs[len(outs) - len(sums) :]
    return list(outs[0::2]), list(outs[1::2]), small


def step_kernel(groups, merge, mode, *refs):
    kept, got = refs[:groups], refs[groups : 2 * groups]
    outs = refs[2 * groups + (2 if mode == "alone" else 1 if mode else 0) :]
    count = kept[0].shape[0]
    half = count // 2
    row = 0
    for g in range(groups):
        total = (kept[g][...].astype(f32) + got[g][:count].astype(f32)).astype(bf16)
        keep, send = outs[:2] if merge else outs[2 * g : 2 * g + 2]
        size = total.shape[1]
        keep[:, row : row + size, :] = total[:half]
        send[:half, row : row + size, :] = total[half:]
        row += size if merge else 0
    if mode == "rides":
        total = refs[2 * groups][...] + got_sums(got[0].at[count])
        put_sums(total, outs[-1], outs[1].at[half])
    elif mode:
        outs[-1][...] = refs[2 * groups][...] + refs[2 * groups + 1][...]


def step_sum(kept, got, small, merge, rides):
    groups = len(kept)
    half = kept[0].shape[0] // 2
    rows = [a.shape[1] for a in kept]
    width = kept[0].shape[2]
    args = [*kept, *got, *small]
    sums = []
    for g, r in enumerate([sum(rows)] if merge else rows):
        sums += [shape((half, r, width), bf16), shape((half + (rides and g == 0), r, width), bf16)]
    outs = pl.pallas_call(
        functools.partial(step_kernel, groups, merge, "rides" if rides else "alone" if small else ""),
        in_specs=[IN_VMEM] * len(args),
        out_specs=[IN_VMEM] * (len(sums) + len(small[:1])),
        out_shape=sums + [shape(a.shape, f32) for a in small[:1]],
        compiler_params=params(16),
        cost_estimate=COST if small else LONG,
        name="step_sum",
    )(*args)
    return list(outs[0 : len(sums) : 2]), list(outs[1 : len(sums) : 2]), list(outs[len(sums) :])


def feed_end_kernel(kept, got, down, up, out):
    total = kept[0].astype(f32) + got[0].astype(f32)
    tall, few = down.shape[0] // GROUPS, out.shape[0] // GROUPS
    ups = []
    for g in range(GROUPS):
        row = g * (2 * tall + few)
        down[g * tall : (g + 1) * tall, :] = total[row : row + tall]
        ups.append(total[row + tall : row + 2 * tall])
        out[g * few : (g + 1) * few, :] = total[row + 2 * tall : row + 2 * tall + few]
    up[...] = jnp.concatenate(ups, axis=0).T


def feed_end(kept, got, tall, few):
    width = kept.shape[2]
    return pl.pallas_call(
        feed_end_kernel,
        in_specs=[IN_VMEM] * 2,
        out_specs=[IN_VMEM] * 3,
        out_shape=[shape((tall, width), f32), shape((width, tall), f32), shape((few, width), f32)],
        compiler_params=params(16),
        cost_estimate=COST,
        name="feed_end",
    )(kept, got)


def qkv_end_kernel(rides, gain_line, kept, got, *refs):
    out, gain1, gain2, rms = refs[-4:]
    tall = out.shape[0]
    width = gain1.shape[0]
    cols = kept.shape[2]
    total = kept[0].astype(f32) + got[0].astype(f32)
    for i in range(total.shape[0] // tall):
        part, third = i // 3, i % 3
        at = third * width + part * cols
        out[:, at : at + cols] = total[i * tall : (i + 1) * tall]
    if rides:
        sums = refs[0][...] + got_sums(got.at[1])
        sums = jnp.concatenate([sums[: LINES // 2], sums[LINES // 2 :]], axis=1)
    else:
        sums = refs[0][...] + refs[1][...]
    gain2[...] = sums[3:4, :].reshape(width)
    gain1[...] = (sums[4:5, :] / gain_line[...].reshape(1, width)).reshape(width)
    count = jnp.max(sums[5:6, :], axis=1, keepdims=True) * width
    rms[...] = jnp.broadcast_to(jnp.sqrt(jnp.sum(sums, axis=1, keepdims=True) / count), rms.shape)


def qkv_end(gain, kept, got, small, tall, wide, rides):
    return pl.pallas_call(
        functools.partial(qkv_end_kernel, rides),
        in_specs=[IN_VMEM] * (3 + len(small)),
        out_specs=[IN_VMEM] * 4,
        out_shape=[shape((tall, wide), f32), shape(gain.shape, f32), shape(gain.shape, f32), shape((8, 128), f32)],
        compiler_params=params(16),
        cost_estimate=COST,
        name="qkv_end",
    )(gain, kept, got, *small)


def after(value, *earlier):
    return lax.optimization_barrier((value, earlier))[0]


def sum_parts(me, kept, got, sources, small, rides):
    orders = bit_orders(lax.axis_size("batch"), len(sources))
    steps = len(orders[0])
    common = min(i for i in range(steps + 1) if all(order[i:] == orders[0][i:] for order in orders))
    keep, send, small = start_sum(me, kept, got, sources, orders, small, rides)
    for i in range(steps):
        got = [exchange(s, "batch", order[i]) for s, order in zip(send, orders[: len(send)], strict=True)]
        if small and not rides:
            small = [small[0], exchange(small[0], "batch", orders[0][i])]
        earlier = yield send[0], got
        if i == steps - 1:
            break
        if earlier is not None:
            keep = after(keep, earlier)
        keep, send, small = step_sum(keep, got, small, i + 1 == common, rides)
    yield keep[0], got[0], small


def on_device(
    inputs, lengths, cotangent, qkv_weight, out_weight, up_weight, down_weight, attn_gain, mlp_gain
):
    seq, width = inputs.shape[2:]
    x = inputs[0, 0]
    dy = cotangent[0, 0]
    count = lax.axis_size("batch")
    stream = lax.axis_index("stream").astype(jnp.int32)
    me = lax.axis_index("batch").astype(jnp.int32).reshape(1)
    info = jnp.stack([stream, lengths[0]])
    cosine, sine = rotary_tables(seq)
    tables = (
        jnp.asarray(np.concatenate([cosine] * 4, axis=1)),
        jnp.asarray(np.concatenate([-sine, sine] * 2, axis=1)),
    )
    tables_t = (jnp.asarray(cosine.T), jnp.asarray(sine.T))

    received = lax.ppermute(x, "stream", [(0, 1)])
    (
        q, ko, vo, kc, vc, h1t, o, lse, outputs, dx2, do,
        up_send, up_keep, down_send, down_keep, out_send, out_keep, sums,
    ) = layer(
        info, attn_gain, mlp_gain, received, x, qkv_weight, tables, out_weight, dy, up_weight, down_weight
    )
    down_got, up_got, out_got = (exchange(a, "stream", 1) for a in (down_send, up_send, out_send))

    def by_rows(array):
        return array.reshape(count * GROUPS, array.shape[0] // (count * GROUPS), width)

    heads = (q, ko, vo, kc, vc, o)
    pairs = width // PW // 2
    dq1, keep1, send1 = attend_back(info, 0, pairs, *heads, do, lse, *tables_t)
    got1 = lax.ppermute(send1, "stream", [(1, 0)])
    early = sum_parts(
        me,
        [by_rows(after(a, dq1)) for a in (down_keep, up_keep, out_keep)],
        [by_rows(a) for a in (down_got, up_got, out_got)],
        [[(a, lambda part, g=g: part * GROUPS + g) for a in range(3)] for g in range(GROUPS)],
        [],
        False,
    )
    token = next(early)[0]
    dq2, keep2, send2 = attend_back(info, pairs, pairs, *heads, after(do, token), lse, *tables_t)
    got2 = lax.ppermute(send2, "stream", [(1, 0)])
    token = early.send(dq2)[0]
    dkv1, qkv_send1, qkv_keep1, small = weigh(info, 0, dq1, after(keep1, token), got1, tables, h1t, qkv_weight, sums)
    qkv_got1 = exchange(qkv_send1, "stream", 1)
    dkv2, qkv_send2, qkv_keep2, small = weigh(info, pairs, dq2, keep2, got2, tables, h1t, qkv_weight, small)
    qkv_got2 = exchange(qkv_send2, "stream", 1)
    small_got = exchange(small, "stream", 1)
    token = early.send(dkv2)[0]

    tall = width // (2 * count)
    split = lambda a: a.reshape(3 * count, tall, a.shape[2])
    rides = 3 * tall >= 2 * LINES
    late = sum_parts(
        me,
        [split(after(a, token)) for a in (qkv_keep1, qkv_keep2)],
        [split(a) for a in (qkv_got1, qkv_got2)],
        [[(g, lambda part, i=i: i * count + part) for i in range(3)] for g in range(2)],
        [small, small_got],
        rides,
    )
    token, came = next(late)
    dx = finish(after(x, token), dx2, [dq1, dq2], [dkv1, dkv2], qkv_weight, attn_gain)
    early_out = early.send((dx, came))
    late_out = late.send(early_out[0])
    while len(late_out) == 2:
        last = late_out[0].shape[0] <= 3
        late_out = late.send(early_out[1] if last and len(early_out) == 2 else None)
    while len(early_out) == 2:
        early_out = early.send(None)
    up_cols = down_keep.shape[0] // count
    down_grad, up_grad, out_grad = feed_end(*early_out[:2], up_cols, tall)
    qkv_grad, gain1_grad, gain2_grad, rms = qkv_end(attn_gain, *late_out, tall, 3 * width, rides)
    return (
        outputs[None, None],
        dx[None, None],
        qkv_grad,
        out_grad,
        up_grad,
        down_grad,
        gain1_grad,
        gain2_grad,
        rms[:3, 0],
    )


def solution(mesh):
    rows = P("stream", "batch", None, None)
    both = ("stream", "batch")
    return jax.shard_map(
        on_device,
        mesh=mesh,
        in_specs=(rows, P("batch"), rows, P(), P(), P(), P(), P(), P()),
        out_specs=(rows, rows, P(both, None), P(both, None), P(None, both), P(both, None), P(), P(), P()),
        check_vma=False,
    )
```

```python
import functools

import jax
import jax.numpy as jnp
import numpy as np
from jax import lax
from jax.experimental import pallas as pl
from jax.experimental.pallas import tpu as pltpu
from jax.sharding import PartitionSpec as P

f32 = jnp.float32
bf16 = jnp.bfloat16

HD = 64
BLK = 16
EPS = 1e-06
NEG = -1e30
PW = 2 * HD
T = 128
R = 256
AHEAD = 2
FC = 512
SCALE = HD**-0.5
BIG = 57
GROUPS = 3

COST = pl.CostEstimate(flops=1 << 20, bytes_accessed=1 << 16, transcendentals=0)
LONG = pl.CostEstimate(flops=1 << 35, bytes_accessed=1 << 26, transcendentals=0)

SMEM = pl.BlockSpec(memory_space=pltpu.SMEM)
IN_VMEM = pl.BlockSpec(memory_space=pltpu.VMEM)


def params(mib):
    return pltpu.CompilerParams(vmem_limit_bytes=mib << 20)


def shape(dims, dtype):
    return jax.ShapeDtypeStruct(dims, dtype)


def pinned(*arrays):
    return [pltpu.with_memory_space_constraint(a, pltpu.HBM) for a in arrays]


def nn(a, b):
    return jnp.dot(a, b, preferred_element_type=f32)


def nt(a, b):
    return lax.dot_general(a, b, (((1,), (1,)), ((), ())), preferred_element_type=f32)


def tn(a, b):
    return lax.dot_general(a, b, (((0,), (0,)), ((), ())), preferred_element_type=f32)


def whole(dims):
    return pl.BlockSpec(dims, lambda *_: (0,) * len(dims), pipeline_mode=pl.Buffered(1))


def inv_rms(v):
    return lax.rsqrt(jnp.mean(v * v, axis=-1, keepdims=True) + EPS)


def norm_back(v, gain, grad):
    r = inv_rms(v)
    unit = v * r
    scaled = grad * gain
    inner = jnp.mean(scaled * unit, axis=-1, keepdims=True)
    return r * (scaled - unit * inner), grad * unit


def rotary_tables(length):
    half = HD // 2
    freqs = np.exp(-np.log(10000.0) * np.arange(half) / half).astype(np.float32)
    angles = (np.arange(length, dtype=np.float32)[:, None] * freqs[None, :]).astype(np.float64)
    return np.cos(angles).astype(np.float32), np.sin(angles).astype(np.float32)


def rotated(v, cosine, signed, sign):
    first = lax.broadcasted_iota(jnp.int32, (1, PW), 1) % HD < HD // 2
    outs = []
    for c in range(0, v.shape[1], PW):
        part = v[:, c : c + PW]
        partner = jnp.where(first, pltpu.roll(part, PW - HD // 2, 1), pltpu.roll(part, HD // 2, 1))
        outs.append(part * cosine + partner * (signed * sign))
    return outs[0] if len(outs) == 1 else jnp.concatenate(outs, axis=1)


def token_weight(start, length, rows):
    return lax.broadcasted_iota(jnp.int32, (rows, 1), 0) + start < length


def row_sum(v):
    return jnp.sum(v, axis=0, keepdims=True)


def by_pairs(ref, rows, value):
    for p in range(ref.shape[0]):
        ref[p, rows, :] = value[:, p * PW : (p + 1) * PW].astype(ref.dtype)


def stacked(tile, low):
    zero = jnp.zeros_like(tile)
    return jnp.concatenate([jnp.where(low, tile, zero), jnp.where(low, zero, tile)], axis=0)


def unstacked(tile_t):
    half = lax.broadcasted_iota(jnp.int32, (PW, 1), 0) < HD
    return jnp.where(half, tile_t[:, :T], tile_t[:, T:])


def chunks_of(i):
    out, j = [], 0
    while j < i:
        n = 2 if i - j >= 2 else 1
        out.append((j * T, n * T))
        j += n
    return out


def edge_bias(ref, noisy):
    row = lax.broadcasted_iota(jnp.int32, (T, 2 * T), 0) // BLK
    col = (lax.broadcasted_iota(jnp.int32, (T, 2 * T), 1) % T) // BLK
    own = jnp.logical_or(row == col, jnp.logical_and(row < col, noisy == 0))
    other = jnp.logical_and(row < col, noisy == 1)
    ref[:T, :] = jnp.where(own, 0.0, NEG)
    ref[T:, :] = jnp.where(other, 0.0, NEG)


def masked(s, start, length):
    pos = lax.broadcasted_iota(jnp.int32, s.shape, 0) + start
    return jnp.where(pos < length, s, NEG)


def over_rows(op, v):
    return op(v.reshape(v.shape[0] // 8, 8, v.shape[1]), axis=0)


def attend_pair(length, q, ko, vo, kc, vc, store, lse, vo_t, vc_t, scores, bias):
    seq = q.shape[0]
    low = lax.broadcasted_iota(jnp.int32, (1, PW), 1) < HD
    vo_t[...] = vo[...].T
    vc_t[...] = vc[...].T

    def score(i):
        at = pl.ds(i * T, T)
        q2 = stacked(q[at, :] * bf16(SCALE), low)
        buf = scores.at[i % AHEAD]
        edge = nt(jnp.concatenate([ko[at, :], kc[at, :]], 0), q2) + bias[...]
        own = masked(edge[:T], i * T, length)
        other = masked(edge[T:], i * T, length)
        buf[pl.ds(0, T), :] = own
        buf[pl.ds(T, T), :] = other
        top = over_rows(jnp.max, jnp.maximum(own, other))
        for start, size in chunks_of(i):
            s = masked(nt(kc[pl.ds(start, size), :], q2), start, length)
            buf[pl.ds(2 * T + start, size), :] = s
            top = jnp.maximum(top, over_rows(jnp.max, s))
        return jnp.max(top, axis=0, keepdims=True)

    def mix(i, top):
        at = pl.ds(i * T, T)
        buf = scores.at[i % AHEAD]
        p = jnp.exp(buf[pl.ds(0, 2 * T), :] - top)
        total = over_rows(jnp.sum, p)
        acc = nn(jnp.concatenate([vo_t[:, at], vc_t[:, at]], 1), p.astype(bf16))
        for start, size in chunks_of(i):
            p = jnp.exp(buf[pl.ds(2 * T + start, size), :] - top)
            total = total + over_rows(jnp.sum, p)
            acc = acc + nn(vc_t[:, pl.ds(start, size)], p.astype(bf16))
        total = row_sum(total)
        lse[0, pl.ds(i, 1), :] = top + jnp.log(total)
        store(at, unstacked(acc * (1.0 / total)))

    tops = {}
    for i in range(seq // T + AHEAD - 1):
        if i < seq // T:
            tops[i] = score(i)
        if i >= AHEAD - 1:
            mix(i - AHEAD + 1, tops.pop(i - AHEAD + 1))


def turned_back(v, cosine, sine):
    quarter = HD // 2
    a, b, c, d = (v[i * quarter : (i + 1) * quarter] for i in range(4))
    return jnp.concatenate(
        [a * cosine + b * sine, b * cosine - a * sine, c * cosine + d * sine, d * cosine - c * sine]
    )


def attend_back_kernel(
    info, q, ko, vo, kc, vc, o, do, lse, cosine, sine, dq, keep, send, ko_t, kc_t, dko, dvo, dkc, dvc, bias
):
    noisy, length = info[0], info[1]
    q, ko, vo, kc, vc = (ref.at[0] for ref in (q, ko, vo, kc, vc))
    seq = q.shape[0]
    low = lax.broadcasted_iota(jnp.int32, (1, PW), 1) < HD

    @pl.when(pl.program_id(0) == 0)
    def _():
        edge_bias(bias, noisy)

    ko_t[...] = ko[...].T
    kc_t[...] = kc[...].T

    def tile(i):
        at = pl.ds(i * T, T)
        prod = (do[at, :].astype(f32) * o[at, :].astype(f32)).T
        delta = jnp.concatenate([row_sum(prod[:HD]), row_sum(prod[HD:])], 1)
        q2 = stacked(q[at, :] * bf16(SCALE), low)
        return q2, stacked(do[at, :], low), lse[0, pl.ds(i, 1), :], delta

    def products(i, start, size, q2, do2):
        if start is None:
            at = pl.ds(i * T, T)
            s = nt(jnp.concatenate([ko[at, :], kc[at, :]], 0), q2) + bias[...]
            s = jnp.concatenate([masked(s[:T], i * T, length), masked(s[T:], i * T, length)], 0)
            return s, nt(jnp.concatenate([vo[at, :], vc[at, :]], 0), do2)
        rows = pl.ds(start, size)
        return masked(nt(kc[rows, :], q2), start, length), nt(vc[rows, :], do2)

    def gather(i, start, size, q2, do2, p, ds, dq_t):
        at = pl.ds(i * T, T)
        dv, dk = nn(p, do2), nn(ds, q2)
        if start is None:
            dvo[at, :] = dv[:T]
            dko[at, :] = dk[:T]
            dvc[at, :] = dv[T:]
            dkc[at, :] = dk[T:]
            return nn(jnp.concatenate([ko_t[:, at], kc_t[:, at]], 1), ds)
        rows = pl.ds(start, size)
        dvc[rows, :] += dv
        dkc[rows, :] += dk
        return dq_t + nn(kc_t[:, rows], ds)

    work = [(i, *c) for i in range(seq // T) for c in [(None, None)] + chunks_of(i)]
    tiles, made, weighed, dq_t = {}, {}, {}, None
    for n in range(len(work) + 2):
        if n < len(work):
            i = work[n][0]
            if i not in tiles:
                tiles[i] = tile(i)
            made[n] = products(*work[n], *tiles[i][:2])
        if 0 <= n - 1 < len(work):
            _, _, norm, delta = tiles[work[n - 1][0]]
            s, dp = made.pop(n - 1)
            p = jnp.exp(s - norm)
            weighed[n - 1] = p.astype(bf16), (p * (dp - delta)).astype(bf16)
        if n >= 2:
            i, start, size = work[n - 2]
            dq_t = gather(i, start, size, *tiles[i][:2], *weighed.pop(n - 2), dq_t)
            if n == len(work) + 1 or work[n - 1][0] != i:
                at = pl.ds(i * T, T)
                out = turned_back(unstacked(dq_t), cosine[:, at], sine[:, at]) * SCALE
                dq[at, :] = out.T.astype(bf16)
    clean = (1 - noisy).astype(f32)
    for at, own, other in ((0, dko, dkc), (1, dvo, dvc)):
        keep[at] = (own[...] + clean * other[...]).astype(bf16)
        send[at] = other[...].astype(bf16)


def attend_back(info, first, pairs, q, ko, vo, kc, vc, o, do, lse, cosine, sine):
    seq = q.shape[1]
    width = pairs * PW
    heads = pl.BlockSpec((1, seq, PW), lambda h: (first + h, 0, 0))
    source = pl.BlockSpec((seq, PW), lambda h: (0, first + h))
    both = pl.BlockSpec((2, seq, PW), lambda h: (0, 0, h))
    lines = pl.BlockSpec((1, seq // T, 2 * T), lambda h: (first + h, 0, 0))
    table = whole((HD // 2, seq))
    return pl.pallas_call(
        attend_back_kernel,
        grid=(pairs,),
        in_specs=[SMEM] + [heads] * 5 + [source] * 2 + [lines, table, table],
        out_specs=[pl.BlockSpec((seq, PW), lambda h: (0, h)), both, both],
        out_shape=[shape((seq, width), bf16)] + [shape((2, seq, width), bf16)] * 2,
        scratch_shapes=[pltpu.VMEM((PW, seq), bf16)] * 2
        + [pltpu.VMEM((seq, PW), f32)] * 4
        + [pltpu.VMEM((2 * T, 2 * T), f32)],
        compiler_params=params(24),
        cost_estimate=LONG,
        name="attend_back",
    )(info, *pinned(q, ko, vo, kc, vc, o, do), lse, cosine, sine)


C0 = 0.7978845608028654
C1 = C0 * 0.044715


def layer_kernel(
    info, gain1_line, gain2_line, received_any, x_any, wqkv_any, cosine_any, signed_any, wo_any, dy_any,
    w1_any, w2_any,
    q_out, ko_out, vo_out, kc_out, vc_out, h1t_out, o_out, lse_out, out_any, dx2_any, do_any,
    up_send, up_keep, down_send, down_keep, g_send, g_keep, sums,
    x, received, wqkv, cosine, signed, q, ko, vo, h1t, wo, dy, w1, w2,
    kc, vc, vo_t, vc_t, scores, bias, o, o_t, lse, x2, h2, m, dh, act, du, up_grad, down_grad, half_grads,
    sem_in, sem_1, sem_2, sem_out, sem_up, sem_down, sem_tile,
):
    noisy, length = info[0], info[1]
    seq, width = x.shape
    chunks, pairs, tiles = w1.shape[0], kc.shape[0], seq // R
    copy = pltpu.make_async_copy
    gain1, gain2 = gain1_line[...].reshape(1, width), gain2_line[...].reshape(1, width)

    def weights(c):
        place = lax.rem(c + (chunks // 2) * (1 - noisy), chunks) * FC
        place = pl.multiple_of(place, FC)
        return (
            copy(w1_any.at[:, pl.ds(place, FC)], w1.at[c], sem_1.at[c]),
            copy(w2_any.at[pl.ds(place, FC), :], w2.at[c], sem_2.at[c]),
        )

    sources = (
        (x_any, x),
        (wqkv_any, wqkv),
        (cosine_any, cosine),
        (signed_any, signed),
        (received_any, received),
        (wo_any, wo),
        (dy_any, dy),
    )
    loads = [copy(a, b, sem_in.at[i]) for i, (a, b) in enumerate(sources)]
    for load in loads[:5]:
        load.start()
    sums[...] = jnp.zeros_like(sums)
    edge_bias(bias, noisy)

    for load in loads[:4]:
        load.wait()

    def own_rows(t, carry):
        start = pl.multiple_of(t * R, R)
        rows = pl.ds(start, R)
        value = x[rows, :].astype(f32)
        h1 = (value * inv_rms(value) * gain1).astype(bf16)
        h1t[:, rows] = h1.T
        tables = (cosine[rows, :], signed[rows, :], 1.0)
        by_pairs(q, rows, rotated(nn(h1, wqkv[:, :width]), *tables))
        by_pairs(ko, rows, rotated(nn(h1, wqkv[:, width : 2 * width]), *tables))
        by_pairs(vo, rows, nn(h1, wqkv[:, 2 * width :]))
        weight = token_weight(start, length, R)
        sums[0:1, :] += row_sum(jnp.where(weight, value * value, 0.0))
        return carry

    lax.fori_loop(0, tiles, own_rows, 0)
    stores = [copy(a, b, sem_out.at[6 + i]) for i, (a, b) in enumerate(((q, q_out), (ko, ko_out), (vo, vo_out), (h1t, h1t_out)))]
    for store in stores:
        store.start()
    loads[4].wait()

    def clean_rows(t, carry):
        rows = pl.ds(pl.multiple_of(t * R, R), R)
        value = jnp.where(noisy == 1, received[rows, :].astype(f32), x[rows, :].astype(f32))
        h1 = (value * inv_rms(value) * gain1).astype(bf16)
        by_pairs(kc, rows, rotated(nn(h1, wqkv[:, width : 2 * width]), cosine[rows, :], signed[rows, :], 1.0))
        by_pairs(vc, rows, nn(h1, wqkv[:, 2 * width :]))
        return carry

    lax.fori_loop(0, tiles, clean_rows, 0)
    for load in loads[5:]:
        load.start()
    more = [copy(kc, kc_out, sem_out.at[0]), copy(vc, vc_out, sem_out.at[1])]
    for store in more:
        store.start()
    stores += more

    for c in range(chunks):
        for load in weights(c):
            load.start()

    def one_pair(p, carry):
        lanes = pl.ds(pl.multiple_of(p * PW, PW), PW)

        def keep(at, tile_t):
            o_t[lanes, at] = tile_t.astype(bf16)
            o[at, lanes] = tile_t.T.astype(bf16)

        heads = (ref.at[p] for ref in (q, ko, vo, kc, vc))
        attend_pair(length, *heads, keep, lse.at[pl.ds(p, 1)], vo_t, vc_t, scores, bias)
        return carry

    lax.fori_loop(0, pairs, one_pair, 0)
    more = [copy(o, o_out, sem_out.at[2]), copy(lse, lse_out, sem_out.at[3])]
    for store in more:
        store.start()
    stores += more

    for load in loads[5:]:
        load.wait()

    def joined_rows(t, carry):
        start = pl.multiple_of(t * R, R)
        rows = pl.ds(start, R)
        branch = nn(o[rows, :], wo[...])
        value = x[rows, :].astype(f32) + branch
        x2[rows, :] = value
        h2[rows, :] = (value * inv_rms(value) * gain2).astype(bf16)
        m[rows, :] = jnp.zeros_like(value)
        dh[rows, :] = jnp.zeros_like(value)
        weight = token_weight(start, length, R)
        sums[1:2, :] += row_sum(jnp.where(weight, branch * branch, 0.0))
        return carry

    lax.fori_loop(0, tiles, joined_rows, 0)

    def grad_stores(c, up, down):
        slot = lax.rem(c, 2)
        rows = pl.ds(pl.multiple_of(lax.rem(c, chunks // 2) * FC, FC), FC)
        return (
            copy(up_grad.at[slot], up.at[rows, :], sem_up.at[slot]),
            copy(down_grad.at[slot], down.at[rows, :], sem_down.at[slot]),
        )

    def one_chunk(c, carry):
        for load in weights(c):
            load.wait()
        up, down = w1.at[c], w2.at[c]
        for t in range(0, seq, R):
            rows = pl.ds(t, R)
            u = nn(h2[rows, :], up[...])
            da = nt(dy[rows, :], down[...])
            sq = u * u
            half = 0.5 * jnp.tanh(u * (C0 + C1 * sq)) + 0.5
            low = (u * half).astype(bf16)
            slope = half + u * (2.0 * half * (1.0 - half)) * (C0 + 3.0 * C1 * sq)
            back = (da * slope).astype(bf16)
            act[rows, :] = low
            du[rows, :] = back
            m[rows, :] += nn(low, down[...])
            dh[rows, :] += nt(back, up[...])

        @pl.when(c >= 2)
        def _():
            for store in grad_stores(c, up_send, down_send):
                store.wait()

        slot = lax.rem(c, 2)
        down_grad[slot] = tn(act[...], dy[...]).astype(bf16)
        up_grad[slot] = tn(du[...], h2[...]).astype(bf16)

        @pl.when(c < chunks // 2)
        def _():
            for store in grad_stores(c, up_send, down_send):
                store.start()

        @pl.when(c >= chunks // 2)
        def _():
            for store in grad_stores(c, up_keep, down_keep):
                store.start()

        return carry

    lax.fori_loop(0, chunks, one_chunk, 0)

    def tile_stores(t):
        rows = pl.ds(pl.multiple_of(t * R, R), R)
        return (
            copy(h2.at[rows, :], out_any.at[rows, :], sem_tile.at[t, 0]),
            copy(x2.at[rows, :], dx2_any.at[rows, :], sem_tile.at[t, 1]),
            copy(received.at[rows, :], do_any.at[rows, :], sem_tile.at[t, 2]),
        )

    def middle_rows(t, carry):
        start = pl.multiple_of(t * R, R)
        rows = pl.ds(start, R)
        value = x2[rows, :]
        mixed = m[rows, :]
        weight = token_weight(start, length, R)
        sums[2:3, :] += row_sum(jnp.where(weight, mixed * mixed, 0.0))
        grad, gain_terms = norm_back(value, gain2, dh[rows, :])
        sums[3:4, :] += row_sum(gain_terms)
        grad = grad + dy[rows, :].astype(f32)
        da = grad.astype(bf16)
        h2[rows, :] = (value + mixed).astype(bf16)
        x2[rows, :] = grad
        received[rows, :] = nt(da, wo[...]).astype(bf16)
        x[rows, :] = da
        for store in tile_stores(t):
            store.start()
        return carry

    lax.fori_loop(0, tiles, middle_rows, 0)
    half = width // 2
    mine = pl.multiple_of(noisy * half, half)
    half_grads[0] = nn(o_t[pl.ds(half - mine, half), :], x[...]).astype(bf16)
    half_grads[1] = nn(o_t[pl.ds(mine, half), :], x[...]).astype(bf16)
    more = [copy(half_grads.at[0], g_send, sem_out.at[4]), copy(half_grads.at[1], g_keep, sem_out.at[5])]
    for store in more:
        store.start()
    stores += more
    for c in range(chunks - 2, chunks):
        stores += grad_stores(c, up_keep, down_keep)
    for t in range(tiles):
        stores += tile_stores(t)
    for store in stores:
        store.wait()


def layer(info, gain1, gain2, received, x, wqkv, tables, wo, dy, w1, w2):
    seq, width = x.shape
    hidden = w1.shape[1]
    tiles, pairs, chunks = seq // R, width // PW, hidden // FC
    anywhere = pl.BlockSpec(memory_space=pl.ANY)
    vmem = pltpu.VMEM
    dma = pltpu.SemaphoreType.DMA
    heads = (pairs, seq, PW)
    flat = (seq, width)
    outs = (
        [shape(heads, bf16)] * 5
        + [shape((width, seq), bf16), shape(flat, bf16), shape((pairs, seq // T, 2 * T), f32)]
        + [shape(flat, bf16), shape(flat, f32), shape(flat, bf16)]
        + [shape((hidden // 2, width), bf16)] * 4
        + [shape((width // 2, width), bf16)] * 2
        + [shape((8, width), f32)]
    )
    return pl.pallas_call(
        layer_kernel,
        in_specs=[SMEM, IN_VMEM, IN_VMEM] + [anywhere] * 9,
        out_specs=[anywhere] * 17 + [IN_VMEM],
        out_shape=outs,
        scratch_shapes=[vmem(flat, bf16)] * 2
        + [vmem(wqkv.shape, bf16), vmem((seq, PW), f32), vmem((seq, PW), f32)]
        + [vmem(heads, bf16)] * 3
        + [vmem((width, seq), bf16), vmem((width, width), bf16), vmem(flat, bf16)]
        + [vmem((chunks, width, FC), bf16), vmem((chunks, FC, width), bf16)]
        + [vmem(heads, bf16)] * 2
        + [vmem((PW, seq), bf16)] * 2
        + [vmem((AHEAD, seq + T, 2 * T), f32), vmem((2 * T, 2 * T), f32)]
        + [vmem(flat, bf16), vmem((width, seq), bf16)]
        + [vmem((pairs, seq // T, 2 * T), f32)]
        + [vmem(flat, f32), vmem(flat, bf16)]
        + [vmem(flat, f32)] * 2
        + [vmem((seq, FC), bf16)] * 2
        + [vmem((2, FC, width), bf16)] * 2
        + [vmem((2, width // 2, width), bf16)]
        + [dma((7,)), dma((chunks,)), dma((chunks,)), dma((10,)), dma((2,)), dma((2,)), dma((tiles, 3))],
        compiler_params=params(BIG),
        cost_estimate=LONG,
        name="layer",
    )(info, gain1, gain2, received, *pinned(x, wqkv, *tables, wo, dy, w1, w2))


def weigh_kernel(first, info, dq, keep, got, cosine, signed, h1t, wqkv, sums, dkv, g_send, g_keep, small):
    width, half = wqkv.shape[0], wqkv.shape[0] // 2
    mine = pl.multiple_of(info[0] * half, half)
    dk = keep[0].astype(f32) + got[0].astype(f32)
    dkv[0] = rotated(dk, cosine[...], signed[...], -1.0).astype(bf16)
    dkv[1] = (keep[1].astype(f32) + got[1].astype(f32)).astype(bf16)
    small[...] = sums[...]
    for out, start in ((g_send, half - mine), (g_keep, mine)):
        rows = pl.ds(start, half)
        terms = 0.0
        for i, part in enumerate((dq, dkv.at[0], dkv.at[1])):
            total = nn(h1t[rows, :], part[...])
            out[i] = total.astype(bf16)
            at = i * width + first * PW
            weighted = total * wqkv[rows, at : at + total.shape[1]].astype(f32)
            for c in range(0, total.shape[1], PW):
                terms = terms + weighted[:, c : c + PW]
        line = jnp.sum(terms.T, axis=0, keepdims=True)
        lanes = lax.broadcasted_iota(jnp.int32, (1, width), 1)
        inside = jnp.logical_and(lanes >= start, lanes < start + half)
        small[4:5, :] += jnp.where(inside, jnp.concatenate([line, line], axis=1), 0.0)
    small[5:6, :] = jnp.full((1, width), info[1].astype(f32))


def weigh(info, first, dq, keep, got, tables, h1t, wqkv, sums):
    seq, width = dq.shape
    tall = h1t.shape[0]
    return pl.pallas_call(
        functools.partial(weigh_kernel, first),
        in_specs=[SMEM] + [IN_VMEM] * 8,
        out_specs=[IN_VMEM] * 4,
        out_shape=[shape((2, seq, width), bf16)]
        + [shape((3, tall // 2, width), bf16)] * 2
        + [shape(sums.shape, f32)],
        compiler_params=params(24),
        cost_estimate=LONG,
        name="weigh",
    )(info, dq, keep, got, *tables, h1t, wqkv, sums)


def finish_kernel(parts, tiles, x, dx2, wqkv, gain_line, *refs):
    dx_any, dx, sem = refs[-3:]
    dqs, dkvs = refs[:parts], refs[parts : 2 * parts]
    gain = gain_line[...].reshape(1, x.shape[1])

    def store(t):
        rows = pl.ds(pl.multiple_of(t * R, R), R)
        return pltpu.make_async_copy(dx.at[rows, :], dx_any.at[rows, :], sem.at[t])

    def some_rows(t, carry):
        rows = pl.ds(pl.multiple_of(t * R, R), R)
        grads = [r[rows, :] for r in dqs] + [r[0, rows, :] for r in dkvs] + [r[1, rows, :] for r in dkvs]
        dh = nt(jnp.concatenate(grads, axis=1), wqkv[...])
        grad, _ = norm_back(x[rows, :].astype(f32), gain, dh)
        dx[rows, :] = (dx2[rows, :] + grad).astype(bf16)
        store(t).start()
        return carry

    lax.fori_loop(*tiles, some_rows, 0)
    for t in range(*tiles):
        store(t).wait()


def finish(tiles, x, dx2, dqs, dkvs, weight, gain, before):
    anywhere = pl.BlockSpec(memory_space=pl.ANY)
    ins = 4 + len(dqs) + len(dkvs)
    return pl.pallas_call(
        functools.partial(finish_kernel, len(dqs), tiles),
        in_specs=[IN_VMEM] * ins + [anywhere] * len(before),
        out_specs=anywhere,
        out_shape=shape(x.shape, bf16),
        scratch_shapes=[pltpu.VMEM(x.shape, bf16), pltpu.SemaphoreType.DMA((x.shape[0] // R,))],
        input_output_aliases={ins: 0} if before else {},
        compiler_params=params(24),
        cost_estimate=COST if before else LONG,
        name="finish",
    )(x, dx2, weight, gain, *dqs, *dkvs, *before)


def bit_orders(count, groups):
    bits = [1 << i for i in range(count.bit_length() - 1)]
    if groups == 2:
        return [bits, bits[1::-1] + bits[2:]]
    return [bits[g:-1] + bits[:g] + bits[-1:] for g in range(groups)]


def exchange(value, axis, bit):
    size = lax.axis_size(axis)
    return lax.ppermute(value, axis, [(i, i ^ bit) for i in range(size)])


def distance(order, place):
    out = 0
    for i, bit in enumerate(order):
        out = out + ((place >> (len(order) - 1 - i)) & 1) * bit
    return out


LINES = 16


def halves(value):
    high = value.astype(bf16)
    return high, (value - high.astype(f32)).astype(bf16)


def put_sums(value, kept, block):
    high, low = halves(value)
    block[:LINES, :] = high
    block[LINES : 2 * LINES, :] = low
    kept[...] = high.astype(f32) + low.astype(f32)


def got_sums(block):
    return block[:LINES, :].astype(f32) + block[LINES : 2 * LINES, :].astype(f32)


def start_kernel(orders, sources, small, me, *refs):
    groups = len(orders)
    arrays = max(a for source in sources for a, _ in source) + 1
    ins, outs = refs[: 2 * arrays], refs[len(refs) - 2 * groups :]
    half = outs[0].shape[0]
    for g, order in enumerate(orders):
        for side in range(2):

            def one(r, carry, g=g, order=order, side=side):
                part = me[0] ^ distance(order, r + side * half)
                row = 0
                for a, where in sources[g]:
                    kept, got = ins[2 * a : 2 * a + 2]
                    place = where(part)
                    size = kept.shape[1]
                    total = kept[place].astype(f32) + got[place].astype(f32)
                    outs[2 * g + side][r, row : row + size, :] = total.astype(bf16)
                    row += size
                return carry

            lax.fori_loop(0, half, one, 0)
    if small:
        here, there, kept = refs[2 * arrays : 2 * arrays + 3]
        total = here[...] + there[...]
        if small == "rides":
            wide = total.shape[1] // 2
            total = jnp.concatenate([total[:, :wide], total[:, wide:]], axis=0)
            put_sums(total, kept, outs[1].at[half])
        else:
            kept[...] = total


def start_sum(me, kept, got, sources, orders, small, rides):
    count = 1 << len(orders[0])
    half = count // 2
    rows = [sum(kept[a].shape[1] for a, _ in source) for source in sources]
    width = kept[0].shape[2]
    cols = width // 3
    args = [a for pair in zip(kept, got, strict=True) for a in pair]
    sums = []
    for g in range(len(orders)):
        sums += [shape((half, rows[g], width), bf16), shape((half + (rides and g == 0), rows[g], width), bf16)]
    mode = "rides" if rides else "alone" if small else ""
    if small:
        lines = (LINES, width) if rides else small[0].shape
        specs = dict(
            in_specs=[SMEM] + [IN_VMEM] * (len(args) + 2),
            out_specs=[IN_VMEM] * (1 + len(sums)),
            out_shape=[shape(lines, f32)] + sums,
        )
    else:
        block = lambda a: pl.BlockSpec((a.shape[0], a.shape[1], cols), lambda c: (0, 0, c))
        specs = dict(
            grid=(width // cols,),
            in_specs=[SMEM] + [block(a) for a in args],
            out_specs=[block(a) for a in sums],
            out_shape=sums,
        )
    outs = pl.pallas_call(
        functools.partial(start_kernel, orders, sources, mode),
        compiler_params=params(30),
        cost_estimate=COST,
        name="start_sum",
        **specs,
    )(me, *args, *small)
    small, outs = list(outs[: len(outs) - len(sums)]), outs[len(outs) - len(sums) :]
    return list(outs[0::2]), list(outs[1::2]), small


def step_kernel(groups, merge, mode, *refs):
    kept, got = refs[:groups], refs[groups : 2 * groups]
    outs = refs[2 * groups + (2 if mode == "alone" else 1 if mode else 0) :]
    count = kept[0].shape[0]
    half = count // 2
    row = 0
    for g in range(groups):
        total = (kept[g][...].astype(f32) + got[g][:count].astype(f32)).astype(bf16)
        keep, send = outs[:2] if merge else outs[2 * g : 2 * g + 2]
        size = total.shape[1]
        keep[:, row : row + size, :] = total[:half]
        send[:half, row : row + size, :] = total[half:]
        row += size if merge else 0
    if mode == "rides":
        total = refs[2 * groups][...] + got_sums(got[0].at[count])
        put_sums(total, outs[-1], outs[1].at[half])
    elif mode:
        outs[-1][...] = refs[2 * groups][...] + refs[2 * groups + 1][...]


def step_sum(kept, got, small, merge, rides):
    groups = len(kept)
    half = kept[0].shape[0] // 2
    rows = [a.shape[1] for a in kept]
    width = kept[0].shape[2]
    args = [*kept, *got, *small]
    sums = []
    for g, r in enumerate([sum(rows)] if merge else rows):
        sums += [shape((half, r, width), bf16), shape((half + (rides and g == 0), r, width), bf16)]
    outs = pl.pallas_call(
        functools.partial(step_kernel, groups, merge, "rides" if rides else "alone" if small else ""),
        in_specs=[IN_VMEM] * len(args),
        out_specs=[IN_VMEM] * (len(sums) + len(small[:1])),
        out_shape=sums + [shape(a.shape, f32) for a in small[:1]],
        compiler_params=params(16),
        cost_estimate=COST if small or half == 1 else LONG,
        name="step_sum",
    )(*args)
    return list(outs[0 : len(sums) : 2]), list(outs[1 : len(sums) : 2]), list(outs[len(sums) :])


def feed_end_kernel(kept, got, down, up, out):
    total = kept[0].astype(f32) + got[0].astype(f32)
    tall, few = down.shape[0] // GROUPS, out.shape[0] // GROUPS
    ups = []
    for g in range(GROUPS):
        row = g * (2 * tall + few)
        down[g * tall : (g + 1) * tall, :] = total[row : row + tall]
        ups.append(total[row + tall : row + 2 * tall])
        out[g * few : (g + 1) * few, :] = total[row + 2 * tall : row + 2 * tall + few]
    up[...] = jnp.concatenate(ups, axis=0).T


def feed_end(kept, got, tall, few):
    width = kept.shape[2]
    return pl.pallas_call(
        feed_end_kernel,
        in_specs=[IN_VMEM] * 2,
        out_specs=[IN_VMEM] * 3,
        out_shape=[shape((tall, width), f32), shape((width, tall), f32), shape((few, width), f32)],
        compiler_params=params(16),
        cost_estimate=COST,
        name="feed_end",
    )(kept, got)


def qkv_end_kernel(rides, gain_line, kept, got, *refs):
    out, gain1, gain2, rms = refs[-4:]
    tall = out.shape[0]
    width = gain1.shape[0]
    cols = kept.shape[2]
    total = kept[0].astype(f32) + got[0].astype(f32)
    for i in range(total.shape[0] // tall):
        part, third = i // 3, i % 3
        at = third * width + part * cols
        out[:, at : at + cols] = total[i * tall : (i + 1) * tall]
    if rides:
        sums = refs[0][...] + got_sums(got.at[1])
        sums = jnp.concatenate([sums[: LINES // 2], sums[LINES // 2 :]], axis=1)
    else:
        sums = refs[0][...] + refs[1][...]
    gain2[...] = sums[3:4, :].reshape(width)
    gain1[...] = (sums[4:5, :] / gain_line[...].reshape(1, width)).reshape(width)
    count = jnp.max(sums[5:6, :], axis=1, keepdims=True) * width
    rms[...] = jnp.broadcast_to(jnp.sqrt(jnp.sum(sums, axis=1, keepdims=True) / count), rms.shape)


def qkv_end(gain, kept, got, small, tall, wide, rides):
    return pl.pallas_call(
        functools.partial(qkv_end_kernel, rides),
        in_specs=[IN_VMEM] * (3 + len(small)),
        out_specs=[IN_VMEM] * 4,
        out_shape=[shape((tall, wide), f32), shape(gain.shape, f32), shape(gain.shape, f32), shape((8, 128), f32)],
        compiler_params=params(16),
        cost_estimate=COST,
        name="qkv_end",
    )(gain, kept, got, *small)


def after(value, *earlier):
    return lax.optimization_barrier((value, earlier))[0]


def sum_parts(me, kept, got, sources, small, rides):
    orders = bit_orders(lax.axis_size("batch"), len(sources))
    steps = len(orders[0])
    common = min(i for i in range(steps + 1) if all(order[i:] == orders[0][i:] for order in orders))
    keep, send, small = start_sum(me, kept, got, sources, orders, small, rides)
    for i in range(steps):
        got = [exchange(s, "batch", order[i]) for s, order in zip(send, orders[: len(send)], strict=True)]
        if small and not rides:
            small = [small[0], exchange(small[0], "batch", orders[0][i])]
        earlier = yield send[0], got
        if i == steps - 1:
            break
        if earlier is not None:
            keep = after(keep, earlier)
        keep, send, small = step_sum(keep, got, small, i + 1 == common, rides)
    yield keep[0], got[0], small


def on_device(
    inputs, lengths, cotangent, qkv_weight, out_weight, up_weight, down_weight, attn_gain, mlp_gain
):
    seq, width = inputs.shape[2:]
    x = inputs[0, 0]
    dy = cotangent[0, 0]
    count = lax.axis_size("batch")
    stream = lax.axis_index("stream").astype(jnp.int32)
    me = lax.axis_index("batch").astype(jnp.int32).reshape(1)
    info = jnp.stack([stream, lengths[0]])
    cosine, sine = rotary_tables(seq)
    tables = (
        jnp.asarray(np.concatenate([cosine] * 4, axis=1)),
        jnp.asarray(np.concatenate([-sine, sine] * 2, axis=1)),
    )
    tables_t = (jnp.asarray(cosine.T), jnp.asarray(sine.T))

    received = lax.ppermute(x, "stream", [(0, 1)])
    (
        q, ko, vo, kc, vc, h1t, o, lse, outputs, dx2, do,
        up_send, up_keep, down_send, down_keep, out_send, out_keep, sums,
    ) = layer(
        info, attn_gain, mlp_gain, received, x, qkv_weight, tables, out_weight, dy, up_weight, down_weight
    )
    down_got, up_got, out_got = (exchange(a, "stream", 1) for a in (down_send, up_send, out_send))

    def by_rows(array):
        return array.reshape(count * GROUPS, array.shape[0] // (count * GROUPS), width)

    heads = (q, ko, vo, kc, vc, o)
    pairs = width // PW // 2
    dq1, keep1, send1 = attend_back(info, 0, pairs, *heads, do, lse, *tables_t)
    got1 = lax.ppermute(send1, "stream", [(1, 0)])
    early = sum_parts(
        me,
        [by_rows(after(a, dq1)) for a in (down_keep, up_keep, out_keep)],
        [by_rows(a) for a in (down_got, up_got, out_got)],
        [[(a, lambda part, g=g: part * GROUPS + g) for a in range(3)] for g in range(GROUPS)],
        [],
        False,
    )
    token = next(early)[0]
    dq2, keep2, send2 = attend_back(info, pairs, pairs, *heads, after(do, token), lse, *tables_t)
    got2 = lax.ppermute(send2, "stream", [(1, 0)])
    token = early.send(dq2)[0]
    dkv1, qkv_send1, qkv_keep1, small = weigh(info, 0, dq1, after(keep1, token), got1, tables, h1t, qkv_weight, sums)
    qkv_got1 = exchange(qkv_send1, "stream", 1)
    dkv2, qkv_send2, qkv_keep2, small = weigh(info, pairs, dq2, keep2, got2, tables, h1t, qkv_weight, small)
    qkv_got2 = exchange(qkv_send2, "stream", 1)
    small_got = exchange(small, "stream", 1)
    token = early.send(dkv2)[0]

    tall = width // (2 * count)
    split = lambda a: a.reshape(3 * count, tall, a.shape[2])
    rides = 3 * tall >= 2 * LINES
    late = sum_parts(
        me,
        [split(after(a, token)) for a in (qkv_keep1, qkv_keep2)],
        [split(a) for a in (qkv_got1, qkv_got2)],
        [[(g, lambda part, i=i: i * count + part) for i in range(3)] for g in range(2)],
        [small, small_got],
        rides,
    )
    token = next(late)[0]
    ends = [dq1, dq2], [dkv1, dkv2], qkv_weight, attn_gain
    tiles = seq // R
    dx = finish((0, tiles // 2), after(x, token), dx2, *ends, [])
    early_out = early.send(dx)
    dx = finish((tiles // 2, tiles), x, after(dx2, early_out[0]), *ends, [dx])
    late.send(dx)
    late_out = late.send(early_out[1])
    while len(late_out) == 2:
        late_out = late.send(None)
    while len(early_out) == 2:
        early_out = early.send(None)
    up_cols = down_keep.shape[0] // count
    down_grad, up_grad, out_grad = feed_end(*early_out[:2], up_cols, tall)
    qkv_grad, gain1_grad, gain2_grad, rms = qkv_end(attn_gain, *late_out, tall, 3 * width, rides)
    return (
        outputs[None, None],
        dx[None, None],
        qkv_grad,
        out_grad,
        up_grad,
        down_grad,
        gain1_grad,
        gain2_grad,
        rms[:3, 0],
    )


def solution(mesh):
    rows = P("stream", "batch", None, None)
    both = ("stream", "batch")
    return jax.shard_map(
        on_device,
        mesh=mesh,
        in_specs=(rows, P("batch"), rows, P(), P(), P(), P(), P(), P()),
        out_specs=(rows, rows, P(both, None), P(both, None), P(None, both), P(both, None), P(), P(), P()),
        check_vma=False,
    )
```

```python
import functools

import jax
import jax.numpy as jnp
import numpy as np
from jax import lax
from jax.experimental import pallas as pl
from jax.experimental.pallas import tpu as pltpu
from jax.sharding import PartitionSpec as P

f32 = jnp.float32
bf16 = jnp.bfloat16

HD = 64
BLK = 16
EPS = 1e-06
NEG = -1e30
PW = 2 * HD
T = 128
R = 256
AHEAD = 2
FC = 512
SCALE = HD**-0.5
BIG = 57
GROUPS = 3

COST = pl.CostEstimate(flops=1 << 20, bytes_accessed=1 << 16, transcendentals=0)
LONG = pl.CostEstimate(flops=1 << 35, bytes_accessed=1 << 26, transcendentals=0)

SMEM = pl.BlockSpec(memory_space=pltpu.SMEM)
IN_VMEM = pl.BlockSpec(memory_space=pltpu.VMEM)


def params(mib):
    return pltpu.CompilerParams(vmem_limit_bytes=mib << 20)


def shape(dims, dtype):
    return jax.ShapeDtypeStruct(dims, dtype)


def pinned(*arrays):
    return [pltpu.with_memory_space_constraint(a, pltpu.HBM) for a in arrays]


def nn(a, b):
    return jnp.dot(a, b, preferred_element_type=f32)


def nt(a, b):
    return lax.dot_general(a, b, (((1,), (1,)), ((), ())), preferred_element_type=f32)


def tn(a, b):
    return lax.dot_general(a, b, (((0,), (0,)), ((), ())), preferred_element_type=f32)


def whole(dims):
    return pl.BlockSpec(dims, lambda *_: (0,) * len(dims), pipeline_mode=pl.Buffered(1))


def inv_rms(v):
    return lax.rsqrt(jnp.mean(v * v, axis=-1, keepdims=True) + EPS)


def norm_back(v, gain, grad):
    r = inv_rms(v)
    unit = v * r
    scaled = grad * gain
    inner = jnp.mean(scaled * unit, axis=-1, keepdims=True)
    return r * (scaled - unit * inner), grad * unit


def rotary_tables(length):
    half = HD // 2
    freqs = np.exp(-np.log(10000.0) * np.arange(half) / half).astype(np.float32)
    angles = (np.arange(length, dtype=np.float32)[:, None] * freqs[None, :]).astype(np.float64)
    return np.cos(angles).astype(np.float32), np.sin(angles).astype(np.float32)


def rotated(v, cosine, signed, sign):
    first = lax.broadcasted_iota(jnp.int32, (1, PW), 1) % HD < HD // 2
    outs = []
    for c in range(0, v.shape[1], PW):
        part = v[:, c : c + PW]
        partner = jnp.where(first, pltpu.roll(part, PW - HD // 2, 1), pltpu.roll(part, HD // 2, 1))
        outs.append(part * cosine + partner * (signed * sign))
    return outs[0] if len(outs) == 1 else jnp.concatenate(outs, axis=1)


def token_weight(start, length, rows):
    return lax.broadcasted_iota(jnp.int32, (rows, 1), 0) + start < length


def row_sum(v):
    return jnp.sum(v, axis=0, keepdims=True)


def by_pairs(ref, rows, value):
    for p in range(ref.shape[0]):
        ref[p, rows, :] = value[:, p * PW : (p + 1) * PW].astype(ref.dtype)


def stacked(tile, low):
    zero = jnp.zeros_like(tile)
    return jnp.concatenate([jnp.where(low, tile, zero), jnp.where(low, zero, tile)], axis=0)


def unstacked(tile_t):
    half = lax.broadcasted_iota(jnp.int32, (PW, 1), 0) < HD
    return jnp.where(half, tile_t[:, :T], tile_t[:, T:])


def chunks_of(i):
    out, j = [], 0
    while j < i:
        n = 2 if i - j >= 2 else 1
        out.append((j * T, n * T))
        j += n
    return out


def edge_bias(ref, noisy):
    row = lax.broadcasted_iota(jnp.int32, (T, 2 * T), 0) // BLK
    col = (lax.broadcasted_iota(jnp.int32, (T, 2 * T), 1) % T) // BLK
    own = jnp.logical_or(row == col, jnp.logical_and(row < col, noisy == 0))
    other = jnp.logical_and(row < col, noisy == 1)
    ref[:T, :] = jnp.where(own, 0.0, NEG)
    ref[T:, :] = jnp.where(other, 0.0, NEG)


def masked(s, start, length):
    pos = lax.broadcasted_iota(jnp.int32, s.shape, 0) + start
    return jnp.where(pos < length, s, NEG)


def over_rows(op, v):
    return op(v.reshape(v.shape[0] // 8, 8, v.shape[1]), axis=0)


def attend_pair(length, q, ko, vo, kc, vc, store, lse, vo_t, vc_t, scores, bias):
    seq = q.shape[0]
    low = lax.broadcasted_iota(jnp.int32, (1, PW), 1) < HD
    vo_t[...] = vo[...].T
    vc_t[...] = vc[...].T

    def score(i):
        at = pl.ds(i * T, T)
        q2 = stacked(q[at, :] * bf16(SCALE), low)
        buf = scores.at[i % AHEAD]
        edge = nt(jnp.concatenate([ko[at, :], kc[at, :]], 0), q2) + bias[...]
        own = masked(edge[:T], i * T, length)
        other = masked(edge[T:], i * T, length)
        buf[pl.ds(0, T), :] = own
        buf[pl.ds(T, T), :] = other
        top = over_rows(jnp.max, jnp.maximum(own, other))
        for start, size in chunks_of(i):
            s = masked(nt(kc[pl.ds(start, size), :], q2), start, length)
            buf[pl.ds(2 * T + start, size), :] = s
            top = jnp.maximum(top, over_rows(jnp.max, s))
        return jnp.max(top, axis=0, keepdims=True)

    def mix(i, top):
        at = pl.ds(i * T, T)
        buf = scores.at[i % AHEAD]
        p = jnp.exp(buf[pl.ds(0, 2 * T), :] - top)
        total = over_rows(jnp.sum, p)
        acc = nn(jnp.concatenate([vo_t[:, at], vc_t[:, at]], 1), p.astype(bf16))
        for start, size in chunks_of(i):
            p = jnp.exp(buf[pl.ds(2 * T + start, size), :] - top)
            total = total + over_rows(jnp.sum, p)
            acc = acc + nn(vc_t[:, pl.ds(start, size)], p.astype(bf16))
        total = row_sum(total)
        lse[0, pl.ds(i, 1), :] = top + jnp.log(total)
        store(at, unstacked(acc * (1.0 / total)))

    tops = {}
    for i in range(seq // T + AHEAD - 1):
        if i < seq // T:
            tops[i] = score(i)
        if i >= AHEAD - 1:
            mix(i - AHEAD + 1, tops.pop(i - AHEAD + 1))


def turned_back(v, cosine, sine):
    quarter = HD // 2
    a, b, c, d = (v[i * quarter : (i + 1) * quarter] for i in range(4))
    return jnp.concatenate(
        [a * cosine + b * sine, b * cosine - a * sine, c * cosine + d * sine, d * cosine - c * sine]
    )


def attend_back_kernel(
    info, q, ko, vo, kc, vc, o, do, lse, cosine, sine, dq, keep, send, ko_t, kc_t, dko, dvo, dkc, dvc, bias
):
    noisy, length = info[0], info[1]
    q, ko, vo, kc, vc = (ref.at[0] for ref in (q, ko, vo, kc, vc))
    seq = q.shape[0]
    low = lax.broadcasted_iota(jnp.int32, (1, PW), 1) < HD

    @pl.when(pl.program_id(0) == 0)
    def _():
        edge_bias(bias, noisy)

    ko_t[...] = ko[...].T
    kc_t[...] = kc[...].T

    def tile(i):
        at = pl.ds(i * T, T)
        prod = (do[at, :].astype(f32) * o[at, :].astype(f32)).T
        delta = jnp.concatenate([row_sum(prod[:HD]), row_sum(prod[HD:])], 1)
        q2 = stacked(q[at, :] * bf16(SCALE), low)
        return q2, stacked(do[at, :], low), lse[0, pl.ds(i, 1), :], delta

    def products(i, start, size, q2, do2):
        if start is None:
            at = pl.ds(i * T, T)
            s = nt(jnp.concatenate([ko[at, :], kc[at, :]], 0), q2) + bias[...]
            s = jnp.concatenate([masked(s[:T], i * T, length), masked(s[T:], i * T, length)], 0)
            return s, nt(jnp.concatenate([vo[at, :], vc[at, :]], 0), do2)
        rows = pl.ds(start, size)
        return masked(nt(kc[rows, :], q2), start, length), nt(vc[rows, :], do2)

    def gather(i, start, size, q2, do2, p, ds, dq_t):
        at = pl.ds(i * T, T)
        dv, dk = nn(p, do2), nn(ds, q2)
        if start is None:
            dvo[at, :] = dv[:T]
            dko[at, :] = dk[:T]
            dvc[at, :] = dv[T:]
            dkc[at, :] = dk[T:]
            return nn(jnp.concatenate([ko_t[:, at], kc_t[:, at]], 1), ds)
        rows = pl.ds(start, size)
        dvc[rows, :] += dv
        dkc[rows, :] += dk
        return dq_t + nn(kc_t[:, rows], ds)

    work = [(i, *c) for i in range(seq // T) for c in [(None, None)] + chunks_of(i)]
    tiles, made, weighed, dq_t = {}, {}, {}, None
    for n in range(len(work) + 2):
        if n < len(work):
            i = work[n][0]
            if i not in tiles:
                tiles[i] = tile(i)
            made[n] = products(*work[n], *tiles[i][:2])
        if 0 <= n - 1 < len(work):
            _, _, norm, delta = tiles[work[n - 1][0]]
            s, dp = made.pop(n - 1)
            p = jnp.exp(s - norm)
            weighed[n - 1] = p.astype(bf16), (p * (dp - delta)).astype(bf16)
        if n >= 2:
            i, start, size = work[n - 2]
            dq_t = gather(i, start, size, *tiles[i][:2], *weighed.pop(n - 2), dq_t)
            if n == len(work) + 1 or work[n - 1][0] != i:
                at = pl.ds(i * T, T)
                out = turned_back(unstacked(dq_t), cosine[:, at], sine[:, at]) * SCALE
                dq[at, :] = out.T.astype(bf16)
    clean = (1 - noisy).astype(f32)
    for at, own, other in ((0, dko, dkc), (1, dvo, dvc)):
        keep[at] = (own[...] + clean * other[...]).astype(bf16)
        send[at] = other[...].astype(bf16)


def attend_back(info, first, pairs, q, ko, vo, kc, vc, o, do, lse, cosine, sine):
    seq = q.shape[1]
    width = pairs * PW
    heads = pl.BlockSpec((1, seq, PW), lambda h: (first + h, 0, 0))
    source = pl.BlockSpec((seq, PW), lambda h: (0, first + h))
    both = pl.BlockSpec((2, seq, PW), lambda h: (0, 0, h))
    lines = pl.BlockSpec((1, seq // T, 2 * T), lambda h: (first + h, 0, 0))
    table = whole((HD // 2, seq))
    return pl.pallas_call(
        attend_back_kernel,
        grid=(pairs,),
        in_specs=[SMEM] + [heads] * 5 + [source] * 2 + [lines, table, table],
        out_specs=[pl.BlockSpec((seq, PW), lambda h: (0, h)), both, both],
        out_shape=[shape((seq, width), bf16)] + [shape((2, seq, width), bf16)] * 2,
        scratch_shapes=[pltpu.VMEM((PW, seq), bf16)] * 2
        + [pltpu.VMEM((seq, PW), f32)] * 4
        + [pltpu.VMEM((2 * T, 2 * T), f32)],
        compiler_params=params(24),
        cost_estimate=LONG,
        name="attend_back",
    )(info, *pinned(q, ko, vo, kc, vc, o, do), lse, cosine, sine)


C0 = 0.7978845608028654
C1 = C0 * 0.044715


def layer_kernel(
    info, gain1_line, gain2_line, received_any, x_any, wqkv_any, cosine_any, signed_any, wo_any, dy_any,
    w1_any, w2_any,
    q_out, ko_out, vo_out, kc_out, vc_out, h1t_out, o_out, lse_out, out_any, dx2_any, do_any,
    up_send, up_keep, down_send, down_keep, g_send, g_keep, sums,
    x, received, wqkv, cosine, signed, q, ko, vo, h1t, wo, dy, w1, w2,
    kc, vc, vo_t, vc_t, scores, bias, o, o_t, lse, x2, h2, m, dh, act, du, up_grad, down_grad, half_grads,
    sem_in, sem_1, sem_2, sem_out, sem_up, sem_down, sem_tile,
):
    noisy, length = info[0], info[1]
    seq, width = x.shape
    chunks, pairs, tiles = w1.shape[0], kc.shape[0], seq // R
    copy = pltpu.make_async_copy
    gain1, gain2 = gain1_line[...].reshape(1, width), gain2_line[...].reshape(1, width)

    def weights(c):
        place = lax.rem(c + (chunks // 2) * (1 - noisy), chunks) * FC
        place = pl.multiple_of(place, FC)
        return (
            copy(w1_any.at[:, pl.ds(place, FC)], w1.at[c], sem_1.at[c]),
            copy(w2_any.at[pl.ds(place, FC), :], w2.at[c], sem_2.at[c]),
        )

    sources = (
        (x_any, x),
        (wqkv_any, wqkv),
        (cosine_any, cosine),
        (signed_any, signed),
        (received_any, received),
        (wo_any, wo),
        (dy_any, dy),
    )
    loads = [copy(a, b, sem_in.at[i]) for i, (a, b) in enumerate(sources)]
    for load in loads[:5]:
        load.start()
    sums[...] = jnp.zeros_like(sums)
    edge_bias(bias, noisy)

    for load in loads[:4]:
        load.wait()

    def own_rows(t, carry):
        start = pl.multiple_of(t * R, R)
        rows = pl.ds(start, R)
        value = x[rows, :].astype(f32)
        h1 = (value * inv_rms(value) * gain1).astype(bf16)
        h1t[:, rows] = h1.T
        tables = (cosine[rows, :], signed[rows, :], 1.0)
        by_pairs(q, rows, rotated(nn(h1, wqkv[:, :width]), *tables))
        by_pairs(ko, rows, rotated(nn(h1, wqkv[:, width : 2 * width]), *tables))
        by_pairs(vo, rows, nn(h1, wqkv[:, 2 * width :]))
        weight = token_weight(start, length, R)
        sums[0:1, :] += row_sum(jnp.where(weight, value * value, 0.0))
        return carry

    lax.fori_loop(0, tiles, own_rows, 0)
    stores = [copy(a, b, sem_out.at[6 + i]) for i, (a, b) in enumerate(((q, q_out), (ko, ko_out), (vo, vo_out), (h1t, h1t_out)))]
    for store in stores:
        store.start()
    loads[4].wait()

    def clean_rows(t, carry):
        rows = pl.ds(pl.multiple_of(t * R, R), R)
        value = jnp.where(noisy == 1, received[rows, :].astype(f32), x[rows, :].astype(f32))
        h1 = (value * inv_rms(value) * gain1).astype(bf16)
        by_pairs(kc, rows, rotated(nn(h1, wqkv[:, width : 2 * width]), cosine[rows, :], signed[rows, :], 1.0))
        by_pairs(vc, rows, nn(h1, wqkv[:, 2 * width :]))
        return carry

    lax.fori_loop(0, tiles, clean_rows, 0)
    for load in loads[5:]:
        load.start()
    more = [copy(kc, kc_out, sem_out.at[0]), copy(vc, vc_out, sem_out.at[1])]
    for store in more:
        store.start()
    stores += more

    for c in range(chunks):
        for load in weights(c):
            load.start()

    def one_pair(p, carry):
        lanes = pl.ds(pl.multiple_of(p * PW, PW), PW)

        def keep(at, tile_t):
            o_t[lanes, at] = tile_t.astype(bf16)
            o[at, lanes] = tile_t.T.astype(bf16)

        heads = (ref.at[p] for ref in (q, ko, vo, kc, vc))
        attend_pair(length, *heads, keep, lse.at[pl.ds(p, 1)], vo_t, vc_t, scores, bias)
        return carry

    lax.fori_loop(0, pairs, one_pair, 0)
    more = [copy(o, o_out, sem_out.at[2]), copy(lse, lse_out, sem_out.at[3])]
    for store in more:
        store.start()
    stores += more

    for load in loads[5:]:
        load.wait()

    def joined_rows(t, carry):
        start = pl.multiple_of(t * R, R)
        rows = pl.ds(start, R)
        branch = nn(o[rows, :], wo[...])
        value = x[rows, :].astype(f32) + branch
        x2[rows, :] = value
        h2[rows, :] = (value * inv_rms(value) * gain2).astype(bf16)
        m[rows, :] = jnp.zeros_like(value)
        dh[rows, :] = jnp.zeros_like(value)
        weight = token_weight(start, length, R)
        sums[1:2, :] += row_sum(jnp.where(weight, branch * branch, 0.0))
        return carry

    lax.fori_loop(0, tiles, joined_rows, 0)

    def grad_stores(c, up, down):
        slot = lax.rem(c, 2)
        rows = pl.ds(pl.multiple_of(lax.rem(c, chunks // 2) * FC, FC), FC)
        return (
            copy(up_grad.at[slot], up.at[rows, :], sem_up.at[slot]),
            copy(down_grad.at[slot], down.at[rows, :], sem_down.at[slot]),
        )

    def one_chunk(c, carry):
        for load in weights(c):
            load.wait()
        up, down = w1.at[c], w2.at[c]
        for t in range(0, seq, R):
            rows = pl.ds(t, R)
            u = nn(h2[rows, :], up[...])
            da = nt(dy[rows, :], down[...])
            sq = u * u
            half = 0.5 * jnp.tanh(u * (C0 + C1 * sq)) + 0.5
            low = (u * half).astype(bf16)
            slope = half + u * (2.0 * half * (1.0 - half)) * (C0 + 3.0 * C1 * sq)
            back = (da * slope).astype(bf16)
            act[rows, :] = low
            du[rows, :] = back
            m[rows, :] += nn(low, down[...])
            dh[rows, :] += nt(back, up[...])

        @pl.when(c >= 2)
        def _():
            for store in grad_stores(c, up_send, down_send):
                store.wait()

        slot = lax.rem(c, 2)
        down_grad[slot] = tn(act[...], dy[...]).astype(bf16)
        up_grad[slot] = tn(du[...], h2[...]).astype(bf16)

        @pl.when(c < chunks // 2)
        def _():
            for store in grad_stores(c, up_send, down_send):
                store.start()

        @pl.when(c >= chunks // 2)
        def _():
            for store in grad_stores(c, up_keep, down_keep):
                store.start()

        return carry

    lax.fori_loop(0, chunks, one_chunk, 0)

    def tile_stores(t):
        rows = pl.ds(pl.multiple_of(t * R, R), R)
        return (
            copy(h2.at[rows, :], out_any.at[rows, :], sem_tile.at[t, 0]),
            copy(x2.at[rows, :], dx2_any.at[rows, :], sem_tile.at[t, 1]),
            copy(received.at[rows, :], do_any.at[rows, :], sem_tile.at[t, 2]),
        )

    def middle_rows(t, carry):
        start = pl.multiple_of(t * R, R)
        rows = pl.ds(start, R)
        value = x2[rows, :]
        mixed = m[rows, :]
        weight = token_weight(start, length, R)
        sums[2:3, :] += row_sum(jnp.where(weight, mixed * mixed, 0.0))
        grad, gain_terms = norm_back(value, gain2, dh[rows, :])
        sums[3:4, :] += row_sum(gain_terms)
        grad = grad + dy[rows, :].astype(f32)
        da = grad.astype(bf16)
        h2[rows, :] = (value + mixed).astype(bf16)
        x2[rows, :] = grad
        received[rows, :] = nt(da, wo[...]).astype(bf16)
        x[rows, :] = da
        for store in tile_stores(t):
            store.start()
        return carry

    lax.fori_loop(0, tiles, middle_rows, 0)
    half = width // 2
    mine = pl.multiple_of(noisy * half, half)
    half_grads[0] = nn(o_t[pl.ds(half - mine, half), :], x[...]).astype(bf16)
    half_grads[1] = nn(o_t[pl.ds(mine, half), :], x[...]).astype(bf16)
    more = [copy(half_grads.at[0], g_send, sem_out.at[4]), copy(half_grads.at[1], g_keep, sem_out.at[5])]
    for store in more:
        store.start()
    stores += more
    for c in range(chunks - 2, chunks):
        stores += grad_stores(c, up_keep, down_keep)
    for t in range(tiles):
        stores += tile_stores(t)
    for store in stores:
        store.wait()


def layer(info, gain1, gain2, received, x, wqkv, tables, wo, dy, w1, w2):
    seq, width = x.shape
    hidden = w1.shape[1]
    tiles, pairs, chunks = seq // R, width // PW, hidden // FC
    anywhere = pl.BlockSpec(memory_space=pl.ANY)
    vmem = pltpu.VMEM
    dma = pltpu.SemaphoreType.DMA
    heads = (pairs, seq, PW)
    flat = (seq, width)
    outs = (
        [shape(heads, bf16)] * 5
        + [shape((width, seq), bf16), shape(flat, bf16), shape((pairs, seq // T, 2 * T), f32)]
        + [shape(flat, bf16), shape(flat, f32), shape(flat, bf16)]
        + [shape((hidden // 2, width), bf16)] * 4
        + [shape((width // 2, width), bf16)] * 2
        + [shape((8, width), f32)]
    )
    return pl.pallas_call(
        layer_kernel,
        in_specs=[SMEM, IN_VMEM, IN_VMEM] + [anywhere] * 9,
        out_specs=[anywhere] * 17 + [IN_VMEM],
        out_shape=outs,
        scratch_shapes=[vmem(flat, bf16)] * 2
        + [vmem(wqkv.shape, bf16), vmem((seq, PW), f32), vmem((seq, PW), f32)]
        + [vmem(heads, bf16)] * 3
        + [vmem((width, seq), bf16), vmem((width, width), bf16), vmem(flat, bf16)]
        + [vmem((chunks, width, FC), bf16), vmem((chunks, FC, width), bf16)]
        + [vmem(heads, bf16)] * 2
        + [vmem((PW, seq), bf16)] * 2
        + [vmem((AHEAD, seq + T, 2 * T), f32), vmem((2 * T, 2 * T), f32)]
        + [vmem(flat, bf16), vmem((width, seq), bf16)]
        + [vmem((pairs, seq // T, 2 * T), f32)]
        + [vmem(flat, f32), vmem(flat, bf16)]
        + [vmem(flat, f32)] * 2
        + [vmem((seq, FC), bf16)] * 2
        + [vmem((2, FC, width), bf16)] * 2
        + [vmem((2, width // 2, width), bf16)]
        + [dma((7,)), dma((chunks,)), dma((chunks,)), dma((10,)), dma((2,)), dma((2,)), dma((tiles, 3))],
        compiler_params=params(BIG),
        cost_estimate=LONG,
        name="layer",
    )(info, gain1, gain2, received, *pinned(x, wqkv, *tables, wo, dy, w1, w2))


def weigh_kernel(first, info, dq, keep, got, cosine, signed, h1t, wqkv, sums, dkv, g_send, g_keep, small):
    width, half = wqkv.shape[0], wqkv.shape[0] // 2
    mine = pl.multiple_of(info[0] * half, half)
    dk = keep[0].astype(f32) + got[0].astype(f32)
    dkv[0] = rotated(dk, cosine[...], signed[...], -1.0).astype(bf16)
    dkv[1] = (keep[1].astype(f32) + got[1].astype(f32)).astype(bf16)
    small[...] = sums[...]
    for out, start in ((g_send, half - mine), (g_keep, mine)):
        rows = pl.ds(start, half)
        terms = 0.0
        for i, part in enumerate((dq, dkv.at[0], dkv.at[1])):
            total = nn(h1t[rows, :], part[...])
            out[i] = total.astype(bf16)
            at = i * width + first * PW
            weighted = total * wqkv[rows, at : at + total.shape[1]].astype(f32)
            for c in range(0, total.shape[1], PW):
                terms = terms + weighted[:, c : c + PW]
        line = jnp.sum(terms.T, axis=0, keepdims=True)
        lanes = lax.broadcasted_iota(jnp.int32, (1, width), 1)
        inside = jnp.logical_and(lanes >= start, lanes < start + half)
        small[4:5, :] += jnp.where(inside, jnp.concatenate([line, line], axis=1), 0.0)
    small[5:6, :] = jnp.full((1, width), info[1].astype(f32))


def weigh(info, first, dq, keep, got, tables, h1t, wqkv, sums):
    seq, width = dq.shape
    tall = h1t.shape[0]
    return pl.pallas_call(
        functools.partial(weigh_kernel, first),
        in_specs=[SMEM] + [IN_VMEM] * 8,
        out_specs=[IN_VMEM] * 4,
        out_shape=[shape((2, seq, width), bf16)]
        + [shape((3, tall // 2, width), bf16)] * 2
        + [shape(sums.shape, f32)],
        compiler_params=params(24),
        cost_estimate=LONG,
        name="weigh",
    )(info, dq, keep, got, *tables, h1t, wqkv, sums)


def finish_kernel(parts, tiles, x, dx2, wqkv, gain_line, *refs):
    dx_any, dx, sem = refs[-3:]
    dqs, dkvs = refs[:parts], refs[parts : 2 * parts]
    gain = gain_line[...].reshape(1, x.shape[1])

    def store(t):
        rows = pl.ds(pl.multiple_of(t * R, R), R)
        return pltpu.make_async_copy(dx.at[rows, :], dx_any.at[rows, :], sem.at[t])

    def some_rows(t, carry):
        rows = pl.ds(pl.multiple_of(t * R, R), R)
        grads = [r[rows, :] for r in dqs] + [r[0, rows, :] for r in dkvs] + [r[1, rows, :] for r in dkvs]
        dh = nt(jnp.concatenate(grads, axis=1), wqkv[...])
        grad, _ = norm_back(x[rows, :].astype(f32), gain, dh)
        dx[rows, :] = (dx2[rows, :] + grad).astype(bf16)
        store(t).start()
        return carry

    lax.fori_loop(*tiles, some_rows, 0)
    for t in range(*tiles):
        store(t).wait()


def finish(tiles, x, dx2, dqs, dkvs, weight, gain, before):
    anywhere = pl.BlockSpec(memory_space=pl.ANY)
    ins = 4 + len(dqs) + len(dkvs)
    return pl.pallas_call(
        functools.partial(finish_kernel, len(dqs), tiles),
        in_specs=[IN_VMEM] * ins + [anywhere] * len(before),
        out_specs=anywhere,
        out_shape=shape(x.shape, bf16),
        scratch_shapes=[pltpu.VMEM(x.shape, bf16), pltpu.SemaphoreType.DMA((x.shape[0] // R,))],
        input_output_aliases={ins: 0} if before else {},
        compiler_params=params(24),
        cost_estimate=COST if before else LONG,
        name="finish",
    )(x, dx2, weight, gain, *dqs, *dkvs, *before)


def bit_orders(count, groups):
    bits = [1 << i for i in range(count.bit_length() - 1)]
    if groups == 2:
        return [bits, bits[1::-1] + bits[2:]]
    return [bits[g:-1] + bits[:g] + bits[-1:] for g in range(groups)]


def exchange(value, axis, bit):
    size = lax.axis_size(axis)
    return lax.ppermute(value, axis, [(i, i ^ bit) for i in range(size)])


def distance(order, place):
    out = 0
    for i, bit in enumerate(order):
        out = out + ((place >> (len(order) - 1 - i)) & 1) * bit
    return out


LINES = 16


def halves(value):
    high = value.astype(bf16)
    return high, (value - high.astype(f32)).astype(bf16)


def put_sums(value, kept, block):
    high, low = halves(value)
    block[:LINES, :] = high
    block[LINES : 2 * LINES, :] = low
    kept[...] = high.astype(f32) + low.astype(f32)


def got_sums(block):
    return block[:LINES, :].astype(f32) + block[LINES : 2 * LINES, :].astype(f32)


def start_kernel(orders, sources, small, me, *refs):
    groups = len(orders)
    arrays = max(a for source in sources for a, _ in source) + 1
    ins, outs = refs[: 2 * arrays], refs[len(refs) - 2 * groups :]
    half = outs[0].shape[0]
    for g, order in enumerate(orders):
        for side in range(2):

            def one(r, carry, g=g, order=order, side=side):
                part = me[0] ^ distance(order, r + side * half)
                out = outs[2 * g + side]
                row = 0
                for a, where in sources[g]:
                    kept, got = ins[2 * a : 2 * a + 2]
                    place = where(part)
                    size = kept.shape[1]
                    total = kept[place].astype(f32) + got[place].astype(f32)
                    if len(out.shape) == 3:
                        out[r, row : row + size, :] = total.astype(bf16)
                    else:
                        start = pl.multiple_of(r * outs[0].shape[1] + row, 8)
                        out[pl.ds(start, size), :] = total.astype(bf16)
                    row += size
                return carry

            lax.fori_loop(0, half, one, 0)
    if small:
        here, there, kept = refs[2 * arrays : 2 * arrays + 3]
        total = here[...] + there[...]
        if small == "rides":
            wide = total.shape[1] // 2
            total = jnp.concatenate([total[:, :wide], total[:, wide:]], axis=0)
            put_sums(total, kept, outs[1].at[pl.ds(half * outs[0].shape[1], 2 * LINES), :])
        else:
            kept[...] = total


def travelling(count, rows, width, rides):
    return shape((count * rows + 2 * LINES, width) if rides else (count, rows, width), bf16)


def start_sum(me, kept, got, sources, orders, small, rides):
    count = 1 << len(orders[0])
    half = count // 2
    rows = [sum(kept[a].shape[1] for a, _ in source) for source in sources]
    width = kept[0].shape[2]
    cols = width // 3
    args = [a for pair in zip(kept, got, strict=True) for a in pair]
    sums = []
    for g in range(len(orders)):
        sums += [shape((half, rows[g], width), bf16), travelling(half, rows[g], width, rides and g == 0)]
    mode = "rides" if rides else "alone" if small else ""
    if small:
        lines = (LINES, width) if rides else small[0].shape
        specs = dict(
            in_specs=[SMEM] + [IN_VMEM] * (len(args) + 2),
            out_specs=[IN_VMEM] * (1 + len(sums)),
            out_shape=[shape(lines, f32)] + sums,
        )
    else:
        block = lambda a: pl.BlockSpec((a.shape[0], a.shape[1], cols), lambda c: (0, 0, c))
        specs = dict(
            grid=(width // cols,),
            in_specs=[SMEM] + [block(a) for a in args],
            out_specs=[block(a) for a in sums],
            out_shape=sums,
        )
    outs = pl.pallas_call(
        functools.partial(start_kernel, orders, sources, mode),
        compiler_params=params(30),
        cost_estimate=COST,
        name="start_sum",
        **specs,
    )(me, *args, *small)
    small, outs = list(outs[: len(outs) - len(sums)]), outs[len(outs) - len(sums) :]
    return list(outs[0::2]), list(outs[1::2]), small


def step_kernel(groups, merge, mode, *refs):
    kept, got = refs[:groups], refs[groups : 2 * groups]
    outs = refs[2 * groups + (2 if mode == "alone" else 1 if mode else 0) :]
    count = kept[0].shape[0]
    half = count // 2
    row = 0
    for g in range(groups):
        keep, send = outs[:2] if merge else outs[2 * g : 2 * g + 2]
        size = kept[g].shape[1]
        for r in range(count):
            there = got[g][r] if len(got[g].shape) == 3 else got[g][r * size : (r + 1) * size]
            total = (kept[g][r].astype(f32) + there.astype(f32)).astype(bf16)
            if r < half:
                keep[r, row : row + size, :] = total
            elif len(send.shape) == 3:
                send[r - half, row : row + size, :] = total
            else:
                start = (r - half) * keep.shape[1] + row
                send[start : start + size, :] = total
        row += size if merge else 0
    if mode == "rides":
        total = refs[2 * groups][...] + got_sums(got[0][count * kept[0].shape[1] :])
        put_sums(total, outs[-1], outs[1].at[pl.ds(half * outs[0].shape[1], 2 * LINES), :])
    elif mode:
        outs[-1][...] = refs[2 * groups][...] + refs[2 * groups + 1][...]


def step_sum(kept, got, small, merge, rides):
    groups = len(kept)
    half = kept[0].shape[0] // 2
    rows = [a.shape[1] for a in kept]
    width = kept[0].shape[2]
    args = [*kept, *got, *small]
    sums = []
    for g, r in enumerate([sum(rows)] if merge else rows):
        sums += [shape((half, r, width), bf16), travelling(half, r, width, rides and g == 0)]
    outs = pl.pallas_call(
        functools.partial(step_kernel, groups, merge, "rides" if rides else "alone" if small else ""),
        in_specs=[IN_VMEM] * len(args),
        out_specs=[IN_VMEM] * (len(sums) + len(small[:1])),
        out_shape=sums + [shape(a.shape, f32) for a in small[:1]],
        compiler_params=params(16),
        cost_estimate=COST if small or half == 1 else LONG,
        name="step_sum",
    )(*args)
    return list(outs[0 : len(sums) : 2]), list(outs[1 : len(sums) : 2]), list(outs[len(sums) :])


def feed_end_kernel(kept, got, down, up, out):
    total = kept[0].astype(f32) + got[0].astype(f32)
    tall, few = down.shape[0] // GROUPS, out.shape[0] // GROUPS
    ups = []
    for g in range(GROUPS):
        row = g * (2 * tall + few)
        down[g * tall : (g + 1) * tall, :] = total[row : row + tall]
        ups.append(total[row + tall : row + 2 * tall])
        out[g * few : (g + 1) * few, :] = total[row + 2 * tall : row + 2 * tall + few]
    up[...] = jnp.concatenate(ups, axis=0).T


def feed_end(kept, got, tall, few):
    width = kept.shape[2]
    return pl.pallas_call(
        feed_end_kernel,
        in_specs=[IN_VMEM] * 2,
        out_specs=[IN_VMEM] * 3,
        out_shape=[shape((tall, width), f32), shape((width, tall), f32), shape((few, width), f32)],
        compiler_params=params(16),
        cost_estimate=COST,
        name="feed_end",
    )(kept, got)


def qkv_end_kernel(rides, gain_line, kept, got, *refs):
    out, gain1, gain2, rms = refs[-4:]
    tall = out.shape[0]
    width = gain1.shape[0]
    cols = kept.shape[2]
    there = got[: kept.shape[1]] if rides else got[0]
    total = kept[0].astype(f32) + there.astype(f32)
    for i in range(total.shape[0] // tall):
        part, third = i // 3, i % 3
        at = third * width + part * cols
        out[:, at : at + cols] = total[i * tall : (i + 1) * tall]
    if rides:
        sums = refs[0][...] + got_sums(got[kept.shape[1] :])
        sums = jnp.concatenate([sums[: LINES // 2], sums[LINES // 2 :]], axis=1)
    else:
        sums = refs[0][...] + refs[1][...]
    gain2[...] = sums[3:4, :].reshape(width)
    gain1[...] = (sums[4:5, :] / gain_line[...].reshape(1, width)).reshape(width)
    count = jnp.max(sums[5:6, :], axis=1, keepdims=True) * width
    rms[...] = jnp.broadcast_to(jnp.sqrt(jnp.sum(sums, axis=1, keepdims=True) / count), rms.shape)


def qkv_end(gain, kept, got, small, tall, wide, rides):
    return pl.pallas_call(
        functools.partial(qkv_end_kernel, rides),
        in_specs=[IN_VMEM] * (3 + len(small)),
        out_specs=[IN_VMEM] * 4,
        out_shape=[shape((tall, wide), f32), shape(gain.shape, f32), shape(gain.shape, f32), shape((8, 128), f32)],
        compiler_params=params(16),
        cost_estimate=COST,
        name="qkv_end",
    )(gain, kept, got, *small)


def after(value, *earlier):
    return lax.optimization_barrier((value, earlier))[0]


def sum_parts(me, kept, got, sources, small, rides):
    orders = bit_orders(lax.axis_size("batch"), len(sources))
    steps = len(orders[0])
    common = min(i for i in range(steps + 1) if all(order[i:] == orders[0][i:] for order in orders))
    keep, send, small = start_sum(me, kept, got, sources, orders, small, rides)
    for i in range(steps):
        got = [exchange(s, "batch", order[i]) for s, order in zip(send, orders[: len(send)], strict=True)]
        if small and not rides:
            small = [small[0], exchange(small[0], "batch", orders[0][i])]
        earlier = yield send[0], got
        if i == steps - 1:
            break
        if earlier is not None:
            keep = after(keep, earlier)
        keep, send, small = step_sum(keep, got, small, i + 1 == common, rides)
    yield keep[0], got[0], small


def on_device(
    inputs, lengths, cotangent, qkv_weight, out_weight, up_weight, down_weight, attn_gain, mlp_gain
):
    seq, width = inputs.shape[2:]
    x = inputs[0, 0]
    dy = cotangent[0, 0]
    count = lax.axis_size("batch")
    stream = lax.axis_index("stream").astype(jnp.int32)
    me = lax.axis_index("batch").astype(jnp.int32).reshape(1)
    info = jnp.stack([stream, lengths[0]])
    cosine, sine = rotary_tables(seq)
    tables = (
        jnp.asarray(np.concatenate([cosine] * 4, axis=1)),
        jnp.asarray(np.concatenate([-sine, sine] * 2, axis=1)),
    )
    tables_t = (jnp.asarray(cosine.T), jnp.asarray(sine.T))

    received = lax.ppermute(x, "stream", [(0, 1)])
    (
        q, ko, vo, kc, vc, h1t, o, lse, outputs, dx2, do,
        up_send, up_keep, down_send, down_keep, out_send, out_keep, sums,
    ) = layer(
        info, attn_gain, mlp_gain, received, x, qkv_weight, tables, out_weight, dy, up_weight, down_weight
    )
    down_got, up_got, out_got = (exchange(a, "stream", 1) for a in (down_send, up_send, out_send))

    def by_rows(array):
        return array.reshape(count * GROUPS, array.shape[0] // (count * GROUPS), width)

    heads = (q, ko, vo, kc, vc, o)
    pairs = width // PW // 2
    dq1, keep1, send1 = attend_back(info, 0, pairs, *heads, do, lse, *tables_t)
    got1 = lax.ppermute(send1, "stream", [(1, 0)])
    early = sum_parts(
        me,
        [by_rows(after(a, dq1)) for a in (down_keep, up_keep, out_keep)],
        [by_rows(a) for a in (down_got, up_got, out_got)],
        [[(a, lambda part, g=g: part * GROUPS + g) for a in range(3)] for g in range(GROUPS)],
        [],
        False,
    )
    token = next(early)[0]
    dq2, keep2, send2 = attend_back(info, pairs, pairs, *heads, after(do, token), lse, *tables_t)
    got2 = lax.ppermute(send2, "stream", [(1, 0)])
    token = early.send(dq2)[0]
    dkv1, qkv_send1, qkv_keep1, small = weigh(info, 0, dq1, after(keep1, token), got1, tables, h1t, qkv_weight, sums)
    qkv_got1 = exchange(qkv_send1, "stream", 1)
    dkv2, qkv_send2, qkv_keep2, small = weigh(info, pairs, dq2, keep2, got2, tables, h1t, qkv_weight, small)
    qkv_got2 = exchange(qkv_send2, "stream", 1)
    small_got = exchange(small, "stream", 1)
    token = early.send(dkv2)[0]

    tall = width // (2 * count)
    split = lambda a: a.reshape(3 * count, tall, a.shape[2])
    rides = 3 * tall >= 2 * LINES
    late = sum_parts(
        me,
        [split(after(a, token)) for a in (qkv_keep1, qkv_keep2)],
        [split(a) for a in (qkv_got1, qkv_got2)],
        [[(g, lambda part, i=i: i * count + part) for i in range(3)] for g in range(2)],
        [small, small_got],
        rides,
    )
    token = next(late)[0]
    ends = [dq1, dq2], [dkv1, dkv2], qkv_weight, attn_gain
    tiles = seq // R
    dx = finish((0, tiles // 2), after(x, token), dx2, *ends, [])
    early_out = early.send(dx)
    dx = finish((tiles // 2, tiles), x, after(dx2, early_out[0]), *ends, [dx])
    late.send(dx)
    late_out = late.send(early_out[1])
    while len(late_out) == 2:
        late_out = late.send(None)
    while len(early_out) == 2:
        early_out = early.send(None)
    up_cols = down_keep.shape[0] // count
    down_grad, up_grad, out_grad = feed_end(*early_out[:2], up_cols, tall)
    qkv_grad, gain1_grad, gain2_grad, rms = qkv_end(attn_gain, *late_out, tall, 3 * width, rides)
    return (
        outputs[None, None],
        dx[None, None],
        qkv_grad,
        out_grad,
        up_grad,
        down_grad,
        gain1_grad,
        gain2_grad,
        rms[:3, 0],
    )


def solution(mesh):
    rows = P("stream", "batch", None, None)
    both = ("stream", "batch")
    return jax.shard_map(
        on_device,
        mesh=mesh,
        in_specs=(rows, P("batch"), rows, P(), P(), P(), P(), P(), P()),
        out_specs=(rows, rows, P(both, None), P(both, None), P(None, both), P(both, None), P(), P(), P()),
        check_vma=False,
    )
```

```python
import functools

import jax
import jax.numpy as jnp
import numpy as np
from jax import lax
from jax.experimental import pallas as pl
from jax.experimental.pallas import tpu as pltpu
from jax.sharding import PartitionSpec as P

f32 = jnp.float32
bf16 = jnp.bfloat16

HD = 64
BLK = 16
EPS = 1e-06
NEG = -1e30
PW = 2 * HD
T = 128
R = 256
AHEAD = 2
FC = 768
SCALE = HD**-0.5
BIG = 62
GROUPS = 3

COST = pl.CostEstimate(flops=1 << 20, bytes_accessed=1 << 16, transcendentals=0)
LONG = pl.CostEstimate(flops=1 << 35, bytes_accessed=1 << 26, transcendentals=0)

SMEM = pl.BlockSpec(memory_space=pltpu.SMEM)
IN_VMEM = pl.BlockSpec(memory_space=pltpu.VMEM)


def params(mib):
    return pltpu.CompilerParams(vmem_limit_bytes=mib << 20)


def shape(dims, dtype):
    return jax.ShapeDtypeStruct(dims, dtype)


def pinned(*arrays):
    return [pltpu.with_memory_space_constraint(a, pltpu.HBM) for a in arrays]


def nn(a, b):
    return jnp.dot(a, b, preferred_element_type=f32)


def nt(a, b):
    return lax.dot_general(a, b, (((1,), (1,)), ((), ())), preferred_element_type=f32)


def tn(a, b):
    return lax.dot_general(a, b, (((0,), (0,)), ((), ())), preferred_element_type=f32)


def whole(dims):
    return pl.BlockSpec(dims, lambda *_: (0,) * len(dims), pipeline_mode=pl.Buffered(1))


def inv_rms(v):
    return lax.rsqrt(jnp.mean(v * v, axis=-1, keepdims=True) + EPS)


def norm_back(v, gain, grad):
    r = inv_rms(v)
    unit = v * r
    scaled = grad * gain
    inner = jnp.mean(scaled * unit, axis=-1, keepdims=True)
    return r * (scaled - unit * inner), grad * unit


def rotary_tables(length):
    half = HD // 2
    freqs = np.exp(-np.log(10000.0) * np.arange(half) / half).astype(np.float32)
    angles = (np.arange(length, dtype=np.float32)[:, None] * freqs[None, :]).astype(np.float64)
    return np.cos(angles).astype(np.float32), np.sin(angles).astype(np.float32)


def rotated(v, cosine, signed, sign):
    first = lax.broadcasted_iota(jnp.int32, (1, PW), 1) % HD < HD // 2
    outs = []
    for c in range(0, v.shape[1], PW):
        part = v[:, c : c + PW]
        partner = jnp.where(first, pltpu.roll(part, PW - HD // 2, 1), pltpu.roll(part, HD // 2, 1))
        outs.append(part * cosine + partner * (signed * sign))
    return outs[0] if len(outs) == 1 else jnp.concatenate(outs, axis=1)


def staggered(count, *stages):
    state = [()] * count
    for step in range(count + len(stages) - 1):
        for k, stage in enumerate(stages):
            if 0 <= step - k < count:
                state[step - k] = stage(step - k, *state[step - k])


def token_weight(start, length, rows):
    return lax.broadcasted_iota(jnp.int32, (rows, 1), 0) + start < length


def row_sum(v):
    return jnp.sum(v, axis=0, keepdims=True)


def by_pairs(ref, rows, value):
    for p in range(ref.shape[0]):
        ref[p, rows, :] = value[:, p * PW : (p + 1) * PW].astype(ref.dtype)


def stacked(tile, low):
    zero = jnp.zeros_like(tile)
    return jnp.concatenate([jnp.where(low, tile, zero), jnp.where(low, zero, tile)], axis=0)


def unstacked(tile_t):
    half = lax.broadcasted_iota(jnp.int32, (PW, 1), 0) < HD
    return jnp.where(half, tile_t[:, :T], tile_t[:, T:])


def chunks_of(i):
    out, j = [], 0
    while j < i:
        n = 2 if i - j >= 2 else 1
        out.append((j * T, n * T))
        j += n
    return out


def edge_bias(ref, noisy):
    row = lax.broadcasted_iota(jnp.int32, (T, 2 * T), 0) // BLK
    col = (lax.broadcasted_iota(jnp.int32, (T, 2 * T), 1) % T) // BLK
    own = jnp.logical_or(row == col, jnp.logical_and(row < col, noisy == 0))
    other = jnp.logical_and(row < col, noisy == 1)
    ref[:T, :] = jnp.where(own, 0.0, NEG)
    ref[T:, :] = jnp.where(other, 0.0, NEG)


def masked(s, start, length):
    pos = lax.broadcasted_iota(jnp.int32, s.shape, 0) + start
    return jnp.where(pos < length, s, NEG)


def over_rows(op, v):
    return op(v.reshape(v.shape[0] // 8, 8, v.shape[1]), axis=0)


def attend_pair(length, q, ko, vo, kc, vc, store, lse, vo_t, vc_t, scores, bias):
    seq = q.shape[0]
    low = lax.broadcasted_iota(jnp.int32, (1, PW), 1) < HD
    vo_t[...] = vo[...].T
    vc_t[...] = vc[...].T

    def score(i):
        at = pl.ds(i * T, T)
        q2 = stacked(q[at, :] * bf16(SCALE), low)
        buf = scores.at[i % AHEAD]
        edge = nt(jnp.concatenate([ko[at, :], kc[at, :]], 0), q2) + bias[...]
        own = masked(edge[:T], i * T, length)
        other = masked(edge[T:], i * T, length)
        buf[pl.ds(0, T), :] = own
        buf[pl.ds(T, T), :] = other
        top = over_rows(jnp.max, jnp.maximum(own, other))
        for start, size in chunks_of(i):
            s = masked(nt(kc[pl.ds(start, size), :], q2), start, length)
            buf[pl.ds(2 * T + start, size), :] = s
            top = jnp.maximum(top, over_rows(jnp.max, s))
        return jnp.max(top, axis=0, keepdims=True)

    def mix(i, top):
        at = pl.ds(i * T, T)
        buf = scores.at[i % AHEAD]
        p = jnp.exp(buf[pl.ds(0, 2 * T), :] - top)
        total = over_rows(jnp.sum, p)
        acc = nn(jnp.concatenate([vo_t[:, at], vc_t[:, at]], 1), p.astype(bf16))
        for start, size in chunks_of(i):
            p = jnp.exp(buf[pl.ds(2 * T + start, size), :] - top)
            total = total + over_rows(jnp.sum, p)
            acc = acc + nn(vc_t[:, pl.ds(start, size)], p.astype(bf16))
        total = row_sum(total)
        lse[0, pl.ds(i, 1), :] = top + jnp.log(total)
        store(at, unstacked(acc * (1.0 / total)))

    tops = {}
    for i in range(seq // T + AHEAD - 1):
        if i < seq // T:
            tops[i] = score(i)
        if i >= AHEAD - 1:
            mix(i - AHEAD + 1, tops.pop(i - AHEAD + 1))


def turned_back(v, cosine, sine):
    quarter = HD // 2
    a, b, c, d = (v[i * quarter : (i + 1) * quarter] for i in range(4))
    return jnp.concatenate(
        [a * cosine + b * sine, b * cosine - a * sine, c * cosine + d * sine, d * cosine - c * sine]
    )


def attend_back_kernel(
    info, q, ko, vo, kc, vc, o, do, lse, cosine, sine, dq, keep, send, ko_t, kc_t, dko, dvo, dkc, dvc, bias
):
    noisy, length = info[0], info[1]
    q, ko, vo, kc, vc = (ref.at[0] for ref in (q, ko, vo, kc, vc))
    seq = q.shape[0]
    low = lax.broadcasted_iota(jnp.int32, (1, PW), 1) < HD

    @pl.when(pl.program_id(0) == 0)
    def _():
        edge_bias(bias, noisy)

    ko_t[...] = ko[...].T
    kc_t[...] = kc[...].T

    def tile(i):
        at = pl.ds(i * T, T)
        prod = (do[at, :].astype(f32) * o[at, :].astype(f32)).T
        delta = jnp.concatenate([row_sum(prod[:HD]), row_sum(prod[HD:])], 1)
        q2 = stacked(q[at, :] * bf16(SCALE), low)
        return q2, stacked(do[at, :], low), lse[0, pl.ds(i, 1), :], delta

    def products(i, start, size, q2, do2):
        if start is None:
            at = pl.ds(i * T, T)
            s = nt(jnp.concatenate([ko[at, :], kc[at, :]], 0), q2) + bias[...]
            s = jnp.concatenate([masked(s[:T], i * T, length), masked(s[T:], i * T, length)], 0)
            return s, nt(jnp.concatenate([vo[at, :], vc[at, :]], 0), do2)
        rows = pl.ds(start, size)
        return masked(nt(kc[rows, :], q2), start, length), nt(vc[rows, :], do2)

    def gather(i, start, size, q2, do2, p, ds, dq_t):
        at = pl.ds(i * T, T)
        dv, dk = nn(p, do2), nn(ds, q2)
        if start is None:
            dvo[at, :] = dv[:T]
            dko[at, :] = dk[:T]
            dvc[at, :] = dv[T:]
            dkc[at, :] = dk[T:]
            return nn(jnp.concatenate([ko_t[:, at], kc_t[:, at]], 1), ds)
        rows = pl.ds(start, size)
        dvc[rows, :] += dv
        dkc[rows, :] += dk
        return dq_t + nn(kc_t[:, rows], ds)

    work = [(i, *c) for i in range(seq // T) for c in [(None, None)] + chunks_of(i)]
    tiles, made, weighed, dq_t = {}, {}, {}, None
    for n in range(len(work) + 2):
        if n < len(work):
            i = work[n][0]
            if i not in tiles:
                tiles[i] = tile(i)
            made[n] = products(*work[n], *tiles[i][:2])
        if 0 <= n - 1 < len(work):
            _, _, norm, delta = tiles[work[n - 1][0]]
            s, dp = made.pop(n - 1)
            p = jnp.exp(s - norm)
            weighed[n - 1] = p.astype(bf16), (p * (dp - delta)).astype(bf16)
        if n >= 2:
            i, start, size = work[n - 2]
            dq_t = gather(i, start, size, *tiles[i][:2], *weighed.pop(n - 2), dq_t)
            if n == len(work) + 1 or work[n - 1][0] != i:
                at = pl.ds(i * T, T)
                out = turned_back(unstacked(dq_t), cosine[:, at], sine[:, at]) * SCALE
                dq[at, :] = out.T.astype(bf16)
    clean = (1 - noisy).astype(f32)
    for at, own, other in ((0, dko, dkc), (1, dvo, dvc)):
        keep[at] = (own[...] + clean * other[...]).astype(bf16)
        send[at] = other[...].astype(bf16)


def attend_back(info, first, pairs, q, ko, vo, kc, vc, o, do, lse, cosine, sine):
    seq = q.shape[1]
    width = pairs * PW
    heads = pl.BlockSpec((1, seq, PW), lambda h: (first + h, 0, 0))
    source = pl.BlockSpec((seq, PW), lambda h: (0, first + h))
    both = pl.BlockSpec((2, seq, PW), lambda h: (0, 0, h))
    lines = pl.BlockSpec((1, seq // T, 2 * T), lambda h: (first + h, 0, 0))
    table = whole((HD // 2, seq))
    return pl.pallas_call(
        attend_back_kernel,
        grid=(pairs,),
        in_specs=[SMEM] + [heads] * 5 + [source] * 2 + [lines, table, table],
        out_specs=[pl.BlockSpec((seq, PW), lambda h: (0, h)), both, both],
        out_shape=[shape((seq, width), bf16)] + [shape((2, seq, width), bf16)] * 2,
        scratch_shapes=[pltpu.VMEM((PW, seq), bf16)] * 2
        + [pltpu.VMEM((seq, PW), f32)] * 4
        + [pltpu.VMEM((2 * T, 2 * T), f32)],
        compiler_params=params(24),
        cost_estimate=LONG,
        name="attend_back",
    )(info, *pinned(q, ko, vo, kc, vc, o, do), lse, cosine, sine)


C0 = 0.7978845608028654
C1 = C0 * 0.044715


def layer_kernel(
    info, gain1_line, gain2_line, received_any, x_any, wqkv_any, cosine_any, signed_any, wo_any, dy_any,
    w1_any, w2_any,
    q_out, ko_out, vo_out, kc_out, vc_out, h1t_out, o_out, lse_out, out_any, dx2_any, do_any,
    up_send, up_keep, down_send, down_keep, g_send, g_keep, sums,
    x, received, wqkv, cosine, signed, q, ko, vo, h1t, wo, dy, w1, w2,
    kc, vc, vo_t, vc_t, scores, bias, o, o_t, lse, x2, h2, m, dh, act, du, up_grad, down_grad, half_grads,
    sem_in, sem_1, sem_2, sem_out, sem_up, sem_down, sem_tile,
):
    noisy, length = info[0], info[1]
    seq, width = x.shape
    chunks, pairs, tiles = w1.shape[0], kc.shape[0], seq // R
    copy = pltpu.make_async_copy
    gain1, gain2 = gain1_line[...].reshape(1, width), gain2_line[...].reshape(1, width)

    def weights(c):
        place = lax.rem(c + (chunks // 2) * (1 - noisy), chunks) * FC
        place = pl.multiple_of(place, FC)
        return (
            copy(w1_any.at[:, pl.ds(place, FC)], w1.at[c], sem_1.at[c]),
            copy(w2_any.at[pl.ds(place, FC), :], w2.at[c], sem_2.at[c]),
        )

    sources = (
        (x_any, x),
        (wqkv_any, wqkv),
        (cosine_any, cosine),
        (signed_any, signed),
        (received_any, received),
        (wo_any, wo),
        (dy_any, dy),
    )
    loads = [copy(a, b, sem_in.at[i]) for i, (a, b) in enumerate(sources)]
    for load in loads[:5]:
        load.start()
    sums[...] = jnp.zeros_like(sums)
    edge_bias(bias, noisy)
    span = lambda t: pl.ds(t * R, R)

    loads[0].wait()

    def own_norm(t):
        value = x[span(t), :].astype(f32)
        h1 = (value * inv_rms(value) * gain1).astype(bf16)
        h2[span(t), :] = h1
        h1t[:, span(t)] = h1.T
        weight = token_weight(t * R, length, R)
        sums[0:1, :] += row_sum(jnp.where(weight, value * value, 0.0))
        return ()

    for t in range(tiles):
        own_norm(t)
    for load in loads[1:5]:
        load.wait()
    for load in loads[5:]:
        load.start()

    def own_product(t):
        return tuple(nn(h2[span(t), :], wqkv[:, i * width : (i + 1) * width]) for i in range(3))

    def own_turn(t, a, b, c):
        tables = (cosine[span(t), :], signed[span(t), :], 1.0)
        by_pairs(q, span(t), rotated(a, *tables))
        by_pairs(ko, span(t), rotated(b, *tables))
        by_pairs(vo, span(t), c)
        return ()

    def clean_norm(t):
        value = jnp.where(noisy == 1, received[span(t), :].astype(f32), x[span(t), :].astype(f32))
        received[span(t), :] = (value * inv_rms(value) * gain1).astype(bf16)
        return ()

    def clean_product(t):
        return tuple(nn(received[span(t), :], wqkv[:, i * width : (i + 1) * width]) for i in (1, 2))

    def clean_turn(t, a, b):
        by_pairs(kc, span(t), rotated(a, cosine[span(t), :], signed[span(t), :], 1.0))
        by_pairs(vc, span(t), b)
        return ()

    staggered(tiles, own_product, own_turn)
    stores = [
        copy(a, b, sem_out.at[6 + i])
        for i, (a, b) in enumerate(((q, q_out), (ko, ko_out), (vo, vo_out), (h1t, h1t_out)))
    ]
    for store in stores:
        store.start()
    staggered(tiles, clean_norm, clean_product, clean_turn)
    more = [copy(kc, kc_out, sem_out.at[0]), copy(vc, vc_out, sem_out.at[1])]
    for store in more:
        store.start()
    stores += more

    for c in range(chunks):
        for load in weights(c):
            load.start()

    def one_pair(p, carry):
        lanes = pl.ds(pl.multiple_of(p * PW, PW), PW)

        def keep(at, tile_t):
            o_t[lanes, at] = tile_t.astype(bf16)
            o[at, lanes] = tile_t.T.astype(bf16)

        heads = (ref.at[p] for ref in (q, ko, vo, kc, vc))
        attend_pair(length, *heads, keep, lse.at[pl.ds(p, 1)], vo_t, vc_t, scores, bias)
        return carry

    lax.fori_loop(0, pairs, one_pair, 0)
    more = [copy(o, o_out, sem_out.at[2]), copy(lse, lse_out, sem_out.at[3])]
    for store in more:
        store.start()
    stores += more

    for load in loads[5:]:
        load.wait()

    def join_product(t):
        return (nn(o[span(t), :], wo[...]),)

    def join_norm(t, branch):
        value = x[span(t), :].astype(f32) + branch
        x2[span(t), :] = value
        h2[span(t), :] = (value * inv_rms(value) * gain2).astype(bf16)
        m[span(t), :] = jnp.zeros_like(value)
        dh[span(t), :] = jnp.zeros_like(value)
        weight = token_weight(t * R, length, R)
        sums[1:2, :] += row_sum(jnp.where(weight, branch * branch, 0.0))
        return ()

    staggered(tiles, join_product, join_norm)

    def grad_stores(c, up, down):
        slot = lax.rem(c, 2)
        rows = pl.ds(pl.multiple_of(lax.rem(c, chunks // 2) * FC, FC), FC)
        return (
            copy(up_grad.at[slot], up.at[rows, :], sem_up.at[slot]),
            copy(down_grad.at[slot], down.at[rows, :], sem_down.at[slot]),
        )

    def one_chunk(c, carry):
        for load in weights(c):
            load.wait()
        up, down = w1.at[c], w2.at[c]
        made = {}
        for t in range(-R, seq, R):
            if t + R < seq:
                rows = pl.ds(t + R, R)
                made[t + R] = nn(h2[rows, :], up[...]), nt(dy[rows, :], down[...])
            if t < 0:
                continue
            rows = pl.ds(t, R)
            u, da = made.pop(t)
            sq = u * u
            half = 0.5 * jnp.tanh(u * (C0 + C1 * sq)) + 0.5
            low = (u * half).astype(bf16)
            slope = half + u * (2.0 * half * (1.0 - half)) * (C0 + 3.0 * C1 * sq)
            back = (da * slope).astype(bf16)
            act[rows, :] = low
            du[rows, :] = back
            m[rows, :] += nn(low, down[...])
            dh[rows, :] += nt(back, up[...])

        @pl.when(c >= 2)
        def _():
            for store in grad_stores(c, up_send, down_send):
                store.wait()

        slot = lax.rem(c, 2)
        down_grad[slot] = tn(act[...], dy[...]).astype(bf16)
        up_grad[slot] = tn(du[...], h2[...]).astype(bf16)

        @pl.when(c < chunks // 2)
        def _():
            for store in grad_stores(c, up_send, down_send):
                store.start()

        @pl.when(c >= chunks // 2)
        def _():
            for store in grad_stores(c, up_keep, down_keep):
                store.start()

        return carry

    lax.fori_loop(0, chunks, one_chunk, 0)

    def tile_stores(t):
        return (
            copy(h2.at[span(t), :], out_any.at[span(t), :], sem_tile.at[t, 0]),
            copy(x2.at[span(t), :], dx2_any.at[span(t), :], sem_tile.at[t, 1]),
            copy(received.at[span(t), :], do_any.at[span(t), :], sem_tile.at[t, 2]),
        )

    def middle_norm(t):
        value = x2[span(t), :]
        mixed = m[span(t), :]
        weight = token_weight(t * R, length, R)
        sums[2:3, :] += row_sum(jnp.where(weight, mixed * mixed, 0.0))
        grad, gain_terms = norm_back(value, gain2, dh[span(t), :])
        sums[3:4, :] += row_sum(gain_terms)
        grad = grad + dy[span(t), :].astype(f32)
        h2[span(t), :] = (value + mixed).astype(bf16)
        x2[span(t), :] = grad
        x[span(t), :] = grad.astype(bf16)
        return ()

    def middle_product(t):
        received[span(t), :] = nt(x[span(t), :], wo[...]).astype(bf16)
        for store in tile_stores(t):
            store.start()
        return ()

    staggered(tiles, middle_norm, middle_product)
    half = width // 2
    mine = pl.multiple_of(noisy * half, half)
    half_grads[0] = nn(o_t[pl.ds(half - mine, half), :], x[...]).astype(bf16)
    half_grads[1] = nn(o_t[pl.ds(mine, half), :], x[...]).astype(bf16)
    more = [copy(half_grads.at[0], g_send, sem_out.at[4]), copy(half_grads.at[1], g_keep, sem_out.at[5])]
    for store in more:
        store.start()
    stores += more
    for c in range(chunks - 2, chunks):
        stores += grad_stores(c, up_keep, down_keep)
    for t in range(tiles):
        stores += tile_stores(t)
    for store in stores:
        store.wait()


def layer(info, gain1, gain2, received, x, wqkv, tables, wo, dy, w1, w2):
    seq, width = x.shape
    hidden = w1.shape[1]
    tiles, pairs, chunks = seq // R, width // PW, hidden // FC
    anywhere = pl.BlockSpec(memory_space=pl.ANY)
    vmem = pltpu.VMEM
    dma = pltpu.SemaphoreType.DMA
    heads = (pairs, seq, PW)
    flat = (seq, width)
    outs = (
        [shape(heads, bf16)] * 5
        + [shape((width, seq), bf16), shape(flat, bf16), shape((pairs, seq // T, 2 * T), f32)]
        + [shape(flat, bf16), shape(flat, f32), shape(flat, bf16)]
        + [shape((hidden // 2, width), bf16)] * 4
        + [shape((width // 2, width), bf16)] * 2
        + [shape((8, width), f32)]
    )
    return pl.pallas_call(
        layer_kernel,
        in_specs=[SMEM, IN_VMEM, IN_VMEM] + [anywhere] * 9,
        out_specs=[anywhere] * 17 + [IN_VMEM],
        out_shape=outs,
        scratch_shapes=[vmem(flat, bf16)] * 2
        + [vmem(wqkv.shape, bf16), vmem((seq, PW), f32), vmem((seq, PW), f32)]
        + [vmem(heads, bf16)] * 3
        + [vmem((width, seq), bf16), vmem((width, width), bf16), vmem(flat, bf16)]
        + [vmem((chunks, width, FC), bf16), vmem((chunks, FC, width), bf16)]
        + [vmem(heads, bf16)] * 2
        + [vmem((PW, seq), bf16)] * 2
        + [vmem((AHEAD, seq + T, 2 * T), f32), vmem((2 * T, 2 * T), f32)]
        + [vmem(flat, bf16), vmem((width, seq), bf16)]
        + [vmem((pairs, seq // T, 2 * T), f32)]
        + [vmem(flat, f32), vmem(flat, bf16)]
        + [vmem(flat, f32)] * 2
        + [vmem((seq, FC), bf16)] * 2
        + [vmem((2, FC, width), bf16)] * 2
        + [vmem((2, width // 2, width), bf16)]
        + [dma((7,)), dma((chunks,)), dma((chunks,)), dma((10,)), dma((2,)), dma((2,)), dma((tiles, 3))],
        compiler_params=params(BIG),
        cost_estimate=LONG,
        name="layer",
    )(info, gain1, gain2, received, *pinned(x, wqkv, *tables, wo, dy, w1, w2))


def weigh_kernel(first, info, dq, keep, got, cosine, signed, h1t, wqkv, sums, dkv, g_send, g_keep, small):
    width, half = wqkv.shape[0], wqkv.shape[0] // 2
    mine = pl.multiple_of(info[0] * half, half)
    dk = keep[0].astype(f32) + got[0].astype(f32)
    dkv[0] = rotated(dk, cosine[...], signed[...], -1.0).astype(bf16)
    dkv[1] = (keep[1].astype(f32) + got[1].astype(f32)).astype(bf16)
    small[...] = sums[...]
    for out, start in ((g_send, half - mine), (g_keep, mine)):
        rows = pl.ds(start, half)
        terms = 0.0
        for i, part in enumerate((dq, dkv.at[0], dkv.at[1])):
            total = nn(h1t[rows, :], part[...])
            out[i] = total.astype(bf16)
            at = i * width + first * PW
            weighted = total * wqkv[rows, at : at + total.shape[1]].astype(f32)
            for c in range(0, total.shape[1], PW):
                terms = terms + weighted[:, c : c + PW]
        line = jnp.sum(terms.T, axis=0, keepdims=True)
        lanes = lax.broadcasted_iota(jnp.int32, (1, width), 1)
        inside = jnp.logical_and(lanes >= start, lanes < start + half)
        small[4:5, :] += jnp.where(inside, jnp.concatenate([line, line], axis=1), 0.0)
    small[5:6, :] = jnp.full((1, width), info[1].astype(f32))


def weigh(info, first, dq, keep, got, tables, h1t, wqkv, sums):
    seq, width = dq.shape
    tall = h1t.shape[0]
    return pl.pallas_call(
        functools.partial(weigh_kernel, first),
        in_specs=[SMEM] + [IN_VMEM] * 8,
        out_specs=[IN_VMEM] * 4,
        out_shape=[shape((2, seq, width), bf16)]
        + [shape((3, tall // 2, width), bf16)] * 2
        + [shape(sums.shape, f32)],
        compiler_params=params(24),
        cost_estimate=LONG,
        name="weigh",
    )(info, dq, keep, got, *tables, h1t, wqkv, sums)


def finish_kernel(parts, tiles, x, dx2, wqkv, gain_line, *refs):
    dx_any, dx, sem = refs[-3:]
    dqs, dkvs = refs[:parts], refs[parts : 2 * parts]
    gain = gain_line[...].reshape(1, x.shape[1])

    def store(t):
        rows = pl.ds(pl.multiple_of(t * R, R), R)
        return pltpu.make_async_copy(dx.at[rows, :], dx_any.at[rows, :], sem.at[t])

    def some_rows(t, carry):
        rows = pl.ds(pl.multiple_of(t * R, R), R)
        grads = [r[rows, :] for r in dqs] + [r[0, rows, :] for r in dkvs] + [r[1, rows, :] for r in dkvs]
        dh = nt(jnp.concatenate(grads, axis=1), wqkv[...])
        grad, _ = norm_back(x[rows, :].astype(f32), gain, dh)
        dx[rows, :] = (dx2[rows, :] + grad).astype(bf16)
        store(t).start()
        return carry

    lax.fori_loop(*tiles, some_rows, 0)
    for t in range(*tiles):
        store(t).wait()


def finish(tiles, x, dx2, dqs, dkvs, weight, gain, before):
    anywhere = pl.BlockSpec(memory_space=pl.ANY)
    ins = 4 + len(dqs) + len(dkvs)
    return pl.pallas_call(
        functools.partial(finish_kernel, len(dqs), tiles),
        in_specs=[IN_VMEM] * ins + [anywhere] * len(before),
        out_specs=anywhere,
        out_shape=shape(x.shape, bf16),
        scratch_shapes=[pltpu.VMEM(x.shape, bf16), pltpu.SemaphoreType.DMA((x.shape[0] // R,))],
        input_output_aliases={ins: 0} if before else {},
        compiler_params=params(24),
        cost_estimate=COST if before else LONG,
        name="finish",
    )(x, dx2, weight, gain, *dqs, *dkvs, *before)


def bit_orders(count, groups):
    bits = [1 << i for i in range(count.bit_length() - 1)]
    if groups == 2:
        return [bits, bits[1::-1] + bits[2:]]
    return [bits[g:-1] + bits[:g] + bits[-1:] for g in range(groups)]


def exchange(value, axis, bit):
    size = lax.axis_size(axis)
    return lax.ppermute(value, axis, [(i, i ^ bit) for i in range(size)])


def distance(order, place):
    out = 0
    for i, bit in enumerate(order):
        out = out + ((place >> (len(order) - 1 - i)) & 1) * bit
    return out


SUMS = 8


def halves(value):
    high = value.astype(bf16)
    return high, (value - high.astype(f32)).astype(bf16)


def put_sums(value, kept, block):
    high, low = halves(value)
    lines = kept.shape[0]
    block[:lines, :] = high
    block[lines : 2 * lines, :] = low
    kept[...] = high.astype(f32) + low.astype(f32)


def got_sums(block):
    lines = block.shape[0] // 2
    return block[:lines, :].astype(f32) + block[lines:, :].astype(f32)


def start_kernel(orders, sources, small, me, *refs):
    groups = len(orders)
    arrays = max(a for source in sources for a, _, _ in source) + 1
    ins, outs = refs[: 2 * arrays], refs[len(refs) - 2 * groups :]
    half = outs[0].shape[0]
    for g, order in enumerate(orders):
        for side in range(2):

            def one(r, carry, g=g, order=order, side=side):
                part = me[0] ^ distance(order, r + side * half)
                out = outs[2 * g + side]
                row = 0
                for a, where, unit in sources[g]:
                    kept, got = ins[2 * a : 2 * a + 2]
                    place = where(part)
                    size, wide = kept.shape[1], out.shape[-1]
                    lanes = slice(unit * wide, (unit + 1) * wide)
                    total = kept[place, :, lanes].astype(f32) + got[place, :, lanes].astype(f32)
                    if len(out.shape) == 3:
                        out[r, row : row + size, :] = total.astype(bf16)
                    else:
                        start = pl.multiple_of(r * outs[0].shape[1] + row, 8)
                        out[pl.ds(start, size), :] = total.astype(bf16)
                    row += size
                return carry

            lax.fori_loop(0, half, one, 0)
    if small:
        here, there, kept = refs[2 * arrays : 2 * arrays + 3]
        total = here[...] + there[...]
        if small == "rides":
            wide = kept.shape[1]
            total = jnp.concatenate([total[:, c : c + wide] for c in range(0, total.shape[1], wide)], axis=0)
            put_sums(total, kept, outs[1].at[pl.ds(half * outs[0].shape[1], 2 * kept.shape[0]), :])
        else:
            kept[...] = total


def travelling(count, rows, width, lines):
    return shape((count * rows + 2 * lines, width) if lines else (count, rows, width), bf16)


def start_sum(me, kept, got, sources, width, orders, small, rides):
    count = 1 << len(orders[0])
    half = count // 2
    rows = [sum(kept[a].shape[1] for a, _, _ in source) for source in sources]
    lines = small[0].size // width if rides else 0
    cols = width // 3
    args = [a for pair in zip(kept, got, strict=True) for a in pair]
    sums = []
    for g in range(len(orders)):
        sums += [shape((half, rows[g], width), bf16), travelling(half, rows[g], width, 0 if g else lines)]
    mode = "rides" if rides else "alone" if small else ""
    if small:
        specs = dict(
            in_specs=[SMEM] + [IN_VMEM] * (len(args) + 2),
            out_specs=[IN_VMEM] * (1 + len(sums)),
            out_shape=[shape((lines, width) if rides else small[0].shape, f32)] + sums,
        )
    else:
        block = lambda a: pl.BlockSpec((a.shape[0], a.shape[1], cols), lambda c: (0, 0, c))
        specs = dict(
            grid=(width // cols,),
            in_specs=[SMEM] + [block(a) for a in args],
            out_specs=[block(a) for a in sums],
            out_shape=sums,
        )
    outs = pl.pallas_call(
        functools.partial(start_kernel, orders, sources, mode),
        compiler_params=params(30),
        cost_estimate=COST,
        name="start_sum",
        **specs,
    )(me, *args, *small)
    small, outs = list(outs[: len(outs) - len(sums)]), outs[len(outs) - len(sums) :]
    return list(outs[0::2]), list(outs[1::2]), small


def step_kernel(groups, merge, mode, *refs):
    kept, got = refs[:groups], refs[groups : 2 * groups]
    outs = refs[2 * groups + (2 if mode == "alone" else 1 if mode else 0) :]
    count = kept[0].shape[0]
    half = count // 2
    row = 0
    for g in range(groups):
        keep, send = outs[:2] if merge else outs[2 * g : 2 * g + 2]
        size = kept[g].shape[1]
        for r in range(count):
            there = got[g][r] if len(got[g].shape) == 3 else got[g][r * size : (r + 1) * size]
            total = (kept[g][r].astype(f32) + there.astype(f32)).astype(bf16)
            if r < half:
                keep[r, row : row + size, :] = total
            elif len(send.shape) == 3:
                send[r - half, row : row + size, :] = total
            else:
                start = (r - half) * keep.shape[1] + row
                send[start : start + size, :] = total
        row += size if merge else 0
    if mode == "rides":
        total = refs[2 * groups][...] + got_sums(got[0][count * kept[0].shape[1] :])
        put_sums(total, outs[-1], outs[1].at[pl.ds(half * outs[0].shape[1], 2 * total.shape[0]), :])
    elif mode:
        outs[-1][...] = refs[2 * groups][...] + refs[2 * groups + 1][...]


def step_sum(kept, got, small, merge, rides):
    groups = len(kept)
    half = kept[0].shape[0] // 2
    rows = [a.shape[1] for a in kept]
    width = kept[0].shape[2]
    args = [*kept, *got, *small]
    sums = []
    for g, r in enumerate([sum(rows)] if merge else rows):
        sums += [shape((half, r, width), bf16), travelling(half, r, width, 0 if g or not rides else small[0].shape[0])]
    outs = pl.pallas_call(
        functools.partial(step_kernel, groups, merge, "rides" if rides else "alone" if small else ""),
        in_specs=[IN_VMEM] * len(args),
        out_specs=[IN_VMEM] * (len(sums) + len(small[:1])),
        out_shape=sums + [shape(a.shape, f32) for a in small[:1]],
        compiler_params=params(16),
        cost_estimate=COST if small or half == 1 else LONG,
        name="step_sum",
    )(*args)
    return list(outs[0 : len(sums) : 2]), list(outs[1 : len(sums) : 2]), list(outs[len(sums) :])


def feed_end_kernel(kept, got, down, up, out):
    total = kept[0].astype(f32) + got[0].astype(f32)
    tall, few = down.shape[0] // GROUPS, out.shape[0] // GROUPS
    ups = []
    for g in range(GROUPS):
        row = g * (2 * tall + few)
        down[g * tall : (g + 1) * tall, :] = total[row : row + tall]
        ups.append(total[row + tall : row + 2 * tall])
        out[g * few : (g + 1) * few, :] = total[row + 2 * tall : row + 2 * tall + few]
    up[...] = jnp.concatenate(ups, axis=0).T


def feed_end(kept, got, tall, few):
    width = kept.shape[2]
    return pl.pallas_call(
        feed_end_kernel,
        in_specs=[IN_VMEM] * 2,
        out_specs=[IN_VMEM] * 3,
        out_shape=[shape((tall, width), f32), shape((width, tall), f32), shape((few, width), f32)],
        compiler_params=params(16),
        cost_estimate=COST,
        name="feed_end",
    )(kept, got)


def qkv_end_kernel(places, rides, gain_line, kept, got, *refs):
    out, gain1, gain2, rms = refs[-4:]
    tall = out.shape[0]
    width = gain1.shape[0]
    cols = kept.shape[2]
    there = got[: kept.shape[1]] if rides else got[0]
    total = kept[0].astype(f32) + there.astype(f32)
    for i, at in enumerate(places):
        out[:, at : at + cols] = total[i * tall : (i + 1) * tall]
    if rides:
        sums = refs[0][...] + got_sums(got[kept.shape[1] :])
        sums = jnp.concatenate([sums[r : r + SUMS] for r in range(0, sums.shape[0], SUMS)], axis=1)
    else:
        sums = refs[0][...] + refs[1][...]
    gain2[...] = sums[3:4, :].reshape(width)
    gain1[...] = (sums[4:5, :] / gain_line[...].reshape(1, width)).reshape(width)
    count = jnp.max(sums[5:6, :], axis=1, keepdims=True) * width
    rms[...] = jnp.broadcast_to(jnp.sqrt(jnp.sum(sums, axis=1, keepdims=True) / count), rms.shape)


def qkv_end(places, gain, kept, got, small, tall, wide, rides):
    return pl.pallas_call(
        functools.partial(qkv_end_kernel, places, rides),
        in_specs=[IN_VMEM] * (3 + len(small)),
        out_specs=[IN_VMEM] * 4,
        out_shape=[shape((tall, wide), f32), shape(gain.shape, f32), shape(gain.shape, f32), shape((SUMS, 128), f32)],
        compiler_params=params(16),
        cost_estimate=COST,
        name="qkv_end",
    )(gain, kept, got, *small)


def after(value, *earlier):
    return lax.optimization_barrier((value, earlier))[0]


def sum_parts(me, kept, got, sources, width, small, rides):
    orders = bit_orders(lax.axis_size("batch"), len(sources))
    steps = len(orders[0])
    common = min(i for i in range(steps + 1) if all(order[i:] == orders[0][i:] for order in orders))
    keep, send, small = start_sum(me, kept, got, sources, width, orders, small, rides)
    for i in range(steps):
        got = [exchange(s, "batch", order[i]) for s, order in zip(send, orders[: len(send)], strict=True)]
        if small and not rides:
            small = [small[0], exchange(small[0], "batch", orders[0][i])]
        earlier = yield send[0], got
        if i == steps - 1:
            break
        if earlier is not None:
            keep = after(keep, earlier)
        keep, send, small = step_sum(keep, got, small, i + 1 == common, rides)
    yield keep[0], got[0], small


def on_device(
    inputs, lengths, cotangent, qkv_weight, out_weight, up_weight, down_weight, attn_gain, mlp_gain
):
    seq, width = inputs.shape[2:]
    x = inputs[0, 0]
    dy = cotangent[0, 0]
    count = lax.axis_size("batch")
    stream = lax.axis_index("stream").astype(jnp.int32)
    me = lax.axis_index("batch").astype(jnp.int32).reshape(1)
    info = jnp.stack([stream, lengths[0]])
    cosine, sine = rotary_tables(seq)
    tables = (
        jnp.asarray(np.concatenate([cosine] * 4, axis=1)),
        jnp.asarray(np.concatenate([-sine, sine] * 2, axis=1)),
    )
    tables_t = (jnp.asarray(cosine.T), jnp.asarray(sine.T))

    received = lax.ppermute(x, "stream", [(0, 1)])
    (
        q, ko, vo, kc, vc, h1t, o, lse, outputs, dx2, do,
        up_send, up_keep, down_send, down_keep, out_send, out_keep, sums,
    ) = layer(
        info, attn_gain, mlp_gain, received, x, qkv_weight, tables, out_weight, dy, up_weight, down_weight
    )
    down_got, up_got, out_got = (exchange(a, "stream", 1) for a in (down_send, up_send, out_send))

    def by_rows(array):
        return array.reshape(count * GROUPS, array.shape[0] // (count * GROUPS), width)

    heads = (q, ko, vo, kc, vc, o)
    pairs = width // PW // 3
    dq1, keep1, send1 = attend_back(info, 0, pairs, *heads, do, lse, *tables_t)
    got1 = lax.ppermute(send1, "stream", [(1, 0)])
    early = sum_parts(
        me,
        [by_rows(after(a, dq1)) for a in (down_keep, up_keep, out_keep)],
        [by_rows(a) for a in (down_got, up_got, out_got)],
        [[(a, lambda part, g=g: part * GROUPS + g, 0) for a in range(3)] for g in range(GROUPS)],
        width,
        [],
        False,
    )
    token = next(early)[0]
    dq2, keep2, send2 = attend_back(info, pairs, 2 * pairs, *heads, after(do, token), lse, *tables_t)
    got2 = lax.ppermute(send2, "stream", [(1, 0)])
    token = early.send(dq2)[0]
    dkv1, qkv_send1, qkv_keep1, small = weigh(info, 0, dq1, after(keep1, token), got1, tables, h1t, qkv_weight, sums)
    qkv_got1 = exchange(qkv_send1, "stream", 1)
    dkv2, qkv_send2, qkv_keep2, small = weigh(info, pairs, dq2, keep2, got2, tables, h1t, qkv_weight, small)
    qkv_got2 = exchange(qkv_send2, "stream", 1)
    small_got = exchange(small, "stream", 1)
    token = early.send(dkv2)[0]

    tall = width // (2 * count)
    split = lambda a: a.reshape(3 * count, tall, a.shape[2])
    rides = tall % 8 == 0
    runs = [(0, i, 0) for i in range(3)] + [(1, i, c) for i in range(3) for c in range(2)]
    groups = runs[:4], runs[4:]
    late = sum_parts(
        me,
        [split(after(a, token)) for a in (qkv_keep1, qkv_keep2)],
        [split(a) for a in (qkv_got1, qkv_got2)],
        [[(a, lambda part, i=i: i * count + part, c) for a, i, c in group] for group in groups],
        pairs * PW,
        [small, small_got],
        rides,
    )
    token = next(late)[0]
    ends = [dq1, dq2], [dkv1, dkv2], qkv_weight, attn_gain
    tiles = seq // R
    dx = finish((0, tiles // 2), after(x, token), dx2, *ends, [])
    early_out = early.send(dx)
    dx = finish((tiles // 2, tiles), x, after(dx2, early_out[0]), *ends, [dx])
    late.send(dx)
    late_out = late.send(early_out[1])
    while len(late_out) == 2:
        late_out = late.send(None)
    while len(early_out) == 2:
        early_out = early.send(None)
    up_cols = down_keep.shape[0] // count
    down_grad, up_grad, out_grad = feed_end(*early_out[:2], up_cols, tall)
    places = [i * width + (a + c) * pairs * PW for a, i, c in runs]
    qkv_grad, gain1_grad, gain2_grad, rms = qkv_end(places, attn_gain, *late_out, tall, 3 * width, rides)
    return (
        outputs[None, None],
        dx[None, None],
        qkv_grad,
        out_grad,
        up_grad,
        down_grad,
        gain1_grad,
        gain2_grad,
        rms[:3, 0],
    )


def solution(mesh):
    rows = P("stream", "batch", None, None)
    both = ("stream", "batch")
    return jax.shard_map(
        on_device,
        mesh=mesh,
        in_specs=(rows, P("batch"), rows, P(), P(), P(), P(), P(), P()),
        out_specs=(rows, rows, P(both, None), P(both, None), P(None, both), P(both, None), P(), P(), P()),
        check_vma=False,
    )
```

```python
import functools

import jax
import jax.numpy as jnp
import numpy as np
from jax import lax
from jax.experimental import pallas as pl
from jax.experimental.pallas import tpu as pltpu
from jax.sharding import PartitionSpec as P

f32 = jnp.float32
bf16 = jnp.bfloat16

HD = 64
BLK = 16
EPS = 1e-06
NEG = -1e30
PW = 2 * HD
T = 128
R = 256
AHEAD = 2
FC = 768
SCALE = HD**-0.5
BIG = 61
GROUPS = 3

COST = pl.CostEstimate(flops=1 << 20, bytes_accessed=1 << 16, transcendentals=0)
LONG = pl.CostEstimate(flops=1 << 35, bytes_accessed=1 << 26, transcendentals=0)

SMEM = pl.BlockSpec(memory_space=pltpu.SMEM)
IN_VMEM = pl.BlockSpec(memory_space=pltpu.VMEM)


def params(mib):
    return pltpu.CompilerParams(vmem_limit_bytes=mib << 20)


def shape(dims, dtype):
    return jax.ShapeDtypeStruct(dims, dtype)


def pinned(*arrays):
    return [pltpu.with_memory_space_constraint(a, pltpu.HBM) for a in arrays]


def nn(a, b):
    return jnp.dot(a, b, preferred_element_type=f32)


def nt(a, b):
    return lax.dot_general(a, b, (((1,), (1,)), ((), ())), preferred_element_type=f32)


def tn(a, b):
    return lax.dot_general(a, b, (((0,), (0,)), ((), ())), preferred_element_type=f32)


def whole(dims):
    return pl.BlockSpec(dims, lambda *_: (0,) * len(dims), pipeline_mode=pl.Buffered(1))


def inv_rms(v):
    return lax.rsqrt(jnp.mean(v * v, axis=-1, keepdims=True) + EPS)


def norm_back(v, gain, grad):
    r = inv_rms(v)
    unit = v * r
    scaled = grad * gain
    inner = jnp.mean(scaled * unit, axis=-1, keepdims=True)
    return r * (scaled - unit * inner), grad * unit


def rotary_tables(length):
    half = HD // 2
    freqs = np.exp(-np.log(10000.0) * np.arange(half) / half).astype(np.float32)
    angles = (np.arange(length, dtype=np.float32)[:, None] * freqs[None, :]).astype(np.float64)
    return np.cos(angles).astype(np.float32), np.sin(angles).astype(np.float32)


def rotated(v, cosine, signed, sign):
    first = lax.broadcasted_iota(jnp.int32, (1, PW), 1) % HD < HD // 2
    outs = []
    for c in range(0, v.shape[1], PW):
        part = v[:, c : c + PW]
        partner = jnp.where(first, pltpu.roll(part, PW - HD // 2, 1), pltpu.roll(part, HD // 2, 1))
        outs.append(part * cosine + partner * (signed * sign))
    return outs[0] if len(outs) == 1 else jnp.concatenate(outs, axis=1)


def staggered(count, *stages):
    state = [()] * count
    for step in range(count + len(stages) - 1):
        for k, stage in enumerate(stages):
            if 0 <= step - k < count:
                state[step - k] = stage(step - k, *state[step - k])


def token_weight(start, length, rows):
    return lax.broadcasted_iota(jnp.int32, (rows, 1), 0) + start < length


def row_sum(v):
    return jnp.sum(v, axis=0, keepdims=True)


def by_pairs(ref, rows, value):
    for p in range(ref.shape[0]):
        ref[p, rows, :] = value[:, p * PW : (p + 1) * PW].astype(ref.dtype)


def stacked(tile, low):
    zero = jnp.zeros_like(tile)
    return jnp.concatenate([jnp.where(low, tile, zero), jnp.where(low, zero, tile)], axis=0)


def unstacked(tile_t):
    half = lax.broadcasted_iota(jnp.int32, (PW, 1), 0) < HD
    return jnp.where(half, tile_t[:, :T], tile_t[:, T:])


def chunks_of(i):
    out, j = [], 0
    while j < i:
        n = 2 if i - j >= 2 else 1
        out.append((j * T, n * T))
        j += n
    return out


def edge_bias(ref, noisy):
    row = lax.broadcasted_iota(jnp.int32, (T, 2 * T), 0) // BLK
    col = (lax.broadcasted_iota(jnp.int32, (T, 2 * T), 1) % T) // BLK
    own = jnp.logical_or(row == col, jnp.logical_and(row < col, noisy == 0))
    other = jnp.logical_and(row < col, noisy == 1)
    ref[:T, :] = jnp.where(own, 0.0, NEG)
    ref[T:, :] = jnp.where(other, 0.0, NEG)


def masked(s, start, length):
    pos = lax.broadcasted_iota(jnp.int32, s.shape, 0) + start
    return jnp.where(pos < length, s, NEG)


def over_rows(op, v):
    return op(v.reshape(v.shape[0] // 8, 8, v.shape[1]), axis=0)


def attend_pair(length, q, ko, vo, kc, vc, store, lse, vo_t, vc_t, scores, bias):
    seq = q.shape[0]
    low = lax.broadcasted_iota(jnp.int32, (1, PW), 1) < HD
    vo_t[...] = vo[...].T
    vc_t[...] = vc[...].T

    def score(i):
        at = pl.ds(i * T, T)
        q2 = stacked(q[at, :] * bf16(SCALE), low)
        buf = scores.at[i % AHEAD]
        edge = nt(jnp.concatenate([ko[at, :], kc[at, :]], 0), q2) + bias[...]
        own = masked(edge[:T], i * T, length)
        other = masked(edge[T:], i * T, length)
        buf[pl.ds(0, T), :] = own
        buf[pl.ds(T, T), :] = other
        top = over_rows(jnp.max, jnp.maximum(own, other))
        for start, size in chunks_of(i):
            s = masked(nt(kc[pl.ds(start, size), :], q2), start, length)
            buf[pl.ds(2 * T + start, size), :] = s
            top = jnp.maximum(top, over_rows(jnp.max, s))
        return jnp.max(top, axis=0, keepdims=True)

    def mix(i, top):
        at = pl.ds(i * T, T)
        buf = scores.at[i % AHEAD]
        p = jnp.exp(buf[pl.ds(0, 2 * T), :] - top)
        total = over_rows(jnp.sum, p)
        acc = nn(jnp.concatenate([vo_t[:, at], vc_t[:, at]], 1), p.astype(bf16))
        for start, size in chunks_of(i):
            p = jnp.exp(buf[pl.ds(2 * T + start, size), :] - top)
            total = total + over_rows(jnp.sum, p)
            acc = acc + nn(vc_t[:, pl.ds(start, size)], p.astype(bf16))
        total = row_sum(total)
        lse[0, pl.ds(i, 1), :] = top + jnp.log(total)
        store(at, unstacked(acc * (1.0 / total)))

    tops = {}
    for i in range(seq // T + AHEAD - 1):
        if i < seq // T:
            tops[i] = score(i)
        if i >= AHEAD - 1:
            mix(i - AHEAD + 1, tops.pop(i - AHEAD + 1))


def turned_back(v, cosine, sine):
    quarter = HD // 2
    a, b, c, d = (v[i * quarter : (i + 1) * quarter] for i in range(4))
    return jnp.concatenate(
        [a * cosine + b * sine, b * cosine - a * sine, c * cosine + d * sine, d * cosine - c * sine]
    )


def attend_back_kernel(
    info, q, ko, vo, kc, vc, o, do, lse, cosine, sine, dq, keep, send, ko_t, kc_t, dko, dvo, dkc, dvc, bias
):
    noisy, length = info[0], info[1]
    q, ko, vo, kc, vc = (ref.at[0] for ref in (q, ko, vo, kc, vc))
    seq = q.shape[0]
    low = lax.broadcasted_iota(jnp.int32, (1, PW), 1) < HD

    @pl.when(pl.program_id(0) == 0)
    def _():
        edge_bias(bias, noisy)

    ko_t[...] = ko[...].T
    kc_t[...] = kc[...].T

    def tile(i):
        at = pl.ds(i * T, T)
        prod = (do[at, :].astype(f32) * o[at, :].astype(f32)).T
        delta = jnp.concatenate([row_sum(prod[:HD]), row_sum(prod[HD:])], 1)
        q2 = stacked(q[at, :] * bf16(SCALE), low)
        return q2, stacked(do[at, :], low), lse[0, pl.ds(i, 1), :], delta

    def products(i, start, size, q2, do2):
        if start is None:
            at = pl.ds(i * T, T)
            s = nt(jnp.concatenate([ko[at, :], kc[at, :]], 0), q2) + bias[...]
            s = jnp.concatenate([masked(s[:T], i * T, length), masked(s[T:], i * T, length)], 0)
            return s, nt(jnp.concatenate([vo[at, :], vc[at, :]], 0), do2)
        rows = pl.ds(start, size)
        return masked(nt(kc[rows, :], q2), start, length), nt(vc[rows, :], do2)

    def gather(i, start, size, q2, do2, p, ds, dq_t):
        at = pl.ds(i * T, T)
        dv, dk = nn(p, do2), nn(ds, q2)
        if start is None:
            dvo[at, :] = dv[:T]
            dko[at, :] = dk[:T]
            dvc[at, :] = dv[T:]
            dkc[at, :] = dk[T:]
            return nn(jnp.concatenate([ko_t[:, at], kc_t[:, at]], 1), ds)
        rows = pl.ds(start, size)
        dvc[rows, :] += dv
        dkc[rows, :] += dk
        return dq_t + nn(kc_t[:, rows], ds)

    work = [(i, *c) for i in range(seq // T) for c in [(None, None)] + chunks_of(i)]
    tiles, made, weighed, dq_t = {}, {}, {}, None
    for n in range(len(work) + 2):
        if n < len(work):
            i = work[n][0]
            if i not in tiles:
                tiles[i] = tile(i)
            made[n] = products(*work[n], *tiles[i][:2])
        if 0 <= n - 1 < len(work):
            _, _, norm, delta = tiles[work[n - 1][0]]
            s, dp = made.pop(n - 1)
            p = jnp.exp(s - norm)
            weighed[n - 1] = p.astype(bf16), (p * (dp - delta)).astype(bf16)
        if n >= 2:
            i, start, size = work[n - 2]
            dq_t = gather(i, start, size, *tiles[i][:2], *weighed.pop(n - 2), dq_t)
            if n == len(work) + 1 or work[n - 1][0] != i:
                at = pl.ds(i * T, T)
                out = turned_back(unstacked(dq_t), cosine[:, at], sine[:, at]) * SCALE
                dq[at, :] = out.T.astype(bf16)
    clean = (1 - noisy).astype(f32)
    for at, own, other in ((0, dko, dkc), (1, dvo, dvc)):
        keep[at] = (own[...] + clean * other[...]).astype(bf16)
        send[at] = other[...].astype(bf16)


def attend_back(info, first, pairs, q, ko, vo, kc, vc, o, do, lse, cosine, sine):
    seq = q.shape[1]
    width = pairs * PW
    heads = pl.BlockSpec((1, seq, PW), lambda h: (first + h, 0, 0))
    source = pl.BlockSpec((seq, PW), lambda h: (0, first + h))
    both = pl.BlockSpec((2, seq, PW), lambda h: (0, 0, h))
    lines = pl.BlockSpec((1, seq // T, 2 * T), lambda h: (first + h, 0, 0))
    table = whole((HD // 2, seq))
    return pl.pallas_call(
        attend_back_kernel,
        grid=(pairs,),
        in_specs=[SMEM] + [heads] * 5 + [source] * 2 + [lines, table, table],
        out_specs=[pl.BlockSpec((seq, PW), lambda h: (0, h)), both, both],
        out_shape=[shape((seq, width), bf16)] + [shape((2, seq, width), bf16)] * 2,
        scratch_shapes=[pltpu.VMEM((PW, seq), bf16)] * 2
        + [pltpu.VMEM((seq, PW), f32)] * 4
        + [pltpu.VMEM((2 * T, 2 * T), f32)],
        compiler_params=params(24),
        cost_estimate=LONG,
        name="attend_back",
    )(info, *pinned(q, ko, vo, kc, vc, o, do), lse, cosine, sine)


C0 = 0.7978845608028654
C1 = C0 * 0.044715


def layer_kernel(
    info, gain1_line, gain2_line, cosine_t, sine_t, received, x_any, wqkv_any, wo_any, dy_any,
    w1_any, w2_any,
    q_out, ko_out, vo_out, kc_out, vc_out, h1t_out, o_out, lse_out, out_any, dx2_any, do_any,
    up_send, up_keep, down_send, down_keep, g_send, g_keep, cosine_out, signed_out, sums,
    x, wqkv, cosine, signed, q, ko, vo, h1t, wo, dy, w1, w2,
    kc, vc, vo_t, vc_t, scores, bias, o, o_t, lse, x2, h2, m, dh, act, du, up_grad, down_grad, half_grads,
    sem_in, sem_1, sem_2, sem_out, sem_up, sem_down, sem_tile,
):
    noisy, length = info[0], info[1]
    seq, width = x.shape
    chunks, pairs, tiles = w1.shape[0], kc.shape[0], seq // R
    copy = pltpu.make_async_copy
    gain1, gain2 = gain1_line[...].reshape(1, width), gain2_line[...].reshape(1, width)

    def weights(c):
        place = lax.rem(c + (chunks // 2) * (1 - noisy), chunks) * FC
        place = pl.multiple_of(place, FC)
        return (
            copy(w1_any.at[:, pl.ds(place, FC)], w1.at[c], sem_1.at[c]),
            copy(w2_any.at[pl.ds(place, FC), :], w2.at[c], sem_2.at[c]),
        )

    sources = (
        (x_any, x),
        (wqkv_any, wqkv),
        (wo_any, wo),
        (dy_any, dy),
    )
    loads = [copy(a, b, sem_in.at[i]) for i, (a, b) in enumerate(sources)]
    for load in loads[:2]:
        load.start()
    sums[...] = jnp.zeros_like(sums)
    edge_bias(bias, noisy)
    for t in range(0, seq, R):
        c, d = cosine_t[:, t : t + R].T, sine_t[:, t : t + R].T
        cosine[pl.ds(t, R), :] = jnp.concatenate([c, c, c, c], axis=1)
        signed[pl.ds(t, R), :] = jnp.concatenate([-d, d, -d, d], axis=1)
    tables_out = [copy(cosine, cosine_out, sem_out.at[10]), copy(signed, signed_out, sem_out.at[11])]
    span = lambda t: pl.ds(t * R, R)

    loads[0].wait()

    def own_norm(t):
        value = x[span(t), :].astype(f32)
        h1 = (value * inv_rms(value) * gain1).astype(bf16)
        h2[span(t), :] = h1
        h1t[:, span(t)] = h1.T
        weight = token_weight(t * R, length, R)
        sums[0:1, :] += row_sum(jnp.where(weight, value * value, 0.0))
        return ()

    for t in range(tiles):
        own_norm(t)
    loads[1].wait()
    for load in loads[2:]:
        load.start()

    def own_product(t):
        return tuple(nn(h2[span(t), :], wqkv[:, i * width : (i + 1) * width]) for i in range(3))

    def own_turn(t, a, b, c):
        tables = (cosine[span(t), :], signed[span(t), :], 1.0)
        by_pairs(q, span(t), rotated(a, *tables))
        by_pairs(ko, span(t), rotated(b, *tables))
        by_pairs(vo, span(t), c)
        return ()

    def clean_norm(t):
        value = jnp.where(noisy == 1, received[span(t), :].astype(f32), x[span(t), :].astype(f32))
        o[span(t), :] = (value * inv_rms(value) * gain1).astype(bf16)
        return ()

    def clean_product(t):
        return tuple(nn(o[span(t), :], wqkv[:, i * width : (i + 1) * width]) for i in (1, 2))

    def clean_turn(t, a, b):
        by_pairs(kc, span(t), rotated(a, cosine[span(t), :], signed[span(t), :], 1.0))
        by_pairs(vc, span(t), b)
        return ()

    staggered(tiles, own_product, own_turn)
    stores = [
        copy(a, b, sem_out.at[6 + i])
        for i, (a, b) in enumerate(((q, q_out), (ko, ko_out), (vo, vo_out), (h1t, h1t_out)))
    ]
    stores += tables_out
    for store in stores:
        store.start()
    staggered(tiles, clean_norm, clean_product, clean_turn)
    more = [copy(kc, kc_out, sem_out.at[0]), copy(vc, vc_out, sem_out.at[1])]
    for store in more:
        store.start()
    stores += more

    for c in range(chunks):
        for load in weights(c):
            load.start()

    def one_pair(p, carry):
        lanes = pl.ds(pl.multiple_of(p * PW, PW), PW)

        def keep(at, tile_t):
            o_t[lanes, at] = tile_t.astype(bf16)
            o[at, lanes] = tile_t.T.astype(bf16)

        heads = (ref.at[p] for ref in (q, ko, vo, kc, vc))
        attend_pair(length, *heads, keep, lse.at[pl.ds(p, 1)], vo_t, vc_t, scores, bias)
        return carry

    lax.fori_loop(0, pairs, one_pair, 0)
    mixed_out = copy(o, o_out, sem_out.at[2])
    mixed_out.start()
    stores += [copy(lse, lse_out, sem_out.at[3])]
    stores[-1].start()

    for load in loads[2:]:
        load.wait()

    def join_product(t):
        return (nn(o[span(t), :], wo[...]),)

    def join_norm(t, branch):
        value = x[span(t), :].astype(f32) + branch
        x2[span(t), :] = value
        h2[span(t), :] = (value * inv_rms(value) * gain2).astype(bf16)
        m[span(t), :] = jnp.zeros_like(value)
        dh[span(t), :] = jnp.zeros_like(value)
        weight = token_weight(t * R, length, R)
        sums[1:2, :] += row_sum(jnp.where(weight, branch * branch, 0.0))
        return ()

    staggered(tiles, join_product, join_norm)

    def grad_stores(c, up, down):
        slot = lax.rem(c, 2)
        rows = pl.ds(pl.multiple_of(lax.rem(c, chunks // 2) * FC, FC), FC)
        return (
            copy(up_grad.at[slot], up.at[rows, :], sem_up.at[slot]),
            copy(down_grad.at[slot], down.at[rows, :], sem_down.at[slot]),
        )

    def one_chunk(c, carry):
        for load in weights(c):
            load.wait()
        up, down = w1.at[c], w2.at[c]
        made = {}
        for t in range(-R, seq, R):
            if t + R < seq:
                rows = pl.ds(t + R, R)
                made[t + R] = nn(h2[rows, :], up[...]), nt(dy[rows, :], down[...])
            if t < 0:
                continue
            rows = pl.ds(t, R)
            u, da = made.pop(t)
            sq = u * u
            half = 0.5 * jnp.tanh(u * (C0 + C1 * sq)) + 0.5
            low = (u * half).astype(bf16)
            slope = half + u * (2.0 * half * (1.0 - half)) * (C0 + 3.0 * C1 * sq)
            back = (da * slope).astype(bf16)
            act[rows, :] = low
            du[rows, :] = back
            m[rows, :] += nn(low, down[...])
            dh[rows, :] += nt(back, up[...])

        @pl.when(c >= 2)
        def _():
            for store in grad_stores(c, up_send, down_send):
                store.wait()

        slot = lax.rem(c, 2)
        down_grad[slot] = tn(act[...], dy[...]).astype(bf16)
        up_grad[slot] = tn(du[...], h2[...]).astype(bf16)

        @pl.when(c < chunks // 2)
        def _():
            for store in grad_stores(c, up_send, down_send):
                store.start()

        @pl.when(c >= chunks // 2)
        def _():
            for store in grad_stores(c, up_keep, down_keep):
                store.start()

        return carry

    lax.fori_loop(0, chunks, one_chunk, 0)

    mixed_out.wait()

    def tile_stores(t):
        return (
            copy(h2.at[span(t), :], out_any.at[span(t), :], sem_tile.at[t, 0]),
            copy(x2.at[span(t), :], dx2_any.at[span(t), :], sem_tile.at[t, 1]),
            copy(o.at[span(t), :], do_any.at[span(t), :], sem_tile.at[t, 2]),
        )

    def middle_norm(t):
        value = x2[span(t), :]
        mixed = m[span(t), :]
        weight = token_weight(t * R, length, R)
        sums[2:3, :] += row_sum(jnp.where(weight, mixed * mixed, 0.0))
        grad, gain_terms = norm_back(value, gain2, dh[span(t), :])
        sums[3:4, :] += row_sum(gain_terms)
        grad = grad + dy[span(t), :].astype(f32)
        h2[span(t), :] = (value + mixed).astype(bf16)
        x2[span(t), :] = grad
        x[span(t), :] = grad.astype(bf16)
        return ()

    def middle_product(t):
        o[span(t), :] = nt(x[span(t), :], wo[...]).astype(bf16)
        for store in tile_stores(t):
            store.start()
        return ()

    staggered(tiles, middle_norm, middle_product)
    half = width // 2
    mine = pl.multiple_of(noisy * half, half)
    half_grads[0] = nn(o_t[pl.ds(half - mine, half), :], x[...]).astype(bf16)
    half_grads[1] = nn(o_t[pl.ds(mine, half), :], x[...]).astype(bf16)
    more = [copy(half_grads.at[0], g_send, sem_out.at[4]), copy(half_grads.at[1], g_keep, sem_out.at[5])]
    for store in more:
        store.start()
    stores += more
    for c in range(chunks - 2, chunks):
        stores += grad_stores(c, up_keep, down_keep)
    for t in range(tiles):
        stores += tile_stores(t)
    for store in stores:
        store.wait()


def layer(info, gain1, gain2, cosine_t, sine_t, received, x, wqkv, wo, dy, w1, w2):
    seq, width = x.shape
    hidden = w1.shape[1]
    tiles, pairs, chunks = seq // R, width // PW, hidden // FC
    anywhere = pl.BlockSpec(memory_space=pl.ANY)
    vmem = pltpu.VMEM
    dma = pltpu.SemaphoreType.DMA
    heads = (pairs, seq, PW)
    flat = (seq, width)
    outs = (
        [shape(heads, bf16)] * 5
        + [shape((width, seq), bf16), shape(flat, bf16), shape((pairs, seq // T, 2 * T), f32)]
        + [shape(flat, bf16), shape(flat, f32), shape(flat, bf16)]
        + [shape((hidden // 2, width), bf16)] * 4
        + [shape((width // 2, width), bf16)] * 2
        + [shape((seq, PW), f32)] * 2
        + [shape((8, width), f32)]
    )
    return pl.pallas_call(
        layer_kernel,
        in_specs=[SMEM] + [IN_VMEM] * 5 + [anywhere] * 6,
        out_specs=[anywhere] * 19 + [IN_VMEM],
        out_shape=outs,
        scratch_shapes=[vmem(flat, bf16)]
        + [vmem(wqkv.shape, bf16), vmem((seq, PW), f32), vmem((seq, PW), f32)]
        + [vmem(heads, bf16)] * 3
        + [vmem((width, seq), bf16), vmem((width, width), bf16), vmem(flat, bf16)]
        + [vmem((chunks, width, FC), bf16), vmem((chunks, FC, width), bf16)]
        + [vmem(heads, bf16)] * 2
        + [vmem((PW, seq), bf16)] * 2
        + [vmem((AHEAD, seq + T, 2 * T), f32), vmem((2 * T, 2 * T), f32)]
        + [vmem(flat, bf16), vmem((width, seq), bf16)]
        + [vmem((pairs, seq // T, 2 * T), f32)]
        + [vmem(flat, f32), vmem(flat, bf16)]
        + [vmem(flat, f32)] * 2
        + [vmem((seq, FC), bf16)] * 2
        + [vmem((2, FC, width), bf16)] * 2
        + [vmem((2, width // 2, width), bf16)]
        + [dma((4,)), dma((chunks,)), dma((chunks,)), dma((12,)), dma((2,)), dma((2,)), dma((tiles, 3))],
        compiler_params=params(BIG),
        cost_estimate=LONG,
        name="layer",
    )(info, gain1, gain2, cosine_t, sine_t, received, *pinned(x, wqkv, wo, dy, w1, w2))


def weigh_kernel(first, info, dq, keep, got, cosine, signed, h1t, wqkv, sums, dkv, g_send, g_keep, small):
    width, half = wqkv.shape[0], wqkv.shape[0] // 2
    mine = pl.multiple_of(info[0] * half, half)
    dk = keep[0].astype(f32) + got[0].astype(f32)
    dkv[0] = rotated(dk, cosine[...], signed[...], -1.0).astype(bf16)
    dkv[1] = (keep[1].astype(f32) + got[1].astype(f32)).astype(bf16)
    small[...] = sums[...]
    for out, start in ((g_send, half - mine), (g_keep, mine)):
        rows = pl.ds(start, half)
        terms = 0.0
        for i, part in enumerate((dq, dkv.at[0], dkv.at[1])):
            total = nn(h1t[rows, :], part[...])
            out[i] = total.astype(bf16)
            at = i * width + first * PW
            weighted = total * wqkv[rows, at : at + total.shape[1]].astype(f32)
            for c in range(0, total.shape[1], PW):
                terms = terms + weighted[:, c : c + PW]
        line = jnp.sum(terms.T, axis=0, keepdims=True)
        lanes = lax.broadcasted_iota(jnp.int32, (1, width), 1)
        inside = jnp.logical_and(lanes >= start, lanes < start + half)
        small[4:5, :] += jnp.where(inside, jnp.concatenate([line, line], axis=1), 0.0)
    small[5:6, :] = jnp.full((1, width), info[1].astype(f32))


def weigh(info, first, dq, keep, got, tables, h1t, wqkv, sums):
    seq, width = dq.shape
    tall = h1t.shape[0]
    return pl.pallas_call(
        functools.partial(weigh_kernel, first),
        in_specs=[SMEM] + [IN_VMEM] * 8,
        out_specs=[IN_VMEM] * 4,
        out_shape=[shape((2, seq, width), bf16)]
        + [shape((3, tall // 2, width), bf16)] * 2
        + [shape(sums.shape, f32)],
        compiler_params=params(24),
        cost_estimate=LONG,
        name="weigh",
    )(info, dq, keep, got, *tables, h1t, wqkv, sums)


def finish_kernel(parts, tiles, x, dx2, wqkv, gain_line, *refs):
    dx_any, dx, sem = refs[-3:]
    dqs, dkvs = refs[:parts], refs[parts : 2 * parts]
    gain = gain_line[...].reshape(1, x.shape[1])

    def store(t):
        rows = pl.ds(pl.multiple_of(t * R, R), R)
        return pltpu.make_async_copy(dx.at[rows, :], dx_any.at[rows, :], sem.at[t])

    def some_rows(t, carry):
        rows = pl.ds(pl.multiple_of(t * R, R), R)
        grads = [r[rows, :] for r in dqs] + [r[0, rows, :] for r in dkvs] + [r[1, rows, :] for r in dkvs]
        dh = nt(jnp.concatenate(grads, axis=1), wqkv[...])
        grad, _ = norm_back(x[rows, :].astype(f32), gain, dh)
        dx[rows, :] = (dx2[rows, :] + grad).astype(bf16)
        store(t).start()
        return carry

    lax.fori_loop(*tiles, some_rows, 0)
    for t in range(*tiles):
        store(t).wait()


def finish(tiles, x, dx2, dqs, dkvs, weight, gain, before):
    anywhere = pl.BlockSpec(memory_space=pl.ANY)
    ins = 4 + len(dqs) + len(dkvs)
    return pl.pallas_call(
        functools.partial(finish_kernel, len(dqs), tiles),
        in_specs=[IN_VMEM] * ins + [anywhere] * len(before),
        out_specs=anywhere,
        out_shape=shape(x.shape, bf16),
        scratch_shapes=[pltpu.VMEM(x.shape, bf16), pltpu.SemaphoreType.DMA((x.shape[0] // R,))],
        input_output_aliases={ins: 0} if before else {},
        compiler_params=params(24),
        cost_estimate=COST if before else LONG,
        name="finish",
    )(x, dx2, weight, gain, *dqs, *dkvs, *before)


def bit_orders(count, groups):
    bits = [1 << i for i in range(count.bit_length() - 1)]
    if groups == 2:
        return [bits, bits[1::-1] + bits[2:]]
    return [bits[g:-1] + bits[:g] + bits[-1:] for g in range(groups)]


def exchange(value, axis, bit):
    size = lax.axis_size(axis)
    return lax.ppermute(value, axis, [(i, i ^ bit) for i in range(size)])


def distance(order, place):
    out = 0
    for i, bit in enumerate(order):
        out = out + ((place >> (len(order) - 1 - i)) & 1) * bit
    return out


SUMS = 8


def halves(value):
    high = value.astype(bf16)
    return high, (value - high.astype(f32)).astype(bf16)


def put_sums(value, kept, block):
    high, low = halves(value)
    lines = kept.shape[0]
    block[:lines, :] = high
    block[lines : 2 * lines, :] = low
    kept[...] = high.astype(f32) + low.astype(f32)


def got_sums(block):
    lines = block.shape[0] // 2
    return block[:lines, :].astype(f32) + block[lines:, :].astype(f32)


def start_kernel(orders, sources, small, me, *refs):
    groups = len(orders)
    arrays = max(a for source in sources for a, _, _ in source) + 1
    ins, outs = refs[: 2 * arrays], refs[len(refs) - 2 * groups :]
    half = outs[0].shape[0]
    for g, order in enumerate(orders):
        for side in range(2):

            def one(r, carry, g=g, order=order, side=side):
                part = me[0] ^ distance(order, r + side * half)
                out = outs[2 * g + side]
                row = 0
                for a, where, unit in sources[g]:
                    kept, got = ins[2 * a : 2 * a + 2]
                    place = where(part)
                    size, wide = kept.shape[1], out.shape[-1]
                    lanes = slice(unit * wide, (unit + 1) * wide)
                    total = kept[place, :, lanes].astype(f32) + got[place, :, lanes].astype(f32)
                    if len(out.shape) == 3:
                        out[r, row : row + size, :] = total.astype(bf16)
                    else:
                        start = pl.multiple_of(r * outs[0].shape[1] + row, 8)
                        out[pl.ds(start, size), :] = total.astype(bf16)
                    row += size
                return carry

            lax.fori_loop(0, half, one, 0)
    if small:
        here, there, kept = refs[2 * arrays : 2 * arrays + 3]
        total = here[...] + there[...]
        if small == "rides":
            wide = kept.shape[1]
            total = jnp.concatenate([total[:, c : c + wide] for c in range(0, total.shape[1], wide)], axis=0)
            put_sums(total, kept, outs[1].at[pl.ds(half * outs[0].shape[1], 2 * kept.shape[0]), :])
        else:
            kept[...] = total


def travelling(count, rows, width, lines):
    return shape((count * rows + 2 * lines, width) if lines else (count, rows, width), bf16)


def start_sum(me, kept, got, sources, width, orders, small, rides):
    count = 1 << len(orders[0])
    half = count // 2
    rows = [sum(kept[a].shape[1] for a, _, _ in source) for source in sources]
    lines = small[0].size // width if rides else 0
    cols = width // 3
    args = [a for pair in zip(kept, got, strict=True) for a in pair]
    sums = []
    for g in range(len(orders)):
        sums += [shape((half, rows[g], width), bf16), travelling(half, rows[g], width, 0 if g else lines)]
    mode = "rides" if rides else "alone" if small else ""
    if small:
        specs = dict(
            in_specs=[SMEM] + [IN_VMEM] * (len(args) + 2),
            out_specs=[IN_VMEM] * (1 + len(sums)),
            out_shape=[shape((lines, width) if rides else small[0].shape, f32)] + sums,
        )
    else:
        block = lambda a: pl.BlockSpec((a.shape[0], a.shape[1], cols), lambda c: (0, 0, c))
        specs = dict(
            grid=(width // cols,),
            in_specs=[SMEM] + [block(a) for a in args],
            out_specs=[block(a) for a in sums],
            out_shape=sums,
        )
    outs = pl.pallas_call(
        functools.partial(start_kernel, orders, sources, mode),
        compiler_params=params(30),
        cost_estimate=COST,
        name="start_sum",
        **specs,
    )(me, *args, *small)
    small, outs = list(outs[: len(outs) - len(sums)]), outs[len(outs) - len(sums) :]
    return list(outs[0::2]), list(outs[1::2]), small


def step_kernel(groups, merge, mode, *refs):
    kept, got = refs[:groups], refs[groups : 2 * groups]
    outs = refs[2 * groups + (2 if mode == "alone" else 1 if mode else 0) :]
    count = kept[0].shape[0]
    half = count // 2
    row = 0
    for g in range(groups):
        keep, send = outs[:2] if merge else outs[2 * g : 2 * g + 2]
        size = kept[g].shape[1]
        for r in range(count):
            there = got[g][r] if len(got[g].shape) == 3 else got[g][r * size : (r + 1) * size]
            total = (kept[g][r].astype(f32) + there.astype(f32)).astype(bf16)
            if r < half:
                keep[r, row : row + size, :] = total
            elif len(send.shape) == 3:
                send[r - half, row : row + size, :] = total
            else:
                start = (r - half) * keep.shape[1] + row
                send[start : start + size, :] = total
        row += size if merge else 0
    if mode == "rides":
        total = refs[2 * groups][...] + got_sums(got[0][count * kept[0].shape[1] :])
        put_sums(total, outs[-1], outs[1].at[pl.ds(half * outs[0].shape[1], 2 * total.shape[0]), :])
    elif mode:
        outs[-1][...] = refs[2 * groups][...] + refs[2 * groups + 1][...]


def step_sum(kept, got, small, merge, rides):
    groups = len(kept)
    half = kept[0].shape[0] // 2
    rows = [a.shape[1] for a in kept]
    width = kept[0].shape[2]
    args = [*kept, *got, *small]
    sums = []
    for g, r in enumerate([sum(rows)] if merge else rows):
        sums += [shape((half, r, width), bf16), travelling(half, r, width, 0 if g or not rides else small[0].shape[0])]
    outs = pl.pallas_call(
        functools.partial(step_kernel, groups, merge, "rides" if rides else "alone" if small else ""),
        in_specs=[IN_VMEM] * len(args),
        out_specs=[IN_VMEM] * (len(sums) + len(small[:1])),
        out_shape=sums + [shape(a.shape, f32) for a in small[:1]],
        compiler_params=params(16),
        cost_estimate=COST if small or half == 1 else LONG,
        name="step_sum",
    )(*args)
    return list(outs[0 : len(sums) : 2]), list(outs[1 : len(sums) : 2]), list(outs[len(sums) :])


def feed_end_kernel(kept, got, down, up, out):
    total = kept[0].astype(f32) + got[0].astype(f32)
    tall, few = down.shape[0] // GROUPS, out.shape[0] // GROUPS
    ups = []
    for g in range(GROUPS):
        row = g * (2 * tall + few)
        down[g * tall : (g + 1) * tall, :] = total[row : row + tall]
        ups.append(total[row + tall : row + 2 * tall])
        out[g * few : (g + 1) * few, :] = total[row + 2 * tall : row + 2 * tall + few]
    up[...] = jnp.concatenate(ups, axis=0).T


def feed_end(kept, got, tall, few):
    width = kept.shape[2]
    return pl.pallas_call(
        feed_end_kernel,
        in_specs=[IN_VMEM] * 2,
        out_specs=[IN_VMEM] * 3,
        out_shape=[shape((tall, width), f32), shape((width, tall), f32), shape((few, width), f32)],
        compiler_params=params(16),
        cost_estimate=COST,
        name="feed_end",
    )(kept, got)


def qkv_end_kernel(places, rides, gain_line, kept, got, *refs):
    out, gain1, gain2, rms = refs[-4:]
    tall = out.shape[0]
    width = gain1.shape[0]
    cols = kept.shape[2]
    there = got[: kept.shape[1]] if rides else got[0]
    total = kept[0].astype(f32) + there.astype(f32)
    for i, at in enumerate(places):
        out[:, at : at + cols] = total[i * tall : (i + 1) * tall]
    if rides:
        sums = refs[0][...] + got_sums(got[kept.shape[1] :])
        sums = jnp.concatenate([sums[r : r + SUMS] for r in range(0, sums.shape[0], SUMS)], axis=1)
    else:
        sums = refs[0][...] + refs[1][...]
    gain2[...] = sums[3:4, :].reshape(width)
    gain1[...] = (sums[4:5, :] / gain_line[...].reshape(1, width)).reshape(width)
    count = jnp.max(sums[5:6, :], axis=1, keepdims=True) * width
    rms[...] = jnp.broadcast_to(jnp.sqrt(jnp.sum(sums, axis=1, keepdims=True) / count), rms.shape)


def qkv_end(places, gain, kept, got, small, tall, wide, rides):
    return pl.pallas_call(
        functools.partial(qkv_end_kernel, places, rides),
        in_specs=[IN_VMEM] * (3 + len(small)),
        out_specs=[IN_VMEM] * 4,
        out_shape=[shape((tall, wide), f32), shape(gain.shape, f32), shape(gain.shape, f32), shape((SUMS, 128), f32)],
        compiler_params=params(16),
        cost_estimate=COST,
        name="qkv_end",
    )(gain, kept, got, *small)


def after(value, *earlier):
    return lax.optimization_barrier((value, earlier))[0]


def sum_parts(me, kept, got, sources, width, small, rides):
    orders = bit_orders(lax.axis_size("batch"), len(sources))
    steps = len(orders[0])
    common = min(i for i in range(steps + 1) if all(order[i:] == orders[0][i:] for order in orders))
    keep, send, small = start_sum(me, kept, got, sources, width, orders, small, rides)
    for i in range(steps):
        got = [exchange(s, "batch", order[i]) for s, order in zip(send, orders[: len(send)], strict=True)]
        if small and not rides:
            small = [small[0], exchange(small[0], "batch", orders[0][i])]
        earlier = yield send[0], got
        if i == steps - 1:
            break
        if earlier is not None:
            keep = after(keep, earlier)
        keep, send, small = step_sum(keep, got, small, i + 1 == common, rides)
    yield keep[0], got[0], small


def on_device(
    inputs, lengths, cotangent, qkv_weight, out_weight, up_weight, down_weight, attn_gain, mlp_gain
):
    seq, width = inputs.shape[2:]
    x = inputs[0, 0]
    dy = cotangent[0, 0]
    count = lax.axis_size("batch")
    stream = lax.axis_index("stream").astype(jnp.int32)
    me = lax.axis_index("batch").astype(jnp.int32).reshape(1)
    info = jnp.stack([stream, lengths[0]])
    cosine, sine = rotary_tables(seq)
    tables_t = (jnp.asarray(cosine.T), jnp.asarray(sine.T))

    received = lax.ppermute(x, "stream", [(0, 1)])
    (
        q, ko, vo, kc, vc, h1t, o, lse, outputs, dx2, do,
        up_send, up_keep, down_send, down_keep, out_send, out_keep, *tables, sums,
    ) = layer(
        info, attn_gain, mlp_gain, *tables_t, received, x, qkv_weight, out_weight, dy, up_weight, down_weight
    )
    down_got, up_got, out_got = (exchange(a, "stream", 1) for a in (down_send, up_send, out_send))

    def by_rows(array):
        return array.reshape(count * GROUPS, array.shape[0] // (count * GROUPS), width)

    heads = (q, ko, vo, kc, vc, o)
    pairs = width // PW // 3
    dq1, keep1, send1 = attend_back(info, 0, pairs, *heads, do, lse, *tables_t)
    got1 = lax.ppermute(send1, "stream", [(1, 0)])
    early = sum_parts(
        me,
        [by_rows(after(a, dq1)) for a in (down_keep, up_keep, out_keep)],
        [by_rows(a) for a in (down_got, up_got, out_got)],
        [[(a, lambda part, g=g: part * GROUPS + g, 0) for a in range(3)] for g in range(GROUPS)],
        width,
        [],
        False,
    )
    token = next(early)[0]
    dq2, keep2, send2 = attend_back(info, pairs, 2 * pairs, *heads, after(do, token), lse, *tables_t)
    got2 = lax.ppermute(send2, "stream", [(1, 0)])
    token = early.send(dq2)[0]
    dkv1, qkv_send1, qkv_keep1, small = weigh(info, 0, dq1, after(keep1, token), got1, tables, h1t, qkv_weight, sums)
    qkv_got1 = exchange(qkv_send1, "stream", 1)
    dkv2, qkv_send2, qkv_keep2, small = weigh(info, pairs, dq2, keep2, got2, tables, h1t, qkv_weight, small)
    qkv_got2 = exchange(qkv_send2, "stream", 1)
    small_got = exchange(small, "stream", 1)
    token = early.send(dkv2)[0]

    tall = width // (2 * count)
    split = lambda a: a.reshape(3 * count, tall, a.shape[2])
    rides = tall % 8 == 0
    runs = [(0, i, 0) for i in range(3)] + [(1, i, c) for i in range(3) for c in range(2)]
    groups = runs[:4], runs[4:]
    late = sum_parts(
        me,
        [split(after(a, token)) for a in (qkv_keep1, qkv_keep2)],
        [split(a) for a in (qkv_got1, qkv_got2)],
        [[(a, lambda part, i=i: i * count + part, c) for a, i, c in group] for group in groups],
        pairs * PW,
        [small, small_got],
        rides,
    )
    token = next(late)[0]
    ends = [dq1, dq2], [dkv1, dkv2], qkv_weight, attn_gain
    tiles = seq // R
    dx = finish((0, tiles // 2), after(x, token), dx2, *ends, [])
    early_out = early.send(dx)
    dx = finish((tiles // 2, tiles), x, after(dx2, early_out[0]), *ends, [dx])
    late.send(dx)
    late_out = late.send(early_out[1])
    while len(late_out) == 2:
        late_out = late.send(None)
    while len(early_out) == 2:
        early_out = early.send(None)
    up_cols = down_keep.shape[0] // count
    down_grad, up_grad, out_grad = feed_end(*early_out[:2], up_cols, tall)
    places = [i * width + (a + c) * pairs * PW for a, i, c in runs]
    qkv_grad, gain1_grad, gain2_grad, rms = qkv_end(places, attn_gain, *late_out, tall, 3 * width, rides)
    return (
        outputs[None, None],
        dx[None, None],
        qkv_grad,
        out_grad,
        up_grad,
        down_grad,
        gain1_grad,
        gain2_grad,
        rms[:3, 0],
    )


def solution(mesh):
    rows = P("stream", "batch", None, None)
    both = ("stream", "batch")
    return jax.shard_map(
        on_device,
        mesh=mesh,
        in_specs=(rows, P("batch"), rows, P(), P(), P(), P(), P(), P()),
        out_specs=(rows, rows, P(both, None), P(both, None), P(None, both), P(both, None), P(), P(), P()),
        check_vma=False,
    )
```

```python
import functools

import jax
import jax.numpy as jnp
import numpy as np
from jax import lax
from jax.experimental import pallas as pl
from jax.experimental.pallas import tpu as pltpu
from jax.sharding import PartitionSpec as P

f32 = jnp.float32
bf16 = jnp.bfloat16

HD = 64
BLK = 16
EPS = 1e-06
NEG = -1e30
PW = 2 * HD
T = 128
R = 256
AHEAD = 2
FC = 768
SCALE = HD**-0.5
BIG = 61
GROUPS = 3

COST = pl.CostEstimate(flops=1 << 20, bytes_accessed=1 << 16, transcendentals=0)
LONG = pl.CostEstimate(flops=1 << 35, bytes_accessed=1 << 26, transcendentals=0)

SMEM = pl.BlockSpec(memory_space=pltpu.SMEM)
IN_VMEM = pl.BlockSpec(memory_space=pltpu.VMEM)


def params(mib):
    return pltpu.CompilerParams(vmem_limit_bytes=mib << 20)


def shape(dims, dtype):
    return jax.ShapeDtypeStruct(dims, dtype)


def pinned(*arrays):
    return [pltpu.with_memory_space_constraint(a, pltpu.HBM) for a in arrays]


def nn(a, b):
    return jnp.dot(a, b, preferred_element_type=f32)


def nt(a, b):
    return lax.dot_general(a, b, (((1,), (1,)), ((), ())), preferred_element_type=f32)


def tn(a, b):
    return lax.dot_general(a, b, (((0,), (0,)), ((), ())), preferred_element_type=f32)


def whole(dims):
    return pl.BlockSpec(dims, lambda *_: (0,) * len(dims), pipeline_mode=pl.Buffered(1))


def inv_rms(v):
    return lax.rsqrt(jnp.mean(v * v, axis=-1, keepdims=True) + EPS)


def norm_back(v, gain, grad):
    r = inv_rms(v)
    unit = v * r
    scaled = grad * gain
    inner = jnp.mean(scaled * unit, axis=-1, keepdims=True)
    return r * (scaled - unit * inner), grad * unit


def rotary_tables(length):
    half = HD // 2
    freqs = np.exp(-np.log(10000.0) * np.arange(half) / half).astype(np.float32)
    angles = (np.arange(length, dtype=np.float32)[:, None] * freqs[None, :]).astype(np.float64)
    return np.cos(angles).astype(np.float32), np.sin(angles).astype(np.float32)


def rotated(v, cosine, signed, sign):
    first = lax.broadcasted_iota(jnp.int32, (1, PW), 1) % HD < HD // 2
    outs = []
    for c in range(0, v.shape[1], PW):
        part = v[:, c : c + PW]
        partner = jnp.where(first, pltpu.roll(part, PW - HD // 2, 1), pltpu.roll(part, HD // 2, 1))
        outs.append(part * cosine + partner * (signed * sign))
    return outs[0] if len(outs) == 1 else jnp.concatenate(outs, axis=1)


def staggered(count, *stages):
    state = [()] * count
    for step in range(count + len(stages) - 1):
        for k, stage in enumerate(stages):
            if 0 <= step - k < count:
                state[step - k] = stage(step - k, *state[step - k])


def in_pairs(count, *stages):
    def turn(n, carry):
        staggered(2, *(lambda t, *state, stage=stage: stage(2 * n + t, *state) for stage in stages))
        return carry

    lax.fori_loop(0, count // 2, turn, 0)


def token_weight(start, length, rows):
    return lax.broadcasted_iota(jnp.int32, (rows, 1), 0) + start < length


def row_sum(v):
    return jnp.sum(v, axis=0, keepdims=True)


def by_pairs(ref, rows, value):
    for p in range(ref.shape[0]):
        ref[p, rows, :] = value[:, p * PW : (p + 1) * PW].astype(ref.dtype)


def stacked(tile, low):
    zero = jnp.zeros_like(tile)
    return jnp.concatenate([jnp.where(low, tile, zero), jnp.where(low, zero, tile)], axis=0)


def unstacked(tile_t):
    half = lax.broadcasted_iota(jnp.int32, (PW, 1), 0) < HD
    return jnp.where(half, tile_t[:, :T], tile_t[:, T:])


def chunks_of(i):
    out, j = [], 0
    while j < i:
        n = 2 if i - j >= 2 else 1
        out.append((j * T, n * T))
        j += n
    return out


def edge_bias(ref, noisy):
    row = lax.broadcasted_iota(jnp.int32, (T, 2 * T), 0) // BLK
    col = (lax.broadcasted_iota(jnp.int32, (T, 2 * T), 1) % T) // BLK
    own = jnp.logical_or(row == col, jnp.logical_and(row < col, noisy == 0))
    other = jnp.logical_and(row < col, noisy == 1)
    ref[:T, :] = jnp.where(own, 0.0, NEG)
    ref[T:, :] = jnp.where(other, 0.0, NEG)


def masked(s, start, length):
    pos = lax.broadcasted_iota(jnp.int32, s.shape, 0) + start
    return jnp.where(pos < length, s, NEG)


def over_rows(op, v):
    return op(v.reshape(v.shape[0] // 8, 8, v.shape[1]), axis=0)


def attend_pair(length, q, ko, vo, kc, vc, store, lse, vo_t, vc_t, scores, bias):
    seq = q.shape[0]
    low = lax.broadcasted_iota(jnp.int32, (1, PW), 1) < HD
    vo_t[...] = vo[...].T
    vc_t[...] = vc[...].T

    def score(i):
        at = pl.ds(i * T, T)
        q2 = stacked(q[at, :] * bf16(SCALE), low)
        buf = scores.at[i % AHEAD]
        edge = nt(jnp.concatenate([ko[at, :], kc[at, :]], 0), q2) + bias[...]
        own = masked(edge[:T], i * T, length)
        other = masked(edge[T:], i * T, length)
        buf[pl.ds(0, T), :] = own
        buf[pl.ds(T, T), :] = other
        top = over_rows(jnp.max, jnp.maximum(own, other))
        for start, size in chunks_of(i):
            s = masked(nt(kc[pl.ds(start, size), :], q2), start, length)
            buf[pl.ds(2 * T + start, size), :] = s
            top = jnp.maximum(top, over_rows(jnp.max, s))
        return jnp.max(top, axis=0, keepdims=True)

    def mix(i, top):
        at = pl.ds(i * T, T)
        buf = scores.at[i % AHEAD]
        p = jnp.exp(buf[pl.ds(0, 2 * T), :] - top)
        total = over_rows(jnp.sum, p)
        acc = nn(jnp.concatenate([vo_t[:, at], vc_t[:, at]], 1), p.astype(bf16))
        for start, size in chunks_of(i):
            p = jnp.exp(buf[pl.ds(2 * T + start, size), :] - top)
            total = total + over_rows(jnp.sum, p)
            acc = acc + nn(vc_t[:, pl.ds(start, size)], p.astype(bf16))
        total = row_sum(total)
        lse[0, pl.ds(i, 1), :] = top + jnp.log(total)
        store(at, unstacked(acc * (1.0 / total)))

    tops = {}
    for i in range(seq // T + AHEAD - 1):
        if i < seq // T:
            tops[i] = score(i)
        if i >= AHEAD - 1:
            mix(i - AHEAD + 1, tops.pop(i - AHEAD + 1))


def turned_back(v, cosine, sine):
    quarter = HD // 2
    a, b, c, d = (v[i * quarter : (i + 1) * quarter] for i in range(4))
    return jnp.concatenate(
        [a * cosine + b * sine, b * cosine - a * sine, c * cosine + d * sine, d * cosine - c * sine]
    )


def attend_back_kernel(
    info, q, ko, vo, kc, vc, o, do, lse, cosine, sine, dq, keep, send, ko_t, kc_t, dko, dvo, dkc, dvc, bias
):
    noisy, length = info[0], info[1]
    q, ko, vo, kc, vc = (ref.at[0] for ref in (q, ko, vo, kc, vc))
    seq = q.shape[0]
    low = lax.broadcasted_iota(jnp.int32, (1, PW), 1) < HD

    @pl.when(pl.program_id(0) == 0)
    def _():
        edge_bias(bias, noisy)

    ko_t[...] = ko[...].T
    kc_t[...] = kc[...].T

    def tile(i):
        at = pl.ds(i * T, T)
        prod = (do[at, :].astype(f32) * o[at, :].astype(f32)).T
        delta = jnp.concatenate([row_sum(prod[:HD]), row_sum(prod[HD:])], 1)
        q2 = stacked(q[at, :] * bf16(SCALE), low)
        return q2, stacked(do[at, :], low), lse[0, pl.ds(i, 1), :], delta

    def products(i, start, size, q2, do2):
        if start is None:
            at = pl.ds(i * T, T)
            s = nt(jnp.concatenate([ko[at, :], kc[at, :]], 0), q2) + bias[...]
            s = jnp.concatenate([masked(s[:T], i * T, length), masked(s[T:], i * T, length)], 0)
            return s, nt(jnp.concatenate([vo[at, :], vc[at, :]], 0), do2)
        rows = pl.ds(start, size)
        return masked(nt(kc[rows, :], q2), start, length), nt(vc[rows, :], do2)

    def gather(i, start, size, q2, do2, p, ds, dq_t):
        at = pl.ds(i * T, T)
        dv, dk = nn(p, do2), nn(ds, q2)
        if start is None:
            dvo[at, :] = dv[:T]
            dko[at, :] = dk[:T]
            dvc[at, :] = dv[T:]
            dkc[at, :] = dk[T:]
            return nn(jnp.concatenate([ko_t[:, at], kc_t[:, at]], 1), ds)
        rows = pl.ds(start, size)
        dvc[rows, :] += dv
        dkc[rows, :] += dk
        return dq_t + nn(kc_t[:, rows], ds)

    work = [(i, *c) for i in range(seq // T) for c in [(None, None)] + chunks_of(i)]
    tiles, made, weighed, dq_t = {}, {}, {}, None
    for n in range(len(work) + 2):
        if n < len(work):
            i = work[n][0]
            if i not in tiles:
                tiles[i] = tile(i)
            made[n] = products(*work[n], *tiles[i][:2])
        if 0 <= n - 1 < len(work):
            _, _, norm, delta = tiles[work[n - 1][0]]
            s, dp = made.pop(n - 1)
            p = jnp.exp(s - norm)
            weighed[n - 1] = p.astype(bf16), (p * (dp - delta)).astype(bf16)
        if n >= 2:
            i, start, size = work[n - 2]
            dq_t = gather(i, start, size, *tiles[i][:2], *weighed.pop(n - 2), dq_t)
            if n == len(work) + 1 or work[n - 1][0] != i:
                at = pl.ds(i * T, T)
                out = turned_back(unstacked(dq_t), cosine[:, at], sine[:, at]) * SCALE
                dq[at, :] = out.T.astype(bf16)
    clean = (1 - noisy).astype(f32)
    for at, own, other in ((0, dko, dkc), (1, dvo, dvc)):
        keep[at] = (own[...] + clean * other[...]).astype(bf16)
        send[at] = other[...].astype(bf16)


def attend_back(info, first, pairs, q, ko, vo, kc, vc, o, do, lse, cosine, sine):
    seq = q.shape[1]
    width = pairs * PW
    heads = pl.BlockSpec((1, seq, PW), lambda h: (first + h, 0, 0))
    source = pl.BlockSpec((seq, PW), lambda h: (0, first + h))
    both = pl.BlockSpec((2, seq, PW), lambda h: (0, 0, h))
    lines = pl.BlockSpec((1, seq // T, 2 * T), lambda h: (first + h, 0, 0))
    table = whole((HD // 2, seq))
    return pl.pallas_call(
        attend_back_kernel,
        grid=(pairs,),
        in_specs=[SMEM] + [heads] * 5 + [source] * 2 + [lines, table, table],
        out_specs=[pl.BlockSpec((seq, PW), lambda h: (0, h)), both, both],
        out_shape=[shape((seq, width), bf16)] + [shape((2, seq, width), bf16)] * 2,
        scratch_shapes=[pltpu.VMEM((PW, seq), bf16)] * 2
        + [pltpu.VMEM((seq, PW), f32)] * 4
        + [pltpu.VMEM((2 * T, 2 * T), f32)],
        compiler_params=params(24),
        cost_estimate=LONG,
        name="attend_back",
    )(info, *pinned(q, ko, vo, kc, vc, o, do), lse, cosine, sine)


C0 = 0.7978845608028654
C1 = C0 * 0.044715


def layer_kernel(
    info, gain1_line, gain2_line, cosine_t, sine_t, received, x_any, wqkv_any, wo_any, dy_any,
    w1_any, w2_any,
    q_out, ko_out, vo_out, kc_out, vc_out, h1t_out, o_out, lse_out, out_any, dx2_any, do_any,
    up_send, up_keep, down_send, down_keep, g_send, g_keep, cosine_out, signed_out, sums,
    x, wqkv, cosine, signed, q, ko, vo, h1t, wo, dy, w1, w2,
    kc, vc, vo_t, vc_t, scores, bias, o, o_t, lse, x2, h2, m, dh, act, du, up_grad, down_grad, half_grads,
    sem_in, sem_1, sem_2, sem_out, sem_up, sem_down, sem_tile,
):
    noisy, length = info[0], info[1]
    seq, width = x.shape
    chunks, pairs, tiles = w1.shape[0], kc.shape[0], seq // R
    copy = pltpu.make_async_copy
    gain1, gain2 = gain1_line[...].reshape(1, width), gain2_line[...].reshape(1, width)

    def weights(c):
        place = lax.rem(c + (chunks // 2) * (1 - noisy), chunks) * FC
        place = pl.multiple_of(place, FC)
        return (
            copy(w1_any.at[:, pl.ds(place, FC)], w1.at[c], sem_1.at[c]),
            copy(w2_any.at[pl.ds(place, FC), :], w2.at[c], sem_2.at[c]),
        )

    sources = (
        (x_any, x),
        (wqkv_any, wqkv),
        (wo_any, wo),
        (dy_any, dy),
    )
    loads = [copy(a, b, sem_in.at[i]) for i, (a, b) in enumerate(sources)]
    for load in loads[:2]:
        load.start()
    sums[...] = jnp.zeros_like(sums)
    edge_bias(bias, noisy)
    for t in range(0, seq, R):
        c, d = cosine_t[:, t : t + R].T, sine_t[:, t : t + R].T
        cosine[pl.ds(t, R), :] = jnp.concatenate([c, c, c, c], axis=1)
        signed[pl.ds(t, R), :] = jnp.concatenate([-d, d, -d, d], axis=1)
    tables_out = [copy(cosine, cosine_out, sem_out.at[10]), copy(signed, signed_out, sem_out.at[11])]
    span = lambda t: pl.ds(pl.multiple_of(t * R, R), R)

    loads[0].wait()

    def own_norm(t):
        value = x[span(t), :].astype(f32)
        h1 = (value * inv_rms(value) * gain1).astype(bf16)
        h2[span(t), :] = h1
        h1t[:, span(t)] = h1.T
        weight = token_weight(t * R, length, R)
        sums[0:1, :] += row_sum(jnp.where(weight, value * value, 0.0))
        return ()

    for t in range(tiles):
        own_norm(t)
    loads[1].wait()
    for load in loads[2:]:
        load.start()

    def own_product(t):
        return tuple(nn(h2[span(t), :], wqkv[:, i * width : (i + 1) * width]) for i in range(3))

    def own_turn(t, a, b, c):
        tables = (cosine[span(t), :], signed[span(t), :], 1.0)
        by_pairs(q, span(t), rotated(a, *tables))
        by_pairs(ko, span(t), rotated(b, *tables))
        by_pairs(vo, span(t), c)
        return ()

    def clean_norm(t):
        value = jnp.where(noisy == 1, received[span(t), :].astype(f32), x[span(t), :].astype(f32))
        o[span(t), :] = (value * inv_rms(value) * gain1).astype(bf16)
        return ()

    def clean_product(t):
        return tuple(nn(o[span(t), :], wqkv[:, i * width : (i + 1) * width]) for i in (1, 2))

    def clean_turn(t, a, b):
        by_pairs(kc, span(t), rotated(a, cosine[span(t), :], signed[span(t), :], 1.0))
        by_pairs(vc, span(t), b)
        return ()

    in_pairs(tiles, own_product, own_turn)
    stores = [
        copy(a, b, sem_out.at[6 + i])
        for i, (a, b) in enumerate(((q, q_out), (ko, ko_out), (vo, vo_out), (h1t, h1t_out)))
    ]
    stores += tables_out
    for store in stores:
        store.start()
    in_pairs(tiles, clean_norm, clean_product, clean_turn)
    more = [copy(kc, kc_out, sem_out.at[0]), copy(vc, vc_out, sem_out.at[1])]
    for store in more:
        store.start()
    stores += more

    for c in range(chunks):
        for load in weights(c):
            load.start()

    def one_pair(p, carry):
        lanes = pl.ds(pl.multiple_of(p * PW, PW), PW)

        def keep(at, tile_t):
            o_t[lanes, at] = tile_t.astype(bf16)
            o[at, lanes] = tile_t.T.astype(bf16)

        heads = (ref.at[p] for ref in (q, ko, vo, kc, vc))
        attend_pair(length, *heads, keep, lse.at[pl.ds(p, 1)], vo_t, vc_t, scores, bias)
        return carry

    lax.fori_loop(0, pairs, one_pair, 0)
    mixed_out = copy(o, o_out, sem_out.at[2])
    mixed_out.start()
    stores += [copy(lse, lse_out, sem_out.at[3])]
    stores[-1].start()

    for load in loads[2:]:
        load.wait()

    def join_product(t):
        return (nn(o[span(t), :], wo[...]),)

    def join_norm(t, branch):
        value = x[span(t), :].astype(f32) + branch
        x2[span(t), :] = value
        h2[span(t), :] = (value * inv_rms(value) * gain2).astype(bf16)
        m[span(t), :] = jnp.zeros_like(value)
        dh[span(t), :] = jnp.zeros_like(value)
        weight = token_weight(t * R, length, R)
        sums[1:2, :] += row_sum(jnp.where(weight, branch * branch, 0.0))
        return ()

    staggered(tiles, join_product, join_norm)

    def grad_stores(c, up, down):
        slot = lax.rem(c, 2)
        rows = pl.ds(pl.multiple_of(lax.rem(c, chunks // 2) * FC, FC), FC)
        return (
            copy(up_grad.at[slot], up.at[rows, :], sem_up.at[slot]),
            copy(down_grad.at[slot], down.at[rows, :], sem_down.at[slot]),
        )

    def one_chunk(c, carry):
        for load in weights(c):
            load.wait()
        up, down = w1.at[c], w2.at[c]
        made = {}
        for t in range(-R, seq, R):
            if t + R < seq:
                rows = pl.ds(t + R, R)
                made[t + R] = nn(h2[rows, :], up[...]), nt(dy[rows, :], down[...])
            if t < 0:
                continue
            rows = pl.ds(t, R)
            u, da = made.pop(t)
            sq = u * u
            half = 0.5 * jnp.tanh(u * (C0 + C1 * sq)) + 0.5
            low = (u * half).astype(bf16)
            slope = half + u * (2.0 * half * (1.0 - half)) * (C0 + 3.0 * C1 * sq)
            back = (da * slope).astype(bf16)
            act[rows, :] = low
            du[rows, :] = back
            m[rows, :] += nn(low, down[...])
            dh[rows, :] += nt(back, up[...])

        @pl.when(c >= 2)
        def _():
            for store in grad_stores(c, up_send, down_send):
                store.wait()

        slot = lax.rem(c, 2)
        down_grad[slot] = tn(act[...], dy[...]).astype(bf16)
        up_grad[slot] = tn(du[...], h2[...]).astype(bf16)

        @pl.when(c < chunks // 2)
        def _():
            for store in grad_stores(c, up_send, down_send):
                store.start()

        @pl.when(c >= chunks // 2)
        def _():
            for store in grad_stores(c, up_keep, down_keep):
                store.start()

        return carry

    lax.fori_loop(0, chunks, one_chunk, 0)

    mixed_out.wait()

    def tile_stores(t):
        return (
            copy(h2.at[span(t), :], out_any.at[span(t), :], sem_tile.at[t, 0]),
            copy(x2.at[span(t), :], dx2_any.at[span(t), :], sem_tile.at[t, 1]),
            copy(o.at[span(t), :], do_any.at[span(t), :], sem_tile.at[t, 2]),
        )

    def middle_norm(t):
        value = x2[span(t), :]
        mixed = m[span(t), :]
        weight = token_weight(t * R, length, R)
        sums[2:3, :] += row_sum(jnp.where(weight, mixed * mixed, 0.0))
        grad, gain_terms = norm_back(value, gain2, dh[span(t), :])
        sums[3:4, :] += row_sum(gain_terms)
        grad = grad + dy[span(t), :].astype(f32)
        h2[span(t), :] = (value + mixed).astype(bf16)
        x2[span(t), :] = grad
        x[span(t), :] = grad.astype(bf16)
        return ()

    def middle_product(t):
        o[span(t), :] = nt(x[span(t), :], wo[...]).astype(bf16)
        for store in tile_stores(t):
            store.start()
        return ()

    staggered(tiles, middle_norm, middle_product)
    half = width // 2
    mine = pl.multiple_of(noisy * half, half)
    half_grads[0] = nn(o_t[pl.ds(half - mine, half), :], x[...]).astype(bf16)
    half_grads[1] = nn(o_t[pl.ds(mine, half), :], x[...]).astype(bf16)
    more = [copy(half_grads.at[0], g_send, sem_out.at[4]), copy(half_grads.at[1], g_keep, sem_out.at[5])]
    for store in more:
        store.start()
    stores += more
    for c in range(chunks - 2, chunks):
        stores += grad_stores(c, up_keep, down_keep)
    for t in range(tiles):
        stores += tile_stores(t)
    for store in stores:
        store.wait()


def layer(info, gain1, gain2, cosine_t, sine_t, received, x, wqkv, wo, dy, w1, w2):
    seq, width = x.shape
    hidden = w1.shape[1]
    tiles, pairs, chunks = seq // R, width // PW, hidden // FC
    anywhere = pl.BlockSpec(memory_space=pl.ANY)
    vmem = pltpu.VMEM
    dma = pltpu.SemaphoreType.DMA
    heads = (pairs, seq, PW)
    flat = (seq, width)
    outs = (
        [shape(heads, bf16)] * 5
        + [shape((width, seq), bf16), shape(flat, bf16), shape((pairs, seq // T, 2 * T), f32)]
        + [shape(flat, bf16), shape(flat, f32), shape(flat, bf16)]
        + [shape((hidden // 2, width), bf16)] * 4
        + [shape((width // 2, width), bf16)] * 2
        + [shape((seq, PW), f32)] * 2
        + [shape((8, width), f32)]
    )
    return pl.pallas_call(
        layer_kernel,
        in_specs=[SMEM] + [IN_VMEM] * 5 + [anywhere] * 6,
        out_specs=[anywhere] * 19 + [IN_VMEM],
        out_shape=outs,
        scratch_shapes=[vmem(flat, bf16)]
        + [vmem(wqkv.shape, bf16), vmem((seq, PW), f32), vmem((seq, PW), f32)]
        + [vmem(heads, bf16)] * 3
        + [vmem((width, seq), bf16), vmem((width, width), bf16), vmem(flat, bf16)]
        + [vmem((chunks, width, FC), bf16), vmem((chunks, FC, width), bf16)]
        + [vmem(heads, bf16)] * 2
        + [vmem((PW, seq), bf16)] * 2
        + [vmem((AHEAD, seq + T, 2 * T), f32), vmem((2 * T, 2 * T), f32)]
        + [vmem(flat, bf16), vmem((width, seq), bf16)]
        + [vmem((pairs, seq // T, 2 * T), f32)]
        + [vmem(flat, f32), vmem(flat, bf16)]
        + [vmem(flat, f32)] * 2
        + [vmem((seq, FC), bf16)] * 2
        + [vmem((2, FC, width), bf16)] * 2
        + [vmem((2, width // 2, width), bf16)]
        + [dma((4,)), dma((chunks,)), dma((chunks,)), dma((12,)), dma((2,)), dma((2,)), dma((tiles, 3))],
        compiler_params=params(BIG),
        cost_estimate=LONG,
        name="layer",
    )(info, gain1, gain2, cosine_t, sine_t, received, *pinned(x, wqkv, wo, dy, w1, w2))


def weigh_kernel(first, info, dq, keep, got, cosine, signed, h1t, wqkv, sums, dkv, g_send, g_keep, small):
    width, half = wqkv.shape[0], wqkv.shape[0] // 2
    mine = pl.multiple_of(info[0] * half, half)
    dk = keep[0].astype(f32) + got[0].astype(f32)
    dkv[0] = rotated(dk, cosine[...], signed[...], -1.0).astype(bf16)
    dkv[1] = (keep[1].astype(f32) + got[1].astype(f32)).astype(bf16)
    small[...] = sums[...]
    for out, start in ((g_send, half - mine), (g_keep, mine)):
        rows = pl.ds(start, half)
        terms = 0.0
        for i, part in enumerate((dq, dkv.at[0], dkv.at[1])):
            total = nn(h1t[rows, :], part[...])
            out[i] = total.astype(bf16)
            at = i * width + first * PW
            weighted = total * wqkv[rows, at : at + total.shape[1]].astype(f32)
            for c in range(0, total.shape[1], PW):
                terms = terms + weighted[:, c : c + PW]
        line = jnp.sum(terms.T, axis=0, keepdims=True)
        lanes = lax.broadcasted_iota(jnp.int32, (1, width), 1)
        inside = jnp.logical_and(lanes >= start, lanes < start + half)
        small[4:5, :] += jnp.where(inside, jnp.concatenate([line, line], axis=1), 0.0)
    small[5:6, :] = jnp.full((1, width), info[1].astype(f32))


def weigh(info, first, dq, keep, got, tables, h1t, wqkv, sums):
    seq, width = dq.shape
    tall = h1t.shape[0]
    return pl.pallas_call(
        functools.partial(weigh_kernel, first),
        in_specs=[SMEM] + [IN_VMEM] * 8,
        out_specs=[IN_VMEM] * 4,
        out_shape=[shape((2, seq, width), bf16)]
        + [shape((3, tall // 2, width), bf16)] * 2
        + [shape(sums.shape, f32)],
        compiler_params=params(24),
        cost_estimate=LONG,
        name="weigh",
    )(info, dq, keep, got, *tables, h1t, wqkv, sums)


def finish_kernel(parts, tiles, x, dx2, wqkv, gain_line, *refs):
    dx_any, dx, sem = refs[-3:]
    dqs, dkvs = refs[:parts], refs[parts : 2 * parts]
    gain = gain_line[...].reshape(1, x.shape[1])

    def store(t):
        rows = pl.ds(pl.multiple_of(t * R, R), R)
        return pltpu.make_async_copy(dx.at[rows, :], dx_any.at[rows, :], sem.at[t])

    def some_rows(t, carry):
        rows = pl.ds(pl.multiple_of(t * R, R), R)
        grads = [r[rows, :] for r in dqs] + [r[0, rows, :] for r in dkvs] + [r[1, rows, :] for r in dkvs]
        dh = nt(jnp.concatenate(grads, axis=1), wqkv[...])
        grad, _ = norm_back(x[rows, :].astype(f32), gain, dh)
        dx[rows, :] = (dx2[rows, :] + grad).astype(bf16)
        store(t).start()
        return carry

    lax.fori_loop(*tiles, some_rows, 0)
    for t in range(*tiles):
        store(t).wait()


def finish(tiles, x, dx2, dqs, dkvs, weight, gain, before):
    anywhere = pl.BlockSpec(memory_space=pl.ANY)
    ins = 4 + len(dqs) + len(dkvs)
    return pl.pallas_call(
        functools.partial(finish_kernel, len(dqs), tiles),
        in_specs=[IN_VMEM] * ins + [anywhere] * len(before),
        out_specs=anywhere,
        out_shape=shape(x.shape, bf16),
        scratch_shapes=[pltpu.VMEM(x.shape, bf16), pltpu.SemaphoreType.DMA((x.shape[0] // R,))],
        input_output_aliases={ins: 0} if before else {},
        compiler_params=params(24),
        cost_estimate=COST if before else LONG,
        name="finish",
    )(x, dx2, weight, gain, *dqs, *dkvs, *before)


def bit_orders(count, groups):
    bits = [1 << i for i in range(count.bit_length() - 1)]
    if groups == 2:
        return [bits, bits[1::-1] + bits[2:]]
    return [bits[g:-1] + bits[:g] + bits[-1:] for g in range(groups)]


def exchange(value, axis, bit):
    size = lax.axis_size(axis)
    return lax.ppermute(value, axis, [(i, i ^ bit) for i in range(size)])


def distance(order, place):
    out = 0
    for i, bit in enumerate(order):
        out = out + ((place >> (len(order) - 1 - i)) & 1) * bit
    return out


SUMS = 8


def halves(value):
    high = value.astype(bf16)
    return high, (value - high.astype(f32)).astype(bf16)


def put_sums(value, kept, block):
    high, low = halves(value)
    lines = kept.shape[0]
    block[:lines, :] = high
    block[lines : 2 * lines, :] = low
    kept[...] = high.astype(f32) + low.astype(f32)


def got_sums(block):
    lines = block.shape[0] // 2
    return block[:lines, :].astype(f32) + block[lines:, :].astype(f32)


def start_kernel(orders, sources, small, me, *refs):
    groups = len(orders)
    arrays = max(a for source in sources for a, _, _ in source) + 1
    ins, outs = refs[: 2 * arrays], refs[len(refs) - 2 * groups :]
    half = outs[0].shape[0]
    for g, order in enumerate(orders):
        for side in range(2):

            def one(r, carry, g=g, order=order, side=side):
                part = me[0] ^ distance(order, r + side * half)
                out = outs[2 * g + side]
                row = 0
                for a, where, unit in sources[g]:
                    kept, got = ins[2 * a : 2 * a + 2]
                    place = where(part)
                    size, wide = kept.shape[1], out.shape[-1]
                    lanes = slice(unit * wide, (unit + 1) * wide)
                    total = kept[place, :, lanes].astype(f32) + got[place, :, lanes].astype(f32)
                    if len(out.shape) == 3:
                        out[r, row : row + size, :] = total.astype(bf16)
                    else:
                        start = pl.multiple_of(r * outs[0].shape[1] + row, 8)
                        out[pl.ds(start, size), :] = total.astype(bf16)
                    row += size
                return carry

            lax.fori_loop(0, half, one, 0)
    if small:
        here, there, kept = refs[2 * arrays : 2 * arrays + 3]
        total = here[...] + there[...]
        if small == "rides":
            wide = kept.shape[1]
            total = jnp.concatenate([total[:, c : c + wide] for c in range(0, total.shape[1], wide)], axis=0)
            put_sums(total, kept, outs[1].at[pl.ds(half * outs[0].shape[1], 2 * kept.shape[0]), :])
        else:
            kept[...] = total


def travelling(count, rows, width, lines):
    return shape((count * rows + 2 * lines, width) if lines else (count, rows, width), bf16)


def start_sum(me, kept, got, sources, width, orders, small, rides):
    count = 1 << len(orders[0])
    half = count // 2
    rows = [sum(kept[a].shape[1] for a, _, _ in source) for source in sources]
    lines = small[0].size // width if rides else 0
    cols = width // 3
    args = [a for pair in zip(kept, got, strict=True) for a in pair]
    sums = []
    for g in range(len(orders)):
        sums += [shape((half, rows[g], width), bf16), travelling(half, rows[g], width, 0 if g else lines)]
    mode = "rides" if rides else "alone" if small else ""
    if small:
        specs = dict(
            in_specs=[SMEM] + [IN_VMEM] * (len(args) + 2),
            out_specs=[IN_VMEM] * (1 + len(sums)),
            out_shape=[shape((lines, width) if rides else small[0].shape, f32)] + sums,
        )
    else:
        block = lambda a: pl.BlockSpec((a.shape[0], a.shape[1], cols), lambda c: (0, 0, c))
        specs = dict(
            grid=(width // cols,),
            in_specs=[SMEM] + [block(a) for a in args],
            out_specs=[block(a) for a in sums],
            out_shape=sums,
        )
    outs = pl.pallas_call(
        functools.partial(start_kernel, orders, sources, mode),
        compiler_params=params(30),
        cost_estimate=COST,
        name="start_sum",
        **specs,
    )(me, *args, *small)
    small, outs = list(outs[: len(outs) - len(sums)]), outs[len(outs) - len(sums) :]
    return list(outs[0::2]), list(outs[1::2]), small


def step_kernel(groups, merge, mode, *refs):
    kept, got = refs[:groups], refs[groups : 2 * groups]
    outs = refs[2 * groups + (2 if mode == "alone" else 1 if mode else 0) :]
    count = kept[0].shape[0]
    half = count // 2
    row = 0
    for g in range(groups):
        keep, send = outs[:2] if merge else outs[2 * g : 2 * g + 2]
        size = kept[g].shape[1]
        for r in range(count):
            there = got[g][r] if len(got[g].shape) == 3 else got[g][r * size : (r + 1) * size]
            total = (kept[g][r].astype(f32) + there.astype(f32)).astype(bf16)
            if r < half:
                keep[r, row : row + size, :] = total
            elif len(send.shape) == 3:
                send[r - half, row : row + size, :] = total
            else:
                start = (r - half) * keep.shape[1] + row
                send[start : start + size, :] = total
        row += size if merge else 0
    if mode == "rides":
        total = refs[2 * groups][...] + got_sums(got[0][count * kept[0].shape[1] :])
        put_sums(total, outs[-1], outs[1].at[pl.ds(half * outs[0].shape[1], 2 * total.shape[0]), :])
    elif mode:
        outs[-1][...] = refs[2 * groups][...] + refs[2 * groups + 1][...]


def step_sum(kept, got, small, merge, rides):
    groups = len(kept)
    half = kept[0].shape[0] // 2
    rows = [a.shape[1] for a in kept]
    width = kept[0].shape[2]
    args = [*kept, *got, *small]
    sums = []
    for g, r in enumerate([sum(rows)] if merge else rows):
        sums += [shape((half, r, width), bf16), travelling(half, r, width, 0 if g or not rides else small[0].shape[0])]
    outs = pl.pallas_call(
        functools.partial(step_kernel, groups, merge, "rides" if rides else "alone" if small else ""),
        in_specs=[IN_VMEM] * len(args),
        out_specs=[IN_VMEM] * (len(sums) + len(small[:1])),
        out_shape=sums + [shape(a.shape, f32) for a in small[:1]],
        compiler_params=params(16),
        cost_estimate=COST if small or half == 1 else LONG,
        name="step_sum",
    )(*args)
    return list(outs[0 : len(sums) : 2]), list(outs[1 : len(sums) : 2]), list(outs[len(sums) :])


def feed_end_kernel(kept, got, down, up, out):
    total = kept[0].astype(f32) + got[0].astype(f32)
    tall, few = down.shape[0] // GROUPS, out.shape[0] // GROUPS
    ups = []
    for g in range(GROUPS):
        row = g * (2 * tall + few)
        down[g * tall : (g + 1) * tall, :] = total[row : row + tall]
        ups.append(total[row + tall : row + 2 * tall])
        out[g * few : (g + 1) * few, :] = total[row + 2 * tall : row + 2 * tall + few]
    up[...] = jnp.concatenate(ups, axis=0).T


def feed_end(kept, got, tall, few):
    width = kept.shape[2]
    return pl.pallas_call(
        feed_end_kernel,
        in_specs=[IN_VMEM] * 2,
        out_specs=[IN_VMEM] * 3,
        out_shape=[shape((tall, width), f32), shape((width, tall), f32), shape((few, width), f32)],
        compiler_params=params(16),
        cost_estimate=COST,
        name="feed_end",
    )(kept, got)


def qkv_end_kernel(places, rides, gain_line, kept, got, *refs):
    out, gain1, gain2, rms = refs[-4:]
    tall = out.shape[0]
    width = gain1.shape[0]
    cols = kept.shape[2]
    there = got[: kept.shape[1]] if rides else got[0]
    total = kept[0].astype(f32) + there.astype(f32)
    for i, at in enumerate(places):
        out[:, at : at + cols] = total[i * tall : (i + 1) * tall]
    if rides:
        sums = refs[0][...] + got_sums(got[kept.shape[1] :])
        sums = jnp.concatenate([sums[r : r + SUMS] for r in range(0, sums.shape[0], SUMS)], axis=1)
    else:
        sums = refs[0][...] + refs[1][...]
    gain2[...] = sums[3:4, :].reshape(width)
    gain1[...] = (sums[4:5, :] / gain_line[...].reshape(1, width)).reshape(width)
    count = jnp.max(sums[5:6, :], axis=1, keepdims=True) * width
    rms[...] = jnp.broadcast_to(jnp.sqrt(jnp.sum(sums, axis=1, keepdims=True) / count), rms.shape)


def qkv_end(places, gain, kept, got, small, tall, wide, rides):
    return pl.pallas_call(
        functools.partial(qkv_end_kernel, places, rides),
        in_specs=[IN_VMEM] * (3 + len(small)),
        out_specs=[IN_VMEM] * 4,
        out_shape=[shape((tall, wide), f32), shape(gain.shape, f32), shape(gain.shape, f32), shape((SUMS, 128), f32)],
        compiler_params=params(16),
        cost_estimate=COST,
        name="qkv_end",
    )(gain, kept, got, *small)


def after(value, *earlier):
    return lax.optimization_barrier((value, earlier))[0]


def sum_parts(me, kept, got, sources, width, small, rides):
    orders = bit_orders(lax.axis_size("batch"), len(sources))
    steps = len(orders[0])
    common = min(i for i in range(steps + 1) if all(order[i:] == orders[0][i:] for order in orders))
    keep, send, small = start_sum(me, kept, got, sources, width, orders, small, rides)
    for i in range(steps):
        got = [exchange(s, "batch", order[i]) for s, order in zip(send, orders[: len(send)], strict=True)]
        if small and not rides:
            small = [small[0], exchange(small[0], "batch", orders[0][i])]
        earlier = yield send[0], got
        if i == steps - 1:
            break
        if earlier is not None:
            keep = after(keep, earlier)
        keep, send, small = step_sum(keep, got, small, i + 1 == common, rides)
    yield keep[0], got[0], small


def on_device(
    inputs, lengths, cotangent, qkv_weight, out_weight, up_weight, down_weight, attn_gain, mlp_gain
):
    seq, width = inputs.shape[2:]
    x = inputs[0, 0]
    dy = cotangent[0, 0]
    count = lax.axis_size("batch")
    stream = lax.axis_index("stream").astype(jnp.int32)
    me = lax.axis_index("batch").astype(jnp.int32).reshape(1)
    info = jnp.stack([stream, lengths[0]])
    cosine, sine = rotary_tables(seq)
    tables_t = (jnp.asarray(cosine.T), jnp.asarray(sine.T))

    received = lax.ppermute(x, "stream", [(0, 1)])
    (
        q, ko, vo, kc, vc, h1t, o, lse, outputs, dx2, do,
        up_send, up_keep, down_send, down_keep, out_send, out_keep, *tables, sums,
    ) = layer(
        info, attn_gain, mlp_gain, *tables_t, received, x, qkv_weight, out_weight, dy, up_weight, down_weight
    )
    down_got, up_got, out_got = (exchange(a, "stream", 1) for a in (down_send, up_send, out_send))

    def by_rows(array):
        return array.reshape(count * GROUPS, array.shape[0] // (count * GROUPS), width)

    heads = (q, ko, vo, kc, vc, o)
    pairs = width // PW // 3
    dq1, keep1, send1 = attend_back(info, 0, pairs, *heads, do, lse, *tables_t)
    got1 = lax.ppermute(send1, "stream", [(1, 0)])
    early = sum_parts(
        me,
        [by_rows(after(a, dq1)) for a in (down_keep, up_keep, out_keep)],
        [by_rows(a) for a in (down_got, up_got, out_got)],
        [[(a, lambda part, g=g: part * GROUPS + g, 0) for a in range(3)] for g in range(GROUPS)],
        width,
        [],
        False,
    )
    token = next(early)[0]
    dq2, keep2, send2 = attend_back(info, pairs, 2 * pairs, *heads, after(do, token), lse, *tables_t)
    got2 = lax.ppermute(send2, "stream", [(1, 0)])
    token = early.send(dq2)[0]
    dkv1, qkv_send1, qkv_keep1, small = weigh(info, 0, dq1, after(keep1, token), got1, tables, h1t, qkv_weight, sums)
    qkv_got1 = exchange(qkv_send1, "stream", 1)
    dkv2, qkv_send2, qkv_keep2, small = weigh(info, pairs, dq2, keep2, got2, tables, h1t, qkv_weight, small)
    qkv_got2 = exchange(qkv_send2, "stream", 1)
    small_got = exchange(small, "stream", 1)
    token = early.send(dkv2)[0]

    tall = width // (2 * count)
    split = lambda a: a.reshape(3 * count, tall, a.shape[2])
    rides = tall % 8 == 0
    runs = [(0, i, 0) for i in range(3)] + [(1, i, c) for i in range(3) for c in range(2)]
    groups = runs[:4], runs[4:]
    late = sum_parts(
        me,
        [split(after(a, token)) for a in (qkv_keep1, qkv_keep2)],
        [split(a) for a in (qkv_got1, qkv_got2)],
        [[(a, lambda part, i=i: i * count + part, c) for a, i, c in group] for group in groups],
        pairs * PW,
        [small, small_got],
        rides,
    )
    token = next(late)[0]
    ends = [dq1, dq2], [dkv1, dkv2], qkv_weight, attn_gain
    tiles = seq // R
    dx = finish((0, tiles // 2), after(x, token), dx2, *ends, [])
    early_out = early.send(dx)
    dx = finish((tiles // 2, tiles), x, after(dx2, early_out[0]), *ends, [dx])
    late.send(dx)
    late_out = late.send(early_out[1])
    while len(late_out) == 2:
        late_out = late.send(None)
    while len(early_out) == 2:
        early_out = early.send(None)
    up_cols = down_keep.shape[0] // count
    down_grad, up_grad, out_grad = feed_end(*early_out[:2], up_cols, tall)
    places = [i * width + (a + c) * pairs * PW for a, i, c in runs]
    qkv_grad, gain1_grad, gain2_grad, rms = qkv_end(places, attn_gain, *late_out, tall, 3 * width, rides)
    return (
        outputs[None, None],
        dx[None, None],
        qkv_grad,
        out_grad,
        up_grad,
        down_grad,
        gain1_grad,
        gain2_grad,
        rms[:3, 0],
    )


def solution(mesh):
    rows = P("stream", "batch", None, None)
    both = ("stream", "batch")
    return jax.shard_map(
        on_device,
        mesh=mesh,
        in_specs=(rows, P("batch"), rows, P(), P(), P(), P(), P(), P()),
        out_specs=(rows, rows, P(both, None), P(both, None), P(None, both), P(both, None), P(), P(), P()),
        check_vma=False,
    )
```

```python
import functools

import jax
import jax.numpy as jnp
import numpy as np
from jax import lax
from jax.experimental import pallas as pl
from jax.experimental.pallas import tpu as pltpu
from jax.sharding import PartitionSpec as P

f32 = jnp.float32
bf16 = jnp.bfloat16

HD = 64
BLK = 16
EPS = 1e-06
NEG = -1e30
PW = 2 * HD
T = 128
R = 256
AHEAD = 2
FC = 768
SCALE = HD**-0.5
BIG = 61
GROUPS = 3

COST = pl.CostEstimate(flops=1 << 20, bytes_accessed=1 << 16, transcendentals=0)
LONG = pl.CostEstimate(flops=1 << 35, bytes_accessed=1 << 26, transcendentals=0)

SMEM = pl.BlockSpec(memory_space=pltpu.SMEM)
IN_VMEM = pl.BlockSpec(memory_space=pltpu.VMEM)


def params(mib):
    return pltpu.CompilerParams(vmem_limit_bytes=mib << 20)


def shape(dims, dtype):
    return jax.ShapeDtypeStruct(dims, dtype)


def pinned(*arrays):
    return [pltpu.with_memory_space_constraint(a, pltpu.HBM) for a in arrays]


def nn(a, b):
    return jnp.dot(a, b, preferred_element_type=f32)


def nt(a, b):
    return lax.dot_general(a, b, (((1,), (1,)), ((), ())), preferred_element_type=f32)


def tn(a, b):
    return lax.dot_general(a, b, (((0,), (0,)), ((), ())), preferred_element_type=f32)


def whole(dims):
    return pl.BlockSpec(dims, lambda *_: (0,) * len(dims), pipeline_mode=pl.Buffered(1))


def inv_rms(v):
    return lax.rsqrt(jnp.mean(v * v, axis=-1, keepdims=True) + EPS)


def norm_back(v, gain, grad):
    r = inv_rms(v)
    unit = v * r
    scaled = grad * gain
    inner = jnp.mean(scaled * unit, axis=-1, keepdims=True)
    return r * (scaled - unit * inner), grad * unit


def rotary_tables(length):
    half = HD // 2
    freqs = np.exp(-np.log(10000.0) * np.arange(half) / half).astype(np.float32)
    angles = (np.arange(length, dtype=np.float32)[:, None] * freqs[None, :]).astype(np.float64)
    return np.cos(angles).astype(np.float32), np.sin(angles).astype(np.float32)


def rotated(v, cosine, signed, sign):
    first = lax.broadcasted_iota(jnp.int32, (1, PW), 1) % HD < HD // 2
    outs = []
    for c in range(0, v.shape[1], PW):
        part = v[:, c : c + PW]
        partner = jnp.where(first, pltpu.roll(part, PW - HD // 2, 1), pltpu.roll(part, HD // 2, 1))
        outs.append(part * cosine + partner * (signed * sign))
    return outs[0] if len(outs) == 1 else jnp.concatenate(outs, axis=1)


def in_turn(count, *stages):
    def turn(t, carry):
        state = ()
        for stage in stages:
            state = stage(t, *state)
        return carry

    lax.fori_loop(0, count, turn, 0)


def token_weight(start, length, rows):
    return lax.broadcasted_iota(jnp.int32, (rows, 1), 0) + start < length


def row_sum(v):
    return jnp.sum(v, axis=0, keepdims=True)


def by_pairs(ref, rows, value):
    for p in range(ref.shape[0]):
        ref[p, rows, :] = value[:, p * PW : (p + 1) * PW].astype(ref.dtype)


def stacked(tile, low):
    zero = jnp.zeros_like(tile)
    return jnp.concatenate([jnp.where(low, tile, zero), jnp.where(low, zero, tile)], axis=0)


def unstacked(tile_t):
    half = lax.broadcasted_iota(jnp.int32, (PW, 1), 0) < HD
    return jnp.where(half, tile_t[:, :T], tile_t[:, T:])


def chunks_of(i):
    out, j = [], 0
    while j < i:
        n = 2 if i - j >= 2 else 1
        out.append((j * T, n * T))
        j += n
    return out


def edge_bias(ref, noisy):
    row = lax.broadcasted_iota(jnp.int32, (T, 2 * T), 0) // BLK
    col = (lax.broadcasted_iota(jnp.int32, (T, 2 * T), 1) % T) // BLK
    own = jnp.logical_or(row == col, jnp.logical_and(row < col, noisy == 0))
    other = jnp.logical_and(row < col, noisy == 1)
    ref[:T, :] = jnp.where(own, 0.0, NEG)
    ref[T:, :] = jnp.where(other, 0.0, NEG)


def masked(s, start, length):
    pos = lax.broadcasted_iota(jnp.int32, s.shape, 0) + start
    return jnp.where(pos < length, s, NEG)


def over_rows(op, v):
    return op(v.reshape(v.shape[0] // 8, 8, v.shape[1]), axis=0)


def attend_pair(length, q, ko, vo, kc, vc, store, lse, vo_t, vc_t, scores, bias):
    seq = q.shape[0]
    low = lax.broadcasted_iota(jnp.int32, (1, PW), 1) < HD
    vo_t[...] = vo[...].T
    vc_t[...] = vc[...].T

    def score(i):
        at = pl.ds(i * T, T)
        q2 = stacked(q[at, :] * bf16(SCALE), low)
        buf = scores.at[i % AHEAD]
        edge = nt(jnp.concatenate([ko[at, :], kc[at, :]], 0), q2) + bias[...]
        own = masked(edge[:T], i * T, length)
        other = masked(edge[T:], i * T, length)
        buf[pl.ds(0, T), :] = own
        buf[pl.ds(T, T), :] = other
        top = over_rows(jnp.max, jnp.maximum(own, other))
        for start, size in chunks_of(i):
            s = masked(nt(kc[pl.ds(start, size), :], q2), start, length)
            buf[pl.ds(2 * T + start, size), :] = s
            top = jnp.maximum(top, over_rows(jnp.max, s))
        return jnp.max(top, axis=0, keepdims=True)

    def mix(i, top):
        at = pl.ds(i * T, T)
        buf = scores.at[i % AHEAD]
        p = jnp.exp(buf[pl.ds(0, 2 * T), :] - top)
        total = over_rows(jnp.sum, p)
        acc = nn(jnp.concatenate([vo_t[:, at], vc_t[:, at]], 1), p.astype(bf16))
        for start, size in chunks_of(i):
            p = jnp.exp(buf[pl.ds(2 * T + start, size), :] - top)
            total = total + over_rows(jnp.sum, p)
            acc = acc + nn(vc_t[:, pl.ds(start, size)], p.astype(bf16))
        total = row_sum(total)
        lse[0, pl.ds(i, 1), :] = top + jnp.log(total)
        store(at, unstacked(acc * (1.0 / total)))

    tops = {}
    for i in range(seq // T + AHEAD - 1):
        if i < seq // T:
            tops[i] = score(i)
        if i >= AHEAD - 1:
            mix(i - AHEAD + 1, tops.pop(i - AHEAD + 1))


def turned_back(v, cosine, sine):
    quarter = HD // 2
    a, b, c, d = (v[i * quarter : (i + 1) * quarter] for i in range(4))
    return jnp.concatenate(
        [a * cosine + b * sine, b * cosine - a * sine, c * cosine + d * sine, d * cosine - c * sine]
    )


def attend_back_kernel(
    info, q, ko, vo, kc, vc, o, do, lse, cosine, sine, dq, keep, send, ko_t, kc_t, dko, dvo, dkc, dvc, bias
):
    noisy, length = info[0], info[1]
    q, ko, vo, kc, vc = (ref.at[0] for ref in (q, ko, vo, kc, vc))
    seq = q.shape[0]
    low = lax.broadcasted_iota(jnp.int32, (1, PW), 1) < HD

    @pl.when(pl.program_id(0) == 0)
    def _():
        edge_bias(bias, noisy)

    ko_t[...] = ko[...].T
    kc_t[...] = kc[...].T

    def tile(i):
        at = pl.ds(i * T, T)
        prod = (do[at, :].astype(f32) * o[at, :].astype(f32)).T
        delta = jnp.concatenate([row_sum(prod[:HD]), row_sum(prod[HD:])], 1)
        q2 = stacked(q[at, :] * bf16(SCALE), low)
        return q2, stacked(do[at, :], low), lse[0, pl.ds(i, 1), :], delta

    def products(i, start, size, q2, do2):
        if start is None:
            at = pl.ds(i * T, T)
            s = nt(jnp.concatenate([ko[at, :], kc[at, :]], 0), q2) + bias[...]
            s = jnp.concatenate([masked(s[:T], i * T, length), masked(s[T:], i * T, length)], 0)
            return s, nt(jnp.concatenate([vo[at, :], vc[at, :]], 0), do2)
        rows = pl.ds(start, size)
        return masked(nt(kc[rows, :], q2), start, length), nt(vc[rows, :], do2)

    def gather(i, start, size, q2, do2, p, ds, dq_t):
        at = pl.ds(i * T, T)
        dv, dk = nn(p, do2), nn(ds, q2)
        if start is None:
            dvo[at, :] = dv[:T]
            dko[at, :] = dk[:T]
            dvc[at, :] = dv[T:]
            dkc[at, :] = dk[T:]
            return nn(jnp.concatenate([ko_t[:, at], kc_t[:, at]], 1), ds)
        rows = pl.ds(start, size)
        dvc[rows, :] += dv
        dkc[rows, :] += dk
        return dq_t + nn(kc_t[:, rows], ds)

    work = [(i, *c) for i in range(seq // T) for c in [(None, None)] + chunks_of(i)]
    tiles, made, weighed, dq_t = {}, {}, {}, None
    for n in range(len(work) + 2):
        if n < len(work):
            i = work[n][0]
            if i not in tiles:
                tiles[i] = tile(i)
            made[n] = products(*work[n], *tiles[i][:2])
        if 0 <= n - 1 < len(work):
            _, _, norm, delta = tiles[work[n - 1][0]]
            s, dp = made.pop(n - 1)
            p = jnp.exp(s - norm)
            weighed[n - 1] = p.astype(bf16), (p * (dp - delta)).astype(bf16)
        if n >= 2:
            i, start, size = work[n - 2]
            dq_t = gather(i, start, size, *tiles[i][:2], *weighed.pop(n - 2), dq_t)
            if n == len(work) + 1 or work[n - 1][0] != i:
                at = pl.ds(i * T, T)
                out = turned_back(unstacked(dq_t), cosine[:, at], sine[:, at]) * SCALE
                dq[at, :] = out.T.astype(bf16)
    clean = (1 - noisy).astype(f32)
    for at, own, other in ((0, dko, dkc), (1, dvo, dvc)):
        keep[at] = (own[...] + clean * other[...]).astype(bf16)
        send[at] = other[...].astype(bf16)


def attend_back(info, first, pairs, q, ko, vo, kc, vc, o, do, lse, cosine, sine):
    seq = q.shape[1]
    width = pairs * PW
    heads = pl.BlockSpec((1, seq, PW), lambda h: (first + h, 0, 0))
    source = pl.BlockSpec((seq, PW), lambda h: (0, first + h))
    both = pl.BlockSpec((2, seq, PW), lambda h: (0, 0, h))
    lines = pl.BlockSpec((1, seq // T, 2 * T), lambda h: (first + h, 0, 0))
    table = whole((HD // 2, seq))
    return pl.pallas_call(
        attend_back_kernel,
        grid=(pairs,),
        in_specs=[SMEM] + [heads] * 5 + [source] * 2 + [lines, table, table],
        out_specs=[pl.BlockSpec((seq, PW), lambda h: (0, h)), both, both],
        out_shape=[shape((seq, width), bf16)] + [shape((2, seq, width), bf16)] * 2,
        scratch_shapes=[pltpu.VMEM((PW, seq), bf16)] * 2
        + [pltpu.VMEM((seq, PW), f32)] * 4
        + [pltpu.VMEM((2 * T, 2 * T), f32)],
        compiler_params=params(24),
        cost_estimate=LONG,
        name="attend_back",
    )(info, *pinned(q, ko, vo, kc, vc, o, do), lse, cosine, sine)


C0 = 0.7978845608028654
C1 = C0 * 0.044715


def layer_kernel(
    info, gain1_line, gain2_line, cosine_t, sine_t, received, x_any, wqkv_any, wo_any, dy_any,
    w1_any, w2_any,
    q_out, ko_out, vo_out, kc_out, vc_out, h1t_out, o_out, lse_out, out_any, dx2_any, do_any,
    up_send, up_keep, down_send, down_keep, g_send, g_keep, cosine_out, signed_out, sums,
    x, wqkv, cosine, signed, q, ko, vo, h1t, wo, dy, w1, w2,
    kc, vc, vo_t, vc_t, scores, bias, o, o_t, lse, x2, h2, m, dh, act, du, up_grad, down_grad, half_grads,
    sem_in, sem_1, sem_2, sem_out, sem_up, sem_down, sem_tile,
):
    noisy, length = info[0], info[1]
    seq, width = x.shape
    chunks, pairs, tiles = w1.shape[0], kc.shape[0], seq // R
    copy = pltpu.make_async_copy
    gain1, gain2 = gain1_line[...].reshape(1, width), gain2_line[...].reshape(1, width)

    def weights(c):
        place = lax.rem(c + (chunks // 2) * (1 - noisy), chunks) * FC
        place = pl.multiple_of(place, FC)
        return (
            copy(w1_any.at[:, pl.ds(place, FC)], w1.at[c], sem_1.at[c]),
            copy(w2_any.at[pl.ds(place, FC), :], w2.at[c], sem_2.at[c]),
        )

    sources = (
        (x_any, x),
        (wqkv_any, wqkv),
        (wo_any, wo),
        (dy_any, dy),
    )
    loads = [copy(a, b, sem_in.at[i]) for i, (a, b) in enumerate(sources)]
    for load in loads[:2]:
        load.start()
    sums[...] = jnp.zeros_like(sums)
    edge_bias(bias, noisy)
    def widen(t):
        rows = pl.ds(pl.multiple_of(t * PW, PW), PW)
        c, d = cosine_t[:, rows].T, sine_t[:, rows].T
        cosine[rows, :] = jnp.concatenate([c, c, c, c], axis=1)
        signed[rows, :] = jnp.concatenate([-d, d, -d, d], axis=1)
        return ()

    in_turn(seq // PW, widen)
    tables_out = [copy(cosine, cosine_out, sem_out.at[10]), copy(signed, signed_out, sem_out.at[11])]
    span = lambda t: pl.ds(pl.multiple_of(t * R, R), R)

    loads[0].wait()

    def own_norm(t):
        value = x[span(t), :].astype(f32)
        h1 = (value * inv_rms(value) * gain1).astype(bf16)
        h2[span(t), :] = h1
        h1t[:, span(t)] = h1.T
        weight = token_weight(t * R, length, R)
        sums[0:1, :] += row_sum(jnp.where(weight, value * value, 0.0))
        return ()

    in_turn(tiles, own_norm)
    loads[1].wait()
    for load in loads[2:]:
        load.start()

    def own_product(t):
        return tuple(nn(h2[span(t), :], wqkv[:, i * width : (i + 1) * width]) for i in range(3))

    def own_turn(t, a, b, c):
        tables = (cosine[span(t), :], signed[span(t), :], 1.0)
        by_pairs(q, span(t), rotated(a, *tables))
        by_pairs(ko, span(t), rotated(b, *tables))
        by_pairs(vo, span(t), c)
        return ()

    def clean_norm(t):
        value = jnp.where(noisy == 1, received[span(t), :].astype(f32), x[span(t), :].astype(f32))
        o[span(t), :] = (value * inv_rms(value) * gain1).astype(bf16)
        return ()

    def clean_product(t):
        return tuple(nn(o[span(t), :], wqkv[:, i * width : (i + 1) * width]) for i in (1, 2))

    def clean_turn(t, a, b):
        by_pairs(kc, span(t), rotated(a, cosine[span(t), :], signed[span(t), :], 1.0))
        by_pairs(vc, span(t), b)
        return ()

    in_turn(tiles, own_product, own_turn)
    stores = [
        copy(a, b, sem_out.at[6 + i])
        for i, (a, b) in enumerate(((q, q_out), (ko, ko_out), (vo, vo_out), (h1t, h1t_out)))
    ]
    stores += tables_out
    for store in stores:
        store.start()
    in_turn(tiles, clean_norm, clean_product, clean_turn)
    more = [copy(kc, kc_out, sem_out.at[0]), copy(vc, vc_out, sem_out.at[1])]
    for store in more:
        store.start()
    stores += more

    for c in range(chunks):
        for load in weights(c):
            load.start()

    def one_pair(p, carry):
        lanes = pl.ds(pl.multiple_of(p * PW, PW), PW)

        def keep(at, tile_t):
            o_t[lanes, at] = tile_t.astype(bf16)
            o[at, lanes] = tile_t.T.astype(bf16)

        heads = (ref.at[p] for ref in (q, ko, vo, kc, vc))
        attend_pair(length, *heads, keep, lse.at[pl.ds(p, 1)], vo_t, vc_t, scores, bias)
        return carry

    lax.fori_loop(0, pairs, one_pair, 0)
    mixed_out = copy(o, o_out, sem_out.at[2])
    mixed_out.start()
    stores += [copy(lse, lse_out, sem_out.at[3])]
    stores[-1].start()

    for load in loads[2:]:
        load.wait()

    def join_product(t):
        return (nn(o[span(t), :], wo[...]),)

    def join_norm(t, branch):
        value = x[span(t), :].astype(f32) + branch
        x2[span(t), :] = value
        h2[span(t), :] = (value * inv_rms(value) * gain2).astype(bf16)
        m[span(t), :] = jnp.zeros_like(value)
        dh[span(t), :] = jnp.zeros_like(value)
        weight = token_weight(t * R, length, R)
        sums[1:2, :] += row_sum(jnp.where(weight, branch * branch, 0.0))
        return ()

    in_turn(tiles, join_product, join_norm)

    def grad_stores(c, up, down):
        slot = lax.rem(c, 2)
        rows = pl.ds(pl.multiple_of(lax.rem(c, chunks // 2) * FC, FC), FC)
        return (
            copy(up_grad.at[slot], up.at[rows, :], sem_up.at[slot]),
            copy(down_grad.at[slot], down.at[rows, :], sem_down.at[slot]),
        )

    def one_chunk(c, carry):
        for load in weights(c):
            load.wait()
        up, down = w1.at[c], w2.at[c]
        made = {}
        for t in range(-R, seq, R):
            if t + R < seq:
                rows = pl.ds(t + R, R)
                made[t + R] = nn(h2[rows, :], up[...]), nt(dy[rows, :], down[...])
            if t < 0:
                continue
            rows = pl.ds(t, R)
            u, da = made.pop(t)
            sq = u * u
            half = 0.5 * jnp.tanh(u * (C0 + C1 * sq)) + 0.5
            low = (u * half).astype(bf16)
            slope = half + u * (2.0 * half * (1.0 - half)) * (C0 + 3.0 * C1 * sq)
            back = (da * slope).astype(bf16)
            act[rows, :] = low
            du[rows, :] = back
            m[rows, :] += nn(low, down[...])
            dh[rows, :] += nt(back, up[...])

        @pl.when(c >= 2)
        def _():
            for store in grad_stores(c, up_send, down_send):
                store.wait()

        slot = lax.rem(c, 2)
        down_grad[slot] = tn(act[...], dy[...]).astype(bf16)
        up_grad[slot] = tn(du[...], h2[...]).astype(bf16)

        @pl.when(c < chunks // 2)
        def _():
            for store in grad_stores(c, up_send, down_send):
                store.start()

        @pl.when(c >= chunks // 2)
        def _():
            for store in grad_stores(c, up_keep, down_keep):
                store.start()

        return carry

    lax.fori_loop(0, chunks, one_chunk, 0)

    mixed_out.wait()

    def tile_stores(t):
        return (
            copy(h2.at[span(t), :], out_any.at[span(t), :], sem_tile.at[t, 0]),
            copy(x2.at[span(t), :], dx2_any.at[span(t), :], sem_tile.at[t, 1]),
            copy(o.at[span(t), :], do_any.at[span(t), :], sem_tile.at[t, 2]),
        )

    def middle_norm(t):
        value = x2[span(t), :]
        mixed = m[span(t), :]
        weight = token_weight(t * R, length, R)
        sums[2:3, :] += row_sum(jnp.where(weight, mixed * mixed, 0.0))
        grad, gain_terms = norm_back(value, gain2, dh[span(t), :])
        sums[3:4, :] += row_sum(gain_terms)
        grad = grad + dy[span(t), :].astype(f32)
        h2[span(t), :] = (value + mixed).astype(bf16)
        x2[span(t), :] = grad
        x[span(t), :] = grad.astype(bf16)
        return ()

    def middle_product(t):
        o[span(t), :] = nt(x[span(t), :], wo[...]).astype(bf16)
        for store in tile_stores(t):
            store.start()
        return ()

    in_turn(tiles, middle_norm, middle_product)
    half = width // 2
    mine = pl.multiple_of(noisy * half, half)
    half_grads[0] = nn(o_t[pl.ds(half - mine, half), :], x[...]).astype(bf16)
    half_grads[1] = nn(o_t[pl.ds(mine, half), :], x[...]).astype(bf16)
    more = [copy(half_grads.at[0], g_send, sem_out.at[4]), copy(half_grads.at[1], g_keep, sem_out.at[5])]
    for store in more:
        store.start()
    stores += more
    for c in range(chunks - 2, chunks):
        stores += grad_stores(c, up_keep, down_keep)
    for t in range(tiles):
        stores += tile_stores(t)
    for store in stores:
        store.wait()


def layer(info, gain1, gain2, cosine_t, sine_t, received, x, wqkv, wo, dy, w1, w2):
    seq, width = x.shape
    hidden = w1.shape[1]
    tiles, pairs, chunks = seq // R, width // PW, hidden // FC
    anywhere = pl.BlockSpec(memory_space=pl.ANY)
    vmem = pltpu.VMEM
    dma = pltpu.SemaphoreType.DMA
    heads = (pairs, seq, PW)
    flat = (seq, width)
    outs = (
        [shape(heads, bf16)] * 5
        + [shape((width, seq), bf16), shape(flat, bf16), shape((pairs, seq // T, 2 * T), f32)]
        + [shape(flat, bf16), shape(flat, f32), shape(flat, bf16)]
        + [shape((hidden // 2, width), bf16)] * 4
        + [shape((width // 2, width), bf16)] * 2
        + [shape((seq, PW), f32)] * 2
        + [shape((8, width), f32)]
    )
    return pl.pallas_call(
        layer_kernel,
        in_specs=[SMEM] + [IN_VMEM] * 5 + [anywhere] * 6,
        out_specs=[anywhere] * 19 + [IN_VMEM],
        out_shape=outs,
        scratch_shapes=[vmem(flat, bf16)]
        + [vmem(wqkv.shape, bf16), vmem((seq, PW), f32), vmem((seq, PW), f32)]
        + [vmem(heads, bf16)] * 3
        + [vmem((width, seq), bf16), vmem((width, width), bf16), vmem(flat, bf16)]
        + [vmem((chunks, width, FC), bf16), vmem((chunks, FC, width), bf16)]
        + [vmem(heads, bf16)] * 2
        + [vmem((PW, seq), bf16)] * 2
        + [vmem((AHEAD, seq + T, 2 * T), f32), vmem((2 * T, 2 * T), f32)]
        + [vmem(flat, bf16), vmem((width, seq), bf16)]
        + [vmem((pairs, seq // T, 2 * T), f32)]
        + [vmem(flat, f32), vmem(flat, bf16)]
        + [vmem(flat, f32)] * 2
        + [vmem((seq, FC), bf16)] * 2
        + [vmem((2, FC, width), bf16)] * 2
        + [vmem((2, width // 2, width), bf16)]
        + [dma((4,)), dma((chunks,)), dma((chunks,)), dma((12,)), dma((2,)), dma((2,)), dma((tiles, 3))],
        compiler_params=params(BIG),
        cost_estimate=LONG,
        name="layer",
    )(info, gain1, gain2, cosine_t, sine_t, received, *pinned(x, wqkv, wo, dy, w1, w2))


def weigh_kernel(first, info, dq, keep, got, cosine, signed, h1t, wqkv, sums, dkv, g_send, g_keep, small):
    width, half = wqkv.shape[0], wqkv.shape[0] // 2
    mine = pl.multiple_of(info[0] * half, half)
    dk = keep[0].astype(f32) + got[0].astype(f32)
    dkv[0] = rotated(dk, cosine[...], signed[...], -1.0).astype(bf16)
    dkv[1] = (keep[1].astype(f32) + got[1].astype(f32)).astype(bf16)
    small[...] = sums[...]
    for out, start in ((g_send, half - mine), (g_keep, mine)):
        rows = pl.ds(start, half)
        terms = 0.0
        for i, part in enumerate((dq, dkv.at[0], dkv.at[1])):
            total = nn(h1t[rows, :], part[...])
            out[i] = total.astype(bf16)
            at = i * width + first * PW
            weighted = total * wqkv[rows, at : at + total.shape[1]].astype(f32)
            for c in range(0, total.shape[1], PW):
                terms = terms + weighted[:, c : c + PW]
        line = jnp.sum(terms.T, axis=0, keepdims=True)
        lanes = lax.broadcasted_iota(jnp.int32, (1, width), 1)
        inside = jnp.logical_and(lanes >= start, lanes < start + half)
        small[4:5, :] += jnp.where(inside, jnp.concatenate([line, line], axis=1), 0.0)
    small[5:6, :] = jnp.full((1, width), info[1].astype(f32))


def weigh(info, first, dq, keep, got, tables, h1t, wqkv, sums):
    seq, width = dq.shape
    tall = h1t.shape[0]
    return pl.pallas_call(
        functools.partial(weigh_kernel, first),
        in_specs=[SMEM] + [IN_VMEM] * 8,
        out_specs=[IN_VMEM] * 4,
        out_shape=[shape((2, seq, width), bf16)]
        + [shape((3, tall // 2, width), bf16)] * 2
        + [shape(sums.shape, f32)],
        compiler_params=params(24),
        cost_estimate=LONG,
        name="weigh",
    )(info, dq, keep, got, *tables, h1t, wqkv, sums)


def finish_kernel(parts, tiles, x, dx2, wqkv, gain_line, *refs):
    dx_any, dx, sem = refs[-3:]
    dqs, dkvs = refs[:parts], refs[parts : 2 * parts]
    gain = gain_line[...].reshape(1, x.shape[1])

    def store(t):
        rows = pl.ds(pl.multiple_of(t * R, R), R)
        return pltpu.make_async_copy(dx.at[rows, :], dx_any.at[rows, :], sem.at[t])

    def some_rows(t, carry):
        rows = pl.ds(pl.multiple_of(t * R, R), R)
        grads = [r[rows, :] for r in dqs] + [r[0, rows, :] for r in dkvs] + [r[1, rows, :] for r in dkvs]
        dh = nt(jnp.concatenate(grads, axis=1), wqkv[...])
        grad, _ = norm_back(x[rows, :].astype(f32), gain, dh)
        dx[rows, :] = (dx2[rows, :] + grad).astype(bf16)
        store(t).start()
        return carry

    lax.fori_loop(*tiles, some_rows, 0)
    for t in range(*tiles):
        store(t).wait()


def finish(tiles, x, dx2, dqs, dkvs, weight, gain, before):
    anywhere = pl.BlockSpec(memory_space=pl.ANY)
    ins = 4 + len(dqs) + len(dkvs)
    return pl.pallas_call(
        functools.partial(finish_kernel, len(dqs), tiles),
        in_specs=[IN_VMEM] * ins + [anywhere] * len(before),
        out_specs=anywhere,
        out_shape=shape(x.shape, bf16),
        scratch_shapes=[pltpu.VMEM(x.shape, bf16), pltpu.SemaphoreType.DMA((x.shape[0] // R,))],
        input_output_aliases={ins: 0} if before else {},
        compiler_params=params(24),
        cost_estimate=COST if before else LONG,
        name="finish",
    )(x, dx2, weight, gain, *dqs, *dkvs, *before)


def bit_orders(count, groups):
    bits = [1 << i for i in range(count.bit_length() - 1)]
    if groups == 2:
        return [bits, bits[1::-1] + bits[2:]]
    return [bits[g:-1] + bits[:g] + bits[-1:] for g in range(groups)]


def exchange(value, axis, bit):
    size = lax.axis_size(axis)
    return lax.ppermute(value, axis, [(i, i ^ bit) for i in range(size)])


def distance(order, place):
    out = 0
    for i, bit in enumerate(order):
        out = out + ((place >> (len(order) - 1 - i)) & 1) * bit
    return out


SUMS = 8


def halves(value):
    high = value.astype(bf16)
    return high, (value - high.astype(f32)).astype(bf16)


def put_sums(value, kept, block):
    high, low = halves(value)
    lines = kept.shape[0]
    block[:lines, :] = high
    block[lines : 2 * lines, :] = low
    kept[...] = high.astype(f32) + low.astype(f32)


def got_sums(block):
    lines = block.shape[0] // 2
    return block[:lines, :].astype(f32) + block[lines:, :].astype(f32)


def start_kernel(orders, sources, small, me, *refs):
    groups = len(orders)
    arrays = max(a for source in sources for a, _, _ in source) + 1
    ins, outs = refs[: 2 * arrays], refs[len(refs) - 2 * groups :]
    half = outs[0].shape[0]
    for g, order in enumerate(orders):
        for side in range(2):

            def one(r, carry, g=g, order=order, side=side):
                part = me[0] ^ distance(order, r + side * half)
                out = outs[2 * g + side]
                row = 0
                for a, where, unit in sources[g]:
                    kept, got = ins[2 * a : 2 * a + 2]
                    place = where(part)
                    size, wide = kept.shape[1], out.shape[-1]
                    lanes = slice(unit * wide, (unit + 1) * wide)
                    total = kept[place, :, lanes].astype(f32) + got[place, :, lanes].astype(f32)
                    if len(out.shape) == 3:
                        out[r, row : row + size, :] = total.astype(bf16)
                    else:
                        start = pl.multiple_of(r * outs[0].shape[1] + row, 8)
                        out[pl.ds(start, size), :] = total.astype(bf16)
                    row += size
                return carry

            lax.fori_loop(0, half, one, 0)
    if small:
        here, there, kept = refs[2 * arrays : 2 * arrays + 3]
        total = here[...] + there[...]
        if small == "rides":
            wide = kept.shape[1]
            total = jnp.concatenate([total[:, c : c + wide] for c in range(0, total.shape[1], wide)], axis=0)
            put_sums(total, kept, outs[1].at[pl.ds(half * outs[0].shape[1], 2 * kept.shape[0]), :])
        else:
            kept[...] = total


def travelling(count, rows, width, lines):
    return shape((count * rows + 2 * lines, width) if lines else (count, rows, width), bf16)


def start_sum(me, kept, got, sources, width, orders, small, rides):
    count = 1 << len(orders[0])
    half = count // 2
    rows = [sum(kept[a].shape[1] for a, _, _ in source) for source in sources]
    lines = small[0].size // width if rides else 0
    cols = width // 3
    args = [a for pair in zip(kept, got, strict=True) for a in pair]
    sums = []
    for g in range(len(orders)):
        sums += [shape((half, rows[g], width), bf16), travelling(half, rows[g], width, 0 if g else lines)]
    mode = "rides" if rides else "alone" if small else ""
    if small:
        specs = dict(
            in_specs=[SMEM] + [IN_VMEM] * (len(args) + 2),
            out_specs=[IN_VMEM] * (1 + len(sums)),
            out_shape=[shape((lines, width) if rides else small[0].shape, f32)] + sums,
        )
    else:
        block = lambda a: pl.BlockSpec((a.shape[0], a.shape[1], cols), lambda c: (0, 0, c))
        specs = dict(
            grid=(width // cols,),
            in_specs=[SMEM] + [block(a) for a in args],
            out_specs=[block(a) for a in sums],
            out_shape=sums,
        )
    outs = pl.pallas_call(
        functools.partial(start_kernel, orders, sources, mode),
        compiler_params=params(30),
        cost_estimate=COST,
        name="start_sum",
        **specs,
    )(me, *args, *small)
    small, outs = list(outs[: len(outs) - len(sums)]), outs[len(outs) - len(sums) :]
    return list(outs[0::2]), list(outs[1::2]), small


def block_of(ref, r, size, row=0, step=0):
    if len(ref.shape) == 3:
        return ref.at[r, pl.ds(row, size), :]
    start = r * (step or size) + row
    return ref.at[pl.ds(start if isinstance(start, int) else pl.multiple_of(start, 8), size), :]


def step_kernel(groups, merge, mode, *refs):
    kept, got = refs[:groups], refs[groups : 2 * groups]
    outs = refs[2 * groups + (2 if mode == "alone" else 1 if mode else 0) :]
    count = kept[0].shape[0]
    half = count // 2

    def one(r, carry):
        row = 0
        for g in range(groups):
            keep, send = outs[:2] if merge else outs[2 * g : 2 * g + 2]
            size = kept[g].shape[1]
            for out, block in ((keep, r), (send, r + half)):
                total = kept[g][block].astype(f32) + block_of(got[g], block, size)[...].astype(f32)
                block_of(out, r, size, row, keep.shape[1])[...] = total.astype(bf16)
            row += size if merge else 0
        return carry

    lax.fori_loop(0, half, one, 0)
    if mode == "rides":
        total = refs[2 * groups][...] + got_sums(got[0][count * kept[0].shape[1] :])
        put_sums(total, outs[-1], outs[1].at[pl.ds(half * outs[0].shape[1], 2 * total.shape[0]), :])
    elif mode:
        outs[-1][...] = refs[2 * groups][...] + refs[2 * groups + 1][...]


def step_sum(kept, got, small, merge, rides):
    groups = len(kept)
    half = kept[0].shape[0] // 2
    rows = [a.shape[1] for a in kept]
    width = kept[0].shape[2]
    args = [*kept, *got, *small]
    sums = []
    for g, r in enumerate([sum(rows)] if merge else rows):
        sums += [shape((half, r, width), bf16), travelling(half, r, width, 0 if g or not rides else small[0].shape[0])]
    outs = pl.pallas_call(
        functools.partial(step_kernel, groups, merge, "rides" if rides else "alone" if small else ""),
        in_specs=[IN_VMEM] * len(args),
        out_specs=[IN_VMEM] * (len(sums) + len(small[:1])),
        out_shape=sums + [shape(a.shape, f32) for a in small[:1]],
        compiler_params=params(16),
        cost_estimate=COST if small or half == 1 else LONG,
        name="step_sum",
    )(*args)
    return list(outs[0 : len(sums) : 2]), list(outs[1 : len(sums) : 2]), list(outs[len(sums) :])


def feed_end_kernel(kept, got, down, up, out):
    total = kept[0].astype(f32) + got[0].astype(f32)
    tall, few = down.shape[0] // GROUPS, out.shape[0] // GROUPS
    ups = []
    for g in range(GROUPS):
        row = g * (2 * tall + few)
        down[g * tall : (g + 1) * tall, :] = total[row : row + tall]
        ups.append(total[row + tall : row + 2 * tall])
        out[g * few : (g + 1) * few, :] = total[row + 2 * tall : row + 2 * tall + few]
    up[...] = jnp.concatenate(ups, axis=0).T


def feed_end(kept, got, tall, few):
    width = kept.shape[2]
    return pl.pallas_call(
        feed_end_kernel,
        in_specs=[IN_VMEM] * 2,
        out_specs=[IN_VMEM] * 3,
        out_shape=[shape((tall, width), f32), shape((width, tall), f32), shape((few, width), f32)],
        compiler_params=params(16),
        cost_estimate=COST,
        name="feed_end",
    )(kept, got)


def qkv_end_kernel(places, rides, gain_line, kept, got, *refs):
    out, gain1, gain2, rms = refs[-4:]
    tall = out.shape[0]
    width = gain1.shape[0]
    cols = kept.shape[2]
    there = got[: kept.shape[1]] if rides else got[0]
    total = kept[0].astype(f32) + there.astype(f32)
    for i, at in enumerate(places):
        out[:, at : at + cols] = total[i * tall : (i + 1) * tall]
    if rides:
        sums = refs[0][...] + got_sums(got[kept.shape[1] :])
        sums = jnp.concatenate([sums[r : r + SUMS] for r in range(0, sums.shape[0], SUMS)], axis=1)
    else:
        sums = refs[0][...] + refs[1][...]
    gain2[...] = sums[3:4, :].reshape(width)
    gain1[...] = (sums[4:5, :] / gain_line[...].reshape(1, width)).reshape(width)
    count = jnp.max(sums[5:6, :], axis=1, keepdims=True) * width
    rms[...] = jnp.broadcast_to(jnp.sqrt(jnp.sum(sums, axis=1, keepdims=True) / count), rms.shape)


def qkv_end(places, gain, kept, got, small, tall, wide, rides):
    return pl.pallas_call(
        functools.partial(qkv_end_kernel, places, rides),
        in_specs=[IN_VMEM] * (3 + len(small)),
        out_specs=[IN_VMEM] * 4,
        out_shape=[shape((tall, wide), f32), shape(gain.shape, f32), shape(gain.shape, f32), shape((SUMS, 128), f32)],
        compiler_params=params(16),
        cost_estimate=COST,
        name="qkv_end",
    )(gain, kept, got, *small)


def after(value, *earlier):
    return lax.optimization_barrier((value, earlier))[0]


def sum_parts(me, kept, got, sources, width, small, rides):
    orders = bit_orders(lax.axis_size("batch"), len(sources))
    steps = len(orders[0])
    common = min(i for i in range(steps + 1) if all(order[i:] == orders[0][i:] for order in orders))
    keep, send, small = start_sum(me, kept, got, sources, width, orders, small, rides)
    for i in range(steps):
        got = [exchange(s, "batch", order[i]) for s, order in zip(send, orders[: len(send)], strict=True)]
        if small and not rides:
            small = [small[0], exchange(small[0], "batch", orders[0][i])]
        earlier = yield send[0], got
        if i == steps - 1:
            break
        if earlier is not None:
            keep = after(keep, earlier)
        keep, send, small = step_sum(keep, got, small, i + 1 == common, rides)
    yield keep[0], got[0], small


def on_device(
    inputs, lengths, cotangent, qkv_weight, out_weight, up_weight, down_weight, attn_gain, mlp_gain
):
    seq, width = inputs.shape[2:]
    x = inputs[0, 0]
    dy = cotangent[0, 0]
    count = lax.axis_size("batch")
    stream = lax.axis_index("stream").astype(jnp.int32)
    me = lax.axis_index("batch").astype(jnp.int32).reshape(1)
    info = jnp.stack([stream, lengths[0]])
    cosine, sine = rotary_tables(seq)
    tables_t = (jnp.asarray(cosine.T), jnp.asarray(sine.T))

    received = lax.ppermute(x, "stream", [(0, 1)])
    (
        q, ko, vo, kc, vc, h1t, o, lse, outputs, dx2, do,
        up_send, up_keep, down_send, down_keep, out_send, out_keep, *tables, sums,
    ) = layer(
        info, attn_gain, mlp_gain, *tables_t, received, x, qkv_weight, out_weight, dy, up_weight, down_weight
    )
    down_got, up_got, out_got = (exchange(a, "stream", 1) for a in (down_send, up_send, out_send))

    def by_rows(array):
        return array.reshape(count * GROUPS, array.shape[0] // (count * GROUPS), width)

    heads = (q, ko, vo, kc, vc, o)
    pairs = width // PW // 3
    dq1, keep1, send1 = attend_back(info, 0, pairs, *heads, do, lse, *tables_t)
    got1 = lax.ppermute(send1, "stream", [(1, 0)])
    early = sum_parts(
        me,
        [by_rows(after(a, dq1)) for a in (down_keep, up_keep, out_keep)],
        [by_rows(a) for a in (down_got, up_got, out_got)],
        [[(a, lambda part, g=g: part * GROUPS + g, 0) for a in range(3)] for g in range(GROUPS)],
        width,
        [],
        False,
    )
    token = next(early)[0]
    dq2, keep2, send2 = attend_back(info, pairs, 2 * pairs, *heads, after(do, token), lse, *tables_t)
    got2 = lax.ppermute(send2, "stream", [(1, 0)])
    token = early.send(dq2)[0]
    dkv1, qkv_send1, qkv_keep1, small = weigh(info, 0, dq1, after(keep1, token), got1, tables, h1t, qkv_weight, sums)
    qkv_got1 = exchange(qkv_send1, "stream", 1)
    dkv2, qkv_send2, qkv_keep2, small = weigh(info, pairs, dq2, keep2, got2, tables, h1t, qkv_weight, small)
    qkv_got2 = exchange(qkv_send2, "stream", 1)
    small_got = exchange(small, "stream", 1)
    token = early.send(dkv2)[0]

    tall = width // (2 * count)
    split = lambda a: a.reshape(3 * count, tall, a.shape[2])
    rides = tall % 8 == 0
    runs = [(0, i, 0) for i in range(3)] + [(1, i, c) for i in range(3) for c in range(2)]
    groups = runs[:4], runs[4:]
    late = sum_parts(
        me,
        [split(after(a, token)) for a in (qkv_keep1, qkv_keep2)],
        [split(a) for a in (qkv_got1, qkv_got2)],
        [[(a, lambda part, i=i: i * count + part, c) for a, i, c in group] for group in groups],
        pairs * PW,
        [small, small_got],
        rides,
    )
    token = next(late)[0]
    ends = [dq1, dq2], [dkv1, dkv2], qkv_weight, attn_gain
    tiles = seq // R
    dx = finish((0, tiles // 2), after(x, token), dx2, *ends, [])
    early_out = early.send(dx)
    dx = finish((tiles // 2, tiles), x, after(dx2, early_out[0]), *ends, [dx])
    late.send(dx)
    late_out = late.send(early_out[1])
    while len(late_out) == 2:
        late_out = late.send(None)
    while len(early_out) == 2:
        early_out = early.send(None)
    up_cols = down_keep.shape[0] // count
    down_grad, up_grad, out_grad = feed_end(*early_out[:2], up_cols, tall)
    places = [i * width + (a + c) * pairs * PW for a, i, c in runs]
    qkv_grad, gain1_grad, gain2_grad, rms = qkv_end(places, attn_gain, *late_out, tall, 3 * width, rides)
    return (
        outputs[None, None],
        dx[None, None],
        qkv_grad,
        out_grad,
        up_grad,
        down_grad,
        gain1_grad,
        gain2_grad,
        rms[:3, 0],
    )


def solution(mesh):
    rows = P("stream", "batch", None, None)
    both = ("stream", "batch")
    return jax.shard_map(
        on_device,
        mesh=mesh,
        in_specs=(rows, P("batch"), rows, P(), P(), P(), P(), P(), P()),
        out_specs=(rows, rows, P(both, None), P(both, None), P(None, both), P(both, None), P(), P(), P()),
        check_vma=False,
    )
```

```python
import functools

import jax
import jax.numpy as jnp
import numpy as np
from jax import lax
from jax.experimental import pallas as pl
from jax.experimental.pallas import tpu as pltpu
from jax.sharding import PartitionSpec as P

f32 = jnp.float32
bf16 = jnp.bfloat16

HD = 64
BLK = 16
EPS = 1e-06
NEG = -1e30
PW = 2 * HD
T = 128
R = 256
AHEAD = 2
FC = 768
SCALE = HD**-0.5
BIG = 58
GROUPS = 3

COST = pl.CostEstimate(flops=1 << 20, bytes_accessed=1 << 16, transcendentals=0)
LONG = pl.CostEstimate(flops=1 << 35, bytes_accessed=1 << 26, transcendentals=0)

SMEM = pl.BlockSpec(memory_space=pltpu.SMEM)
IN_VMEM = pl.BlockSpec(memory_space=pltpu.VMEM)


def params(mib):
    return pltpu.CompilerParams(vmem_limit_bytes=mib << 20)


def shape(dims, dtype):
    return jax.ShapeDtypeStruct(dims, dtype)


def pinned(*arrays):
    return [pltpu.with_memory_space_constraint(a, pltpu.HBM) for a in arrays]


def nn(a, b):
    return jnp.dot(a, b, preferred_element_type=f32)


def nt(a, b):
    return lax.dot_general(a, b, (((1,), (1,)), ((), ())), preferred_element_type=f32)


def tn(a, b):
    return lax.dot_general(a, b, (((0,), (0,)), ((), ())), preferred_element_type=f32)


def whole(dims):
    return pl.BlockSpec(dims, lambda *_: (0,) * len(dims), pipeline_mode=pl.Buffered(1))


def inv_rms(v):
    return lax.rsqrt(jnp.mean(v * v, axis=-1, keepdims=True) + EPS)


def norm_back(v, gain, grad):
    r = inv_rms(v)
    unit = v * r
    scaled = grad * gain
    inner = jnp.mean(scaled * unit, axis=-1, keepdims=True)
    return r * (scaled - unit * inner), grad * unit


def rotary_tables(length):
    half = HD // 2
    freqs = np.exp(-np.log(10000.0) * np.arange(half) / half).astype(np.float32)
    angles = (np.arange(length, dtype=np.float32)[:, None] * freqs[None, :]).astype(np.float64)
    return np.cos(angles).astype(np.float32), np.sin(angles).astype(np.float32)


def rotated(v, cosine, signed, sign):
    first = lax.broadcasted_iota(jnp.int32, (1, PW), 1) % HD < HD // 2
    outs = []
    for c in range(0, v.shape[1], PW):
        part = v[:, c : c + PW]
        partner = jnp.where(first, pltpu.roll(part, PW - HD // 2, 1), pltpu.roll(part, HD // 2, 1))
        outs.append(part * cosine + partner * (signed * sign))
    return outs[0] if len(outs) == 1 else jnp.concatenate(outs, axis=1)


def in_turn(count, *stages, at_once=1):
    def turn(n, carry):
        state = [()] * at_once
        for step in range(at_once + len(stages) - 1):
            for k, stage in enumerate(stages):
                if 0 <= step - k < at_once:
                    state[step - k] = stage(at_once * n + step - k, *state[step - k])
        return carry

    lax.fori_loop(0, count // at_once, turn, 0)


def token_weight(start, length, rows):
    return lax.broadcasted_iota(jnp.int32, (rows, 1), 0) + start < length


def row_sum(v):
    return jnp.sum(v, axis=0, keepdims=True)


def by_pairs(ref, rows, value):
    for p in range(ref.shape[0]):
        ref[p, rows, :] = value[:, p * PW : (p + 1) * PW].astype(ref.dtype)


def stacked(tile, low):
    zero = jnp.zeros_like(tile)
    return jnp.concatenate([jnp.where(low, tile, zero), jnp.where(low, zero, tile)], axis=0)


def unstacked(tile_t):
    half = lax.broadcasted_iota(jnp.int32, (PW, 1), 0) < HD
    return jnp.where(half, tile_t[:, :T], tile_t[:, T:])


def chunks_of(i):
    out, j = [], 0
    while j < i:
        n = 2 if i - j >= 2 else 1
        out.append((j * T, n * T))
        j += n
    return out


def edge_bias(ref, noisy):
    row = lax.broadcasted_iota(jnp.int32, (T, 2 * T), 0) // BLK
    col = (lax.broadcasted_iota(jnp.int32, (T, 2 * T), 1) % T) // BLK
    own = jnp.logical_or(row == col, jnp.logical_and(row < col, noisy == 0))
    other = jnp.logical_and(row < col, noisy == 1)
    ref[:T, :] = jnp.where(own, 0.0, NEG)
    ref[T:, :] = jnp.where(other, 0.0, NEG)


def masked(s, start, length):
    pos = lax.broadcasted_iota(jnp.int32, s.shape, 0) + start
    return jnp.where(pos < length, s, NEG)


def over_rows(op, v):
    return op(v.reshape(v.shape[0] // 8, 8, v.shape[1]), axis=0)


def attend_pair(length, q, ko, vo, kc, vc, store, lse, vo_t, vc_t, scores, bias):
    seq = q.shape[0]
    low = lax.broadcasted_iota(jnp.int32, (1, PW), 1) < HD
    vo_t[...] = vo[...].T
    vc_t[...] = vc[...].T

    def score(i):
        at = pl.ds(i * T, T)
        q2 = stacked(q[at, :] * bf16(SCALE), low)
        buf = scores.at[i % AHEAD]
        edge = nt(jnp.concatenate([ko[at, :], kc[at, :]], 0), q2) + bias[...]
        own = masked(edge[:T], i * T, length)
        other = masked(edge[T:], i * T, length)
        buf[pl.ds(0, T), :] = own
        buf[pl.ds(T, T), :] = other
        top = over_rows(jnp.max, jnp.maximum(own, other))
        for start, size in chunks_of(i):
            s = masked(nt(kc[pl.ds(start, size), :], q2), start, length)
            buf[pl.ds(2 * T + start, size), :] = s
            top = jnp.maximum(top, over_rows(jnp.max, s))
        return jnp.max(top, axis=0, keepdims=True)

    def mix(i, top):
        at = pl.ds(i * T, T)
        buf = scores.at[i % AHEAD]
        p = jnp.exp(buf[pl.ds(0, 2 * T), :] - top)
        total = over_rows(jnp.sum, p)
        acc = nn(jnp.concatenate([vo_t[:, at], vc_t[:, at]], 1), p.astype(bf16))
        for start, size in chunks_of(i):
            p = jnp.exp(buf[pl.ds(2 * T + start, size), :] - top)
            total = total + over_rows(jnp.sum, p)
            acc = acc + nn(vc_t[:, pl.ds(start, size)], p.astype(bf16))
        total = row_sum(total)
        lse[0, pl.ds(i, 1), :] = top + jnp.log(total)
        store(at, unstacked(acc * (1.0 / total)))

    tops = {}
    for i in range(seq // T + AHEAD - 1):
        if i < seq // T:
            tops[i] = score(i)
        if i >= AHEAD - 1:
            mix(i - AHEAD + 1, tops.pop(i - AHEAD + 1))


def turned_back(v, cosine, sine):
    quarter = HD // 2
    a, b, c, d = (v[i * quarter : (i + 1) * quarter] for i in range(4))
    return jnp.concatenate(
        [a * cosine + b * sine, b * cosine - a * sine, c * cosine + d * sine, d * cosine - c * sine]
    )


def attend_back_kernel(
    info, q, ko, vo, kc, vc, o, do, lse, cosine, sine, dq, keep, send, ko_t, kc_t, dko, dvo, dkc, dvc, bias
):
    noisy, length = info[0], info[1]
    q, ko, vo, kc, vc = (ref.at[0] for ref in (q, ko, vo, kc, vc))
    seq = q.shape[0]
    low = lax.broadcasted_iota(jnp.int32, (1, PW), 1) < HD

    @pl.when(pl.program_id(0) == 0)
    def _():
        edge_bias(bias, noisy)

    ko_t[...] = ko[...].T
    kc_t[...] = kc[...].T

    def tile(i):
        at = pl.ds(i * T, T)
        prod = (do[at, :].astype(f32) * o[at, :].astype(f32)).T
        delta = jnp.concatenate([row_sum(prod[:HD]), row_sum(prod[HD:])], 1)
        q2 = stacked(q[at, :] * bf16(SCALE), low)
        return q2, stacked(do[at, :], low), lse[0, pl.ds(i, 1), :], delta

    def products(i, start, size, q2, do2):
        if start is None:
            at = pl.ds(i * T, T)
            s = nt(jnp.concatenate([ko[at, :], kc[at, :]], 0), q2) + bias[...]
            s = jnp.concatenate([masked(s[:T], i * T, length), masked(s[T:], i * T, length)], 0)
            return s, nt(jnp.concatenate([vo[at, :], vc[at, :]], 0), do2)
        rows = pl.ds(start, size)
        return masked(nt(kc[rows, :], q2), start, length), nt(vc[rows, :], do2)

    def gather(i, start, size, q2, do2, p, ds, dq_t):
        at = pl.ds(i * T, T)
        dv, dk = nn(p, do2), nn(ds, q2)
        if start is None:
            dvo[at, :] = dv[:T]
            dko[at, :] = dk[:T]
            dvc[at, :] = dv[T:]
            dkc[at, :] = dk[T:]
            return nn(jnp.concatenate([ko_t[:, at], kc_t[:, at]], 1), ds)
        rows = pl.ds(start, size)
        dvc[rows, :] += dv
        dkc[rows, :] += dk
        return dq_t + nn(kc_t[:, rows], ds)

    work = [(i, *c) for i in range(seq // T) for c in [(None, None)] + chunks_of(i)]
    tiles, made, weighed, dq_t = {}, {}, {}, None
    for n in range(len(work) + 2):
        if n < len(work):
            i = work[n][0]
            if i not in tiles:
                tiles[i] = tile(i)
            made[n] = products(*work[n], *tiles[i][:2])
        if 0 <= n - 1 < len(work):
            _, _, norm, delta = tiles[work[n - 1][0]]
            s, dp = made.pop(n - 1)
            p = jnp.exp(s - norm)
            weighed[n - 1] = p.astype(bf16), (p * (dp - delta)).astype(bf16)
        if n >= 2:
            i, start, size = work[n - 2]
            dq_t = gather(i, start, size, *tiles[i][:2], *weighed.pop(n - 2), dq_t)
            if n == len(work) + 1 or work[n - 1][0] != i:
                at = pl.ds(i * T, T)
                out = turned_back(unstacked(dq_t), cosine[:, at], sine[:, at]) * SCALE
                dq[at, :] = out.T.astype(bf16)
    clean = (1 - noisy).astype(f32)
    for at, own, other in ((0, dko, dkc), (1, dvo, dvc)):
        keep[at] = (own[...] + clean * other[...]).astype(bf16)
        send[at] = other[...].astype(bf16)


def attend_back(info, first, pairs, q, ko, vo, kc, vc, o, do, lse, cosine, sine):
    seq = q.shape[1]
    width = pairs * PW
    heads = pl.BlockSpec((1, seq, PW), lambda h: (first + h, 0, 0))
    source = pl.BlockSpec((seq, PW), lambda h: (0, first + h))
    both = pl.BlockSpec((2, seq, PW), lambda h: (0, 0, h))
    lines = pl.BlockSpec((1, seq // T, 2 * T), lambda h: (first + h, 0, 0))
    table = whole((HD // 2, seq))
    return pl.pallas_call(
        attend_back_kernel,
        grid=(pairs,),
        in_specs=[SMEM] + [heads] * 5 + [source] * 2 + [lines, table, table],
        out_specs=[pl.BlockSpec((seq, PW), lambda h: (0, h)), both, both],
        out_shape=[shape((seq, width), bf16)] + [shape((2, seq, width), bf16)] * 2,
        scratch_shapes=[pltpu.VMEM((PW, seq), bf16)] * 2
        + [pltpu.VMEM((seq, PW), f32)] * 4
        + [pltpu.VMEM((2 * T, 2 * T), f32)],
        compiler_params=params(24),
        cost_estimate=LONG,
        name="attend_back",
    )(info, *pinned(q, ko, vo, kc, vc, o, do), lse, cosine, sine)


C0 = 0.7978845608028654
C1 = C0 * 0.044715


def layer_kernel(
    info, gain1_line, gain2_line, cosine_t, sine_t, received, x_any, wqkv_any, wo_any, dy_any,
    w1_any, w2_any,
    q_out, ko_out, vo_out, kc_out, vc_out, h1t_out, o_out, lse_out, out_any, dx2_any, do_any,
    up_send, up_keep, down_send, down_keep, g_send, g_keep, cosine_out, signed_out, sums,
    x, wqkv, cosine, signed, q, ko, vo, h1t, wo, dy, w1, w2,
    kc, vc, vo_t, vc_t, scores, bias, o, o_t, lse, x2, h2, m, dh, act, du, up_grad, down_grad, half_grads,
    sem_in, sem_1, sem_2, sem_out, sem_up, sem_down, sem_tile,
):
    noisy, length = info[0], info[1]
    seq, width = x.shape
    chunks, pairs, tiles = w1.shape[0], kc.shape[0], seq // R
    copy = pltpu.make_async_copy
    gain1, gain2 = gain1_line[...].reshape(1, width), gain2_line[...].reshape(1, width)

    def weights(c):
        place = lax.rem(c + (chunks // 2) * (1 - noisy), chunks) * FC
        place = pl.multiple_of(place, FC)
        return (
            copy(w1_any.at[:, pl.ds(place, FC)], w1.at[c], sem_1.at[c]),
            copy(w2_any.at[pl.ds(place, FC), :], w2.at[c], sem_2.at[c]),
        )

    sources = (
        (x_any, x),
        (wqkv_any, wqkv),
        (wo_any, wo),
        (dy_any, dy),
    )
    loads = [copy(a, b, sem_in.at[i]) for i, (a, b) in enumerate(sources)]
    for load in loads[:2]:
        load.start()
    sums[...] = jnp.zeros_like(sums)
    edge_bias(bias, noisy)
    def widen(t):
        rows = pl.ds(pl.multiple_of(t * PW, PW), PW)
        c, d = cosine_t[:, rows].T, sine_t[:, rows].T
        cosine[rows, :] = jnp.concatenate([c, c, c, c], axis=1)
        signed[rows, :] = jnp.concatenate([-d, d, -d, d], axis=1)
        return ()

    in_turn(seq // PW, widen)
    tables_out = [copy(cosine, cosine_out, sem_out.at[10]), copy(signed, signed_out, sem_out.at[11])]
    span = lambda t: pl.ds(pl.multiple_of(t * R, R), R)

    loads[0].wait()

    def own_norm(t):
        value = x[span(t), :].astype(f32)
        h1 = (value * inv_rms(value) * gain1).astype(bf16)
        h2[span(t), :] = h1
        h1t[:, span(t)] = h1.T
        weight = token_weight(t * R, length, R)
        sums[0:1, :] += row_sum(jnp.where(weight, value * value, 0.0))
        return ()

    in_turn(tiles, own_norm)
    loads[1].wait()
    for load in loads[2:]:
        load.start()

    def own_product(t):
        return tuple(nn(h2[span(t), :], wqkv[:, i * width : (i + 1) * width]) for i in range(3))

    def own_turn(t, a, b, c):
        tables = (cosine[span(t), :], signed[span(t), :], 1.0)
        by_pairs(q, span(t), rotated(a, *tables))
        by_pairs(ko, span(t), rotated(b, *tables))
        by_pairs(vo, span(t), c)
        return ()

    def clean_norm(t):
        value = jnp.where(noisy == 1, received[span(t), :].astype(f32), x[span(t), :].astype(f32))
        o[span(t), :] = (value * inv_rms(value) * gain1).astype(bf16)
        return ()

    def clean_product(t):
        return tuple(nn(o[span(t), :], wqkv[:, i * width : (i + 1) * width]) for i in (1, 2))

    def clean_turn(t, a, b):
        by_pairs(kc, span(t), rotated(a, cosine[span(t), :], signed[span(t), :], 1.0))
        by_pairs(vc, span(t), b)
        return ()

    in_turn(tiles, own_product, own_turn)
    stores = [
        copy(a, b, sem_out.at[6 + i])
        for i, (a, b) in enumerate(((q, q_out), (ko, ko_out), (vo, vo_out), (h1t, h1t_out)))
    ]
    stores += tables_out
    for store in stores:
        store.start()
    in_turn(tiles, clean_norm, clean_product, clean_turn)
    more = [copy(kc, kc_out, sem_out.at[0]), copy(vc, vc_out, sem_out.at[1])]
    for store in more:
        store.start()
    stores += more

    for c in range(chunks):
        for load in weights(c):
            load.start()

    def one_pair(p, carry):
        lanes = pl.ds(pl.multiple_of(p * PW, PW), PW)

        def keep(at, tile_t):
            o_t[lanes, at] = tile_t.astype(bf16)
            o[at, lanes] = tile_t.T.astype(bf16)

        heads = (ref.at[p] for ref in (q, ko, vo, kc, vc))
        attend_pair(length, *heads, keep, lse.at[pl.ds(p, 1)], vo_t, vc_t, scores, bias)
        return carry

    lax.fori_loop(0, pairs, one_pair, 0)
    mixed_out = copy(o, o_out, sem_out.at[2])
    mixed_out.start()
    stores += [copy(lse, lse_out, sem_out.at[3])]
    stores[-1].start()

    for load in loads[2:]:
        load.wait()

    def join_product(t):
        return (nn(o[span(t), :], wo[...]),)

    def join_norm(t, branch):
        value = x[span(t), :].astype(f32) + branch
        x2[span(t), :] = value
        h2[span(t), :] = (value * inv_rms(value) * gain2).astype(bf16)
        m[span(t), :] = jnp.zeros_like(value)
        dh[span(t), :] = jnp.zeros_like(value)
        weight = token_weight(t * R, length, R)
        sums[1:2, :] += row_sum(jnp.where(weight, branch * branch, 0.0))
        return ()

    in_turn(tiles, join_product, join_norm, at_once=2)

    def grad_stores(c, up, down):
        slot = lax.rem(c, 2)
        rows = pl.ds(pl.multiple_of(lax.rem(c, chunks // 2) * FC, FC), FC)
        return (
            copy(up_grad.at[slot], up.at[rows, :], sem_up.at[slot]),
            copy(down_grad.at[slot], down.at[rows, :], sem_down.at[slot]),
        )

    def one_chunk(c, carry):
        for load in weights(c):
            load.wait()
        up, down = w1.at[c], w2.at[c]
        made = {}
        for t in range(-R, seq, R):
            if t + R < seq:
                rows = pl.ds(t + R, R)
                made[t + R] = nn(h2[rows, :], up[...]), nt(dy[rows, :], down[...])
            if t < 0:
                continue
            rows = pl.ds(t, R)
            u, da = made.pop(t)
            sq = u * u
            half = 0.5 * jnp.tanh(u * (C0 + C1 * sq)) + 0.5
            low = (u * half).astype(bf16)
            slope = half + u * (2.0 * half * (1.0 - half)) * (C0 + 3.0 * C1 * sq)
            back = (da * slope).astype(bf16)
            act[rows, :] = low
            du[rows, :] = back
            m[rows, :] += nn(low, down[...])
            dh[rows, :] += nt(back, up[...])

        @pl.when(c >= 2)
        def _():
            for store in grad_stores(c, up_send, down_send):
                store.wait()

        slot = lax.rem(c, 2)
        down_grad[slot] = tn(act[...], dy[...]).astype(bf16)
        up_grad[slot] = tn(du[...], h2[...]).astype(bf16)

        @pl.when(c < chunks // 2)
        def _():
            for store in grad_stores(c, up_send, down_send):
                store.start()

        @pl.when(c >= chunks // 2)
        def _():
            for store in grad_stores(c, up_keep, down_keep):
                store.start()

        return carry

    lax.fori_loop(0, chunks, one_chunk, 0)

    mixed_out.wait()

    def tile_stores(t):
        return (
            copy(h2.at[span(t), :], out_any.at[span(t), :], sem_tile.at[t, 0]),
            copy(x2.at[span(t), :], dx2_any.at[span(t), :], sem_tile.at[t, 1]),
            copy(o.at[span(t), :], do_any.at[span(t), :], sem_tile.at[t, 2]),
        )

    def middle_norm(t):
        value = x2[span(t), :]
        mixed = m[span(t), :]
        weight = token_weight(t * R, length, R)
        sums[2:3, :] += row_sum(jnp.where(weight, mixed * mixed, 0.0))
        grad, gain_terms = norm_back(value, gain2, dh[span(t), :])
        sums[3:4, :] += row_sum(gain_terms)
        grad = grad + dy[span(t), :].astype(f32)
        h2[span(t), :] = (value + mixed).astype(bf16)
        x2[span(t), :] = grad
        x[span(t), :] = grad.astype(bf16)
        return ()

    def middle_product(t):
        o[span(t), :] = nt(x[span(t), :], wo[...]).astype(bf16)
        for store in tile_stores(t):
            store.start()
        return ()

    in_turn(tiles, middle_norm, middle_product, at_once=2)
    half = width // 2
    mine = pl.multiple_of(noisy * half, half)
    half_grads[0] = nn(o_t[pl.ds(half - mine, half), :], x[...]).astype(bf16)
    half_grads[1] = nn(o_t[pl.ds(mine, half), :], x[...]).astype(bf16)
    more = [copy(half_grads.at[0], g_send, sem_out.at[4]), copy(half_grads.at[1], g_keep, sem_out.at[5])]
    for store in more:
        store.start()
    stores += more
    for c in range(chunks - 2, chunks):
        stores += grad_stores(c, up_keep, down_keep)
    for t in range(tiles):
        stores += tile_stores(t)
    for store in stores:
        store.wait()


def layer(info, gain1, gain2, cosine_t, sine_t, received, x, wqkv, wo, dy, w1, w2):
    seq, width = x.shape
    hidden = w1.shape[1]
    tiles, pairs, chunks = seq // R, width // PW, hidden // FC
    anywhere = pl.BlockSpec(memory_space=pl.ANY)
    vmem = pltpu.VMEM
    dma = pltpu.SemaphoreType.DMA
    heads = (pairs, seq, PW)
    flat = (seq, width)
    outs = (
        [shape(heads, bf16)] * 5
        + [shape((width, seq), bf16), shape(flat, bf16), shape((pairs, seq // T, 2 * T), f32)]
        + [shape(flat, bf16), shape(flat, f32), shape(flat, bf16)]
        + [shape((hidden // 2, width), bf16)] * 4
        + [shape((width // 2, width), bf16)] * 2
        + [shape((seq, PW), f32)] * 2
        + [shape((8, width), f32)]
    )
    return pl.pallas_call(
        layer_kernel,
        in_specs=[SMEM] + [IN_VMEM] * 5 + [anywhere] * 6,
        out_specs=[anywhere] * 19 + [IN_VMEM],
        out_shape=outs,
        scratch_shapes=[vmem(flat, bf16)]
        + [vmem(wqkv.shape, bf16), vmem((seq, PW), f32), vmem((seq, PW), f32)]
        + [vmem(heads, bf16)] * 3
        + [vmem((width, seq), bf16), vmem((width, width), bf16), vmem(flat, bf16)]
        + [vmem((chunks, width, FC), bf16), vmem((chunks, FC, width), bf16)]
        + [vmem(heads, bf16)] * 2
        + [vmem((PW, seq), bf16)] * 2
        + [vmem((AHEAD, seq + T, 2 * T), f32), vmem((2 * T, 2 * T), f32)]
        + [vmem(flat, bf16), vmem((width, seq), bf16)]
        + [vmem((pairs, seq // T, 2 * T), f32)]
        + [vmem(flat, f32), vmem(flat, bf16)]
        + [vmem(flat, f32)] * 2
        + [vmem((seq, FC), bf16)] * 2
        + [vmem((2, FC, width), bf16)] * 2
        + [vmem((2, width // 2, width), bf16)]
        + [dma((4,)), dma((chunks,)), dma((chunks,)), dma((12,)), dma((2,)), dma((2,)), dma((tiles, 3))],
        compiler_params=params(BIG),
        cost_estimate=LONG,
        name="layer",
    )(info, gain1, gain2, cosine_t, sine_t, received, *pinned(x, wqkv, wo, dy, w1, w2))


def weigh_kernel(first, info, dq, keep, got, cosine, signed, h1t, wqkv, sums, dkv, g_send, g_keep, small):
    width, half = wqkv.shape[0], wqkv.shape[0] // 2
    mine = pl.multiple_of(info[0] * half, half)
    dk = keep[0].astype(f32) + got[0].astype(f32)
    dkv[0] = rotated(dk, cosine[...], signed[...], -1.0).astype(bf16)
    dkv[1] = (keep[1].astype(f32) + got[1].astype(f32)).astype(bf16)
    small[...] = sums[...]
    for out, start in ((g_send, half - mine), (g_keep, mine)):
        rows = pl.ds(start, half)
        terms = 0.0
        for i, part in enumerate((dq, dkv.at[0], dkv.at[1])):
            total = nn(h1t[rows, :], part[...])
            out[i] = total.astype(bf16)
            at = i * width + first * PW
            weighted = total * wqkv[rows, at : at + total.shape[1]].astype(f32)
            for c in range(0, total.shape[1], PW):
                terms = terms + weighted[:, c : c + PW]
        line = jnp.sum(terms.T, axis=0, keepdims=True)
        lanes = lax.broadcasted_iota(jnp.int32, (1, width), 1)
        inside = jnp.logical_and(lanes >= start, lanes < start + half)
        small[4:5, :] += jnp.where(inside, jnp.concatenate([line, line], axis=1), 0.0)
    small[5:6, :] = jnp.full((1, width), info[1].astype(f32))


def weigh(info, first, dq, keep, got, tables, h1t, wqkv, sums):
    seq, width = dq.shape
    tall = h1t.shape[0]
    return pl.pallas_call(
        functools.partial(weigh_kernel, first),
        in_specs=[SMEM] + [IN_VMEM] * 8,
        out_specs=[IN_VMEM] * 4,
        out_shape=[shape((2, seq, width), bf16)]
        + [shape((3, tall // 2, width), bf16)] * 2
        + [shape(sums.shape, f32)],
        compiler_params=params(24),
        cost_estimate=LONG,
        name="weigh",
    )(info, dq, keep, got, *tables, h1t, wqkv, sums)


def finish_kernel(parts, tiles, x, dx2, wqkv, gain_line, *refs):
    dx_any, dx, sem = refs[-3:]
    dqs, dkvs = refs[:parts], refs[parts : 2 * parts]
    gain = gain_line[...].reshape(1, x.shape[1])

    def store(t):
        rows = pl.ds(pl.multiple_of(t * R, R), R)
        return pltpu.make_async_copy(dx.at[rows, :], dx_any.at[rows, :], sem.at[t])

    def some_rows(t, carry):
        rows = pl.ds(pl.multiple_of(t * R, R), R)
        grads = [r[rows, :] for r in dqs] + [r[0, rows, :] for r in dkvs] + [r[1, rows, :] for r in dkvs]
        dh = nt(jnp.concatenate(grads, axis=1), wqkv[...])
        grad, _ = norm_back(x[rows, :].astype(f32), gain, dh)
        dx[rows, :] = (dx2[rows, :] + grad).astype(bf16)
        store(t).start()
        return carry

    lax.fori_loop(*tiles, some_rows, 0)
    for t in range(*tiles):
        store(t).wait()


def finish(tiles, x, dx2, dqs, dkvs, weight, gain, before):
    anywhere = pl.BlockSpec(memory_space=pl.ANY)
    ins = 4 + len(dqs) + len(dkvs)
    return pl.pallas_call(
        functools.partial(finish_kernel, len(dqs), tiles),
        in_specs=[IN_VMEM] * ins + [anywhere] * len(before),
        out_specs=anywhere,
        out_shape=shape(x.shape, bf16),
        scratch_shapes=[pltpu.VMEM(x.shape, bf16), pltpu.SemaphoreType.DMA((x.shape[0] // R,))],
        input_output_aliases={ins: 0} if before else {},
        compiler_params=params(24),
        cost_estimate=COST if before else LONG,
        name="finish",
    )(x, dx2, weight, gain, *dqs, *dkvs, *before)


def bit_orders(count, groups):
    bits = [1 << i for i in range(count.bit_length() - 1)]
    if groups == 2:
        return [bits, bits[1::-1] + bits[2:]]
    return [bits[g:-1] + bits[:g] + bits[-1:] for g in range(groups)]


def exchange(value, axis, bit):
    size = lax.axis_size(axis)
    return lax.ppermute(value, axis, [(i, i ^ bit) for i in range(size)])


def distance(order, place):
    out = 0
    for i, bit in enumerate(order):
        out = out + ((place >> (len(order) - 1 - i)) & 1) * bit
    return out


SUMS = 8


def halves(value):
    high = value.astype(bf16)
    return high, (value - high.astype(f32)).astype(bf16)


def put_sums(value, kept, block):
    high, low = halves(value)
    lines = kept.shape[0]
    block[:lines, :] = high
    block[lines : 2 * lines, :] = low
    kept[...] = high.astype(f32) + low.astype(f32)


def got_sums(block):
    lines = block.shape[0] // 2
    return block[:lines, :].astype(f32) + block[lines:, :].astype(f32)


def start_kernel(orders, sources, small, me, *refs):
    groups = len(orders)
    arrays = max(a for source in sources for a, _, _ in source) + 1
    ins, outs = refs[: 2 * arrays], refs[len(refs) - 2 * groups :]
    half = outs[0].shape[0]
    for g, order in enumerate(orders):
        for side in range(2):

            def one(r, carry, g=g, order=order, side=side):
                part = me[0] ^ distance(order, r + side * half)
                out = outs[2 * g + side]
                row = 0
                for a, where, unit in sources[g]:
                    kept, got = ins[2 * a : 2 * a + 2]
                    place = where(part)
                    size, wide = kept.shape[1], out.shape[-1]
                    lanes = slice(unit * wide, (unit + 1) * wide)
                    total = kept[place, :, lanes].astype(f32) + got[place, :, lanes].astype(f32)
                    if len(out.shape) == 3:
                        out[r, row : row + size, :] = total.astype(bf16)
                    else:
                        start = pl.multiple_of(r * outs[0].shape[1] + row, 8)
                        out[pl.ds(start, size), :] = total.astype(bf16)
                    row += size
                return carry

            lax.fori_loop(0, half, one, 0)
    if small:
        here, there, kept = refs[2 * arrays : 2 * arrays + 3]
        total = here[...] + there[...]
        if small == "rides":
            wide = kept.shape[1]
            total = jnp.concatenate([total[:, c : c + wide] for c in range(0, total.shape[1], wide)], axis=0)
            put_sums(total, kept, outs[1].at[pl.ds(half * outs[0].shape[1], 2 * kept.shape[0]), :])
        else:
            kept[...] = total


def travelling(count, rows, width, lines):
    return shape((count * rows + 2 * lines, width) if lines else (count, rows, width), bf16)


def start_sum(me, kept, got, sources, width, orders, small, rides):
    count = 1 << len(orders[0])
    half = count // 2
    rows = [sum(kept[a].shape[1] for a, _, _ in source) for source in sources]
    lines = small[0].size // width if rides else 0
    cols = width // 3
    args = [a for pair in zip(kept, got, strict=True) for a in pair]
    sums = []
    for g in range(len(orders)):
        sums += [shape((half, rows[g], width), bf16), travelling(half, rows[g], width, 0 if g else lines)]
    mode = "rides" if rides else "alone" if small else ""
    if small:
        specs = dict(
            in_specs=[SMEM] + [IN_VMEM] * (len(args) + 2),
            out_specs=[IN_VMEM] * (1 + len(sums)),
            out_shape=[shape((lines, width) if rides else small[0].shape, f32)] + sums,
        )
    else:
        block = lambda a: pl.BlockSpec((a.shape[0], a.shape[1], cols), lambda c: (0, 0, c))
        specs = dict(
            grid=(width // cols,),
            in_specs=[SMEM] + [block(a) for a in args],
            out_specs=[block(a) for a in sums],
            out_shape=sums,
        )
    outs = pl.pallas_call(
        functools.partial(start_kernel, orders, sources, mode),
        compiler_params=params(30),
        cost_estimate=COST,
        name="start_sum",
        **specs,
    )(me, *args, *small)
    small, outs = list(outs[: len(outs) - len(sums)]), outs[len(outs) - len(sums) :]
    return list(outs[0::2]), list(outs[1::2]), small


def block_of(ref, r, size, row=0, step=0):
    if len(ref.shape) == 3:
        return ref.at[r, pl.ds(row, size), :]
    start = r * (step or size) + row
    return ref.at[pl.ds(start if isinstance(start, int) else pl.multiple_of(start, 8), size), :]


def step_kernel(groups, merge, mode, *refs):
    kept, got = refs[:groups], refs[groups : 2 * groups]
    outs = refs[2 * groups + (2 if mode == "alone" else 1 if mode else 0) :]
    count = kept[0].shape[0]
    half = count // 2

    def one(r, carry):
        row = 0
        for g in range(groups):
            keep, send = outs[:2] if merge else outs[2 * g : 2 * g + 2]
            size = kept[g].shape[1]
            for out, block in ((keep, r), (send, r + half)):
                total = kept[g][block].astype(f32) + block_of(got[g], block, size)[...].astype(f32)
                block_of(out, r, size, row, keep.shape[1])[...] = total.astype(bf16)
            row += size if merge else 0
        return carry

    lax.fori_loop(0, half, one, 0)
    if mode == "rides":
        total = refs[2 * groups][...] + got_sums(got[0][count * kept[0].shape[1] :])
        put_sums(total, outs[-1], outs[1].at[pl.ds(half * outs[0].shape[1], 2 * total.shape[0]), :])
    elif mode:
        outs[-1][...] = refs[2 * groups][...] + refs[2 * groups + 1][...]


def step_sum(kept, got, small, merge, rides):
    groups = len(kept)
    half = kept[0].shape[0] // 2
    rows = [a.shape[1] for a in kept]
    width = kept[0].shape[2]
    args = [*kept, *got, *small]
    sums = []
    for g, r in enumerate([sum(rows)] if merge else rows):
        sums += [shape((half, r, width), bf16), travelling(half, r, width, 0 if g or not rides else small[0].shape[0])]
    outs = pl.pallas_call(
        functools.partial(step_kernel, groups, merge, "rides" if rides else "alone" if small else ""),
        in_specs=[IN_VMEM] * len(args),
        out_specs=[IN_VMEM] * (len(sums) + len(small[:1])),
        out_shape=sums + [shape(a.shape, f32) for a in small[:1]],
        compiler_params=params(16),
        cost_estimate=COST if small or half == 1 else LONG,
        name="step_sum",
    )(*args)
    return list(outs[0 : len(sums) : 2]), list(outs[1 : len(sums) : 2]), list(outs[len(sums) :])


def feed_end_kernel(kept, got, down, up, out):
    total = kept[0].astype(f32) + got[0].astype(f32)
    tall, few = down.shape[0] // GROUPS, out.shape[0] // GROUPS
    ups = []
    for g in range(GROUPS):
        row = g * (2 * tall + few)
        down[g * tall : (g + 1) * tall, :] = total[row : row + tall]
        ups.append(total[row + tall : row + 2 * tall])
        out[g * few : (g + 1) * few, :] = total[row + 2 * tall : row + 2 * tall + few]
    up[...] = jnp.concatenate(ups, axis=0).T


def feed_end(kept, got, tall, few):
    width = kept.shape[2]
    return pl.pallas_call(
        feed_end_kernel,
        in_specs=[IN_VMEM] * 2,
        out_specs=[IN_VMEM] * 3,
        out_shape=[shape((tall, width), f32), shape((width, tall), f32), shape((few, width), f32)],
        compiler_params=params(16),
        cost_estimate=COST,
        name="feed_end",
    )(kept, got)


def qkv_end_kernel(places, rides, gain_line, kept, got, *refs):
    out, gain1, gain2, rms = refs[-4:]
    tall = out.shape[0]
    width = gain1.shape[0]
    cols = kept.shape[2]
    there = got[: kept.shape[1]] if rides else got[0]
    total = kept[0].astype(f32) + there.astype(f32)
    for i, at in enumerate(places):
        out[:, at : at + cols] = total[i * tall : (i + 1) * tall]
    if rides:
        sums = refs[0][...] + got_sums(got[kept.shape[1] :])
        sums = jnp.concatenate([sums[r : r + SUMS] for r in range(0, sums.shape[0], SUMS)], axis=1)
    else:
        sums = refs[0][...] + refs[1][...]
    gain2[...] = sums[3:4, :].reshape(width)
    gain1[...] = (sums[4:5, :] / gain_line[...].reshape(1, width)).reshape(width)
    count = jnp.max(sums[5:6, :], axis=1, keepdims=True) * width
    rms[...] = jnp.broadcast_to(jnp.sqrt(jnp.sum(sums, axis=1, keepdims=True) / count), rms.shape)


def qkv_end(places, gain, kept, got, small, tall, wide, rides):
    return pl.pallas_call(
        functools.partial(qkv_end_kernel, places, rides),
        in_specs=[IN_VMEM] * (3 + len(small)),
        out_specs=[IN_VMEM] * 4,
        out_shape=[shape((tall, wide), f32), shape(gain.shape, f32), shape(gain.shape, f32), shape((SUMS, 128), f32)],
        compiler_params=params(16),
        cost_estimate=COST,
        name="qkv_end",
    )(gain, kept, got, *small)


def after(value, *earlier):
    return lax.optimization_barrier((value, earlier))[0]


def sum_parts(me, kept, got, sources, width, small, rides):
    orders = bit_orders(lax.axis_size("batch"), len(sources))
    steps = len(orders[0])
    common = min(i for i in range(steps + 1) if all(order[i:] == orders[0][i:] for order in orders))
    keep, send, small = start_sum(me, kept, got, sources, width, orders, small, rides)
    for i in range(steps):
        got = [exchange(s, "batch", order[i]) for s, order in zip(send, orders[: len(send)], strict=True)]
        if small and not rides:
            small = [small[0], exchange(small[0], "batch", orders[0][i])]
        earlier = yield send[0], got
        if i == steps - 1:
            break
        if earlier is not None:
            keep = after(keep, earlier)
        keep, send, small = step_sum(keep, got, small, i + 1 == common, rides)
    yield keep[0], got[0], small


def on_device(
    inputs, lengths, cotangent, qkv_weight, out_weight, up_weight, down_weight, attn_gain, mlp_gain
):
    seq, width = inputs.shape[2:]
    x = inputs[0, 0]
    dy = cotangent[0, 0]
    count = lax.axis_size("batch")
    stream = lax.axis_index("stream").astype(jnp.int32)
    me = lax.axis_index("batch").astype(jnp.int32).reshape(1)
    info = jnp.stack([stream, lengths[0]])
    cosine, sine = rotary_tables(seq)
    tables_t = (jnp.asarray(cosine.T), jnp.asarray(sine.T))

    received = lax.ppermute(x, "stream", [(0, 1)])
    (
        q, ko, vo, kc, vc, h1t, o, lse, outputs, dx2, do,
        up_send, up_keep, down_send, down_keep, out_send, out_keep, *tables, sums,
    ) = layer(
        info, attn_gain, mlp_gain, *tables_t, received, x, qkv_weight, out_weight, dy, up_weight, down_weight
    )
    down_got, up_got, out_got = (exchange(a, "stream", 1) for a in (down_send, up_send, out_send))

    def by_rows(array):
        return array.reshape(count * GROUPS, array.shape[0] // (count * GROUPS), width)

    heads = (q, ko, vo, kc, vc, o)
    pairs = width // PW // 3
    dq1, keep1, send1 = attend_back(info, 0, pairs, *heads, do, lse, *tables_t)
    early = sum_parts(
        me,
        [by_rows(after(a, dq1)) for a in (down_keep, up_keep, out_keep)],
        [by_rows(a) for a in (down_got, up_got, out_got)],
        [[(a, lambda part, g=g: part * GROUPS + g, 0) for a in range(3)] for g in range(GROUPS)],
        width,
        [],
        False,
    )
    token = next(early)[0]
    got1 = lax.ppermute(after(send1, token), "stream", [(1, 0)])
    dq2, keep2, send2 = attend_back(info, pairs, 2 * pairs, *heads, after(do, token), lse, *tables_t)
    got2 = lax.ppermute(send2, "stream", [(1, 0)])
    token = early.send(dq2)[0]
    dkv1, qkv_send1, qkv_keep1, small = weigh(info, 0, dq1, after(keep1, token), got1, tables, h1t, qkv_weight, sums)
    qkv_got1 = exchange(qkv_send1, "stream", 1)
    dkv2, qkv_send2, qkv_keep2, small = weigh(info, pairs, dq2, keep2, got2, tables, h1t, qkv_weight, small)
    qkv_got2 = exchange(qkv_send2, "stream", 1)
    small_got = exchange(small, "stream", 1)
    token = early.send(dkv2)[0]

    tall = width // (2 * count)
    split = lambda a: a.reshape(3 * count, tall, a.shape[2])
    rides = tall % 8 == 0
    runs = [(0, i, 0) for i in range(3)] + [(1, i, c) for i in range(3) for c in range(2)]
    groups = runs[:4], runs[4:]
    late = sum_parts(
        me,
        [split(after(a, token)) for a in (qkv_keep1, qkv_keep2)],
        [split(a) for a in (qkv_got1, qkv_got2)],
        [[(a, lambda part, i=i: i * count + part, c) for a, i, c in group] for group in groups],
        pairs * PW,
        [small, small_got],
        rides,
    )
    token = next(late)[0]
    ends = [dq1, dq2], [dkv1, dkv2], qkv_weight, attn_gain
    tiles = seq // R
    dx = finish((0, tiles // 2), after(x, token), dx2, *ends, [])
    early_out = early.send(dx)
    dx = finish((tiles // 2, tiles), x, after(dx2, early_out[0]), *ends, [dx])
    late.send(dx)
    late_out = late.send(early_out[1])
    while len(late_out) == 2:
        late_out = late.send(None)
    while len(early_out) == 2:
        early_out = early.send(None)
    up_cols = down_keep.shape[0] // count
    down_grad, up_grad, out_grad = feed_end(*early_out[:2], up_cols, tall)
    places = [i * width + (a + c) * pairs * PW for a, i, c in runs]
    qkv_grad, gain1_grad, gain2_grad, rms = qkv_end(places, attn_gain, *late_out, tall, 3 * width, rides)
    return (
        outputs[None, None],
        dx[None, None],
        qkv_grad,
        out_grad,
        up_grad,
        down_grad,
        gain1_grad,
        gain2_grad,
        rms[:3, 0],
    )


def solution(mesh):
    rows = P("stream", "batch", None, None)
    both = ("stream", "batch")
    return jax.shard_map(
        on_device,
        mesh=mesh,
        in_specs=(rows, P("batch"), rows, P(), P(), P(), P(), P(), P()),
        out_specs=(rows, rows, P(both, None), P(both, None), P(None, both), P(both, None), P(), P(), P()),
        check_vma=False,
    )
```

```python
import functools

import jax
import jax.numpy as jnp
import numpy as np
from jax import lax
from jax.experimental import pallas as pl
from jax.experimental.pallas import tpu as pltpu
from jax.sharding import PartitionSpec as P

f32 = jnp.float32
bf16 = jnp.bfloat16

HD = 64
BLK = 16
EPS = 1e-06
NEG = -1e30
PW = 2 * HD
T = 128
R = 256
AHEAD = 2
FC = 768
SCALE = HD**-0.5
BIG = 58
GROUPS = 3

COST = pl.CostEstimate(flops=1 << 20, bytes_accessed=1 << 16, transcendentals=0)
LONG = pl.CostEstimate(flops=1 << 35, bytes_accessed=1 << 26, transcendentals=0)

SMEM = pl.BlockSpec(memory_space=pltpu.SMEM)
IN_VMEM = pl.BlockSpec(memory_space=pltpu.VMEM)


def params(mib):
    return pltpu.CompilerParams(vmem_limit_bytes=mib << 20)


def shape(dims, dtype):
    return jax.ShapeDtypeStruct(dims, dtype)


def pinned(*arrays):
    return [pltpu.with_memory_space_constraint(a, pltpu.HBM) for a in arrays]


def nn(a, b):
    return jnp.dot(a, b, preferred_element_type=f32)


def nt(a, b):
    return lax.dot_general(a, b, (((1,), (1,)), ((), ())), preferred_element_type=f32)


def tn(a, b):
    return lax.dot_general(a, b, (((0,), (0,)), ((), ())), preferred_element_type=f32)


def whole(dims):
    return pl.BlockSpec(dims, lambda *_: (0,) * len(dims), pipeline_mode=pl.Buffered(1))


def inv_rms(v):
    return lax.rsqrt(jnp.mean(v * v, axis=-1, keepdims=True) + EPS)


def norm_back(v, gain, grad):
    r = inv_rms(v)
    unit = v * r
    scaled = grad * gain
    inner = jnp.mean(scaled * unit, axis=-1, keepdims=True)
    return r * (scaled - unit * inner), grad * unit


def rotary_tables(length):
    half = HD // 2
    freqs = np.exp(-np.log(10000.0) * np.arange(half) / half).astype(np.float32)
    angles = (np.arange(length, dtype=np.float32)[:, None] * freqs[None, :]).astype(np.float64)
    return np.cos(angles).astype(np.float32), np.sin(angles).astype(np.float32)


def rotated(v, cosine, signed, sign):
    first = lax.broadcasted_iota(jnp.int32, (1, PW), 1) % HD < HD // 2
    outs = []
    for c in range(0, v.shape[1], PW):
        part = v[:, c : c + PW]
        partner = jnp.where(first, pltpu.roll(part, PW - HD // 2, 1), pltpu.roll(part, HD // 2, 1))
        outs.append(part * cosine + partner * (signed * sign))
    return outs[0] if len(outs) == 1 else jnp.concatenate(outs, axis=1)


def in_turn(count, *stages, at_once=1):
    def turn(n, carry):
        state = [()] * at_once
        for step in range(at_once + len(stages) - 1):
            for k, stage in enumerate(stages):
                if 0 <= step - k < at_once:
                    state[step - k] = stage(at_once * n + step - k, *state[step - k])
        return carry

    lax.fori_loop(0, count // at_once, turn, 0)


def token_weight(start, length, rows):
    return lax.broadcasted_iota(jnp.int32, (rows, 1), 0) + start < length


def row_sum(v):
    return jnp.sum(v, axis=0, keepdims=True)


def by_pairs(ref, rows, value):
    for p in range(ref.shape[0]):
        ref[p, rows, :] = value[:, p * PW : (p + 1) * PW].astype(ref.dtype)


def stacked(tile, low):
    zero = jnp.zeros_like(tile)
    return jnp.concatenate([jnp.where(low, tile, zero), jnp.where(low, zero, tile)], axis=0)


def unstacked(tile_t):
    half = lax.broadcasted_iota(jnp.int32, (PW, 1), 0) < HD
    return jnp.where(half, tile_t[:, :T], tile_t[:, T:])


def chunks_of(i):
    out, j = [], 0
    while j < i:
        n = 2 if i - j >= 2 else 1
        out.append((j * T, n * T))
        j += n
    return out


def edge_bias(ref, noisy):
    row = lax.broadcasted_iota(jnp.int32, (T, 2 * T), 0) // BLK
    col = (lax.broadcasted_iota(jnp.int32, (T, 2 * T), 1) % T) // BLK
    own = jnp.logical_or(row == col, jnp.logical_and(row < col, noisy == 0))
    other = jnp.logical_and(row < col, noisy == 1)
    ref[:T, :] = jnp.where(own, 0.0, NEG)
    ref[T:, :] = jnp.where(other, 0.0, NEG)


def masked(s, start, length):
    pos = lax.broadcasted_iota(jnp.int32, s.shape, 0) + start
    return jnp.where(pos < length, s, NEG)


def over_rows(op, v):
    return op(v.reshape(v.shape[0] // 8, 8, v.shape[1]), axis=0)


def attend_pair(length, q, ko, vo, kc, vc, store, lse, vo_t, vc_t, scores, bias):
    seq = q.shape[0]
    low = lax.broadcasted_iota(jnp.int32, (1, PW), 1) < HD
    vo_t[...] = vo[...].T
    vc_t[...] = vc[...].T

    def score(i):
        at = pl.ds(i * T, T)
        q2 = stacked(q[at, :] * bf16(SCALE), low)
        buf = scores.at[i % AHEAD]
        edge = nt(jnp.concatenate([ko[at, :], kc[at, :]], 0), q2) + bias[...]
        own = masked(edge[:T], i * T, length)
        other = masked(edge[T:], i * T, length)
        buf[pl.ds(0, T), :] = own
        buf[pl.ds(T, T), :] = other
        top = over_rows(jnp.max, jnp.maximum(own, other))
        for start, size in chunks_of(i):
            s = masked(nt(kc[pl.ds(start, size), :], q2), start, length)
            buf[pl.ds(2 * T + start, size), :] = s
            top = jnp.maximum(top, over_rows(jnp.max, s))
        return jnp.max(top, axis=0, keepdims=True)

    def mix(i, top):
        at = pl.ds(i * T, T)
        buf = scores.at[i % AHEAD]
        p = jnp.exp(buf[pl.ds(0, 2 * T), :] - top)
        total = over_rows(jnp.sum, p)
        acc = nn(jnp.concatenate([vo_t[:, at], vc_t[:, at]], 1), p.astype(bf16))
        for start, size in chunks_of(i):
            p = jnp.exp(buf[pl.ds(2 * T + start, size), :] - top)
            total = total + over_rows(jnp.sum, p)
            acc = acc + nn(vc_t[:, pl.ds(start, size)], p.astype(bf16))
        total = row_sum(total)
        lse[0, pl.ds(i, 1), :] = top + jnp.log(total)
        store(at, unstacked(acc * (1.0 / total)))

    tops = {}
    for i in range(seq // T + AHEAD - 1):
        if i < seq // T:
            tops[i] = score(i)
        if i >= AHEAD - 1:
            mix(i - AHEAD + 1, tops.pop(i - AHEAD + 1))


def turned_back(v, cosine, sine):
    quarter = HD // 2
    a, b, c, d = (v[i * quarter : (i + 1) * quarter] for i in range(4))
    return jnp.concatenate(
        [a * cosine + b * sine, b * cosine - a * sine, c * cosine + d * sine, d * cosine - c * sine]
    )


def attend_back_kernel(
    info, q, ko, vo, kc, vc, o, do, lse, cosine, sine, dq, keep, send, ko_t, kc_t, dko, dvo, dkc, dvc, bias
):
    noisy, length = info[0], info[1]
    q, ko, vo, kc, vc = (ref.at[0] for ref in (q, ko, vo, kc, vc))
    seq = q.shape[0]
    low = lax.broadcasted_iota(jnp.int32, (1, PW), 1) < HD

    @pl.when(pl.program_id(0) == 0)
    def _():
        edge_bias(bias, noisy)

    ko_t[...] = ko[...].T
    kc_t[...] = kc[...].T

    def tile(i):
        at = pl.ds(i * T, T)
        prod = (do[at, :].astype(f32) * o[at, :].astype(f32)).T
        delta = jnp.concatenate([row_sum(prod[:HD]), row_sum(prod[HD:])], 1)
        q2 = stacked(q[at, :] * bf16(SCALE), low)
        return q2, stacked(do[at, :], low), lse[0, pl.ds(i, 1), :], delta

    def products(i, start, size, q2, do2):
        if start is None:
            at = pl.ds(i * T, T)
            s = nt(jnp.concatenate([ko[at, :], kc[at, :]], 0), q2) + bias[...]
            s = jnp.concatenate([masked(s[:T], i * T, length), masked(s[T:], i * T, length)], 0)
            return s, nt(jnp.concatenate([vo[at, :], vc[at, :]], 0), do2)
        rows = pl.ds(start, size)
        return masked(nt(kc[rows, :], q2), start, length), nt(vc[rows, :], do2)

    def gather(i, start, size, q2, do2, p, ds, dq_t):
        at = pl.ds(i * T, T)
        dv, dk = nn(p, do2), nn(ds, q2)
        if start is None:
            dvo[at, :] = dv[:T]
            dko[at, :] = dk[:T]
            dvc[at, :] = dv[T:]
            dkc[at, :] = dk[T:]
            return nn(jnp.concatenate([ko_t[:, at], kc_t[:, at]], 1), ds)
        rows = pl.ds(start, size)
        dvc[rows, :] += dv
        dkc[rows, :] += dk
        return dq_t + nn(kc_t[:, rows], ds)

    work = [(i, *c) for i in range(seq // T) for c in [(None, None)] + chunks_of(i)]
    tiles, made, weighed, dq_t = {}, {}, {}, None
    for n in range(len(work) + 2):
        if n < len(work):
            i = work[n][0]
            if i not in tiles:
                tiles[i] = tile(i)
            made[n] = products(*work[n], *tiles[i][:2])
        if 0 <= n - 1 < len(work):
            _, _, norm, delta = tiles[work[n - 1][0]]
            s, dp = made.pop(n - 1)
            p = jnp.exp(s - norm)
            weighed[n - 1] = p.astype(bf16), (p * (dp - delta)).astype(bf16)
        if n >= 2:
            i, start, size = work[n - 2]
            dq_t = gather(i, start, size, *tiles[i][:2], *weighed.pop(n - 2), dq_t)
            if n == len(work) + 1 or work[n - 1][0] != i:
                at = pl.ds(i * T, T)
                out = turned_back(unstacked(dq_t), cosine[:, at], sine[:, at]) * SCALE
                dq[at, :] = out.T.astype(bf16)
    clean = (1 - noisy).astype(f32)
    for at, own, other in ((0, dko, dkc), (1, dvo, dvc)):
        keep[at] = (own[...] + clean * other[...]).astype(bf16)
        send[at] = other[...].astype(bf16)


def attend_back(info, first, pairs, q, ko, vo, kc, vc, o, do, lse, cosine, sine):
    seq = q.shape[1]
    width = pairs * PW
    heads = pl.BlockSpec((1, seq, PW), lambda h: (first + h, 0, 0))
    source = pl.BlockSpec((seq, PW), lambda h: (0, first + h))
    both = pl.BlockSpec((2, seq, PW), lambda h: (0, 0, h))
    lines = pl.BlockSpec((1, seq // T, 2 * T), lambda h: (first + h, 0, 0))
    table = whole((HD // 2, seq))
    return pl.pallas_call(
        attend_back_kernel,
        grid=(pairs,),
        in_specs=[SMEM] + [heads] * 5 + [source] * 2 + [lines, table, table],
        out_specs=[pl.BlockSpec((seq, PW), lambda h: (0, h)), both, both],
        out_shape=[shape((seq, width), bf16)] + [shape((2, seq, width), bf16)] * 2,
        scratch_shapes=[pltpu.VMEM((PW, seq), bf16)] * 2
        + [pltpu.VMEM((seq, PW), f32)] * 4
        + [pltpu.VMEM((2 * T, 2 * T), f32)],
        compiler_params=params(24),
        cost_estimate=LONG,
        name="attend_back",
    )(info, *pinned(q, ko, vo, kc, vc, o, do), lse, cosine, sine)


C0 = 0.7978845608028654
C1 = C0 * 0.044715


def layer_kernel(
    info, gain1_line, gain2_line, cosine_t, sine_t, received, x_any, wqkv_any, wo_any, dy_any,
    w1_any, w2_any,
    q_out, ko_out, vo_out, kc_out, vc_out, h1t_out, o_out, lse_out, out_any, dx2_any, do_any,
    up_send, up_keep, down_send, down_keep, g_send, g_keep, cosine_out, signed_out, sums,
    x, wqkv, cosine, signed, q, ko, vo, h1t, wo, dy, w1, w2,
    kc, vc, vo_t, vc_t, scores, bias, o, o_t, lse, x2, h2, m, dh, act, du, up_grad, down_grad, half_grads,
    sem_in, sem_1, sem_2, sem_out, sem_up, sem_down, sem_tile,
):
    noisy, length = info[0], info[1]
    seq, width = x.shape
    chunks, pairs, tiles = w1.shape[0], kc.shape[0], seq // R
    copy = pltpu.make_async_copy
    gain1, gain2 = gain1_line[...].reshape(1, width), gain2_line[...].reshape(1, width)

    def weights(c):
        place = lax.rem(c + (chunks // 2) * (1 - noisy), chunks) * FC
        place = pl.multiple_of(place, FC)
        return (
            copy(w1_any.at[:, pl.ds(place, FC)], w1.at[c], sem_1.at[c]),
            copy(w2_any.at[pl.ds(place, FC), :], w2.at[c], sem_2.at[c]),
        )

    sources = (
        (x_any, x),
        (wqkv_any, wqkv),
        (wo_any, wo),
        (dy_any, dy),
    )
    loads = [copy(a, b, sem_in.at[i]) for i, (a, b) in enumerate(sources)]
    for load in loads[:2]:
        load.start()
    sums[...] = jnp.zeros_like(sums)
    edge_bias(bias, noisy)
    def widen(t):
        rows = pl.ds(pl.multiple_of(t * PW, PW), PW)
        c, d = cosine_t[:, rows].T, sine_t[:, rows].T
        cosine[rows, :] = jnp.concatenate([c, c, c, c], axis=1)
        signed[rows, :] = jnp.concatenate([-d, d, -d, d], axis=1)
        return ()

    in_turn(seq // PW, widen)
    tables_out = [copy(cosine, cosine_out, sem_out.at[10]), copy(signed, signed_out, sem_out.at[11])]
    span = lambda t: pl.ds(pl.multiple_of(t * R, R), R)

    loads[0].wait()

    def own_norm(t):
        value = x[span(t), :].astype(f32)
        h1 = (value * inv_rms(value) * gain1).astype(bf16)
        h2[span(t), :] = h1
        h1t[:, span(t)] = h1.T
        weight = token_weight(t * R, length, R)
        sums[0:1, :] += row_sum(jnp.where(weight, value * value, 0.0))
        return ()

    in_turn(tiles, own_norm)
    loads[1].wait()
    for load in loads[2:]:
        load.start()

    def own_product(t):
        return tuple(nn(h2[span(t), :], wqkv[:, i * width : (i + 1) * width]) for i in range(3))

    def own_turn(t, a, b, c):
        tables = (cosine[span(t), :], signed[span(t), :], 1.0)
        by_pairs(q, span(t), rotated(a, *tables))
        by_pairs(ko, span(t), rotated(b, *tables))
        by_pairs(vo, span(t), c)
        return ()

    def clean_norm(t):
        value = jnp.where(noisy == 1, received[span(t), :].astype(f32), x[span(t), :].astype(f32))
        o[span(t), :] = (value * inv_rms(value) * gain1).astype(bf16)
        return ()

    def clean_product(t):
        return tuple(nn(o[span(t), :], wqkv[:, i * width : (i + 1) * width]) for i in (1, 2))

    def clean_turn(t, a, b):
        by_pairs(kc, span(t), rotated(a, cosine[span(t), :], signed[span(t), :], 1.0))
        by_pairs(vc, span(t), b)
        return ()

    in_turn(tiles, own_product, own_turn)
    stores = [
        copy(a, b, sem_out.at[6 + i])
        for i, (a, b) in enumerate(((q, q_out), (ko, ko_out), (vo, vo_out), (h1t, h1t_out)))
    ]
    stores += tables_out
    for store in stores:
        store.start()
    in_turn(tiles, clean_norm, clean_product, clean_turn)
    more = [copy(kc, kc_out, sem_out.at[0]), copy(vc, vc_out, sem_out.at[1])]
    for store in more:
        store.start()
    stores += more

    for c in range(chunks):
        for load in weights(c):
            load.start()

    def one_pair(p, carry):
        lanes = pl.ds(pl.multiple_of(p * PW, PW), PW)

        def keep(at, tile_t):
            o_t[lanes, at] = tile_t.astype(bf16)
            o[at, lanes] = tile_t.T.astype(bf16)

        heads = (ref.at[p] for ref in (q, ko, vo, kc, vc))
        attend_pair(length, *heads, keep, lse.at[pl.ds(p, 1)], vo_t, vc_t, scores, bias)
        return carry

    lax.fori_loop(0, pairs, one_pair, 0)
    mixed_out = copy(o, o_out, sem_out.at[2])
    mixed_out.start()
    stores += [copy(lse, lse_out, sem_out.at[3])]
    stores[-1].start()

    for load in loads[2:]:
        load.wait()

    def join_product(t):
        return (nn(o[span(t), :], wo[...]),)

    def join_norm(t, branch):
        value = x[span(t), :].astype(f32) + branch
        x2[span(t), :] = value
        h2[span(t), :] = (value * inv_rms(value) * gain2).astype(bf16)
        m[span(t), :] = jnp.zeros_like(value)
        dh[span(t), :] = jnp.zeros_like(value)
        weight = token_weight(t * R, length, R)
        sums[1:2, :] += row_sum(jnp.where(weight, branch * branch, 0.0))
        return ()

    in_turn(tiles, join_product, join_norm, at_once=2)

    def grad_stores(c, up, down):
        slot = lax.rem(c, 2)
        rows = pl.ds(pl.multiple_of(lax.rem(c, chunks // 2) * FC, FC), FC)
        return (
            copy(up_grad.at[slot], up.at[rows, :], sem_up.at[slot]),
            copy(down_grad.at[slot], down.at[rows, :], sem_down.at[slot]),
        )

    def one_chunk(c, carry):
        for load in weights(c):
            load.wait()
        up, down = w1.at[c], w2.at[c]
        made = {}
        for t in range(-R, seq, R):
            if t + R < seq:
                rows = pl.ds(t + R, R)
                made[t + R] = nn(h2[rows, :], up[...]), nt(dy[rows, :], down[...])
            if t < 0:
                continue
            rows = pl.ds(t, R)
            u, da = made.pop(t)
            sq = u * u
            half = 0.5 * jnp.tanh(u * (C0 + C1 * sq)) + 0.5
            low = (u * half).astype(bf16)
            slope = half + u * (2.0 * half * (1.0 - half)) * (C0 + 3.0 * C1 * sq)
            back = (da * slope).astype(bf16)
            act[rows, :] = low
            du[rows, :] = back
            m[rows, :] += nn(low, down[...])
            dh[rows, :] += nt(back, up[...])

        @pl.when(c >= 2)
        def _():
            for store in grad_stores(c, up_send, down_send):
                store.wait()

        slot = lax.rem(c, 2)
        down_grad[slot] = tn(act[...], dy[...]).astype(bf16)
        up_grad[slot] = tn(du[...], h2[...]).astype(bf16)

        @pl.when(c < chunks // 2)
        def _():
            for store in grad_stores(c, up_send, down_send):
                store.start()

        @pl.when(c >= chunks // 2)
        def _():
            for store in grad_stores(c, up_keep, down_keep):
                store.start()

        return carry

    lax.fori_loop(0, chunks, one_chunk, 0)

    mixed_out.wait()

    def tile_stores(t):
        return (
            copy(h2.at[span(t), :], out_any.at[span(t), :], sem_tile.at[t, 0]),
            copy(x2.at[span(t), :], dx2_any.at[span(t), :], sem_tile.at[t, 1]),
            copy(o.at[span(t), :], do_any.at[span(t), :], sem_tile.at[t, 2]),
        )

    def middle_norm(t):
        value = x2[span(t), :]
        mixed = m[span(t), :]
        weight = token_weight(t * R, length, R)
        sums[2:3, :] += row_sum(jnp.where(weight, mixed * mixed, 0.0))
        grad, gain_terms = norm_back(value, gain2, dh[span(t), :])
        sums[3:4, :] += row_sum(gain_terms)
        grad = grad + dy[span(t), :].astype(f32)
        h2[span(t), :] = (value + mixed).astype(bf16)
        x2[span(t), :] = grad
        x[span(t), :] = grad.astype(bf16)
        return ()

    def middle_product(t):
        o[span(t), :] = nt(x[span(t), :], wo[...]).astype(bf16)
        for store in tile_stores(t):
            store.start()
        return ()

    in_turn(tiles, middle_norm, middle_product, at_once=2)
    half = width // 2
    mine = pl.multiple_of(noisy * half, half)
    half_grads[0] = nn(o_t[pl.ds(half - mine, half), :], x[...]).astype(bf16)
    half_grads[1] = nn(o_t[pl.ds(mine, half), :], x[...]).astype(bf16)
    more = [copy(half_grads.at[0], g_send, sem_out.at[4]), copy(half_grads.at[1], g_keep, sem_out.at[5])]
    for store in more:
        store.start()
    stores += more
    for c in range(chunks - 2, chunks):
        stores += grad_stores(c, up_keep, down_keep)
    for t in range(tiles):
        stores += tile_stores(t)
    for store in stores:
        store.wait()


def layer(info, gain1, gain2, cosine_t, sine_t, received, x, wqkv, wo, dy, w1, w2):
    seq, width = x.shape
    hidden = w1.shape[1]
    tiles, pairs, chunks = seq // R, width // PW, hidden // FC
    anywhere = pl.BlockSpec(memory_space=pl.ANY)
    vmem = pltpu.VMEM
    dma = pltpu.SemaphoreType.DMA
    heads = (pairs, seq, PW)
    flat = (seq, width)
    outs = (
        [shape(heads, bf16)] * 5
        + [shape((width, seq), bf16), shape(flat, bf16), shape((pairs, seq // T, 2 * T), f32)]
        + [shape(flat, bf16), shape(flat, f32), shape(flat, bf16)]
        + [shape((hidden // 2, width), bf16)] * 4
        + [shape((width // 2, width), bf16)] * 2
        + [shape((seq, PW), f32)] * 2
        + [shape((8, width), f32)]
    )
    return pl.pallas_call(
        layer_kernel,
        in_specs=[SMEM] + [IN_VMEM] * 5 + [anywhere] * 6,
        out_specs=[anywhere] * 19 + [IN_VMEM],
        out_shape=outs,
        scratch_shapes=[vmem(flat, bf16)]
        + [vmem(wqkv.shape, bf16), vmem((seq, PW), f32), vmem((seq, PW), f32)]
        + [vmem(heads, bf16)] * 3
        + [vmem((width, seq), bf16), vmem((width, width), bf16), vmem(flat, bf16)]
        + [vmem((chunks, width, FC), bf16), vmem((chunks, FC, width), bf16)]
        + [vmem(heads, bf16)] * 2
        + [vmem((PW, seq), bf16)] * 2
        + [vmem((AHEAD, seq + T, 2 * T), f32), vmem((2 * T, 2 * T), f32)]
        + [vmem(flat, bf16), vmem((width, seq), bf16)]
        + [vmem((pairs, seq // T, 2 * T), f32)]
        + [vmem(flat, f32), vmem(flat, bf16)]
        + [vmem(flat, f32)] * 2
        + [vmem((seq, FC), bf16)] * 2
        + [vmem((2, FC, width), bf16)] * 2
        + [vmem((2, width // 2, width), bf16)]
        + [dma((4,)), dma((chunks,)), dma((chunks,)), dma((12,)), dma((2,)), dma((2,)), dma((tiles, 3))],
        compiler_params=params(BIG),
        cost_estimate=LONG,
        name="layer",
    )(info, gain1, gain2, cosine_t, sine_t, received, *pinned(x, wqkv, wo, dy, w1, w2))


def weigh_kernel(first, info, dq, keep, got, cosine, signed, h1t, wqkv, sums, dkv, g_send, g_keep, small):
    width, half = wqkv.shape[0], wqkv.shape[0] // 2
    mine = pl.multiple_of(info[0] * half, half)
    dk = keep[0].astype(f32) + got[0].astype(f32)
    dkv[0] = rotated(dk, cosine[...], signed[...], -1.0).astype(bf16)
    dkv[1] = (keep[1].astype(f32) + got[1].astype(f32)).astype(bf16)
    small[...] = sums[...]
    for out, start in ((g_send, half - mine), (g_keep, mine)):
        rows = pl.ds(start, half)
        terms = 0.0
        for i, part in enumerate((dq, dkv.at[0], dkv.at[1])):
            total = nn(h1t[rows, :], part[...])
            out[i] = total.astype(bf16)
            at = i * width + first * PW
            weighted = total * wqkv[rows, at : at + total.shape[1]].astype(f32)
            for c in range(0, total.shape[1], PW):
                terms = terms + weighted[:, c : c + PW]
        line = jnp.sum(terms.T, axis=0, keepdims=True)
        lanes = lax.broadcasted_iota(jnp.int32, (1, width), 1)
        inside = jnp.logical_and(lanes >= start, lanes < start + half)
        small[4:5, :] += jnp.where(inside, jnp.concatenate([line, line], axis=1), 0.0)
    small[5:6, :] = jnp.full((1, width), info[1].astype(f32))


def weigh(info, first, dq, keep, got, tables, h1t, wqkv, sums):
    seq, width = dq.shape
    tall = h1t.shape[0]
    return pl.pallas_call(
        functools.partial(weigh_kernel, first),
        in_specs=[SMEM] + [IN_VMEM] * 8,
        out_specs=[IN_VMEM] * 4,
        out_shape=[shape((2, seq, width), bf16)]
        + [shape((3, tall // 2, width), bf16)] * 2
        + [shape(sums.shape, f32)],
        compiler_params=params(24),
        cost_estimate=LONG,
        name="weigh",
    )(info, dq, keep, got, *tables, h1t, wqkv, sums)


def finish_kernel(parts, tiles, x, dx2, wqkv, gain_line, *refs):
    dx_any, dx, sem = refs[-3:]
    dqs, dkvs = refs[:parts], refs[parts : 2 * parts]
    gain = gain_line[...].reshape(1, x.shape[1])

    def store(t):
        rows = pl.ds(pl.multiple_of(t * R, R), R)
        return pltpu.make_async_copy(dx.at[rows, :], dx_any.at[rows, :], sem.at[t])

    def some_rows(t, carry):
        rows = pl.ds(pl.multiple_of(t * R, R), R)
        grads = [r[rows, :] for r in dqs] + [r[0, rows, :] for r in dkvs] + [r[1, rows, :] for r in dkvs]
        dh = nt(jnp.concatenate(grads, axis=1), wqkv[...])
        grad, _ = norm_back(x[rows, :].astype(f32), gain, dh)
        dx[rows, :] = (dx2[rows, :] + grad).astype(bf16)
        store(t).start()
        return carry

    lax.fori_loop(*tiles, some_rows, 0)
    for t in range(*tiles):
        store(t).wait()


def finish(tiles, x, dx2, dqs, dkvs, weight, gain, before):
    anywhere = pl.BlockSpec(memory_space=pl.ANY)
    ins = 4 + len(dqs) + len(dkvs)
    return pl.pallas_call(
        functools.partial(finish_kernel, len(dqs), tiles),
        in_specs=[IN_VMEM] * ins + [anywhere] * len(before),
        out_specs=anywhere,
        out_shape=shape(x.shape, bf16),
        scratch_shapes=[pltpu.VMEM(x.shape, bf16), pltpu.SemaphoreType.DMA((x.shape[0] // R,))],
        input_output_aliases={ins: 0} if before else {},
        compiler_params=params(24),
        cost_estimate=COST if before else LONG,
        name="finish",
    )(x, dx2, weight, gain, *dqs, *dkvs, *before)


def bit_orders(count, groups):
    bits = [1 << i for i in range(count.bit_length() - 1)]
    if groups == 2:
        return [bits, bits[1::-1] + bits[2:]]
    return [bits[g:-1] + bits[:g] + bits[-1:] for g in range(groups)]


def exchange(value, axis, bit):
    size = lax.axis_size(axis)
    return lax.ppermute(value, axis, [(i, i ^ bit) for i in range(size)])


def distance(order, place):
    out = 0
    for i, bit in enumerate(order):
        out = out + ((place >> (len(order) - 1 - i)) & 1) * bit
    return out


SUMS = 8


def halves(value):
    high = value.astype(bf16)
    return high, (value - high.astype(f32)).astype(bf16)


def put_sums(value, kept, block):
    high, low = halves(value)
    lines = kept.shape[0]
    block[:lines, :] = high
    block[lines : 2 * lines, :] = low
    kept[...] = high.astype(f32) + low.astype(f32)


def got_sums(block):
    lines = block.shape[0] // 2
    return block[:lines, :].astype(f32) + block[lines:, :].astype(f32)


def start_kernel(orders, sources, small, me, *refs):
    groups = len(orders)
    arrays = max(a for source in sources for a, _, _ in source) + 1
    ins, outs = refs[: 2 * arrays], refs[len(refs) - 2 * groups :]
    half = outs[0].shape[0]
    for g, order in enumerate(orders):
        for side in range(2):

            def one(r, carry, g=g, order=order, side=side):
                part = me[0] ^ distance(order, r + side * half)
                out = outs[2 * g + side]
                row = 0
                for a, where, unit in sources[g]:
                    kept, got = ins[2 * a : 2 * a + 2]
                    place = where(part)
                    size, wide = kept.shape[1], out.shape[-1]
                    lanes = slice(unit * wide, (unit + 1) * wide)
                    total = kept[place, :, lanes].astype(f32) + got[place, :, lanes].astype(f32)
                    if len(out.shape) == 3:
                        out[r, row : row + size, :] = total.astype(bf16)
                    else:
                        start = pl.multiple_of(r * outs[0].shape[1] + row, 8)
                        out[pl.ds(start, size), :] = total.astype(bf16)
                    row += size
                return carry

            lax.fori_loop(0, half, one, 0)
    if small:
        here, there, kept = refs[2 * arrays : 2 * arrays + 3]
        total = here[...] + there[...]
        if small == "rides":
            wide = kept.shape[1]
            total = jnp.concatenate([total[:, c : c + wide] for c in range(0, total.shape[1], wide)], axis=0)
            put_sums(total, kept, outs[1].at[pl.ds(half * outs[0].shape[1], 2 * kept.shape[0]), :])
        else:
            kept[...] = total


def travelling(count, rows, width, lines):
    return shape((count * rows + 2 * lines, width) if lines else (count, rows, width), bf16)


def start_sum(me, kept, got, sources, width, orders, small, rides):
    count = 1 << len(orders[0])
    half = count // 2
    rows = [sum(kept[a].shape[1] for a, _, _ in source) for source in sources]
    lines = small[0].size // width if rides else 0
    cols = width // 3
    args = [a for pair in zip(kept, got, strict=True) for a in pair]
    sums = []
    for g in range(len(orders)):
        sums += [shape((half, rows[g], width), bf16), travelling(half, rows[g], width, 0 if g else lines)]
    mode = "rides" if rides else "alone" if small else ""
    if small:
        specs = dict(
            in_specs=[SMEM] + [IN_VMEM] * (len(args) + 2),
            out_specs=[IN_VMEM] * (1 + len(sums)),
            out_shape=[shape((lines, width) if rides else small[0].shape, f32)] + sums,
        )
    else:
        block = lambda a: pl.BlockSpec((a.shape[0], a.shape[1], cols), lambda c: (0, 0, c))
        specs = dict(
            grid=(width // cols,),
            in_specs=[SMEM] + [block(a) for a in args],
            out_specs=[block(a) for a in sums],
            out_shape=sums,
        )
    outs = pl.pallas_call(
        functools.partial(start_kernel, orders, sources, mode),
        compiler_params=params(30),
        cost_estimate=COST,
        name="start_sum",
        **specs,
    )(me, *args, *small)
    small, outs = list(outs[: len(outs) - len(sums)]), outs[len(outs) - len(sums) :]
    return list(outs[0::2]), list(outs[1::2]), small


def block_of(ref, r, size, row=0, step=0):
    if len(ref.shape) == 3:
        return ref.at[r, pl.ds(row, size), :]
    start = r * (step or size) + row
    return ref.at[pl.ds(start if isinstance(start, int) else pl.multiple_of(start, 8), size), :]


def step_kernel(groups, merge, mode, *refs):
    kept, got = refs[:groups], refs[groups : 2 * groups]
    outs = refs[2 * groups + (2 if mode == "alone" else 1 if mode else 0) :]
    count = kept[0].shape[0]
    half = count // 2

    def one(r, carry):
        row = 0
        for g in range(groups):
            keep, send = outs[:2] if merge else outs[2 * g : 2 * g + 2]
            size = kept[g].shape[1]
            for out, block in ((keep, r), (send, r + half)):
                total = kept[g][block].astype(f32) + block_of(got[g], block, size)[...].astype(f32)
                block_of(out, r, size, row, keep.shape[1])[...] = total.astype(bf16)
            row += size if merge else 0
        return carry

    lax.fori_loop(0, half, one, 0)
    if mode == "rides":
        total = refs[2 * groups][...] + got_sums(got[0][count * kept[0].shape[1] :])
        put_sums(total, outs[-1], outs[1].at[pl.ds(half * outs[0].shape[1], 2 * total.shape[0]), :])
    elif mode:
        outs[-1][...] = refs[2 * groups][...] + refs[2 * groups + 1][...]


def step_sum(kept, got, small, merge, rides):
    groups = len(kept)
    half = kept[0].shape[0] // 2
    rows = [a.shape[1] for a in kept]
    width = kept[0].shape[2]
    args = [*kept, *got, *small]
    sums = []
    for g, r in enumerate([sum(rows)] if merge else rows):
        sums += [shape((half, r, width), bf16), travelling(half, r, width, 0 if g or not rides else small[0].shape[0])]
    outs = pl.pallas_call(
        functools.partial(step_kernel, groups, merge, "rides" if rides else "alone" if small else ""),
        in_specs=[IN_VMEM] * len(args),
        out_specs=[IN_VMEM] * (len(sums) + len(small[:1])),
        out_shape=sums + [shape(a.shape, f32) for a in small[:1]],
        compiler_params=params(16),
        cost_estimate=COST if small or half == 1 else LONG,
        name="step_sum",
    )(*args)
    return list(outs[0 : len(sums) : 2]), list(outs[1 : len(sums) : 2]), list(outs[len(sums) :])


def feed_end_kernel(kept, got, down, up, out):
    total = kept[0].astype(f32) + got[0].astype(f32)
    tall, few = down.shape[0] // GROUPS, out.shape[0] // GROUPS
    ups = []
    for g in range(GROUPS):
        row = g * (2 * tall + few)
        down[g * tall : (g + 1) * tall, :] = total[row : row + tall]
        ups.append(total[row + tall : row + 2 * tall])
        out[g * few : (g + 1) * few, :] = total[row + 2 * tall : row + 2 * tall + few]
    up[...] = jnp.concatenate(ups, axis=0).T


def feed_end(kept, got, tall, few):
    width = kept.shape[2]
    return pl.pallas_call(
        feed_end_kernel,
        in_specs=[IN_VMEM] * 2,
        out_specs=[IN_VMEM] * 3,
        out_shape=[shape((tall, width), f32), shape((width, tall), f32), shape((few, width), f32)],
        compiler_params=params(16),
        cost_estimate=COST,
        name="feed_end",
    )(kept, got)


def qkv_end_kernel(places, rides, gain_line, kept, got, *refs):
    out, gain1, gain2, rms = refs[-4:]
    tall = out.shape[0]
    width = gain1.shape[0]
    cols = kept.shape[2]
    there = got[: kept.shape[1]] if rides else got[0]
    total = kept[0].astype(f32) + there.astype(f32)
    for i, at in enumerate(places):
        out[:, at : at + cols] = total[i * tall : (i + 1) * tall]
    if rides:
        sums = refs[0][...] + got_sums(got[kept.shape[1] :])
        sums = jnp.concatenate([sums[r : r + SUMS] for r in range(0, sums.shape[0], SUMS)], axis=1)
    else:
        sums = refs[0][...] + refs[1][...]
    gain2[...] = sums[3:4, :].reshape(width)
    gain1[...] = (sums[4:5, :] / gain_line[...].reshape(1, width)).reshape(width)
    count = jnp.max(sums[5:6, :], axis=1, keepdims=True) * width
    for i in range(3):
        rms[i] = jnp.sum(jnp.sqrt(jnp.sum(sums[i : i + 1, :], axis=1, keepdims=True) / count))


def qkv_end(places, gain, kept, got, small, tall, wide, rides):
    return pl.pallas_call(
        functools.partial(qkv_end_kernel, places, rides),
        in_specs=[IN_VMEM] * (3 + len(small)),
        out_specs=[IN_VMEM] * 3 + [SMEM],
        out_shape=[shape((tall, wide), f32), shape(gain.shape, f32), shape(gain.shape, f32), shape((3,), f32)],
        compiler_params=params(16),
        cost_estimate=COST,
        name="qkv_end",
    )(gain, kept, got, *small)


def after(value, *earlier):
    return lax.optimization_barrier((value, earlier))[0]


def sum_parts(me, kept, got, sources, width, small, rides):
    orders = bit_orders(lax.axis_size("batch"), len(sources))
    steps = len(orders[0])
    common = min(i for i in range(steps + 1) if all(order[i:] == orders[0][i:] for order in orders))
    keep, send, small = start_sum(me, kept, got, sources, width, orders, small, rides)
    for i in range(steps):
        got = [exchange(s, "batch", order[i]) for s, order in zip(send, orders[: len(send)], strict=True)]
        if small and not rides:
            small = [small[0], exchange(small[0], "batch", orders[0][i])]
        earlier = yield send[0], got
        if i == steps - 1:
            break
        if earlier is not None:
            keep = after(keep, earlier)
        keep, send, small = step_sum(keep, got, small, i + 1 == common, rides)
    yield keep[0], got[0], small


def on_device(
    inputs, lengths, cotangent, qkv_weight, out_weight, up_weight, down_weight, attn_gain, mlp_gain
):
    seq, width = inputs.shape[2:]
    x = inputs[0, 0]
    dy = cotangent[0, 0]
    count = lax.axis_size("batch")
    stream = lax.axis_index("stream").astype(jnp.int32)
    me = lax.axis_index("batch").astype(jnp.int32).reshape(1)
    info = jnp.stack([stream, lengths[0]])
    cosine, sine = rotary_tables(seq)
    tables_t = (jnp.asarray(cosine.T), jnp.asarray(sine.T))

    received = lax.ppermute(x, "stream", [(0, 1)])
    (
        q, ko, vo, kc, vc, h1t, o, lse, outputs, dx2, do,
        up_send, up_keep, down_send, down_keep, out_send, out_keep, *tables, sums,
    ) = layer(
        info, attn_gain, mlp_gain, *tables_t, received, x, qkv_weight, out_weight, dy, up_weight, down_weight
    )
    down_got, up_got, out_got = (exchange(a, "stream", 1) for a in (down_send, up_send, out_send))

    def by_rows(array):
        return array.reshape(count * GROUPS, array.shape[0] // (count * GROUPS), width)

    heads = (q, ko, vo, kc, vc, o)
    pairs = width // PW // 3
    dq1, keep1, send1 = attend_back(info, 0, pairs, *heads, do, lse, *tables_t)
    early = sum_parts(
        me,
        [by_rows(after(a, dq1)) for a in (down_keep, up_keep, out_keep)],
        [by_rows(a) for a in (down_got, up_got, out_got)],
        [[(a, lambda part, g=g: part * GROUPS + g, 0) for a in range(3)] for g in range(GROUPS)],
        width,
        [],
        False,
    )
    token = next(early)[0]
    got1 = lax.ppermute(after(send1, token), "stream", [(1, 0)])
    dq2, keep2, send2 = attend_back(info, pairs, 2 * pairs, *heads, after(do, token), lse, *tables_t)
    got2 = lax.ppermute(send2, "stream", [(1, 0)])
    token = early.send(dq2)[0]
    dkv1, qkv_send1, qkv_keep1, small = weigh(info, 0, dq1, after(keep1, token), got1, tables, h1t, qkv_weight, sums)
    qkv_got1 = exchange(qkv_send1, "stream", 1)
    dkv2, qkv_send2, qkv_keep2, small = weigh(info, pairs, dq2, keep2, got2, tables, h1t, qkv_weight, small)
    qkv_got2 = exchange(qkv_send2, "stream", 1)
    small_got = exchange(small, "stream", 1)
    token = early.send(dkv2)[0]

    tall = width // (2 * count)
    split = lambda a: a.reshape(3 * count, tall, a.shape[2])
    rides = tall % 8 == 0
    runs = [(0, i, 0) for i in range(3)] + [(1, i, c) for i in range(3) for c in range(2)]
    groups = runs[:4], runs[4:]
    late = sum_parts(
        me,
        [split(after(a, token)) for a in (qkv_keep1, qkv_keep2)],
        [split(a) for a in (qkv_got1, qkv_got2)],
        [[(a, lambda part, i=i: i * count + part, c) for a, i, c in group] for group in groups],
        pairs * PW,
        [small, small_got],
        rides,
    )
    token = next(late)[0]
    ends = [dq1, dq2], [dkv1, dkv2], qkv_weight, attn_gain
    dx = finish((0, 1), after(x, token), dx2, *ends, [])
    early_out = early.send(dx)
    dx = finish((1, seq // R), x, after(dx2, early_out[0]), *ends, [dx])
    late.send(dx)
    late_out = late.send(early_out[1])
    while len(late_out) == 2:
        late_out = late.send(None)
    while len(early_out) == 2:
        early_out = early.send(None)
    up_cols = down_keep.shape[0] // count
    down_grad, up_grad, out_grad = feed_end(*early_out[:2], up_cols, tall)
    places = [i * width + (a + c) * pairs * PW for a, i, c in runs]
    qkv_grad, gain1_grad, gain2_grad, rms = qkv_end(places, attn_gain, *late_out, tall, 3 * width, rides)
    return (
        outputs[None, None],
        dx[None, None],
        qkv_grad,
        out_grad,
        up_grad,
        down_grad,
        gain1_grad,
        gain2_grad,
        rms,
    )


def solution(mesh):
    rows = P("stream", "batch", None, None)
    both = ("stream", "batch")
    return jax.shard_map(
        on_device,
        mesh=mesh,
        in_specs=(rows, P("batch"), rows, P(), P(), P(), P(), P(), P()),
        out_specs=(rows, rows, P(both, None), P(both, None), P(None, both), P(both, None), P(), P(), P()),
        check_vma=False,
    )
```

```python
import functools

import jax
import jax.numpy as jnp
import numpy as np
from jax import lax
from jax.experimental import pallas as pl
from jax.experimental.pallas import tpu as pltpu
from jax.sharding import PartitionSpec as P

f32 = jnp.float32
bf16 = jnp.bfloat16

HD = 64
BLK = 16
EPS = 1e-06
NEG = -1e30
PW = 2 * HD
T = 128
R = 256
AHEAD = 2
FC = 768
SCALE = HD**-0.5
BIG = 58
GROUPS = 3

COST = pl.CostEstimate(flops=1 << 20, bytes_accessed=1 << 16, transcendentals=0)
LONG = pl.CostEstimate(flops=1 << 35, bytes_accessed=1 << 26, transcendentals=0)

SMEM = pl.BlockSpec(memory_space=pltpu.SMEM)
IN_VMEM = pl.BlockSpec(memory_space=pltpu.VMEM)


def params(mib):
    return pltpu.CompilerParams(vmem_limit_bytes=mib << 20)


def shape(dims, dtype):
    return jax.ShapeDtypeStruct(dims, dtype)


def pinned(*arrays):
    return [pltpu.with_memory_space_constraint(a, pltpu.HBM) for a in arrays]


def nn(a, b):
    return jnp.dot(a, b, preferred_element_type=f32)


def nt(a, b):
    return lax.dot_general(a, b, (((1,), (1,)), ((), ())), preferred_element_type=f32)


def tn(a, b):
    return lax.dot_general(a, b, (((0,), (0,)), ((), ())), preferred_element_type=f32)


def whole(dims):
    return pl.BlockSpec(dims, lambda *_: (0,) * len(dims), pipeline_mode=pl.Buffered(1))


def inv_rms(v):
    return lax.rsqrt(jnp.mean(v * v, axis=-1, keepdims=True) + EPS)


def norm_back(v, gain, grad):
    r = inv_rms(v)
    unit = v * r
    scaled = grad * gain
    inner = jnp.mean(scaled * unit, axis=-1, keepdims=True)
    return r * (scaled - unit * inner), grad * unit


def rotary_tables(length):
    half = HD // 2
    freqs = np.exp(-np.log(10000.0) * np.arange(half) / half).astype(np.float32)
    angles = (np.arange(length, dtype=np.float32)[:, None] * freqs[None, :]).astype(np.float64)
    return np.cos(angles).astype(np.float32), np.sin(angles).astype(np.float32)


def rotated(v, cosine, signed, sign):
    first = lax.broadcasted_iota(jnp.int32, (1, PW), 1) % HD < HD // 2
    outs = []
    for c in range(0, v.shape[1], PW):
        part = v[:, c : c + PW]
        partner = jnp.where(first, pltpu.roll(part, PW - HD // 2, 1), pltpu.roll(part, HD // 2, 1))
        outs.append(part * cosine + partner * (signed * sign))
    return outs[0] if len(outs) == 1 else jnp.concatenate(outs, axis=1)


def in_turn(count, *stages, at_once=1):
    def turn(n, carry):
        state = [()] * at_once
        for step in range(at_once + len(stages) - 1):
            for k, stage in enumerate(stages):
                if 0 <= step - k < at_once:
                    state[step - k] = stage(at_once * n + step - k, *state[step - k])
        return carry

    lax.fori_loop(0, count // at_once, turn, 0)


def token_weight(start, length, rows):
    return lax.broadcasted_iota(jnp.int32, (rows, 1), 0) + start < length


def row_sum(v):
    return jnp.sum(v, axis=0, keepdims=True)


def by_pairs(ref, rows, value):
    for p in range(ref.shape[0]):
        ref[p, rows, :] = value[:, p * PW : (p + 1) * PW].astype(ref.dtype)


def stacked(tile, low):
    zero = jnp.zeros_like(tile)
    return jnp.concatenate([jnp.where(low, tile, zero), jnp.where(low, zero, tile)], axis=0)


def unstacked(tile_t):
    half = lax.broadcasted_iota(jnp.int32, (PW, 1), 0) < HD
    return jnp.where(half, tile_t[:, :T], tile_t[:, T:])


def chunks_of(i):
    out, j = [], 0
    while j < i:
        n = 2 if i - j >= 2 else 1
        out.append((j * T, n * T))
        j += n
    return out


def edge_bias(ref, noisy):
    row = lax.broadcasted_iota(jnp.int32, (T, 2 * T), 0) // BLK
    col = (lax.broadcasted_iota(jnp.int32, (T, 2 * T), 1) % T) // BLK
    own = jnp.logical_or(row == col, jnp.logical_and(row < col, noisy == 0))
    other = jnp.logical_and(row < col, noisy == 1)
    ref[:T, :] = jnp.where(own, 0.0, NEG)
    ref[T:, :] = jnp.where(other, 0.0, NEG)


def masked(s, start, length):
    pos = lax.broadcasted_iota(jnp.int32, s.shape, 0) + start
    return jnp.where(pos < length, s, NEG)


def over_rows(op, v):
    return op(v.reshape(v.shape[0] // 8, 8, v.shape[1]), axis=0)


def attend_pair(length, q, ko, vo, kc, vc, store, lse, vo_t, vc_t, scores, bias):
    seq = q.shape[0]
    low = lax.broadcasted_iota(jnp.int32, (1, PW), 1) < HD
    vo_t[...] = vo[...].T
    vc_t[...] = vc[...].T

    def score(i):
        at = pl.ds(i * T, T)
        q2 = stacked(q[at, :] * bf16(SCALE), low)
        buf = scores.at[i % AHEAD]
        edge = nt(jnp.concatenate([ko[at, :], kc[at, :]], 0), q2) + bias[...]
        own = masked(edge[:T], i * T, length)
        other = masked(edge[T:], i * T, length)
        buf[pl.ds(0, T), :] = own
        buf[pl.ds(T, T), :] = other
        top = over_rows(jnp.max, jnp.maximum(own, other))
        for start, size in chunks_of(i):
            s = masked(nt(kc[pl.ds(start, size), :], q2), start, length)
            buf[pl.ds(2 * T + start, size), :] = s
            top = jnp.maximum(top, over_rows(jnp.max, s))
        return jnp.max(top, axis=0, keepdims=True)

    def mix(i, top):
        at = pl.ds(i * T, T)
        buf = scores.at[i % AHEAD]
        p = jnp.exp(buf[pl.ds(0, 2 * T), :] - top)
        total = over_rows(jnp.sum, p)
        acc = nn(jnp.concatenate([vo_t[:, at], vc_t[:, at]], 1), p.astype(bf16))
        for start, size in chunks_of(i):
            p = jnp.exp(buf[pl.ds(2 * T + start, size), :] - top)
            total = total + over_rows(jnp.sum, p)
            acc = acc + nn(vc_t[:, pl.ds(start, size)], p.astype(bf16))
        total = row_sum(total)
        lse[0, pl.ds(i, 1), :] = top + jnp.log(total)
        store(at, unstacked(acc * (1.0 / total)))

    tops = {}
    for i in range(seq // T + AHEAD - 1):
        if i < seq // T:
            tops[i] = score(i)
        if i >= AHEAD - 1:
            mix(i - AHEAD + 1, tops.pop(i - AHEAD + 1))


def turned_back(v, cosine, sine):
    quarter = HD // 2
    a, b, c, d = (v[i * quarter : (i + 1) * quarter] for i in range(4))
    return jnp.concatenate(
        [a * cosine + b * sine, b * cosine - a * sine, c * cosine + d * sine, d * cosine - c * sine]
    )


def attend_back_kernel(
    info, q, ko, vo, kc, vc, o, do, lse, cosine, sine, dq, keep, send, ko_t, kc_t, dko, dvo, dkc, dvc, bias
):
    noisy, length = info[0], info[1]
    q, ko, vo, kc, vc = (ref.at[0] for ref in (q, ko, vo, kc, vc))
    seq = q.shape[0]
    low = lax.broadcasted_iota(jnp.int32, (1, PW), 1) < HD

    @pl.when(pl.program_id(0) == 0)
    def _():
        edge_bias(bias, noisy)

    ko_t[...] = ko[...].T
    kc_t[...] = kc[...].T

    def tile(i):
        at = pl.ds(i * T, T)
        prod = (do[at, :].astype(f32) * o[at, :].astype(f32)).T
        delta = jnp.concatenate([row_sum(prod[:HD]), row_sum(prod[HD:])], 1)
        q2 = stacked(q[at, :] * bf16(SCALE), low)
        return q2, stacked(do[at, :], low), lse[0, pl.ds(i, 1), :], delta

    def products(i, start, size, q2, do2):
        if start is None:
            at = pl.ds(i * T, T)
            s = nt(jnp.concatenate([ko[at, :], kc[at, :]], 0), q2) + bias[...]
            s = jnp.concatenate([masked(s[:T], i * T, length), masked(s[T:], i * T, length)], 0)
            return s, nt(jnp.concatenate([vo[at, :], vc[at, :]], 0), do2)
        rows = pl.ds(start, size)
        return masked(nt(kc[rows, :], q2), start, length), nt(vc[rows, :], do2)

    def gather(i, start, size, q2, do2, p, ds, dq_t):
        at = pl.ds(i * T, T)
        dv, dk = nn(p, do2), nn(ds, q2)
        if start is None:
            dvo[at, :] = dv[:T]
            dko[at, :] = dk[:T]
            dvc[at, :] = dv[T:]
            dkc[at, :] = dk[T:]
            return nn(jnp.concatenate([ko_t[:, at], kc_t[:, at]], 1), ds)
        rows = pl.ds(start, size)
        dvc[rows, :] += dv
        dkc[rows, :] += dk
        return dq_t + nn(kc_t[:, rows], ds)

    work = [(i, *c) for i in range(seq // T) for c in [(None, None)] + chunks_of(i)]
    tiles, made, weighed, dq_t = {}, {}, {}, None
    for n in range(len(work) + 2):
        if n < len(work):
            i = work[n][0]
            if i not in tiles:
                tiles[i] = tile(i)
            made[n] = products(*work[n], *tiles[i][:2])
        if 0 <= n - 1 < len(work):
            _, _, norm, delta = tiles[work[n - 1][0]]
            s, dp = made.pop(n - 1)
            p = jnp.exp(s - norm)
            weighed[n - 1] = p.astype(bf16), (p * (dp - delta)).astype(bf16)
        if n >= 2:
            i, start, size = work[n - 2]
            dq_t = gather(i, start, size, *tiles[i][:2], *weighed.pop(n - 2), dq_t)
            if n == len(work) + 1 or work[n - 1][0] != i:
                at = pl.ds(i * T, T)
                out = turned_back(unstacked(dq_t), cosine[:, at], sine[:, at]) * SCALE
                dq[at, :] = out.T.astype(bf16)
    clean = (1 - noisy).astype(f32)
    for at, own, other in ((0, dko, dkc), (1, dvo, dvc)):
        keep[at] = (own[...] + clean * other[...]).astype(bf16)
        send[at] = other[...].astype(bf16)


def attend_back(info, first, pairs, q, ko, vo, kc, vc, o, do, lse, cosine, sine):
    seq = q.shape[1]
    width = pairs * PW
    heads = pl.BlockSpec((1, seq, PW), lambda h: (first + h, 0, 0))
    source = pl.BlockSpec((seq, PW), lambda h: (0, first + h))
    both = pl.BlockSpec((2, seq, PW), lambda h: (0, 0, h))
    lines = pl.BlockSpec((1, seq // T, 2 * T), lambda h: (first + h, 0, 0))
    table = whole((HD // 2, seq))
    return pl.pallas_call(
        attend_back_kernel,
        grid=(pairs,),
        in_specs=[SMEM] + [heads] * 5 + [source] * 2 + [lines, table, table],
        out_specs=[pl.BlockSpec((seq, PW), lambda h: (0, h)), both, both],
        out_shape=[shape((seq, width), bf16)] + [shape((2, seq, width), bf16)] * 2,
        scratch_shapes=[pltpu.VMEM((PW, seq), bf16)] * 2
        + [pltpu.VMEM((seq, PW), f32)] * 4
        + [pltpu.VMEM((2 * T, 2 * T), f32)],
        compiler_params=params(24),
        cost_estimate=LONG,
        name="attend_back",
    )(info, *pinned(q, ko, vo, kc, vc, o, do, lse), cosine, sine)


C0 = 0.7978845608028654
C1 = C0 * 0.044715


def layer_kernel(
    info, gain1_line, gain2_line, cosine_t, sine_t, received, x_any, wqkv_any, wo_any, dy_any,
    w1_any, w2_any,
    q_out, ko_out, vo_out, kc_out, vc_out, h1t_out, o_out, lse_out, out_any, dx2_any, do_any,
    up_send, up_keep, down_send, down_keep, g_send, g_keep, cosine_out, signed_out, sums,
    x, wqkv, cosine, signed, q, ko, vo, h1t, wo, dy, w1, w2,
    kc, vc, vo_t, vc_t, scores, bias, o, o_t, lse, x2, h2, m, dh, act, du, up_grad, down_grad, half_grads,
    sem_in, sem_1, sem_2, sem_out, sem_up, sem_down, sem_tile,
):
    noisy, length = info[0], info[1]
    seq, width = x.shape
    chunks, pairs, tiles = w1.shape[0], kc.shape[0], seq // R
    copy = pltpu.make_async_copy
    gain1, gain2 = gain1_line[...].reshape(1, width), gain2_line[...].reshape(1, width)

    def weights(c):
        place = lax.rem(c + (chunks // 2) * (1 - noisy), chunks) * FC
        place = pl.multiple_of(place, FC)
        return (
            copy(w1_any.at[:, pl.ds(place, FC)], w1.at[c], sem_1.at[c]),
            copy(w2_any.at[pl.ds(place, FC), :], w2.at[c], sem_2.at[c]),
        )

    sources = (
        (x_any, x),
        (wqkv_any, wqkv),
        (wo_any, wo),
        (dy_any, dy),
    )
    loads = [copy(a, b, sem_in.at[i]) for i, (a, b) in enumerate(sources)]
    for load in loads[:2]:
        load.start()
    sums[...] = jnp.zeros_like(sums)
    edge_bias(bias, noisy)
    def widen(t):
        rows = pl.ds(pl.multiple_of(t * PW, PW), PW)
        c, d = cosine_t[:, rows].T, sine_t[:, rows].T
        cosine[rows, :] = jnp.concatenate([c, c, c, c], axis=1)
        signed[rows, :] = jnp.concatenate([-d, d, -d, d], axis=1)
        return ()

    in_turn(seq // PW, widen)
    tables_out = [copy(cosine, cosine_out, sem_out.at[10]), copy(signed, signed_out, sem_out.at[11])]
    span = lambda t: pl.ds(pl.multiple_of(t * R, R), R)

    loads[0].wait()

    def own_norm(t):
        value = x[span(t), :].astype(f32)
        h1 = (value * inv_rms(value) * gain1).astype(bf16)
        h2[span(t), :] = h1
        h1t[:, span(t)] = h1.T
        weight = token_weight(t * R, length, R)
        sums[0:1, :] += row_sum(jnp.where(weight, value * value, 0.0))
        return ()

    in_turn(tiles, own_norm)
    loads[1].wait()
    for load in loads[2:]:
        load.start()

    def own_product(t):
        return tuple(nn(h2[span(t), :], wqkv[:, i * width : (i + 1) * width]) for i in range(3))

    def own_turn(t, a, b, c):
        tables = (cosine[span(t), :], signed[span(t), :], 1.0)
        by_pairs(q, span(t), rotated(a, *tables))
        by_pairs(ko, span(t), rotated(b, *tables))
        by_pairs(vo, span(t), c)
        return ()

    def clean_norm(t):
        value = jnp.where(noisy == 1, received[span(t), :].astype(f32), x[span(t), :].astype(f32))
        o[span(t), :] = (value * inv_rms(value) * gain1).astype(bf16)
        return ()

    def clean_product(t):
        return tuple(nn(o[span(t), :], wqkv[:, i * width : (i + 1) * width]) for i in (1, 2))

    def clean_turn(t, a, b):
        by_pairs(kc, span(t), rotated(a, cosine[span(t), :], signed[span(t), :], 1.0))
        by_pairs(vc, span(t), b)
        return ()

    in_turn(tiles, own_product, own_turn)
    stores = [
        copy(a, b, sem_out.at[6 + i])
        for i, (a, b) in enumerate(((q, q_out), (ko, ko_out), (vo, vo_out), (h1t, h1t_out)))
    ]
    stores += tables_out
    for store in stores:
        store.start()
    in_turn(tiles, clean_norm, clean_product, clean_turn)
    more = [copy(kc, kc_out, sem_out.at[0]), copy(vc, vc_out, sem_out.at[1])]
    for store in more:
        store.start()
    stores += more

    for c in range(chunks):
        for load in weights(c):
            load.start()

    def one_pair(p, carry):
        lanes = pl.ds(pl.multiple_of(p * PW, PW), PW)

        def keep(at, tile_t):
            o_t[lanes, at] = tile_t.astype(bf16)
            o[at, lanes] = tile_t.T.astype(bf16)

        heads = (ref.at[p] for ref in (q, ko, vo, kc, vc))
        attend_pair(length, *heads, keep, lse.at[pl.ds(p, 1)], vo_t, vc_t, scores, bias)
        return carry

    lax.fori_loop(0, pairs, one_pair, 0)
    mixed_out = copy(o, o_out, sem_out.at[2])
    mixed_out.start()
    stores += [copy(lse, lse_out, sem_out.at[3])]
    stores[-1].start()

    for load in loads[2:]:
        load.wait()

    def join_product(t):
        return (nn(o[span(t), :], wo[...]),)

    def join_norm(t, branch):
        value = x[span(t), :].astype(f32) + branch
        x2[span(t), :] = value
        h2[span(t), :] = (value * inv_rms(value) * gain2).astype(bf16)
        m[span(t), :] = jnp.zeros_like(value)
        dh[span(t), :] = jnp.zeros_like(value)
        weight = token_weight(t * R, length, R)
        sums[1:2, :] += row_sum(jnp.where(weight, branch * branch, 0.0))
        return ()

    in_turn(tiles, join_product, join_norm, at_once=2)

    def grad_stores(c, up, down):
        slot = lax.rem(c, 2)
        rows = pl.ds(pl.multiple_of(lax.rem(c, chunks // 2) * FC, FC), FC)
        return (
            copy(up_grad.at[slot], up.at[rows, :], sem_up.at[slot]),
            copy(down_grad.at[slot], down.at[rows, :], sem_down.at[slot]),
        )

    def one_chunk(c, carry):
        for load in weights(c):
            load.wait()
        up, down = w1.at[c], w2.at[c]
        made = {}
        for t in range(-R, seq, R):
            if t + R < seq:
                rows = pl.ds(t + R, R)
                made[t + R] = nn(h2[rows, :], up[...]), nt(dy[rows, :], down[...])
            if t < 0:
                continue
            rows = pl.ds(t, R)
            u, da = made.pop(t)
            sq = u * u
            half = 0.5 * jnp.tanh(u * (C0 + C1 * sq)) + 0.5
            low = (u * half).astype(bf16)
            slope = half + u * (2.0 * half * (1.0 - half)) * (C0 + 3.0 * C1 * sq)
            back = (da * slope).astype(bf16)
            act[rows, :] = low
            du[rows, :] = back
            m[rows, :] += nn(low, down[...])
            dh[rows, :] += nt(back, up[...])

        @pl.when(c >= 2)
        def _():
            for store in grad_stores(c, up_send, down_send):
                store.wait()

        slot = lax.rem(c, 2)
        down_grad[slot] = tn(act[...], dy[...]).astype(bf16)
        up_grad[slot] = tn(du[...], h2[...]).astype(bf16)

        @pl.when(c < chunks // 2)
        def _():
            for store in grad_stores(c, up_send, down_send):
                store.start()

        @pl.when(c >= chunks // 2)
        def _():
            for store in grad_stores(c, up_keep, down_keep):
                store.start()

        return carry

    lax.fori_loop(0, chunks, one_chunk, 0)

    mixed_out.wait()

    def tile_stores(t):
        return (
            copy(h2.at[span(t), :], out_any.at[span(t), :], sem_tile.at[t, 0]),
            copy(x2.at[span(t), :], dx2_any.at[span(t), :], sem_tile.at[t, 1]),
            copy(o.at[span(t), :], do_any.at[span(t), :], sem_tile.at[t, 2]),
        )

    def middle_norm(t):
        value = x2[span(t), :]
        mixed = m[span(t), :]
        weight = token_weight(t * R, length, R)
        sums[2:3, :] += row_sum(jnp.where(weight, mixed * mixed, 0.0))
        grad, gain_terms = norm_back(value, gain2, dh[span(t), :])
        sums[3:4, :] += row_sum(gain_terms)
        grad = grad + dy[span(t), :].astype(f32)
        h2[span(t), :] = (value + mixed).astype(bf16)
        x2[span(t), :] = grad
        x[span(t), :] = grad.astype(bf16)
        return ()

    def middle_product(t):
        o[span(t), :] = nt(x[span(t), :], wo[...]).astype(bf16)
        for store in tile_stores(t):
            store.start()
        return ()

    in_turn(tiles, middle_norm, middle_product, at_once=2)
    half = width // 2
    mine = pl.multiple_of(noisy * half, half)
    half_grads[0] = nn(o_t[pl.ds(half - mine, half), :], x[...]).astype(bf16)
    half_grads[1] = nn(o_t[pl.ds(mine, half), :], x[...]).astype(bf16)
    more = [copy(half_grads.at[0], g_send, sem_out.at[4]), copy(half_grads.at[1], g_keep, sem_out.at[5])]
    for store in more:
        store.start()
    stores += more
    for c in range(chunks - 2, chunks):
        stores += grad_stores(c, up_keep, down_keep)
    for t in range(tiles):
        stores += tile_stores(t)
    for store in stores:
        store.wait()


def layer(info, gain1, gain2, cosine_t, sine_t, received, x, wqkv, wo, dy, w1, w2):
    seq, width = x.shape
    hidden = w1.shape[1]
    tiles, pairs, chunks = seq // R, width // PW, hidden // FC
    anywhere = pl.BlockSpec(memory_space=pl.ANY)
    vmem = pltpu.VMEM
    dma = pltpu.SemaphoreType.DMA
    heads = (pairs, seq, PW)
    flat = (seq, width)
    outs = (
        [shape(heads, bf16)] * 5
        + [shape((width, seq), bf16), shape(flat, bf16), shape((pairs, seq // T, 2 * T), f32)]
        + [shape(flat, bf16), shape(flat, f32), shape(flat, bf16)]
        + [shape((hidden // 2, width), bf16)] * 4
        + [shape((width // 2, width), bf16)] * 2
        + [shape((seq, PW), f32)] * 2
        + [shape((8, width), f32)]
    )
    return pl.pallas_call(
        layer_kernel,
        in_specs=[SMEM] + [IN_VMEM] * 5 + [anywhere] * 6,
        out_specs=[anywhere] * 19 + [IN_VMEM],
        out_shape=outs,
        scratch_shapes=[vmem(flat, bf16)]
        + [vmem(wqkv.shape, bf16), vmem((seq, PW), f32), vmem((seq, PW), f32)]
        + [vmem(heads, bf16)] * 3
        + [vmem((width, seq), bf16), vmem((width, width), bf16), vmem(flat, bf16)]
        + [vmem((chunks, width, FC), bf16), vmem((chunks, FC, width), bf16)]
        + [vmem(heads, bf16)] * 2
        + [vmem((PW, seq), bf16)] * 2
        + [vmem((AHEAD, seq + T, 2 * T), f32), vmem((2 * T, 2 * T), f32)]
        + [vmem(flat, bf16), vmem((width, seq), bf16)]
        + [vmem((pairs, seq // T, 2 * T), f32)]
        + [vmem(flat, f32), vmem(flat, bf16)]
        + [vmem(flat, f32)] * 2
        + [vmem((seq, FC), bf16)] * 2
        + [vmem((2, FC, width), bf16)] * 2
        + [vmem((2, width // 2, width), bf16)]
        + [dma((4,)), dma((chunks,)), dma((chunks,)), dma((12,)), dma((2,)), dma((2,)), dma((tiles, 3))],
        compiler_params=params(BIG),
        cost_estimate=LONG,
        name="layer",
    )(info, gain1, gain2, cosine_t, sine_t, received, *pinned(x, wqkv, wo, dy, w1, w2))


def weigh_kernel(first, info, dq, keep, got, cosine, signed, h1t, wqkv, sums, dkv, g_send, g_keep, small):
    width, half = wqkv.shape[0], wqkv.shape[0] // 2
    mine = pl.multiple_of(info[0] * half, half)
    dk = keep[0].astype(f32) + got[0].astype(f32)
    dkv[0] = rotated(dk, cosine[...], signed[...], -1.0).astype(bf16)
    dkv[1] = (keep[1].astype(f32) + got[1].astype(f32)).astype(bf16)
    small[...] = sums[...]
    for out, start in ((g_send, half - mine), (g_keep, mine)):
        rows = pl.ds(start, half)
        terms = 0.0
        for i, part in enumerate((dq, dkv.at[0], dkv.at[1])):
            total = nn(h1t[rows, :], part[...])
            out[i] = total.astype(bf16)
            at = i * width + first * PW
            weighted = total * wqkv[rows, at : at + total.shape[1]].astype(f32)
            for c in range(0, total.shape[1], PW):
                terms = terms + weighted[:, c : c + PW]
        line = jnp.sum(terms.T, axis=0, keepdims=True)
        lanes = lax.broadcasted_iota(jnp.int32, (1, width), 1)
        inside = jnp.logical_and(lanes >= start, lanes < start + half)
        small[4:5, :] += jnp.where(inside, jnp.concatenate([line, line], axis=1), 0.0)
    small[5:6, :] = jnp.full((1, width), info[1].astype(f32))


def weigh(info, first, dq, keep, got, tables, h1t, wqkv, sums):
    seq, width = dq.shape
    tall = h1t.shape[0]
    return pl.pallas_call(
        functools.partial(weigh_kernel, first),
        in_specs=[SMEM] + [IN_VMEM] * 8,
        out_specs=[IN_VMEM] * 4,
        out_shape=[shape((2, seq, width), bf16)]
        + [shape((3, tall // 2, width), bf16)] * 2
        + [shape(sums.shape, f32)],
        compiler_params=params(24),
        cost_estimate=LONG,
        name="weigh",
    )(info, dq, keep, got, *tables, h1t, wqkv, sums)


def finish_kernel(parts, tiles, x, dx2, wqkv, gain_line, *refs):
    dx_any, dx, sem = refs[-3:]
    dqs, dkvs = refs[:parts], refs[parts : 2 * parts]
    gain = gain_line[...].reshape(1, x.shape[1])

    def store(t):
        rows = pl.ds(pl.multiple_of(t * R, R), R)
        return pltpu.make_async_copy(dx.at[rows, :], dx_any.at[rows, :], sem.at[t])

    def some_rows(t, carry):
        rows = pl.ds(pl.multiple_of(t * R, R), R)
        grads = [r[rows, :] for r in dqs] + [r[0, rows, :] for r in dkvs] + [r[1, rows, :] for r in dkvs]
        dh = nt(jnp.concatenate(grads, axis=1), wqkv[...])
        grad, _ = norm_back(x[rows, :].astype(f32), gain, dh)
        dx[rows, :] = (dx2[rows, :] + grad).astype(bf16)
        store(t).start()
        return carry

    lax.fori_loop(*tiles, some_rows, 0)
    for t in range(*tiles):
        store(t).wait()


def finish(tiles, x, dx2, dqs, dkvs, weight, gain, before):
    anywhere = pl.BlockSpec(memory_space=pl.ANY)
    ins = 4 + len(dqs) + len(dkvs)
    return pl.pallas_call(
        functools.partial(finish_kernel, len(dqs), tiles),
        in_specs=[IN_VMEM] * ins + [anywhere] * len(before),
        out_specs=anywhere,
        out_shape=shape(x.shape, bf16),
        scratch_shapes=[pltpu.VMEM(x.shape, bf16), pltpu.SemaphoreType.DMA((x.shape[0] // R,))],
        input_output_aliases={ins: 0} if before else {},
        compiler_params=params(24),
        cost_estimate=COST if before else LONG,
        name="finish",
    )(x, dx2, weight, gain, *dqs, *dkvs, *before)


def bit_orders(count, groups):
    bits = [1 << i for i in range(count.bit_length() - 1)]
    if groups == 2:
        return [bits, bits[1::-1] + bits[2:]]
    return [bits[g:-1] + bits[:g] + bits[-1:] for g in range(groups)]


def exchange(value, axis, bit):
    size = lax.axis_size(axis)
    return lax.ppermute(value, axis, [(i, i ^ bit) for i in range(size)])


def distance(order, place):
    out = 0
    for i, bit in enumerate(order):
        out = out + ((place >> (len(order) - 1 - i)) & 1) * bit
    return out


SUMS = 8


def halves(value):
    high = value.astype(bf16)
    return high, (value - high.astype(f32)).astype(bf16)


def put_sums(value, kept, block):
    high, low = halves(value)
    lines = kept.shape[0]
    block[:lines, :] = high
    block[lines : 2 * lines, :] = low
    kept[...] = high.astype(f32) + low.astype(f32)


def got_sums(block):
    lines = block.shape[0] // 2
    return block[:lines, :].astype(f32) + block[lines:, :].astype(f32)


def start_kernel(orders, sources, small, me, *refs):
    groups = len(orders)
    arrays = max(a for source in sources for a, _, _ in source) + 1
    ins, outs = refs[: 2 * arrays], refs[len(refs) - 2 * groups :]
    half = outs[0].shape[0]
    for g, order in enumerate(orders):
        for side in range(2):

            def one(r, carry, g=g, order=order, side=side):
                part = me[0] ^ distance(order, r + side * half)
                out = outs[2 * g + side]
                row = 0
                for a, where, unit in sources[g]:
                    kept, got = ins[2 * a : 2 * a + 2]
                    place = where(part)
                    size, wide = kept.shape[1], out.shape[-1]
                    lanes = slice(unit * wide, (unit + 1) * wide)
                    total = kept[place, :, lanes].astype(f32) + got[place, :, lanes].astype(f32)
                    if len(out.shape) == 3:
                        out[r, row : row + size, :] = total.astype(bf16)
                    else:
                        start = pl.multiple_of(r * outs[0].shape[1] + row, 8)
                        out[pl.ds(start, size), :] = total.astype(bf16)
                    row += size
                return carry

            lax.fori_loop(0, half, one, 0)
    if small:
        here, there, kept = refs[2 * arrays : 2 * arrays + 3]
        total = here[...] + there[...]
        if small == "rides":
            wide = kept.shape[1]
            total = jnp.concatenate([total[:, c : c + wide] for c in range(0, total.shape[1], wide)], axis=0)
            put_sums(total, kept, outs[1].at[pl.ds(half * outs[0].shape[1], 2 * kept.shape[0]), :])
        else:
            kept[...] = total


def travelling(count, rows, width, lines):
    return shape((count * rows + 2 * lines, width) if lines else (count, rows, width), bf16)


def start_sum(me, kept, got, sources, width, orders, small, rides):
    count = 1 << len(orders[0])
    half = count // 2
    rows = [sum(kept[a].shape[1] for a, _, _ in source) for source in sources]
    lines = small[0].size // width if rides else 0
    cols = width // 3
    args = [a for pair in zip(kept, got, strict=True) for a in pair]
    sums = []
    for g in range(len(orders)):
        sums += [shape((half, rows[g], width), bf16), travelling(half, rows[g], width, 0 if g else lines)]
    mode = "rides" if rides else "alone" if small else ""
    if small:
        specs = dict(
            in_specs=[SMEM] + [IN_VMEM] * (len(args) + 2),
            out_specs=[IN_VMEM] * (1 + len(sums)),
            out_shape=[shape((lines, width) if rides else small[0].shape, f32)] + sums,
        )
    else:
        block = lambda a: pl.BlockSpec((a.shape[0], a.shape[1], cols), lambda c: (0, 0, c))
        specs = dict(
            grid=(width // cols,),
            in_specs=[SMEM] + [block(a) for a in args],
            out_specs=[block(a) for a in sums],
            out_shape=sums,
        )
    outs = pl.pallas_call(
        functools.partial(start_kernel, orders, sources, mode),
        compiler_params=params(30),
        cost_estimate=COST,
        name="start_sum",
        **specs,
    )(me, *args, *small)
    small, outs = list(outs[: len(outs) - len(sums)]), outs[len(outs) - len(sums) :]
    return list(outs[0::2]), list(outs[1::2]), small


def block_of(ref, r, size, row=0, step=0):
    if len(ref.shape) == 3:
        return ref.at[r, pl.ds(row, size), :]
    start = r * (step or size) + row
    return ref.at[pl.ds(start if isinstance(start, int) else pl.multiple_of(start, 8), size), :]


def step_kernel(groups, merge, mode, *refs):
    kept, got = refs[:groups], refs[groups : 2 * groups]
    outs = refs[2 * groups + (2 if mode == "alone" else 1 if mode else 0) :]
    count = kept[0].shape[0]
    half = count // 2

    def one(r, carry):
        row = 0
        for g in range(groups):
            keep, send = outs[:2] if merge else outs[2 * g : 2 * g + 2]
            size = kept[g].shape[1]
            for out, block in ((keep, r), (send, r + half)):
                total = kept[g][block].astype(f32) + block_of(got[g], block, size)[...].astype(f32)
                block_of(out, r, size, row, keep.shape[1])[...] = total.astype(bf16)
            row += size if merge else 0
        return carry

    lax.fori_loop(0, half, one, 0)
    if mode == "rides":
        total = refs[2 * groups][...] + got_sums(got[0][count * kept[0].shape[1] :])
        put_sums(total, outs[-1], outs[1].at[pl.ds(half * outs[0].shape[1], 2 * total.shape[0]), :])
    elif mode:
        outs[-1][...] = refs[2 * groups][...] + refs[2 * groups + 1][...]


def step_sum(kept, got, small, merge, rides):
    groups = len(kept)
    half = kept[0].shape[0] // 2
    rows = [a.shape[1] for a in kept]
    width = kept[0].shape[2]
    args = [*kept, *got, *small]
    sums = []
    for g, r in enumerate([sum(rows)] if merge else rows):
        sums += [shape((half, r, width), bf16), travelling(half, r, width, 0 if g or not rides else small[0].shape[0])]
    outs = pl.pallas_call(
        functools.partial(step_kernel, groups, merge, "rides" if rides else "alone" if small else ""),
        in_specs=[IN_VMEM] * len(args),
        out_specs=[IN_VMEM] * (len(sums) + len(small[:1])),
        out_shape=sums + [shape(a.shape, f32) for a in small[:1]],
        compiler_params=params(16),
        cost_estimate=COST if small or half == 1 else LONG,
        name="step_sum",
    )(*args)
    return list(outs[0 : len(sums) : 2]), list(outs[1 : len(sums) : 2]), list(outs[len(sums) :])


def feed_end_kernel(kept, got, down, up, out):
    total = kept[0].astype(f32) + got[0].astype(f32)
    tall, few = down.shape[0] // GROUPS, out.shape[0] // GROUPS
    ups = []
    for g in range(GROUPS):
        row = g * (2 * tall + few)
        down[g * tall : (g + 1) * tall, :] = total[row : row + tall]
        ups.append(total[row + tall : row + 2 * tall])
        out[g * few : (g + 1) * few, :] = total[row + 2 * tall : row + 2 * tall + few]
    up[...] = jnp.concatenate(ups, axis=0).T


def feed_end(kept, got, tall, few):
    width = kept.shape[2]
    return pl.pallas_call(
        feed_end_kernel,
        in_specs=[IN_VMEM] * 2,
        out_specs=[IN_VMEM] * 3,
        out_shape=[shape((tall, width), f32), shape((width, tall), f32), shape((few, width), f32)],
        compiler_params=params(16),
        cost_estimate=COST,
        name="feed_end",
    )(kept, got)


def qkv_end_kernel(places, rides, gain_line, kept, got, *refs):
    out, gain1, gain2, rms = refs[-4:]
    tall = out.shape[0]
    width = gain1.shape[0]
    cols = kept.shape[2]
    there = got[: kept.shape[1]] if rides else got[0]
    total = kept[0].astype(f32) + there.astype(f32)
    for i, at in enumerate(places):
        out[:, at : at + cols] = total[i * tall : (i + 1) * tall]
    if rides:
        sums = refs[0][...] + got_sums(got[kept.shape[1] :])
        sums = jnp.concatenate([sums[r : r + SUMS] for r in range(0, sums.shape[0], SUMS)], axis=1)
    else:
        sums = refs[0][...] + refs[1][...]
    gain2[...] = sums[3:4, :].reshape(width)
    gain1[...] = (sums[4:5, :] / gain_line[...].reshape(1, width)).reshape(width)
    count = jnp.max(sums[5:6, :], axis=1, keepdims=True) * width
    for i in range(3):
        rms[i] = jnp.sum(jnp.sqrt(jnp.sum(sums[i : i + 1, :], axis=1, keepdims=True) / count))


def qkv_end(places, gain, kept, got, small, tall, wide, rides):
    return pl.pallas_call(
        functools.partial(qkv_end_kernel, places, rides),
        in_specs=[IN_VMEM] * (3 + len(small)),
        out_specs=[IN_VMEM] * 3 + [SMEM],
        out_shape=[shape((tall, wide), f32), shape(gain.shape, f32), shape(gain.shape, f32), shape((3,), f32)],
        compiler_params=params(16),
        cost_estimate=COST,
        name="qkv_end",
    )(gain, kept, got, *small)


def after(value, *earlier):
    return lax.optimization_barrier((value, earlier))[0]


def sum_parts(me, kept, got, sources, width, small, rides):
    orders = bit_orders(lax.axis_size("batch"), len(sources))
    steps = len(orders[0])
    common = min(i for i in range(steps + 1) if all(order[i:] == orders[0][i:] for order in orders))
    keep, send, small = start_sum(me, kept, got, sources, width, orders, small, rides)
    for i in range(steps):
        got = [exchange(s, "batch", order[i]) for s, order in zip(send, orders[: len(send)], strict=True)]
        if small and not rides:
            small = [small[0], exchange(small[0], "batch", orders[0][i])]
        earlier = yield send[0], got
        if i == steps - 1:
            break
        if earlier is not None:
            keep = after(keep, earlier)
        keep, send, small = step_sum(keep, got, small, i + 1 == common, rides)
    yield keep[0], got[0], small


def on_device(
    inputs, lengths, cotangent, qkv_weight, out_weight, up_weight, down_weight, attn_gain, mlp_gain
):
    seq, width = inputs.shape[2:]
    x = inputs[0, 0]
    dy = cotangent[0, 0]
    count = lax.axis_size("batch")
    stream = lax.axis_index("stream").astype(jnp.int32)
    me = lax.axis_index("batch").astype(jnp.int32).reshape(1)
    info = jnp.stack([stream, lengths[0]])
    cosine, sine = rotary_tables(seq)
    tables_t = (jnp.asarray(cosine.T), jnp.asarray(sine.T))

    received = lax.ppermute(x, "stream", [(0, 1)])
    (
        q, ko, vo, kc, vc, h1t, o, lse, outputs, dx2, do,
        up_send, up_keep, down_send, down_keep, out_send, out_keep, *tables, sums,
    ) = layer(
        info, attn_gain, mlp_gain, *tables_t, received, x, qkv_weight, out_weight, dy, up_weight, down_weight
    )
    down_got, up_got, out_got = (exchange(a, "stream", 1) for a in (down_send, up_send, out_send))

    def by_rows(array):
        return array.reshape(count * GROUPS, array.shape[0] // (count * GROUPS), width)

    heads = (q, ko, vo, kc, vc, o)
    pairs = width // PW // 3
    dq1, keep1, send1 = attend_back(info, 0, pairs, *heads, do, lse, *tables_t)
    early = sum_parts(
        me,
        [by_rows(after(a, dq1)) for a in (down_keep, up_keep, out_keep)],
        [by_rows(a) for a in (down_got, up_got, out_got)],
        [[(a, lambda part, g=g: part * GROUPS + g, 0) for a in range(3)] for g in range(GROUPS)],
        width,
        [],
        False,
    )
    token = next(early)[0]
    got1 = lax.ppermute(after(send1, token), "stream", [(1, 0)])
    dq2, keep2, send2 = attend_back(info, pairs, 2 * pairs, *heads, after(do, token), lse, *tables_t)
    got2 = lax.ppermute(send2, "stream", [(1, 0)])
    token = early.send(dq2)[0]
    dkv1, qkv_send1, qkv_keep1, small = weigh(info, 0, dq1, after(keep1, token), got1, tables, h1t, qkv_weight, sums)
    qkv_got1 = exchange(qkv_send1, "stream", 1)
    dkv2, qkv_send2, qkv_keep2, small = weigh(info, pairs, dq2, keep2, got2, tables, h1t, qkv_weight, small)
    qkv_got2 = exchange(qkv_send2, "stream", 1)
    small_got = exchange(small, "stream", 1)
    token = early.send(dkv2)[0]

    tall = width // (2 * count)
    split = lambda a: a.reshape(3 * count, tall, a.shape[2])
    rides = tall % 8 == 0
    runs = [(0, i, 0) for i in range(3)] + [(1, i, c) for i in range(3) for c in range(2)]
    groups = runs[:4], runs[4:]
    late = sum_parts(
        me,
        [split(after(a, token)) for a in (qkv_keep1, qkv_keep2)],
        [split(a) for a in (qkv_got1, qkv_got2)],
        [[(a, lambda part, i=i: i * count + part, c) for a, i, c in group] for group in groups],
        pairs * PW,
        [small, small_got],
        rides,
    )
    token = next(late)[0]
    ends = [dq1, dq2], [dkv1, dkv2], qkv_weight, attn_gain
    dx = finish((0, 1), after(x, token), dx2, *ends, [])
    early_out = early.send(dx)
    dx = finish((1, seq // R), x, after(dx2, early_out[0]), *ends, [dx])
    late.send(dx)
    late_out = late.send(early_out[1])
    while len(late_out) == 2:
        late_out = late.send(None)
    while len(early_out) == 2:
        early_out = early.send(None)
    up_cols = down_keep.shape[0] // count
    down_grad, up_grad, out_grad = feed_end(*early_out[:2], up_cols, tall)
    places = [i * width + (a + c) * pairs * PW for a, i, c in runs]
    qkv_grad, gain1_grad, gain2_grad, rms = qkv_end(places, attn_gain, *late_out, tall, 3 * width, rides)
    return (
        outputs[None, None],
        dx[None, None],
        qkv_grad,
        out_grad,
        up_grad,
        down_grad,
        gain1_grad,
        gain2_grad,
        rms,
    )


def solution(mesh):
    rows = P("stream", "batch", None, None)
    both = ("stream", "batch")
    return jax.shard_map(
        on_device,
        mesh=mesh,
        in_specs=(rows, P("batch"), rows, P(), P(), P(), P(), P(), P()),
        out_specs=(rows, rows, P(both, None), P(both, None), P(None, both), P(both, None), P(), P(), P()),
        check_vma=False,
    )
```

```python
import functools

import jax
import jax.numpy as jnp
import numpy as np
from jax import lax
from jax.experimental import pallas as pl
from jax.experimental.pallas import tpu as pltpu
from jax.sharding import PartitionSpec as P

f32 = jnp.float32
bf16 = jnp.bfloat16

HD = 64
BLK = 16
EPS = 1e-06
NEG = -1e30
PW = 2 * HD
T = 128
R = 256
AHEAD = 2
FC = 768
SCALE = HD**-0.5
BIG = 58
GROUPS = 3

COST = pl.CostEstimate(flops=1 << 20, bytes_accessed=1 << 16, transcendentals=0)
LONG = pl.CostEstimate(flops=1 << 35, bytes_accessed=1 << 26, transcendentals=0)

FEED = (((0, 0), (1, 0), (2, 0), (2, 1)), ((0, 1), (1, 1), (2, 2)), ((0, 2), (1, 2)))

SMEM = pl.BlockSpec(memory_space=pltpu.SMEM)
IN_VMEM = pl.BlockSpec(memory_space=pltpu.VMEM)


def params(mib):
    return pltpu.CompilerParams(vmem_limit_bytes=mib << 20)


def shape(dims, dtype):
    return jax.ShapeDtypeStruct(dims, dtype)


def pinned(*arrays):
    return [pltpu.with_memory_space_constraint(a, pltpu.HBM) for a in arrays]


def nn(a, b):
    return jnp.dot(a, b, preferred_element_type=f32)


def nt(a, b):
    return lax.dot_general(a, b, (((1,), (1,)), ((), ())), preferred_element_type=f32)


def tn(a, b):
    return lax.dot_general(a, b, (((0,), (0,)), ((), ())), preferred_element_type=f32)


def whole(dims):
    return pl.BlockSpec(dims, lambda *_: (0,) * len(dims), pipeline_mode=pl.Buffered(1))


def inv_rms(v):
    return lax.rsqrt(jnp.mean(v * v, axis=-1, keepdims=True) + EPS)


def norm_back(v, gain, grad):
    r = inv_rms(v)
    unit = v * r
    scaled = grad * gain
    inner = jnp.mean(scaled * unit, axis=-1, keepdims=True)
    return r * (scaled - unit * inner), grad * unit


def rotary_tables(length):
    half = HD // 2
    freqs = np.exp(-np.log(10000.0) * np.arange(half) / half).astype(np.float32)
    angles = (np.arange(length, dtype=np.float32)[:, None] * freqs[None, :]).astype(np.float64)
    return np.cos(angles).astype(np.float32), np.sin(angles).astype(np.float32)


def rotated(v, cosine, signed, sign):
    first = lax.broadcasted_iota(jnp.int32, (1, PW), 1) % HD < HD // 2
    outs = []
    for c in range(0, v.shape[1], PW):
        part = v[:, c : c + PW]
        partner = jnp.where(first, pltpu.roll(part, PW - HD // 2, 1), pltpu.roll(part, HD // 2, 1))
        outs.append(part * cosine + partner * (signed * sign))
    return outs[0] if len(outs) == 1 else jnp.concatenate(outs, axis=1)


def in_turn(count, *stages, at_once=1):
    def turn(n, carry):
        state = [()] * at_once
        for step in range(at_once + len(stages) - 1):
            for k, stage in enumerate(stages):
                if 0 <= step - k < at_once:
                    state[step - k] = stage(at_once * n + step - k, *state[step - k])
        return carry

    lax.fori_loop(0, count // at_once, turn, 0)


def token_weight(start, length, rows):
    return lax.broadcasted_iota(jnp.int32, (rows, 1), 0) + start < length


def row_sum(v):
    return jnp.sum(v, axis=0, keepdims=True)


def by_pairs(ref, rows, value):
    for p in range(ref.shape[0]):
        ref[p, rows, :] = value[:, p * PW : (p + 1) * PW].astype(ref.dtype)


def stacked(tile, low):
    zero = jnp.zeros_like(tile)
    return jnp.concatenate([jnp.where(low, tile, zero), jnp.where(low, zero, tile)], axis=0)


def unstacked(tile_t):
    half = lax.broadcasted_iota(jnp.int32, (PW, 1), 0) < HD
    return jnp.where(half, tile_t[:, :T], tile_t[:, T:])


def chunks_of(i):
    out, j = [], 0
    while j < i:
        n = 2 if i - j >= 2 else 1
        out.append((j * T, n * T))
        j += n
    return out


def edge_bias(ref, noisy):
    row = lax.broadcasted_iota(jnp.int32, (T, 2 * T), 0) // BLK
    col = (lax.broadcasted_iota(jnp.int32, (T, 2 * T), 1) % T) // BLK
    own = jnp.logical_or(row == col, jnp.logical_and(row < col, noisy == 0))
    other = jnp.logical_and(row < col, noisy == 1)
    ref[:T, :] = jnp.where(own, 0.0, NEG)
    ref[T:, :] = jnp.where(other, 0.0, NEG)


def masked(s, start, length):
    pos = lax.broadcasted_iota(jnp.int32, s.shape, 0) + start
    return jnp.where(pos < length, s, NEG)


def over_rows(op, v):
    return op(v.reshape(v.shape[0] // 8, 8, v.shape[1]), axis=0)


def attend_pair(length, q, ko, vo, kc, vc, store, lse, vo_t, vc_t, scores, bias):
    seq = q.shape[0]
    low = lax.broadcasted_iota(jnp.int32, (1, PW), 1) < HD
    vo_t[...] = vo[...].T
    vc_t[...] = vc[...].T

    def score(i):
        at = pl.ds(i * T, T)
        q2 = stacked(q[at, :] * bf16(SCALE), low)
        buf = scores.at[i % AHEAD]
        edge = nt(jnp.concatenate([ko[at, :], kc[at, :]], 0), q2) + bias[...]
        own = masked(edge[:T], i * T, length)
        other = masked(edge[T:], i * T, length)
        buf[pl.ds(0, T), :] = own
        buf[pl.ds(T, T), :] = other
        top = over_rows(jnp.max, jnp.maximum(own, other))
        for start, size in chunks_of(i):
            s = masked(nt(kc[pl.ds(start, size), :], q2), start, length)
            buf[pl.ds(2 * T + start, size), :] = s
            top = jnp.maximum(top, over_rows(jnp.max, s))
        return jnp.max(top, axis=0, keepdims=True)

    def mix(i, top):
        at = pl.ds(i * T, T)
        buf = scores.at[i % AHEAD]
        p = jnp.exp(buf[pl.ds(0, 2 * T), :] - top)
        total = over_rows(jnp.sum, p)
        acc = nn(jnp.concatenate([vo_t[:, at], vc_t[:, at]], 1), p.astype(bf16))
        for start, size in chunks_of(i):
            p = jnp.exp(buf[pl.ds(2 * T + start, size), :] - top)
            total = total + over_rows(jnp.sum, p)
            acc = acc + nn(vc_t[:, pl.ds(start, size)], p.astype(bf16))
        total = row_sum(total)
        lse[0, pl.ds(i, 1), :] = top + jnp.log(total)
        store(at, unstacked(acc * (1.0 / total)))

    tops = {}
    for i in range(seq // T + AHEAD - 1):
        if i < seq // T:
            tops[i] = score(i)
        if i >= AHEAD - 1:
            mix(i - AHEAD + 1, tops.pop(i - AHEAD + 1))


def turned_back(v, cosine, sine):
    quarter = HD // 2
    a, b, c, d = (v[i * quarter : (i + 1) * quarter] for i in range(4))
    return jnp.concatenate(
        [a * cosine + b * sine, b * cosine - a * sine, c * cosine + d * sine, d * cosine - c * sine]
    )


def attend_back_kernel(
    info, q, ko, vo, kc, vc, o, do, lse, cosine, sine, dq, keep, send, ko_t, kc_t, dko, dvo, dkc, dvc, bias
):
    noisy, length = info[0], info[1]
    q, ko, vo, kc, vc = (ref.at[0] for ref in (q, ko, vo, kc, vc))
    seq = q.shape[0]
    low = lax.broadcasted_iota(jnp.int32, (1, PW), 1) < HD

    @pl.when(pl.program_id(0) == 0)
    def _():
        edge_bias(bias, noisy)

    ko_t[...] = ko[...].T
    kc_t[...] = kc[...].T

    def tile(i):
        at = pl.ds(i * T, T)
        prod = (do[at, :].astype(f32) * o[at, :].astype(f32)).T
        delta = jnp.concatenate([row_sum(prod[:HD]), row_sum(prod[HD:])], 1)
        q2 = stacked(q[at, :] * bf16(SCALE), low)
        return q2, stacked(do[at, :], low), lse[0, pl.ds(i, 1), :], delta

    def products(i, start, size, q2, do2):
        if start is None:
            at = pl.ds(i * T, T)
            s = nt(jnp.concatenate([ko[at, :], kc[at, :]], 0), q2) + bias[...]
            s = jnp.concatenate([masked(s[:T], i * T, length), masked(s[T:], i * T, length)], 0)
            return s, nt(jnp.concatenate([vo[at, :], vc[at, :]], 0), do2)
        rows = pl.ds(start, size)
        return masked(nt(kc[rows, :], q2), start, length), nt(vc[rows, :], do2)

    def gather(i, start, size, q2, do2, p, ds, dq_t):
        at = pl.ds(i * T, T)
        dv, dk = nn(p, do2), nn(ds, q2)
        if start is None:
            dvo[at, :] = dv[:T]
            dko[at, :] = dk[:T]
            dvc[at, :] = dv[T:]
            dkc[at, :] = dk[T:]
            return nn(jnp.concatenate([ko_t[:, at], kc_t[:, at]], 1), ds)
        rows = pl.ds(start, size)
        dvc[rows, :] += dv
        dkc[rows, :] += dk
        return dq_t + nn(kc_t[:, rows], ds)

    work = [(i, *c) for i in range(seq // T) for c in [(None, None)] + chunks_of(i)]
    tiles, made, weighed, dq_t = {}, {}, {}, None
    for n in range(len(work) + 2):
        if n < len(work):
            i = work[n][0]
            if i not in tiles:
                tiles[i] = tile(i)
            made[n] = products(*work[n], *tiles[i][:2])
        if 0 <= n - 1 < len(work):
            _, _, norm, delta = tiles[work[n - 1][0]]
            s, dp = made.pop(n - 1)
            p = jnp.exp(s - norm)
            weighed[n - 1] = p.astype(bf16), (p * (dp - delta)).astype(bf16)
        if n >= 2:
            i, start, size = work[n - 2]
            dq_t = gather(i, start, size, *tiles[i][:2], *weighed.pop(n - 2), dq_t)
            if n == len(work) + 1 or work[n - 1][0] != i:
                at = pl.ds(i * T, T)
                out = turned_back(unstacked(dq_t), cosine[:, at], sine[:, at]) * SCALE
                dq[at, :] = out.T.astype(bf16)
    clean = (1 - noisy).astype(f32)
    for at, own, other in ((0, dko, dkc), (1, dvo, dvc)):
        keep[at] = (own[...] + clean * other[...]).astype(bf16)
        send[at] = other[...].astype(bf16)


def attend_back(info, first, pairs, q, ko, vo, kc, vc, o, do, lse, cosine, sine):
    seq = q.shape[1]
    width = pairs * PW
    heads = pl.BlockSpec((1, seq, PW), lambda h: (first + h, 0, 0))
    source = pl.BlockSpec((seq, PW), lambda h: (0, first + h))
    both = pl.BlockSpec((2, seq, PW), lambda h: (0, 0, h))
    lines = pl.BlockSpec((1, seq // T, 2 * T), lambda h: (first + h, 0, 0))
    table = whole((HD // 2, seq))
    return pl.pallas_call(
        attend_back_kernel,
        grid=(pairs,),
        in_specs=[SMEM] + [heads] * 5 + [source] * 2 + [lines, table, table],
        out_specs=[pl.BlockSpec((seq, PW), lambda h: (0, h)), both, both],
        out_shape=[shape((seq, width), bf16)] + [shape((2, seq, width), bf16)] * 2,
        scratch_shapes=[pltpu.VMEM((PW, seq), bf16)] * 2
        + [pltpu.VMEM((seq, PW), f32)] * 4
        + [pltpu.VMEM((2 * T, 2 * T), f32)],
        compiler_params=params(24),
        cost_estimate=LONG,
        name="attend_back",
    )(info, *pinned(q, ko, vo, kc, vc, o, do, lse), cosine, sine)


C0 = 0.7978845608028654
C1 = C0 * 0.044715


def layer_kernel(
    info, gain1_line, gain2_line, cosine_t, sine_t, received, x_any, wqkv_any, wo_any, dy_any,
    w1_any, w2_any,
    q_out, ko_out, vo_out, kc_out, vc_out, h1t_out, o_out, lse_out, out_any, dx2_any, do_any,
    up_send, up_keep, down_send, down_keep, g_send, g_keep, cosine_out, signed_out, sums,
    x, wqkv, cosine, signed, q, ko, vo, h1t, wo, dy, w1, w2,
    kc, vc, vo_t, vc_t, scores, bias, o, o_t, lse, x2, h2, m, dh, act, du, up_grad, down_grad, half_grads,
    sem_in, sem_1, sem_2, sem_out, sem_up, sem_down, sem_tile,
):
    noisy, length = info[0], info[1]
    seq, width = x.shape
    chunks, pairs, tiles = w1.shape[0], kc.shape[0], seq // R
    copy = pltpu.make_async_copy
    gain1, gain2 = gain1_line[...].reshape(1, width), gain2_line[...].reshape(1, width)

    def weights(c):
        place = lax.rem(c + (chunks // 2) * (1 - noisy), chunks) * FC
        place = pl.multiple_of(place, FC)
        return (
            copy(w1_any.at[:, pl.ds(place, FC)], w1.at[c], sem_1.at[c]),
            copy(w2_any.at[pl.ds(place, FC), :], w2.at[c], sem_2.at[c]),
        )

    sources = (
        (x_any, x),
        (wqkv_any, wqkv),
        (wo_any, wo),
        (dy_any, dy),
    )
    loads = [copy(a, b, sem_in.at[i]) for i, (a, b) in enumerate(sources)]
    for load in loads[:2]:
        load.start()
    sums[...] = jnp.zeros_like(sums)
    edge_bias(bias, noisy)
    def widen(t):
        rows = pl.ds(pl.multiple_of(t * PW, PW), PW)
        c, d = cosine_t[:, rows].T, sine_t[:, rows].T
        cosine[rows, :] = jnp.concatenate([c, c, c, c], axis=1)
        signed[rows, :] = jnp.concatenate([-d, d, -d, d], axis=1)
        return ()

    in_turn(seq // PW, widen)
    tables_out = [copy(cosine, cosine_out, sem_out.at[10]), copy(signed, signed_out, sem_out.at[11])]
    span = lambda t: pl.ds(pl.multiple_of(t * R, R), R)

    loads[0].wait()

    def own_norm(t):
        value = x[span(t), :].astype(f32)
        h1 = (value * inv_rms(value) * gain1).astype(bf16)
        h2[span(t), :] = h1
        h1t[:, span(t)] = h1.T
        weight = token_weight(t * R, length, R)
        sums[0:1, :] += row_sum(jnp.where(weight, value * value, 0.0))
        return ()

    in_turn(tiles, own_norm)
    loads[1].wait()
    for load in loads[2:]:
        load.start()

    def own_product(t):
        return tuple(nn(h2[span(t), :], wqkv[:, i * width : (i + 1) * width]) for i in range(3))

    def own_turn(t, a, b, c):
        tables = (cosine[span(t), :], signed[span(t), :], 1.0)
        by_pairs(q, span(t), rotated(a, *tables))
        by_pairs(ko, span(t), rotated(b, *tables))
        by_pairs(vo, span(t), c)
        return ()

    def clean_norm(t):
        value = jnp.where(noisy == 1, received[span(t), :].astype(f32), x[span(t), :].astype(f32))
        o[span(t), :] = (value * inv_rms(value) * gain1).astype(bf16)
        return ()

    def clean_product(t):
        return tuple(nn(o[span(t), :], wqkv[:, i * width : (i + 1) * width]) for i in (1, 2))

    def clean_turn(t, a, b):
        by_pairs(kc, span(t), rotated(a, cosine[span(t), :], signed[span(t), :], 1.0))
        by_pairs(vc, span(t), b)
        return ()

    in_turn(tiles, own_product, own_turn)
    stores = [
        copy(a, b, sem_out.at[6 + i])
        for i, (a, b) in enumerate(((q, q_out), (ko, ko_out), (vo, vo_out), (h1t, h1t_out)))
    ]
    stores += tables_out
    for store in stores:
        store.start()
    in_turn(tiles, clean_norm, clean_product, clean_turn)
    more = [copy(kc, kc_out, sem_out.at[0]), copy(vc, vc_out, sem_out.at[1])]
    for store in more:
        store.start()
    stores += more

    for c in range(chunks):
        for load in weights(c):
            load.start()

    def one_pair(p, carry):
        lanes = pl.ds(pl.multiple_of(p * PW, PW), PW)

        def keep(at, tile_t):
            o_t[lanes, at] = tile_t.astype(bf16)
            o[at, lanes] = tile_t.T.astype(bf16)

        heads = (ref.at[p] for ref in (q, ko, vo, kc, vc))
        attend_pair(length, *heads, keep, lse.at[pl.ds(p, 1)], vo_t, vc_t, scores, bias)
        return carry

    lax.fori_loop(0, pairs, one_pair, 0)
    mixed_out = copy(o, o_out, sem_out.at[2])
    mixed_out.start()
    stores += [copy(lse, lse_out, sem_out.at[3])]
    stores[-1].start()

    for load in loads[2:]:
        load.wait()

    def join_product(t):
        return (nn(o[span(t), :], wo[...]),)

    def join_norm(t, branch):
        value = x[span(t), :].astype(f32) + branch
        x2[span(t), :] = value
        h2[span(t), :] = (value * inv_rms(value) * gain2).astype(bf16)
        m[span(t), :] = jnp.zeros_like(value)
        dh[span(t), :] = jnp.zeros_like(value)
        weight = token_weight(t * R, length, R)
        sums[1:2, :] += row_sum(jnp.where(weight, branch * branch, 0.0))
        return ()

    in_turn(tiles, join_product, join_norm, at_once=2)

    def grad_stores(c, up, down):
        slot = lax.rem(c, 2)
        rows = pl.ds(pl.multiple_of(lax.rem(c, chunks // 2) * FC, FC), FC)
        return (
            copy(up_grad.at[slot], up.at[rows, :], sem_up.at[slot]),
            copy(down_grad.at[slot], down.at[rows, :], sem_down.at[slot]),
        )

    def one_chunk(c, carry):
        for load in weights(c):
            load.wait()
        up, down = w1.at[c], w2.at[c]
        made = {}
        for t in range(-R, seq, R):
            if t + R < seq:
                rows = pl.ds(t + R, R)
                made[t + R] = nn(h2[rows, :], up[...]), nt(dy[rows, :], down[...])
            if t < 0:
                continue
            rows = pl.ds(t, R)
            u, da = made.pop(t)
            sq = u * u
            half = 0.5 * jnp.tanh(u * (C0 + C1 * sq)) + 0.5
            low = (u * half).astype(bf16)
            slope = half + u * (2.0 * half * (1.0 - half)) * (C0 + 3.0 * C1 * sq)
            back = (da * slope).astype(bf16)
            act[rows, :] = low
            du[rows, :] = back
            m[rows, :] += nn(low, down[...])
            dh[rows, :] += nt(back, up[...])

        @pl.when(c >= 2)
        def _():
            for store in grad_stores(c, up_send, down_send):
                store.wait()

        slot = lax.rem(c, 2)
        down_grad[slot] = tn(act[...], dy[...]).astype(bf16)
        up_grad[slot] = tn(du[...], h2[...]).astype(bf16)

        @pl.when(c < chunks // 2)
        def _():
            for store in grad_stores(c, up_send, down_send):
                store.start()

        @pl.when(c >= chunks // 2)
        def _():
            for store in grad_stores(c, up_keep, down_keep):
                store.start()

        return carry

    lax.fori_loop(0, chunks, one_chunk, 0)

    mixed_out.wait()

    def tile_stores(t):
        return (
            copy(h2.at[span(t), :], out_any.at[span(t), :], sem_tile.at[t, 0]),
            copy(x2.at[span(t), :], dx2_any.at[span(t), :], sem_tile.at[t, 1]),
            copy(o.at[span(t), :], do_any.at[span(t), :], sem_tile.at[t, 2]),
        )

    def middle_norm(t):
        value = x2[span(t), :]
        mixed = m[span(t), :]
        weight = token_weight(t * R, length, R)
        sums[2:3, :] += row_sum(jnp.where(weight, mixed * mixed, 0.0))
        grad, gain_terms = norm_back(value, gain2, dh[span(t), :])
        sums[3:4, :] += row_sum(gain_terms)
        grad = grad + dy[span(t), :].astype(f32)
        h2[span(t), :] = (value + mixed).astype(bf16)
        x2[span(t), :] = grad
        x[span(t), :] = grad.astype(bf16)
        return ()

    def middle_product(t):
        o[span(t), :] = nt(x[span(t), :], wo[...]).astype(bf16)
        for store in tile_stores(t):
            store.start()
        return ()

    in_turn(tiles, middle_norm, middle_product, at_once=2)
    half = width // 2
    mine = pl.multiple_of(noisy * half, half)
    half_grads[0] = nn(o_t[pl.ds(half - mine, half), :], x[...]).astype(bf16)
    half_grads[1] = nn(o_t[pl.ds(mine, half), :], x[...]).astype(bf16)
    more = [copy(half_grads.at[0], g_send, sem_out.at[4]), copy(half_grads.at[1], g_keep, sem_out.at[5])]
    for store in more:
        store.start()
    stores += more
    for c in range(chunks - 2, chunks):
        stores += grad_stores(c, up_keep, down_keep)
    for t in range(tiles):
        stores += tile_stores(t)
    for store in stores:
        store.wait()


def layer(info, gain1, gain2, cosine_t, sine_t, received, x, wqkv, wo, dy, w1, w2):
    seq, width = x.shape
    hidden = w1.shape[1]
    tiles, pairs, chunks = seq // R, width // PW, hidden // FC
    anywhere = pl.BlockSpec(memory_space=pl.ANY)
    vmem = pltpu.VMEM
    dma = pltpu.SemaphoreType.DMA
    heads = (pairs, seq, PW)
    flat = (seq, width)
    outs = (
        [shape(heads, bf16)] * 5
        + [shape((width, seq), bf16), shape(flat, bf16), shape((pairs, seq // T, 2 * T), f32)]
        + [shape(flat, bf16), shape(flat, f32), shape(flat, bf16)]
        + [shape((hidden // 2, width), bf16)] * 4
        + [shape((width // 2, width), bf16)] * 2
        + [shape((seq, PW), f32)] * 2
        + [shape((8, width), f32)]
    )
    return pl.pallas_call(
        layer_kernel,
        in_specs=[SMEM] + [IN_VMEM] * 5 + [anywhere] * 6,
        out_specs=[anywhere] * 19 + [IN_VMEM],
        out_shape=outs,
        scratch_shapes=[vmem(flat, bf16)]
        + [vmem(wqkv.shape, bf16), vmem((seq, PW), f32), vmem((seq, PW), f32)]
        + [vmem(heads, bf16)] * 3
        + [vmem((width, seq), bf16), vmem((width, width), bf16), vmem(flat, bf16)]
        + [vmem((chunks, width, FC), bf16), vmem((chunks, FC, width), bf16)]
        + [vmem(heads, bf16)] * 2
        + [vmem((PW, seq), bf16)] * 2
        + [vmem((AHEAD, seq + T, 2 * T), f32), vmem((2 * T, 2 * T), f32)]
        + [vmem(flat, bf16), vmem((width, seq), bf16)]
        + [vmem((pairs, seq // T, 2 * T), f32)]
        + [vmem(flat, f32), vmem(flat, bf16)]
        + [vmem(flat, f32)] * 2
        + [vmem((seq, FC), bf16)] * 2
        + [vmem((2, FC, width), bf16)] * 2
        + [vmem((2, width // 2, width), bf16)]
        + [dma((4,)), dma((chunks,)), dma((chunks,)), dma((12,)), dma((2,)), dma((2,)), dma((tiles, 3))],
        compiler_params=params(BIG),
        cost_estimate=LONG,
        name="layer",
    )(info, gain1, gain2, cosine_t, sine_t, received, *pinned(x, wqkv, wo, dy, w1, w2))


def weigh_kernel(first, info, dq, keep, got, cosine, signed, h1t, wqkv, sums, dkv, g_send, g_keep, small):
    width, half = wqkv.shape[0], wqkv.shape[0] // 2
    mine = pl.multiple_of(info[0] * half, half)
    dk = keep[0].astype(f32) + got[0].astype(f32)
    dkv[0] = rotated(dk, cosine[...], signed[...], -1.0).astype(bf16)
    dkv[1] = (keep[1].astype(f32) + got[1].astype(f32)).astype(bf16)
    small[...] = sums[...]
    for out, start in ((g_send, half - mine), (g_keep, mine)):
        rows = pl.ds(start, half)
        terms = 0.0
        for i, part in enumerate((dq, dkv.at[0], dkv.at[1])):
            total = nn(h1t[rows, :], part[...])
            out[i] = total.astype(bf16)
            at = i * width + first * PW
            weighted = total * wqkv[rows, at : at + total.shape[1]].astype(f32)
            for c in range(0, total.shape[1], PW):
                terms = terms + weighted[:, c : c + PW]
        line = jnp.sum(terms.T, axis=0, keepdims=True)
        lanes = lax.broadcasted_iota(jnp.int32, (1, width), 1)
        inside = jnp.logical_and(lanes >= start, lanes < start + half)
        small[4:5, :] += jnp.where(inside, jnp.concatenate([line, line], axis=1), 0.0)
    small[5:6, :] = jnp.full((1, width), info[1].astype(f32))


def weigh(info, first, dq, keep, got, tables, h1t, wqkv, sums):
    seq, width = dq.shape
    tall = h1t.shape[0]
    return pl.pallas_call(
        functools.partial(weigh_kernel, first),
        in_specs=[SMEM] + [IN_VMEM] * 8,
        out_specs=[IN_VMEM] * 4,
        out_shape=[shape((2, seq, width), bf16)]
        + [shape((3, tall // 2, width), bf16)] * 2
        + [shape(sums.shape, f32)],
        compiler_params=params(24),
        cost_estimate=LONG,
        name="weigh",
    )(info, dq, keep, got, *tables, h1t, wqkv, sums)


def finish_kernel(parts, tiles, x, dx2, wqkv, gain_line, *refs):
    dx_any, dx, sem = refs[-3:]
    dqs, dkvs = refs[:parts], refs[parts : 2 * parts]
    gain = gain_line[...].reshape(1, x.shape[1])

    def store(t):
        rows = pl.ds(pl.multiple_of(t * R, R), R)
        return pltpu.make_async_copy(dx.at[rows, :], dx_any.at[rows, :], sem.at[t])

    def some_rows(t, carry):
        rows = pl.ds(pl.multiple_of(t * R, R), R)
        grads = [r[rows, :] for r in dqs] + [r[0, rows, :] for r in dkvs] + [r[1, rows, :] for r in dkvs]
        dh = nt(jnp.concatenate(grads, axis=1), wqkv[...])
        grad, _ = norm_back(x[rows, :].astype(f32), gain, dh)
        dx[rows, :] = (dx2[rows, :] + grad).astype(bf16)
        store(t).start()
        return carry

    lax.fori_loop(*tiles, some_rows, 0)
    for t in range(*tiles):
        store(t).wait()


def finish(tiles, x, dx2, dqs, dkvs, weight, gain, before):
    anywhere = pl.BlockSpec(memory_space=pl.ANY)
    ins = 4 + len(dqs) + len(dkvs)
    return pl.pallas_call(
        functools.partial(finish_kernel, len(dqs), tiles),
        in_specs=[IN_VMEM] * ins + [anywhere] * len(before),
        out_specs=anywhere,
        out_shape=shape(x.shape, bf16),
        scratch_shapes=[pltpu.VMEM(x.shape, bf16), pltpu.SemaphoreType.DMA((x.shape[0] // R,))],
        input_output_aliases={ins: 0} if before else {},
        compiler_params=params(24),
        cost_estimate=COST if before else LONG,
        name="finish",
    )(x, dx2, weight, gain, *dqs, *dkvs, *before)


def bit_orders(count, groups):
    bits = [1 << i for i in range(count.bit_length() - 1)]
    if groups == 2:
        return [bits, bits[1::-1] + bits[2:]]
    return [bits[g:-1] + bits[:g] + bits[-1:] for g in range(groups)]


def exchange(value, axis, bit):
    size = lax.axis_size(axis)
    return lax.ppermute(value, axis, [(i, i ^ bit) for i in range(size)])


def distance(order, place):
    out = 0
    for i, bit in enumerate(order):
        out = out + ((place >> (len(order) - 1 - i)) & 1) * bit
    return out


SUMS = 8


def halves(value):
    high = value.astype(bf16)
    return high, (value - high.astype(f32)).astype(bf16)


def put_sums(value, kept, block):
    high, low = halves(value)
    lines = kept.shape[0]
    block[:lines, :] = high
    block[lines : 2 * lines, :] = low
    kept[...] = high.astype(f32) + low.astype(f32)


def got_sums(block):
    lines = block.shape[0] // 2
    return block[:lines, :].astype(f32) + block[lines:, :].astype(f32)


def start_kernel(orders, sources, small, me, *refs):
    groups = len(orders)
    arrays = max(a for source in sources for a, _, _ in source) + 1
    ins, outs = refs[: 2 * arrays], refs[len(refs) - 2 * groups :]
    half = outs[0].shape[0]
    for g, order in enumerate(orders):
        for side in range(2):

            def one(r, carry, g=g, order=order, side=side):
                part = me[0] ^ distance(order, r + side * half)
                out = outs[2 * g + side]
                row = 0
                for a, where, unit in sources[g]:
                    kept, got = ins[2 * a : 2 * a + 2]
                    place = where(part)
                    size, wide = kept.shape[1], out.shape[-1]
                    lanes = slice(unit * wide, (unit + 1) * wide)
                    total = kept[place, :, lanes].astype(f32) + got[place, :, lanes].astype(f32)
                    if len(out.shape) == 3:
                        out[r, row : row + size, :] = total.astype(bf16)
                    else:
                        start = pl.multiple_of(r * outs[0].shape[1] + row, 8)
                        out[pl.ds(start, size), :] = total.astype(bf16)
                    row += size
                return carry

            lax.fori_loop(0, half, one, 0)
    if small:
        here, there, kept = refs[2 * arrays : 2 * arrays + 3]
        total = here[...] + there[...]
        if small == "rides":
            wide = kept.shape[1]
            total = jnp.concatenate([total[:, c : c + wide] for c in range(0, total.shape[1], wide)], axis=0)
            put_sums(total, kept, outs[1].at[pl.ds(half * outs[0].shape[1], 2 * kept.shape[0]), :])
        else:
            kept[...] = total


def travelling(count, rows, width, lines):
    return shape((count * rows + 2 * lines, width) if lines else (count, rows, width), bf16)


def start_sum(me, kept, got, sources, width, orders, small, rides):
    count = 1 << len(orders[0])
    half = count // 2
    rows = [sum(kept[a].shape[1] for a, _, _ in source) for source in sources]
    lines = small[0].size // width if rides else 0
    cols = width // 3
    args = [a for pair in zip(kept, got, strict=True) for a in pair]
    sums = []
    for g in range(len(orders)):
        sums += [shape((half, rows[g], width), bf16), travelling(half, rows[g], width, 0 if g else lines)]
    mode = "rides" if rides else "alone" if small else ""
    if small:
        specs = dict(
            in_specs=[SMEM] + [IN_VMEM] * (len(args) + 2),
            out_specs=[IN_VMEM] * (1 + len(sums)),
            out_shape=[shape((lines, width) if rides else small[0].shape, f32)] + sums,
        )
    else:
        block = lambda a: pl.BlockSpec((a.shape[0], a.shape[1], cols), lambda c: (0, 0, c))
        specs = dict(
            grid=(width // cols,),
            in_specs=[SMEM] + [block(a) for a in args],
            out_specs=[block(a) for a in sums],
            out_shape=sums,
        )
    outs = pl.pallas_call(
        functools.partial(start_kernel, orders, sources, mode),
        compiler_params=params(30),
        cost_estimate=COST,
        name="start_sum",
        **specs,
    )(me, *args, *small)
    small, outs = list(outs[: len(outs) - len(sums)]), outs[len(outs) - len(sums) :]
    return list(outs[0::2]), list(outs[1::2]), small


def block_of(ref, r, size, row=0, step=0):
    if len(ref.shape) == 3:
        return ref.at[r, pl.ds(row, size), :]
    start = r * (step or size) + row
    return ref.at[pl.ds(start if isinstance(start, int) else pl.multiple_of(start, 8), size), :]


def step_kernel(groups, merge, mode, *refs):
    kept, got = refs[:groups], refs[groups : 2 * groups]
    outs = refs[2 * groups + (2 if mode == "alone" else 1 if mode else 0) :]
    count = kept[0].shape[0]
    half = count // 2

    def one(r, carry):
        row = 0
        for g in range(groups):
            keep, send = outs[:2] if merge else outs[2 * g : 2 * g + 2]
            size = kept[g].shape[1]
            for out, block in ((keep, r), (send, r + half)):
                total = kept[g][block].astype(f32) + block_of(got[g], block, size)[...].astype(f32)
                block_of(out, r, size, row, keep.shape[1])[...] = total.astype(bf16)
            row += size if merge else 0
        return carry

    lax.fori_loop(0, half, one, 0)
    if mode == "rides":
        total = refs[2 * groups][...] + got_sums(got[0][count * kept[0].shape[1] :])
        put_sums(total, outs[-1], outs[1].at[pl.ds(half * outs[0].shape[1], 2 * total.shape[0]), :])
    elif mode:
        outs[-1][...] = refs[2 * groups][...] + refs[2 * groups + 1][...]


def step_sum(kept, got, small, merge, rides):
    groups = len(kept)
    half = kept[0].shape[0] // 2
    rows = [a.shape[1] for a in kept]
    width = kept[0].shape[2]
    args = [*kept, *got, *small]
    sums = []
    for g, r in enumerate([sum(rows)] if merge else rows):
        sums += [shape((half, r, width), bf16), travelling(half, r, width, 0 if g or not rides else small[0].shape[0])]
    outs = pl.pallas_call(
        functools.partial(step_kernel, groups, merge, "rides" if rides else "alone" if small else ""),
        in_specs=[IN_VMEM] * len(args),
        out_specs=[IN_VMEM] * (len(sums) + len(small[:1])),
        out_shape=sums + [shape(a.shape, f32) for a in small[:1]],
        compiler_params=params(16),
        cost_estimate=COST if small or half == 1 else LONG,
        name="step_sum",
    )(*args)
    return list(outs[0 : len(sums) : 2]), list(outs[1 : len(sums) : 2]), list(outs[len(sums) :])


def feed_end_kernel(kept, got, down, up, out):
    total = kept[0].astype(f32) + got[0].astype(f32)
    tall, few = down.shape[0] // GROUPS, out.shape[0] // GROUPS
    ups, row = [], 0
    for group in FEED:
        for a, j in group:
            size = few if a == 2 else tall
            piece = total[row : row + size]
            row += size
            if a == 1:
                ups.append(piece)
            else:
                (down, None, out)[a][j * size : (j + 1) * size, :] = piece
    up[...] = jnp.concatenate(ups, axis=0).T


def feed_end(kept, got, tall, few):
    width = kept.shape[2]
    return pl.pallas_call(
        feed_end_kernel,
        in_specs=[IN_VMEM] * 2,
        out_specs=[IN_VMEM] * 3,
        out_shape=[shape((tall, width), f32), shape((width, tall), f32), shape((few, width), f32)],
        compiler_params=params(16),
        cost_estimate=COST,
        name="feed_end",
    )(kept, got)


def qkv_end_kernel(places, rides, gain_line, kept, got, *refs):
    out, gain1, gain2, rms = refs[-4:]
    tall = out.shape[0]
    width = gain1.shape[0]
    cols = kept.shape[2]
    there = got[: kept.shape[1]] if rides else got[0]
    total = kept[0].astype(f32) + there.astype(f32)
    for i, at in enumerate(places):
        out[:, at : at + cols] = total[i * tall : (i + 1) * tall]
    if rides:
        sums = refs[0][...] + got_sums(got[kept.shape[1] :])
        sums = jnp.concatenate([sums[r : r + SUMS] for r in range(0, sums.shape[0], SUMS)], axis=1)
    else:
        sums = refs[0][...] + refs[1][...]
    gain2[...] = sums[3:4, :].reshape(width)
    gain1[...] = (sums[4:5, :] / gain_line[...].reshape(1, width)).reshape(width)
    count = jnp.max(sums[5:6, :], axis=1, keepdims=True) * width
    for i in range(3):
        rms[i] = jnp.sum(jnp.sqrt(jnp.sum(sums[i : i + 1, :], axis=1, keepdims=True) / count))


def qkv_end(places, gain, kept, got, small, tall, wide, rides):
    return pl.pallas_call(
        functools.partial(qkv_end_kernel, places, rides),
        in_specs=[IN_VMEM] * (3 + len(small)),
        out_specs=[IN_VMEM] * 3 + [SMEM],
        out_shape=[shape((tall, wide), f32), shape(gain.shape, f32), shape(gain.shape, f32), shape((3,), f32)],
        compiler_params=params(16),
        cost_estimate=COST,
        name="qkv_end",
    )(gain, kept, got, *small)


def after(value, *earlier):
    return lax.optimization_barrier((value, earlier))[0]


def sum_parts(me, kept, got, sources, width, small, rides):
    orders = bit_orders(lax.axis_size("batch"), len(sources))
    steps = len(orders[0])
    common = min(i for i in range(steps + 1) if all(order[i:] == orders[0][i:] for order in orders))
    keep, send, small = start_sum(me, kept, got, sources, width, orders, small, rides)
    for i in range(steps):
        got = [exchange(s, "batch", order[i]) for s, order in zip(send, orders[: len(send)], strict=True)]
        if small and not rides:
            small = [small[0], exchange(small[0], "batch", orders[0][i])]
        earlier = yield send[0], got
        if i == steps - 1:
            break
        if earlier is not None:
            keep = after(keep, earlier)
        keep, send, small = step_sum(keep, got, small, i + 1 == common, rides)
    yield keep[0], got[0], small


def on_device(
    inputs, lengths, cotangent, qkv_weight, out_weight, up_weight, down_weight, attn_gain, mlp_gain
):
    seq, width = inputs.shape[2:]
    x = inputs[0, 0]
    dy = cotangent[0, 0]
    count = lax.axis_size("batch")
    stream = lax.axis_index("stream").astype(jnp.int32)
    me = lax.axis_index("batch").astype(jnp.int32).reshape(1)
    info = jnp.stack([stream, lengths[0]])
    cosine, sine = rotary_tables(seq)
    tables_t = (jnp.asarray(cosine.T), jnp.asarray(sine.T))

    received = lax.ppermute(x, "stream", [(0, 1)])
    (
        q, ko, vo, kc, vc, h1t, o, lse, outputs, dx2, do,
        up_send, up_keep, down_send, down_keep, out_send, out_keep, *tables, sums,
    ) = layer(
        info, attn_gain, mlp_gain, *tables_t, received, x, qkv_weight, out_weight, dy, up_weight, down_weight
    )
    down_got, up_got, out_got = (exchange(a, "stream", 1) for a in (down_send, up_send, out_send))

    def by_rows(array):
        return array.reshape(count * GROUPS, array.shape[0] // (count * GROUPS), width)

    heads = (q, ko, vo, kc, vc, o)
    pairs = width // PW // 3
    dq1, keep1, send1 = attend_back(info, 0, pairs, *heads, do, lse, *tables_t)
    early = sum_parts(
        me,
        [by_rows(after(a, dq1)) for a in (down_keep, up_keep, out_keep)],
        [by_rows(a) for a in (down_got, up_got, out_got)],
        [[(a, lambda part, j=j: part * GROUPS + j, 0) for a, j in group] for group in FEED],
        width,
        [],
        False,
    )
    token = next(early)[0]
    got1 = lax.ppermute(after(send1, token), "stream", [(1, 0)])
    dq2, keep2, send2 = attend_back(info, pairs, 2 * pairs, *heads, after(do, token), lse, *tables_t)
    got2 = lax.ppermute(send2, "stream", [(1, 0)])
    token = early.send(dq2)[0]
    dkv1, qkv_send1, qkv_keep1, small = weigh(info, 0, dq1, after(keep1, token), got1, tables, h1t, qkv_weight, sums)
    qkv_got1 = exchange(qkv_send1, "stream", 1)
    dkv2, qkv_send2, qkv_keep2, small = weigh(info, pairs, dq2, keep2, got2, tables, h1t, qkv_weight, small)
    qkv_got2 = exchange(qkv_send2, "stream", 1)
    small_got = exchange(small, "stream", 1)
    token = early.send(dkv2)[0]

    tall = width // (2 * count)
    split = lambda a: a.reshape(3 * count, tall, a.shape[2])
    rides = tall % 8 == 0
    runs = [(0, i, 0) for i in range(3)] + [(1, i, c) for i in range(3) for c in range(2)]
    groups = runs[:4], runs[4:]
    late = sum_parts(
        me,
        [split(after(a, token)) for a in (qkv_keep1, qkv_keep2)],
        [split(a) for a in (qkv_got1, qkv_got2)],
        [[(a, lambda part, i=i: i * count + part, c) for a, i, c in group] for group in groups],
        pairs * PW,
        [small, small_got],
        rides,
    )
    token = next(late)[0]
    ends = [dq1, dq2], [dkv1, dkv2], qkv_weight, attn_gain
    dx = finish((0, 1), after(x, token), dx2, *ends, [])
    early_out = early.send(dx)
    dx = finish((1, seq // R), x, after(dx2, early_out[0]), *ends, [dx])
    late.send(dx)
    late_out = late.send(early_out[1])
    while len(late_out) == 2:
        late_out = late.send(None)
    while len(early_out) == 2:
        early_out = early.send(None)
    up_cols = down_keep.shape[0] // count
    down_grad, up_grad, out_grad = feed_end(*early_out[:2], up_cols, tall)
    places = [i * width + (a + c) * pairs * PW for a, i, c in runs]
    qkv_grad, gain1_grad, gain2_grad, rms = qkv_end(places, attn_gain, *late_out, tall, 3 * width, rides)
    return (
        outputs[None, None],
        dx[None, None],
        qkv_grad,
        out_grad,
        up_grad,
        down_grad,
        gain1_grad,
        gain2_grad,
        rms,
    )


def solution(mesh):
    rows = P("stream", "batch", None, None)
    both = ("stream", "batch")
    return jax.shard_map(
        on_device,
        mesh=mesh,
        in_specs=(rows, P("batch"), rows, P(), P(), P(), P(), P(), P()),
        out_specs=(rows, rows, P(both, None), P(both, None), P(None, both), P(both, None), P(), P(), P()),
        check_vma=False,
    )
```
